32 devices in a mesh: dp: 4 (over z), gx: 4 (over y, core), gy: 2 (over x).
Axes of the slice: x: 2, y: 2, z: 4, core: 2. Of those that a mesh axis runs over, the one named last changes fastest.
Arguments:
- inputs: bfloat16 [8, 1024, 2048], P('dp', 'gx', 'gy'), may hold values from -6 to 6
- segments: int32 [8, 1024], P('dp'), may hold values from 0 to 3, never falling along the last dimension, each value on 1 to 512 neighbouring positions
- norm_gain: float32 [2048], replicated, may hold values from 0.5 to 1.5
- w_query: bfloat16 [2048, 2048], P('gy', 'gx'), may hold values from -0.125 to 0.125
- w_key: bfloat16 [2048, 2048], P('gy', 'gx'), may hold values from -0.125 to 0.125
- w_value: bfloat16 [2048, 2048], P('gy', 'gx'), may hold values from -0.125 to 0.125
- w_beta: bfloat16 [2048, 16], P('gy', 'gx'), may hold values from -0.125 to 0.125
- w_gate_head: bfloat16 [2048, 2048], P('gy', 'gx'), may hold values from -0.125 to 0.125
- conv_kernel: float32 [3, 4, 2048], replicated, may hold values from -1 to 1
- head_gain: float32 [128], replicated, may hold values from 0.5 to 1.5
- w_out: bfloat16 [2048, 2048], P('gx', 'gy'), may hold values from -0.25 to 0.25
- mlp_gain: float32 [2048], replicated, may hold values from 0.5 to 1.5
- w_gate: bfloat16 [2048, 5632], P('gy', 'gx'), may hold values from -0.125 to 0.125
- w_up: bfloat16 [2048, 5632], P('gy', 'gx'), may hold values from -0.125 to 0.125
- w_down: bfloat16 [5632, 2048], P('gx', 'gy'), may hold values from -0.15625 to 0.15625
- grad_y: bfloat16 [8, 1024, 2048], P('dp', 'gx', 'gy'), may hold values from -6 to 6
Outputs:
- layer_out: bfloat16 [8, 1024, 2048], P('dp', 'gx', 'gy')
- grad_inputs: bfloat16 [8, 1024, 2048], P('dp', 'gx', 'gy')
- grad_norm_gain: float32 [2048], replicated
- grad_query: float32 [2048, 2048], P(('gy', 'dp'), 'gx')
- grad_key: float32 [2048, 2048], P(('gy', 'dp'), 'gx')
- grad_value: float32 [2048, 2048], P(('gy', 'dp'), 'gx')
- grad_beta: float32 [2048, 16], P(('gy', 'dp'), 'gx')
- grad_gate_head: float32 [2048, 2048], P(('gy', 'dp'), 'gx')
- grad_conv: float32 [3, 4, 2048], replicated
- grad_head_gain: float32 [128], replicated
- grad_out: float32 [2048, 2048], P(('gx', 'dp'), 'gy')
- grad_mlp_gain: float32 [2048], replicated
- grad_gate: float32 [2048, 5632], P(('gy', 'dp'), 'gx')
- grad_up: float32 [2048, 5632], P(('gy', 'dp'), 'gx')
- grad_down: float32 [5632, 2048], P(('gx', 'dp'), 'gy')
The draws below stay inside these ranges and needn't reach their ends.
Inputs may be any that keep to these rules, and one draw needn't show every extreme that they name: `segments`: within each sequence the document number starts at 0 and never falls; a document has 1 to 512 tokens, and one of them exactly that many.
All inputs are finite; a program needn't handle non-finite values.
Results may differ from the reference program's by a relative error of at most 0.024.
Values may be sent and summed in bfloat16 or wider, within the bound.
A program may use at most 256 MiB of HBM per device.

```python
import math
import jax
import jax.numpy as jnp
import numpy as np
from jax import lax

D = 2048
HEADS = 16
HEAD_DIM = 128
FF = 5632
CONV = 4
BLOCK = 64
SEQ_LEN = 1024
HD = 2048
SEQUENCES = 8


def block_scale(own_key, extent, cuts, low, top_value):
    loudness, own = 1.0, jax.random.fold_in(own_key, 6)
    for position, parts in cuts:
        steps = jnp.exp(jax.random.uniform(jax.random.fold_in(own, position), (parts,), jnp.float32, low / len(cuts), top_value / len(cuts)))
        loudness = loudness * jnp.repeat(steps, extent[position] // parts).reshape([-1 if axis == position else 1 for axis in range(len(extent))])
    return loudness


def split_up(count, total, bound, slope):
    portions = [(1 << 20) // math.isqrt(rank ** slope) + 1 for rank in range(2, count + 1)]
    spare, given = total - bound - (count - 1), [1] * (count - 1)
    while spare > 0:
        candidates = [i for i in range(count - 1) if given[i] < bound]
        whole, remaining = sum([portions[i] for i in candidates]), spare
        for i in candidates:
            more = min(bound - given[i], max(1, remaining * portions[i] // whole), spare)
            given[i] = given[i] + more
            spare = spare - more
    return np.array([bound] + given)


def uneven_parts(stream_key, number_of, total, limit, lean):
    if number_of == 2:
        one = jax.random.randint(stream_key, (), max(1, total - limit), min(limit, total - 1) + 1)
        return jnp.stack([one, total - one])
    tallies = jnp.asarray(split_up(number_of, total, limit, lean), jnp.int32)
    twos = (number_of - 1) // 2
    donor, taker = tallies[1:1 + 2 * twos:2], tallies[2:2 + 2 * twos:2]
    room = jnp.minimum(donor - 1, limit - taker)
    shifted = jax.random.randint(jax.random.fold_in(stream_key, 1), (twos,), 0, 1 << 20) % (room + 1)
    tallies = tallies.at[1:1 + 2 * twos:2].set(donor - shifted).at[2:2 + 2 * twos:2].set(taker + shifted)
    return tallies[jax.random.permutation(jax.random.fold_in(stream_key, 2), number_of)]


def gaussian(stream_key, extent, deviation, most, shards=(), held_as=jnp.bfloat16):
    level = block_scale(stream_key, extent, shards, -0.22, 0.18) if shards else 1.0
    values = jax.random.normal(stream_key, extent, jnp.float32) * deviation * level
    return jnp.minimum(jnp.maximum(values, -most), most).astype(held_as)


def setup_inputs(seed: int = 0) -> dict:
    arg_keys = jax.random.split(jax.random.key(seed), 17)
    return {
        "inputs": gaussian(arg_keys[0], (SEQUENCES, SEQ_LEN, D), 1.0, 6.0, ((0, 4), (1, 4), (2, 2))),
        "segments": jax.vmap(lambda own: jnp.searchsorted(jnp.cumsum(uneven_parts(own, max(3, SEQ_LEN // 256), SEQ_LEN, SEQ_LEN // 2, 0)), jnp.arange(SEQ_LEN), side="right"))(jax.random.split(arg_keys[1], SEQUENCES)).reshape((SEQUENCES, SEQ_LEN)).astype(jnp.int32),
        "norm_gain": jnp.clip(1.0 + 0.1 * jax.random.normal(arg_keys[2], (D,), jnp.float32), 0.5, 1.5),
        "w_query": gaussian(arg_keys[3], (D, HD), D ** -0.5, 0.125, ((0, 2), (1, 4))),
        "w_key": gaussian(arg_keys[4], (D, HD), D ** -0.5, 0.125, ((0, 2), (1, 4))),
        "w_value": gaussian(arg_keys[5], (D, HD), D ** -0.5, 0.125, ((0, 2), (1, 4))),
        "w_beta": gaussian(arg_keys[6], (D, HEADS), D ** -0.5, 0.125, ((0, 2), (1, 4))),
        "w_gate_head": gaussian(arg_keys[7], (D, HD), D ** -0.5, 0.125, ((0, 2), (1, 4))),
        "conv_kernel": jnp.clip(jax.random.uniform(arg_keys[8], (3, CONV, HD), jnp.float32, -1.0, 1.0), -1.0, 1.0),
        "head_gain": jnp.clip(1.0 + 0.1 * jax.random.normal(arg_keys[9], (HEAD_DIM,), jnp.float32), 0.5, 1.5),
        "w_out": gaussian(arg_keys[10], (HD, D), (HD // 4) ** -0.5, 0.25, ((0, 4), (1, 2))),
        "mlp_gain": jnp.clip(1.0 + 0.1 * jax.random.normal(arg_keys[11], (D,), jnp.float32), 0.5, 1.5),
        "w_gate": gaussian(arg_keys[12], (D, FF), D ** -0.5, 0.125, ((0, 2), (1, 4))),
        "w_up": gaussian(arg_keys[13], (D, FF), D ** -0.5, 0.125, ((0, 2), (1, 4))),
        "w_down": gaussian(arg_keys[14], (FF, D), (FF // 4) ** -0.5, 0.15625, ((0, 4), (1, 2))),
        "grad_y": gaussian(arg_keys[15], (SEQUENCES, SEQ_LEN, D), 1.0, 6.0, ((0, 4), (1, 4), (2, 2))),
    }


EPS = 1e-06
HEAD_EPS = 0.01
HIGH_ACCURACY = lax.Precision.HIGHEST

@jax.custom_vjp
def low(v):
    return lax.optimization_barrier(v.astype(jnp.bfloat16)).astype(jnp.float32)

@jax.custom_vjp
def low_back(v):
    return v

def low_keep(v):
    return (low(v), None)

def low_pass(kept, grad):
    return (grad,)

def back_keep(v):
    return (v, None)

def back_low(kept, grad):
    return (low(grad),)
low.defvjp(low_keep, low_pass)
low_back.defvjp(back_keep, back_low)

def causal_mix(raw_rows, kernel, segment):
    length = raw_rows.shape[0]
    mixed_sum = jnp.zeros(raw_rows.shape, jnp.float32)
    for offset in range(kernel.shape[0]):
        moved_rows = jnp.pad(raw_rows, ((offset, 0), (0, 0)))[:length]
        moved_seg = jnp.pad(segment, (offset, 0), constant_values=-1)[:length]
        keep_mask = (moved_seg == segment).astype(jnp.float32)[:, None]
        mixed_sum = mixed_sum + kernel[offset][None, :] * moved_rows * keep_mask
    return mixed_sum

def unit_norm(value_in):
    return value_in * lax.rsqrt(lax.optimization_barrier(jnp.sum(value_in * value_in, axis=-1, keepdims=True)) + EPS)

def block_step(carry_in, block_data):
    state_now, last_doc = carry_in
    query_rows, key_rows, value_rows, beta_rows, segment = block_data
    block_size = segment.shape[0]
    same_doc = (segment[:, None] == segment[None, :]).astype(jnp.float32)
    strict = jnp.tril(jnp.ones((block_size, block_size), jnp.float32), -1)
    inclusive = jnp.tril(jnp.ones((block_size, block_size), jnp.float32))
    key_inner = jnp.einsum('hid,hjd->hij', key_rows, key_rows, precision=HIGH_ACCURACY)
    system = beta_rows[:, :, None] * key_inner * (same_doc * strict)[None] + jnp.eye(block_size, dtype=jnp.float32)[None]
    stacked = beta_rows[:, :, None] * jnp.concatenate([key_rows, value_rows], axis=-1)
    solved = lax.linalg.triangular_solve(system, stacked, left_side=True, lower=True, unit_diagonal=True)
    dim_key = key_rows.shape[-1]
    weight_rows = solved[..., :dim_key]
    update_rows = solved[..., dim_key:]
    carried = (segment == last_doc).astype(jnp.float32)
    fresh_rows = update_rows - carried[None, :, None] * jnp.einsum('hid,hed->hie', weight_rows, state_now, precision=HIGH_ACCURACY)
    scores = jnp.einsum('hid,hjd->hij', query_rows, key_rows, precision=HIGH_ACCURACY) * (same_doc * inclusive)[None]
    output = carried[None, :, None] * jnp.einsum('hid,hed->hie', query_rows, state_now, precision=HIGH_ACCURACY)
    output = output + jnp.einsum('hij,hje->hie', scores, fresh_rows, precision=HIGH_ACCURACY)
    tail_doc = (segment == segment[-1]).astype(jnp.float32)
    new_state = carried[-1] * state_now + jnp.einsum('hje,hjd->hed', fresh_rows * tail_doc[None, :, None], key_rows, precision=HIGH_ACCURACY)
    return ((new_state, segment[-1]), output)

def delta_rule(query_rows, key_rows, value_rows, beta_rows, segment):
    length, head_count, dim_key = query_rows.shape
    steps_count = length // BLOCK

    def blocked(array_in):
        return array_in.reshape(steps_count, BLOCK, head_count, -1).transpose(0, 2, 1, 3)
    start_carry = (jnp.zeros((head_count, dim_key, dim_key), jnp.float32), jnp.array(-1, jnp.int32))
    block_inputs = (blocked(query_rows), blocked(key_rows), blocked(value_rows), beta_rows.reshape(steps_count, BLOCK, head_count).transpose(0, 2, 1), segment.reshape(steps_count, BLOCK))
    final_carry, outputs = lax.scan(jax.checkpoint(block_step), start_carry, block_inputs)
    return outputs.transpose(0, 2, 1, 3).reshape(length, head_count, dim_key)

def mixer(query_raw, key_raw, value_raw, gate_raw, beta_raw, conv_kernel, head_gain, segment):
    length = query_raw.shape[0]
    head_count = beta_raw.shape[-1]
    dim_key = query_raw.shape[-1] // head_count

    def heads_of(value_in):
        return value_in.reshape(length, head_count, dim_key)
    query_rows = unit_norm(heads_of(jax.nn.silu(causal_mix(query_raw, conv_kernel[0], segment))))
    key_rows = unit_norm(heads_of(jax.nn.silu(causal_mix(key_raw, conv_kernel[1], segment))))
    value_rows = heads_of(jax.nn.silu(causal_mix(value_raw, conv_kernel[2], segment)))
    beta_rows = jax.nn.sigmoid(beta_raw)
    delta_out = delta_rule(query_rows, key_rows, value_rows, beta_rows, segment)
    normed = delta_out * lax.rsqrt(lax.optimization_barrier(jnp.mean(delta_out * delta_out, axis=-1, keepdims=True)) + HEAD_EPS) * head_gain
    return (normed * heads_of(jax.nn.silu(gate_raw))).reshape(length, head_count * dim_key)

def rms_norm(value_in, gain):
    return value_in * lax.rsqrt(lax.optimization_barrier(jnp.mean(value_in * value_in, axis=-1, keepdims=True)) + EPS) * gain

def project(row_total, weight_matrix):
    return jnp.einsum('pnj,ju->pnu', row_total, weight_matrix, precision=HIGH_ACCURACY)

def forward(params, inputs, segments):
    norm_gain, w_query, w_key, w_value, w_beta, w_gate_head, conv_kernel, head_gain, w_out, mlp_gain, w_gate, w_up, w_down = params
    normed = low(rms_norm(inputs, norm_gain))
    query_raw = low_back(project(normed, w_query))
    key_raw = low_back(project(normed, w_key))
    value_raw = low_back(project(normed, w_value))
    beta_raw = low_back(project(normed, w_beta))
    gate_raw = low_back(project(normed, w_gate_head))
    mixed = jax.vmap(mixer, in_axes=(0, 0, 0, 0, 0, None, None, 0))(query_raw, key_raw, value_raw, gate_raw, beta_raw, conv_kernel, head_gain, segments)
    mixed = low(mixed)
    branch = low_back(project(mixed, w_out))
    middle = inputs + branch
    second = low(rms_norm(middle, mlp_gain))
    gate_val = low_back(project(second, w_gate))
    up_val = low_back(project(second, w_up))
    hidden_state = low(jax.nn.silu(gate_val) * up_val)
    return middle + project(hidden_state, w_down)

def reference(inputs, segments, norm_gain, w_query, w_key, w_value, w_beta, w_gate_head, conv_kernel, head_gain, w_out, mlp_gain, w_gate, w_up, w_down, grad_y):
    params = tuple((array_in.astype(jnp.float32) for array_in in (norm_gain, w_query, w_key, w_value, w_beta, w_gate_head, conv_kernel, head_gain, w_out, mlp_gain, w_gate, w_up, w_down)))
    group_size = math.gcd(SEQUENCES, max(1, 4096 // SEQ_LEN))
    group_count = SEQUENCES // group_size

    def shaped(array_in):
        return array_in.reshape((group_count, group_size) + array_in.shape[1:])

    def one_group(totals, block_data):
        in_block, seg_block, cot_block = block_data
        result, pull_back = jax.vjp(lambda prm, val: forward(prm, val, seg_block), params, in_block)
        grad_params, grad_in = pull_back(cot_block)
        return (jax.tree.map(jnp.add, totals, grad_params), (result, grad_in))
    totals, (result, grad_in) = lax.scan(one_group, jax.tree.map(jnp.zeros_like, params), (shaped(inputs.astype(jnp.float32)), shaped(segments), shaped(grad_y.astype(jnp.float32))))
    layer_out = result.reshape(inputs.shape).astype(jnp.bfloat16)
    grad_inputs = grad_in.reshape(inputs.shape).astype(jnp.bfloat16)
    return (layer_out, grad_inputs, totals[0], totals[1], totals[2], totals[3], totals[4], totals[5], totals[6], totals[7], totals[8], totals[9], totals[10], totals[11], totals[12])
```

```python
import jax, jax.numpy as jnp
from jax import lax
from jax.experimental import pallas as pl
from jax.experimental.pallas import tpu as pltpu
import functools
from jax.sharding import PartitionSpec as P
EPS = 1e-6
HEAD_EPS = 0.01
C = 128
bf = jnp.bfloat16
f32 = jnp.float32
GROUP = 8

def nn(a, b):
    return lax.dot_general(a.astype(bf), b.astype(bf), (((1,), (0,)), ((), ())), preferred_element_type=f32)
def nt(a, b):
    return lax.dot_general(a.astype(bf), b.astype(bf), (((1,), (1,)), ((), ())), preferred_element_type=f32)
def tn(a, b):
    return lax.dot_general(a.astype(bf), b.astype(bf), (((0,), (0,)), ((), ())), preferred_element_type=f32)

def level_masks(n):
    row = lax.broadcasted_iota(jnp.int32, (n, n), 0)
    col = lax.broadcasted_iota(jnp.int32, (n, n), 1)
    out = []
    size = 1
    while size < n:
        out.append(((row ^ col) & (-size) == size).astype(f32).astype(bf))
        size *= 2
    return (row == col).astype(f32).astype(bf), out

def inverse_many(many, eye, levels):
    totals = [eye - a * levels[0] for a in many]
    for mask in levels[1:]:
        inner = [nn(a * mask, t).astype(bf) for a, t in zip(many, totals)]
        outer = [nn(t, x).astype(bf) for t, x in zip(totals, inner)]
        totals = [t - x for t, x in zip(totals, outer)]
    return totals

def act_stage(x, prev, aux, w, norm):
    row8 = lax.broadcasted_iota(jnp.int32, (8, 128), 0)
    conv = x * w[0:1]
    sh = []
    for i in range(1, w.shape[0]):
        r = pltpu.roll(x, i, 0)
        p = pltpu.roll(prev, i, 0)
        head = jnp.where(row8 < i, p, r[:8])
        m = jnp.concatenate([head, r[8:]], axis=0) * aux[:, 2 + i:3 + i]
        sh.append(m)
        conv = conv + m * w[i:i + 1]
    s = jax.nn.sigmoid(conv)
    act = conv * s
    if norm:
        rate = lax.rsqrt(jnp.sum(act * act, axis=-1, keepdims=True) + EPS)
        return conv, s, act * rate, rate, sh
    return conv, s, act, None, sh

def masks(aux, segrow):
    n = aux.shape[0]
    row = lax.broadcasted_iota(jnp.int32, (n, n), 0)
    col = lax.broadcasted_iota(jnp.int32, (n, n), 1)
    same = aux[:, 0:1] == segrow
    return same & (row > col), same & (row >= col)

def beta_column(block, h):
    lane = lax.broadcasted_iota(jnp.int32, block.shape, 1)
    return jnp.sum(jnp.where(lane == h, jax.nn.sigmoid(block), 0.0), axis=1, keepdims=True)

def prev_rows(ref, lo):
    start = pl.multiple_of(jnp.maximum(lo - 8, 0), 8)
    return jnp.where(lo > 0, ref[0, pl.ds(start, 8), :].astype(f32), 0.0)

def fwd_kernel(q_ref, k_ref, v_ref, g_ref, b_ref, aux_ref, seg_ref, w_ref, gain_ref,
               mixed_ref, t_ref, w_out, p_ref, f_ref, s_ref, fresh_ref, o_ref,
               q_s, u_s, b_s):
    h = pl.program_id(1)
    length = q_ref.shape[1]
    steps = length // C
    eye, levels = level_masks(C)
    def stage_a(group, _):
        lows = [pl.multiple_of((group * GROUP + n) * C, C) for n in range(GROUP)]
        spans = [pl.ds(lo, C) for lo in lows]
        many, keys, right = [], [], []
        for lo, rows in zip(lows, spans):
            aux = aux_ref[0, rows, :]
            q = act_stage(q_ref[0, rows, :].astype(f32), prev_rows(q_ref, lo), aux, w_ref[0], True)[2]
            k = act_stage(k_ref[0, rows, :].astype(f32), prev_rows(k_ref, lo), aux, w_ref[1], True)[2]
            v = act_stage(v_ref[0, rows, :].astype(f32), prev_rows(v_ref, lo), aux, w_ref[2], False)[2]
            beta = beta_column(b_ref[0, rows, :].astype(f32), h)
            strict, inclusive = masks(aux, seg_ref[0, 0:1, rows])
            kb = k.astype(bf)
            qb = q.astype(bf)
            both = nt(jnp.concatenate([kb, qb], axis=0), kb)
            many.append(jnp.where(strict, beta * both[:C], 0.0).astype(bf))
            p_ref[0, 0, rows, :] = jnp.where(inclusive, both[C:], 0.0).astype(bf)
            q_s[rows, :] = qb
            keys.append((k * aux[:, 2:3]).astype(bf))
            right.append(jnp.concatenate([(beta * k).astype(bf), (beta * v).astype(bf)], axis=1))
        totals = inverse_many(many, eye, levels)
        wus = [nn(t, r) for t, r in zip(totals, right)]
        kwus = [tn(k, wu) for k, wu in zip(keys, wus)]
        for rows, t, wu, kwu in zip(spans, totals, wus, kwus):
            clast = aux_ref[0, rows, :][C - 1:C, 1:2]
            f_ref[0, 0, rows, :] = (clast * (eye.astype(f32) - kwu[:, :C])).astype(bf)
            b_s[rows, :] = kwu[:, C:]
            t_ref[0, 0, rows, :] = t
            w_out[0, 0, rows, :] = wu[:, :C].astype(bf)
            u_s[rows, :] = wu[:, C:]
        return 0
    lax.fori_loop(0, steps // GROUP, stage_a, 0)
    def scan(c, state):
        rows = pl.ds(pl.multiple_of(c * C, C), C)
        sb = state.astype(bf)
        s_ref[0, 0, rows, :] = sb
        return nn(f_ref[0, 0, rows, :], sb) + b_s[rows, :]
    lax.fori_loop(0, steps, scan, jnp.zeros((C, C), f32), unroll=True)
    def stage_c(c, _):
        rows = pl.ds(pl.multiple_of(c * C, C), C)
        aux = aux_ref[0, rows, :]
        carried = aux[:, 1:2]
        ws = nn(jnp.concatenate([w_out[0, 0, rows, :], q_s[rows, :]], axis=0), s_ref[0, 0, rows, :])
        fresh = (u_s[rows, :] - carried * ws[:C]).astype(bf)
        out = carried * ws[C:] + nn(p_ref[0, 0, rows, :], fresh)
        fresh_ref[0, 0, rows, :] = fresh
        o_ref[0, 0, rows, :] = out
        g = g_ref[0, rows, :].astype(f32)
        r = lax.rsqrt(jnp.mean(out * out, axis=-1, keepdims=True) + HEAD_EPS)
        mixed_ref[0, rows, :] = (out * r * gain_ref[0:1] * (g * jax.nn.sigmoid(g))).astype(bf)
        return 0
    lax.fori_loop(0, steps, stage_c, 0, unroll=4)

def specs(length, heads, off):
    return [pl.BlockSpec((1, length, 128), functools.partial(lambda t, b, h: (b, 0, t * heads + h), t)) for t in range(4)] + [
        pl.BlockSpec((1, length, 128), lambda b, h: (b, 0, 4 * heads))]

def mixer_fwd(raw, aux, segrow, conv, gain):
    nb, length, width = raw.shape
    heads = (width - 128) // 512
    per = pl.BlockSpec((1, 1, length, 128), lambda b, h: (b, h, 0, 0))
    sh = lambda d: jax.ShapeDtypeStruct((nb, heads, length, 128), d)
    return pl.pallas_call(
        fwd_kernel,
        grid=(nb, heads),
        in_specs=specs(length, heads, 0) + [
            pl.BlockSpec((1, length, aux.shape[2]), lambda b, h: (b, 0, 0)),
            pl.BlockSpec((1, 1, length), lambda b, h: (b, 0, 0)),
            pl.BlockSpec((3, conv.shape[1], 128), lambda b, h: (0, 0, h)),
            pl.BlockSpec((1, 128), lambda b, h: (0, 0)),
        ],
        out_specs=[pl.BlockSpec((1, length, 128), lambda b, h: (b, 0, h))] + [per] * 7,
        out_shape=[jax.ShapeDtypeStruct((nb, length, heads * 128), bf)] + [sh(bf)] * 6 + [sh(f32)],
        scratch_shapes=[pltpu.VMEM((length, 128), bf), pltpu.VMEM((length, 128), f32), pltpu.VMEM((length, 128), f32)],
        name="mixer_forward",
    )(raw, raw, raw, raw, raw, aux, segrow, conv, gain)

def bwd_kernel(q_ref, k_ref, v_ref, g_ref, b_ref, aux_ref, seg_ref, w_ref, gain_ref,
               t_ref, w_in, p_ref, f_ref, s_ref, fresh_ref, o_ref, dm_ref,
               draw_ref, dconv_ref, dgain_ref,
               do_s, pd_s, base_s, ds_s):
    h = pl.program_id(1)
    heads = pl.num_programs(1)
    length = q_ref.shape[1]
    steps = length // C
    gain = gain_ref[0:1]
    def stage_a(c, dgain):
        lo = pl.multiple_of(c * C, C)
        rows = pl.ds(lo, C)
        aux = aux_ref[0, rows, :]
        carried = aux[:, 1:2]
        q = act_stage(q_ref[0, rows, :].astype(f32), prev_rows(q_ref, lo), aux, w_ref[0], True)[2]
        out = o_ref[0, 0, rows, :]
        g = g_ref[0, rows, :].astype(f32)
        dm = dm_ref[0, rows, :].astype(f32)
        s = jax.nn.sigmoid(g)
        r = lax.rsqrt(jnp.mean(out * out, axis=-1, keepdims=True) + HEAD_EPS)
        scaled = out * r
        dn = dm * (g * s)
        dg = dm * scaled * gain * (s * (1.0 + g * (1.0 - s)))
        draw_ref[0, rows, pl.ds(pl.multiple_of((3 * heads + h) * 128, 128), 128)] = dg.astype(bf)
        e = dn * gain
        do = r * (e - scaled * jnp.mean(e * scaled, axis=-1, keepdims=True))
        pd = tn(p_ref[0, 0, rows, :], do)
        do_s[rows, :] = do
        pd_s[rows, :] = pd
        base_s[rows, :] = tn(jnp.concatenate([q.astype(bf), w_in[0, 0, rows, :]], axis=0),
                             jnp.concatenate([carried * do, -carried * pd], axis=0))
        return dgain + jnp.sum((dn * scaled).reshape(C // 8, 8, 128), axis=0)
    dgain = lax.fori_loop(0, steps, stage_a, jnp.zeros((8, 128), f32), unroll=2)
    dgain_ref[0, 0] = dgain
    def scan(j, state):
        c = steps - 1 - j
        rows = pl.ds(pl.multiple_of(c * C, C), C)
        sb = state.astype(bf)
        ds_s[rows, :] = sb
        return tn(f_ref[0, 0, rows, :], sb) + base_s[rows, :]
    lax.fori_loop(0, steps, scan, jnp.zeros((C, C), f32), unroll=True)
    row8 = lax.broadcasted_iota(jnp.int32, (8, 128), 0)
    lane = lax.broadcasted_iota(jnp.int32, (C, 128), 1)

    def conv_back(dconv, nxt, aux, w, raw, sh):
        d = dconv * w[0:1]
        dw = [jnp.sum((dconv * raw).reshape(C // 8, 8, 128), axis=0)]
        for i in range(1, w.shape[0]):
            r = pltpu.roll(dconv, C - i, 0)
            p = pltpu.roll(nxt, 8 - i, 0)
            tailrows = jnp.where(row8 >= 8 - i, p, r[C - 8:])
            m = jnp.concatenate([r[:C - 8], tailrows], axis=0) * aux[:, 5 + i:6 + i]
            d = d + m * w[i:i + 1]
            dw.append(jnp.sum((dconv * sh[i - 1]).reshape(C // 8, 8, 128), axis=0))
        return d, dw

    def stage_c(j, carry):
        nq, nk, nv, dws = carry
        c = steps - 1 - j
        lo = pl.multiple_of(c * C, C)
        rows = pl.ds(lo, C)
        aux = aux_ref[0, rows, :]
        carried = aux[:, 1:2]
        tail = aux[:, 2:3]
        xq = q_ref[0, rows, :].astype(f32)
        xk = k_ref[0, rows, :].astype(f32)
        xv = v_ref[0, rows, :].astype(f32)
        cq, sq, q, rq, shq = act_stage(xq, prev_rows(q_ref, lo), aux, w_ref[0], True)
        ck, sk, k, rk, shk = act_stage(xk, prev_rows(k_ref, lo), aux, w_ref[1], True)
        cv, sv, v, _, shv = act_stage(xv, prev_rows(v_ref, lo), aux, w_ref[2], False)
        bblock = b_ref[0, rows, :].astype(f32)
        beta = beta_column(bblock, h)
        strict, inclusive = masks(aux, seg_ref[0, 0:1, rows])
        kb = k.astype(bf)
        qb = q.astype(bf)
        st = s_ref[0, 0, rows, :]
        dst = ds_s[rows, :]
        fresh = fresh_ref[0, 0, rows, :]
        do = do_s[rows, :]
        gram = nt(kb, kb)
        kk = nn(kb, jnp.concatenate([dst, st], axis=1))
        dfresh = pd_s[rows, :] + tail * kk[:, :128]
        x = v - carried * kk[:, 128:]
        y = tn(t_ref[0, 0, rows, :], dfresh)
        dx = beta * y
        cdx = (carried * dx).astype(bf)
        yb = y.astype(bf)
        dob = do.astype(bf)
        both = nt(jnp.concatenate([dob, yb], axis=0), fresh)
        dp = jnp.where(inclusive, both[:C], 0.0)
        da = jnp.where(strict, -both[C:], 0.0)
        dbeta = jnp.sum(y * x, axis=-1, keepdims=True) + jnp.sum(da * gram, axis=-1, keepdims=True)
        dg = beta * da
        dgs = dg + dg.T
        through = nt(jnp.concatenate([carried * do, -(carried * dx)], axis=0), st)
        dpb = dp.astype(bf)
        dq = through[:C] + nn(dpb, kb)
        dk = through[C:] + tn(dpb, qb) + nt(tail * fresh.astype(f32), dst) + nn(dgs, kb)
        dv = dx
        db = dbeta * beta * (1.0 - beta)
        bl = pl.ds(4 * heads * 128, 128)
        @pl.when(h == 0)
        def _():
            draw_ref[0, rows, bl] = jnp.where(lane == 0, db, 0.0).astype(bf)
        @pl.when(h > 0)
        def _():
            old = draw_ref[0, rows, bl]
            draw_ref[0, rows, bl] = jnp.where(lane == h, db.astype(bf).astype(f32), old.astype(f32)).astype(bf)
        dq = rq * (dq - q * jnp.sum(q * dq, axis=-1, keepdims=True))
        dk = rk * (dk - k * jnp.sum(k * dk, axis=-1, keepdims=True))
        dcq = dq * (sq * (1.0 + cq * (1.0 - sq)))
        dck = dk * (sk * (1.0 + ck * (1.0 - sk)))
        dcv = dv * (sv * (1.0 + cv * (1.0 - sv)))
        rq_, wq = conv_back(dcq, nq, aux, w_ref[0], xq, shq)
        rk_, wk = conv_back(dck, nk, aux, w_ref[1], xk, shk)
        rv_, wv = conv_back(dcv, nv, aux, w_ref[2], xv, shv)
        for t, val in ((0, rq_), (1, rk_), (2, rv_)):
            draw_ref[0, rows, pl.ds(pl.multiple_of((t * heads + h) * 128, 128), 128)] = val.astype(bf)
        dws = tuple(a + b for a, b in zip(dws, wq + wk + wv))
        return dcq[:8], dck[:8], dcv[:8], dws
    z8 = jnp.zeros((8, 128), f32)
    taps = w_ref.shape[1]
    _, _, _, dws = lax.fori_loop(0, steps, stage_c, (z8, z8, z8, (z8,) * (3 * taps)), unroll=2)
    for n, d in enumerate(dws):
        dconv_ref[0, 0, n] = d

def mixer_bwd(raw, aux, segrow, conv, gain, saved, dmixed):
    nb, length, width = raw.shape
    heads = (width - 128) // 512
    taps = conv.shape[1]
    per = pl.BlockSpec((1, 1, length, 128), lambda b, h: (b, h, 0, 0))
    sh = lambda d: jax.ShapeDtypeStruct((nb, heads, length, 128), d)
    draw, dconv, dgain = pl.pallas_call(
        bwd_kernel,
        grid=(nb, heads),
        in_specs=specs(length, heads, 0) + [
            pl.BlockSpec((1, length, aux.shape[2]), lambda b, h: (b, 0, 0)),
            pl.BlockSpec((1, 1, length), lambda b, h: (b, 0, 0)),
            pl.BlockSpec((3, taps, 128), lambda b, h: (0, 0, h)),
            pl.BlockSpec((1, 128), lambda b, h: (0, 0)),
        ] + [per] * 7 + [pl.BlockSpec((1, length, 128), lambda b, h: (b, 0, h))],
        out_specs=[pl.BlockSpec((1, length, width), lambda b, h: (b, 0, 0)),
                   pl.BlockSpec((1, 1, 3 * taps, 8, 128), lambda b, h: (b, h, 0, 0, 0)),
                   pl.BlockSpec((1, 1, 8, 128), lambda b, h: (b, h, 0, 0))],
        out_shape=[jax.ShapeDtypeStruct((nb, length, width), bf),
                   jax.ShapeDtypeStruct((nb, heads, 3 * taps, 8, 128), f32),
                   jax.ShapeDtypeStruct((nb, heads, 8, 128), f32)],
        scratch_shapes=[pltpu.VMEM((length, 128), f32)] * 3 + [pltpu.VMEM((length, 128), bf)],
        name="mixer_backward",
    )(raw, raw, raw, raw, raw, aux, segrow, conv, gain, *saved, dmixed)
    dconv = jnp.sum(dconv, axis=(0, 3)).reshape(heads, 3, taps, 128).transpose(1, 2, 0, 3).reshape(3, taps, heads * 128)
    return draw, dconv, jnp.sum(dgain, axis=(0, 1, 2))

def make_aux(segments):
    nb, length = segments.shape
    seg = segments.astype(f32)
    blocks = seg.reshape(nb, length // C, C)
    last = blocks[:, :, -1:]
    before = jnp.concatenate([jnp.full((nb, 1, 1), -1.0, f32), last[:, :-1]], axis=1)
    carried = (blocks == before).astype(f32).reshape(nb, length)
    tail = (blocks == last).astype(f32).reshape(nb, length)
    cols = [seg, carried, tail]
    for i in range(1, 4):
        cols.append((jnp.pad(seg, ((0, 0), (i, 0)), constant_values=-1.0)[:, :length] == seg).astype(f32))
    for i in range(1, 4):
        cols.append((jnp.pad(seg, ((0, 0), (0, i)), constant_values=-1.0)[:, i:] == seg).astype(f32))
    cols += [jnp.zeros_like(seg)] * (16 - len(cols))
    return jnp.stack(cols, axis=-1), seg[:, None, :]


TOKENS = ("gy", "gx")
EVERY = ("dp", "gx", "gy")


def dot(a, b):
    return lax.dot_general(a, b, (((1,), (0,)), ((), ())), preferred_element_type=f32)


def dot_t(a, b):
    return lax.dot_general(a, b, (((1,), (1,)), ((), ())), preferred_element_type=f32)


def dot_w(a, b):
    return lax.dot_general(a, b, (((0,), (0,)), ((), ())), preferred_element_type=f32)


def swap(value):
    return lax.ppermute(value, "gy", [(0, 1), (1, 0)])


def in_order(mine, other, axis):
    first = lax.axis_index("gy") == 0
    return jnp.concatenate([jnp.where(first, mine, other), jnp.where(first, other, mine)], axis=axis)


def halves(value, axis):
    size = value.shape[axis] // 2
    mine = lax.axis_index("gy")
    return (
        lax.dynamic_slice_in_dim(value, mine * size, size, axis),
        lax.dynamic_slice_in_dim(value, (1 - mine) * size, size, axis),
    )


def gather_blocks(value):
    nb, rows, width = value.shape
    many = lax.all_gather(value, ("gx", "gy"), axis=0, tiled=False)
    ngx, ngy = lax.axis_size("gx"), lax.axis_size("gy")
    many = many.reshape(ngx, ngy, nb, rows, width)
    return many.transpose(2, 0, 3, 1, 4).reshape(nb, ngx * rows, ngy * width)


def gather_rows(value):
    return lax.all_gather(value, TOKENS, axis=0, tiled=True)


def scatter_rows(value):
    return lax.psum_scatter(value.astype(bf), TOKENS, scatter_dimension=0, tiled=True).astype(f32)


def to_final(own):
    mine, other = halves(own, 1)
    return in_order(mine[None], swap(other)[None], 0)


def rate_of(value):
    return lax.rsqrt(jnp.mean(value * value, axis=-1, keepdims=True) + EPS)


def norm_back(value, rate, gain, incoming):
    scaled = gain * incoming
    inner = jnp.mean(value * scaled, axis=-1, keepdims=True)
    return rate * scaled - value * (rate * rate * rate) * inner, jnp.sum(incoming * value * rate, axis=0)


def scatter_dp(value):
    return lax.psum_scatter(value.astype(bf), "dp", scatter_dimension=0, tiled=True)


def columns_grad(grad, ndp):
    rows, cols = grad.shape
    parts = grad.astype(bf).reshape(2, ndp, rows // (2 * ndp), cols).transpose(1, 0, 2, 3)
    summed = lax.psum_scatter(parts.reshape(rows, cols), "dp", scatter_dimension=0, tiled=True)
    mine, other = halves(summed, 0)
    return mine, swap(other)


def shards(
    inputs,
    segments,
    norm_gain,
    w_query,
    w_key,
    w_value,
    w_beta,
    w_gate_head,
    conv_kernel,
    head_gain,
    w_out,
    mlp_gain,
    w_gate,
    w_up,
    w_down,
    grad_y,
):
    ngx, ngy, ndp = lax.axis_size("gx"), lax.axis_size("gy"), lax.axis_size("dp")
    gx, gy = lax.axis_index("gx"), lax.axis_index("gy")
    x_all = gather_blocks(inputs)
    nb, length, feat = x_all.shape
    tokens = nb * length
    own_rows = tokens // (ngx * ngy)
    own_start = (gy * ngx + gx) * own_rows
    heads = w_beta.shape[1] // ngy
    width = w_query.shape[1] // ngy

    cat = [halves(w, 1) for w in (w_query, w_key, w_value, w_gate_head)]
    pad = ((0, 0), (0, 128 - heads))
    beta_mine, beta_other = halves(w_beta, 1)
    head_w = in_order(
        jnp.concatenate([m for m, _ in cat] + [jnp.pad(beta_mine, pad)], axis=1),
        swap(jnp.concatenate([o for _, o in cat] + [jnp.pad(beta_other, pad)], axis=1)),
        0,
    )

    def own_columns(w):
        mine, other = halves(w, 1)
        return in_order(mine, swap(other), 0)

    aux, segrow = make_aux(segments)
    x_flat = x_all.reshape(tokens, feat)
    x_wide = x_flat.astype(f32)
    rate_first = rate_of(x_wide)
    normed = (x_wide * rate_first * norm_gain).astype(bf)
    raw = dot(normed, head_w).reshape(nb, length, -1)
    conv_start = (gx * ngy + gy) * width
    conv_local = lax.dynamic_slice_in_dim(conv_kernel, conv_start, width, 2)
    gain_row = head_gain[None]
    mixed, *saved = mixer_fwd(raw, aux, segrow, conv_local, gain_row)
    mixed = mixed.reshape(tokens, width)

    out_blocks = lax.all_gather(w_out, ("gx", "gy"), axis=0, tiled=False)
    out_full = (
        out_blocks.reshape(ngx, ngy, ngy, width, -1).transpose(2, 0, 3, 1, 4).reshape(ngx * ngy * width, feat)
    )
    y_all = gather_blocks(grad_y).reshape(tokens, feat)
    gate_w = own_columns(w_gate)
    up_w = own_columns(w_up)
    down_mine, down_other = halves(w_down, 0)
    down_w = in_order(down_mine, swap(down_other), 1)

    mixed_own = lax.all_to_all(mixed, TOKENS, 0, 1, tiled=True)
    x_own = lax.dynamic_slice_in_dim(x_flat, own_start, own_rows, 0).astype(f32)
    middle = x_own + dot(mixed_own, out_full)
    rate_second = rate_of(middle)
    second = gather_rows((middle * rate_second * mlp_gain).astype(bf))
    gate_val = dot(second, gate_w)
    up_val = dot(second, up_w)
    grad_hidden = dot_t(y_all, down_w)
    sig = jax.nn.sigmoid(gate_val)
    act = gate_val * sig
    hidden = (act * up_val).astype(bf)
    grad_up_val = (grad_hidden * act).astype(bf)
    grad_gate_val = (grad_hidden * up_val * sig * (1.0 + gate_val * (1.0 - sig))).astype(bf)
    grad_second = scatter_rows(dot_t(grad_gate_val, gate_w) + dot_t(grad_up_val, up_w))
    norm_two, mlp_gain_grad = norm_back(middle, rate_second, mlp_gain, grad_second)
    y_own = lax.dynamic_slice_in_dim(y_all, own_start, own_rows, 0).astype(f32)
    grad_middle = y_own + norm_two
    mid_low = grad_middle.astype(bf)
    grad_mixed = lax.all_to_all(dot_t(mid_low, out_full).astype(bf), TOKENS, 1, 0, tiled=True)
    draw, conv_grad, gain_grad = mixer_bwd(
        raw, aux, segrow, conv_local, gain_row, saved, grad_mixed.reshape(nb, length, width)
    )
    draw = draw.reshape(tokens, -1)
    grad_normed = scatter_rows(dot_t(draw, head_w))
    rate_own = lax.dynamic_slice_in_dim(rate_first, own_start, own_rows, 0)
    norm_one, norm_gain_grad = norm_back(x_own, rate_own, norm_gain, grad_normed)
    grad_inputs = to_final((grad_middle + norm_one).astype(bf))

    layer_out = to_final((middle + scatter_rows(dot(hidden, down_w))).astype(bf))
    mid_all = gather_rows(mid_low)

    down_keep, down_send = halves(dot_w(hidden, y_all).astype(bf), 1)
    sum_down = scatter_dp(in_order(down_keep, swap(down_send), 0)).astype(f32)
    out_keep, out_send = halves(dot_w(mixed, mid_all).astype(bf), 1)
    sum_out = scatter_dp(in_order(out_keep, swap(out_send), 0)).astype(f32)

    def whole_columns(grad):
        mine, other = columns_grad(grad, ndp)
        return in_order(mine, other, 1).astype(f32)

    sum_gate = whole_columns(dot_w(second, grad_gate_val))
    sum_up = whole_columns(dot_w(second, grad_up_val))
    head_mine, head_other = columns_grad(dot_w(normed, draw), ndp)

    def head_part(i, n):
        return in_order(head_mine[:, i : i + n], head_other[:, i : i + n], 1).astype(f32)

    sum_query, sum_key, sum_value, sum_head_gate = (head_part(i * width, width) for i in range(4))
    sum_beta = head_part(4 * width, heads)

    conv_full = lax.dynamic_update_slice_in_dim(jnp.zeros(conv_kernel.shape, f32), conv_grad, conv_start, 2)
    norm_sum, mlp_sum, conv_sum, gain_sum = lax.psum((norm_gain_grad, mlp_gain_grad, conv_full, gain_grad), EVERY)
    return (
        layer_out,
        grad_inputs,
        norm_sum,
        sum_query,
        sum_key,
        sum_value,
        sum_beta,
        sum_head_gate,
        conv_sum,
        gain_sum,
        sum_out,
        mlp_sum,
        sum_gate,
        sum_up,
        sum_down,
    )


def solution(mesh):
    cols = P("gy", "gx")
    rows = P("gx", "gy")
    acts = P("dp", "gx", "gy")
    cols_out = P(("gy", "dp"), "gx")
    rows_out = P(("gx", "dp"), "gy")
    return jax.shard_map(
        shards,
        mesh=mesh,
        in_specs=(acts, P("dp", None), P(), cols, cols, cols, cols, cols, P(), P(), rows, P(), cols, cols, rows, acts),
        out_specs=(
            acts,
            acts,
            P(),
            cols_out,
            cols_out,
            cols_out,
            cols_out,
            cols_out,
            P(),
            P(),
            rows_out,
            P(),
            cols_out,
            cols_out,
            rows_out,
        ),
        check_vma=False,
    )
```

```python
import jax, jax.numpy as jnp
from jax import lax
from jax.experimental import pallas as pl
from jax.experimental.pallas import tpu as pltpu
import functools
from jax.sharding import PartitionSpec as P
EPS = 1e-6
HEAD_EPS = 0.01
C = 128
bf = jnp.bfloat16
f32 = jnp.float32
GROUP = 8

def nn(a, b):
    return lax.dot_general(a.astype(bf), b.astype(bf), (((1,), (0,)), ((), ())), preferred_element_type=f32)
def nt(a, b):
    return lax.dot_general(a.astype(bf), b.astype(bf), (((1,), (1,)), ((), ())), preferred_element_type=f32)
def tn(a, b):
    return lax.dot_general(a.astype(bf), b.astype(bf), (((0,), (0,)), ((), ())), preferred_element_type=f32)

def level_masks(n):
    row = lax.broadcasted_iota(jnp.int32, (n, n), 0)
    col = lax.broadcasted_iota(jnp.int32, (n, n), 1)
    out = []
    size = 1
    while size < n:
        out.append(((row ^ col) & (-size) == size).astype(f32).astype(bf))
        size *= 2
    return (row == col).astype(f32).astype(bf), out

def inverse_many(many, eye, levels):
    totals = [eye - a * levels[0] for a in many]
    for mask in levels[1:]:
        inner = [nn(a * mask, t).astype(bf) for a, t in zip(many, totals)]
        outer = [nn(t, x).astype(bf) for t, x in zip(totals, inner)]
        totals = [t - x for t, x in zip(totals, outer)]
    return totals

def act_stage(x, prev, aux, w, norm):
    row8 = lax.broadcasted_iota(jnp.int32, (8, 128), 0)
    conv = x * w[0:1]
    sh = []
    for i in range(1, w.shape[0]):
        r = pltpu.roll(x, i, 0)
        p = pltpu.roll(prev, i, 0)
        head = jnp.where(row8 < i, p, r[:8])
        m = jnp.concatenate([head, r[8:]], axis=0) * aux[:, 2 + i:3 + i]
        sh.append(m)
        conv = conv + m * w[i:i + 1]
    s = jax.nn.sigmoid(conv)
    act = conv * s
    if norm:
        rate = lax.rsqrt(jnp.sum(act * act, axis=-1, keepdims=True) + EPS)
        return conv, s, act * rate, rate, sh
    return conv, s, act, None, sh

def masks(aux, segrow):
    n = aux.shape[0]
    row = lax.broadcasted_iota(jnp.int32, (n, n), 0)
    col = lax.broadcasted_iota(jnp.int32, (n, n), 1)
    same = aux[:, 0:1] == segrow
    return same & (row > col), same & (row >= col)

def beta_column(block, h):
    lane = lax.broadcasted_iota(jnp.int32, block.shape, 1)
    return jnp.sum(jnp.where(lane == h, jax.nn.sigmoid(block), 0.0), axis=1, keepdims=True)

def prev_rows(ref, lo):
    start = pl.multiple_of(jnp.maximum(lo - 8, 0), 8)
    return jnp.where(lo > 0, ref[0, pl.ds(start, 8), :].astype(f32), 0.0)

def fwd_kernel(q_ref, k_ref, v_ref, g_ref, b_ref, aux_ref, seg_ref, w_ref, gain_ref,
               mixed_ref, t_ref, w_out, p_ref, f_ref, s_ref, fresh_ref, o_ref,
               q_s, u_s, b_s):
    h = pl.program_id(1)
    length = q_ref.shape[1]
    steps = length // C
    eye, levels = level_masks(C)
    def stage_a(group, _):
        lows = [pl.multiple_of((group * GROUP + n) * C, C) for n in range(GROUP)]
        spans = [pl.ds(lo, C) for lo in lows]
        many, keys, right = [], [], []
        for lo, rows in zip(lows, spans):
            aux = aux_ref[0, rows, :]
            q = act_stage(q_ref[0, rows, :].astype(f32), prev_rows(q_ref, lo), aux, w_ref[0], True)[2]
            k = act_stage(k_ref[0, rows, :].astype(f32), prev_rows(k_ref, lo), aux, w_ref[1], True)[2]
            v = act_stage(v_ref[0, rows, :].astype(f32), prev_rows(v_ref, lo), aux, w_ref[2], False)[2]
            beta = beta_column(b_ref[0, rows, :].astype(f32), h)
            strict, inclusive = masks(aux, seg_ref[0, 0:1, rows])
            kb = k.astype(bf)
            qb = q.astype(bf)
            both = nt(jnp.concatenate([kb, qb], axis=0), kb)
            many.append(jnp.where(strict, beta * both[:C], 0.0).astype(bf))
            p_ref[0, 0, rows, :] = jnp.where(inclusive, both[C:], 0.0).astype(bf)
            q_s[rows, :] = qb
            keys.append((k * aux[:, 2:3]).astype(bf))
            right.append(jnp.concatenate([(beta * k).astype(bf), (beta * v).astype(bf)], axis=1))
        totals = inverse_many(many, eye, levels)
        wus = [nn(t, r) for t, r in zip(totals, right)]
        kwus = [tn(k, wu) for k, wu in zip(keys, wus)]
        for rows, t, wu, kwu in zip(spans, totals, wus, kwus):
            clast = aux_ref[0, rows, :][C - 1:C, 1:2]
            f_ref[0, 0, rows, :] = (clast * (eye.astype(f32) - kwu[:, :C])).astype(bf)
            b_s[rows, :] = kwu[:, C:]
            t_ref[0, 0, rows, :] = t
            w_out[0, 0, rows, :] = wu[:, :C].astype(bf)
            u_s[rows, :] = wu[:, C:]
        return 0
    lax.fori_loop(0, steps // GROUP, stage_a, 0)
    def scan(c, state):
        rows = pl.ds(pl.multiple_of(c * C, C), C)
        sb = state.astype(bf)
        s_ref[0, 0, rows, :] = sb
        return nn(f_ref[0, 0, rows, :], sb) + b_s[rows, :]
    lax.fori_loop(0, steps, scan, jnp.zeros((C, C), f32), unroll=True)
    def stage_c(c, _):
        rows = pl.ds(pl.multiple_of(c * C, C), C)
        aux = aux_ref[0, rows, :]
        carried = aux[:, 1:2]
        ws = nn(jnp.concatenate([w_out[0, 0, rows, :], q_s[rows, :]], axis=0), s_ref[0, 0, rows, :])
        fresh = (u_s[rows, :] - carried * ws[:C]).astype(bf)
        out = carried * ws[C:] + nn(p_ref[0, 0, rows, :], fresh)
        fresh_ref[0, 0, rows, :] = fresh
        o_ref[0, 0, rows, :] = out
        g = g_ref[0, rows, :].astype(f32)
        r = lax.rsqrt(jnp.mean(out * out, axis=-1, keepdims=True) + HEAD_EPS)
        mixed_ref[0, rows, :] = (out * r * gain_ref[0:1] * (g * jax.nn.sigmoid(g))).astype(bf)
        return 0
    lax.fori_loop(0, steps, stage_c, 0, unroll=4)

def specs(length, heads, off):
    return [pl.BlockSpec((1, length, 128), functools.partial(lambda t, b, h: (b, 0, t * heads + h), t)) for t in range(4)] + [
        pl.BlockSpec((1, length, 128), lambda b, h: (b, 0, 4 * heads))]

def mixer_fwd(raw, aux, segrow, conv, gain):
    nb, length, width = raw.shape
    heads = (width - 128) // 512
    per = pl.BlockSpec((1, 1, length, 128), lambda b, h: (b, h, 0, 0))
    sh = lambda d: jax.ShapeDtypeStruct((nb, heads, length, 128), d)
    return pl.pallas_call(
        fwd_kernel,
        grid=(nb, heads),
        in_specs=specs(length, heads, 0) + [
            pl.BlockSpec((1, length, aux.shape[2]), lambda b, h: (b, 0, 0)),
            pl.BlockSpec((1, 1, length), lambda b, h: (b, 0, 0)),
            pl.BlockSpec((3, conv.shape[1], 128), lambda b, h: (0, 0, h)),
            pl.BlockSpec((1, 128), lambda b, h: (0, 0)),
        ],
        out_specs=[pl.BlockSpec((1, length, 128), lambda b, h: (b, 0, h))] + [per] * 7,
        out_shape=[jax.ShapeDtypeStruct((nb, length, heads * 128), bf)] + [sh(bf)] * 6 + [sh(f32)],
        scratch_shapes=[pltpu.VMEM((length, 128), bf), pltpu.VMEM((length, 128), f32), pltpu.VMEM((length, 128), f32)],
        name="mixer_forward",
    )(raw, raw, raw, raw, raw, aux, segrow, conv, gain)

def bwd_kernel(q_ref, k_ref, v_ref, g_ref, b_ref, aux_ref, seg_ref, w_ref, gain_ref,
               t_ref, w_in, p_ref, f_ref, s_ref, fresh_ref, o_ref, dm_ref,
               draw_ref, dconv_ref, dgain_ref,
               do_s, pd_s, base_s, ds_s):
    h = pl.program_id(1)
    heads = pl.num_programs(1)
    length = q_ref.shape[1]
    steps = length // C
    gain = gain_ref[0:1]
    def stage_a(c, dgain):
        lo = pl.multiple_of(c * C, C)
        rows = pl.ds(lo, C)
        aux = aux_ref[0, rows, :]
        carried = aux[:, 1:2]
        q = act_stage(q_ref[0, rows, :].astype(f32), prev_rows(q_ref, lo), aux, w_ref[0], True)[2]
        out = o_ref[0, 0, rows, :]
        g = g_ref[0, rows, :].astype(f32)
        dm = dm_ref[0, rows, :].astype(f32)
        s = jax.nn.sigmoid(g)
        r = lax.rsqrt(jnp.mean(out * out, axis=-1, keepdims=True) + HEAD_EPS)
        scaled = out * r
        dn = dm * (g * s)
        dg = dm * scaled * gain * (s * (1.0 + g * (1.0 - s)))
        draw_ref[0, rows, pl.ds(pl.multiple_of((3 * heads + h) * 128, 128), 128)] = dg.astype(bf)
        e = dn * gain
        do = r * (e - scaled * jnp.mean(e * scaled, axis=-1, keepdims=True))
        pd = tn(p_ref[0, 0, rows, :], do)
        do_s[rows, :] = do
        pd_s[rows, :] = pd
        base_s[rows, :] = tn(jnp.concatenate([q.astype(bf), w_in[0, 0, rows, :]], axis=0),
                             jnp.concatenate([carried * do, -carried * pd], axis=0))
        return dgain + jnp.sum((dn * scaled).reshape(C // 8, 8, 128), axis=0)
    dgain = lax.fori_loop(0, steps, stage_a, jnp.zeros((8, 128), f32), unroll=2)
    dgain_ref[0, 0] = dgain
    def scan(j, state):
        c = steps - 1 - j
        rows = pl.ds(pl.multiple_of(c * C, C), C)
        sb = state.astype(bf)
        ds_s[rows, :] = sb
        return tn(f_ref[0, 0, rows, :], sb) + base_s[rows, :]
    lax.fori_loop(0, steps, scan, jnp.zeros((C, C), f32), unroll=True)
    row8 = lax.broadcasted_iota(jnp.int32, (8, 128), 0)
    lane = lax.broadcasted_iota(jnp.int32, (C, 128), 1)

    def conv_back(dconv, nxt, aux, w, raw, sh):
        d = dconv * w[0:1]
        dw = [jnp.sum((dconv * raw).reshape(C // 8, 8, 128), axis=0)]
        for i in range(1, w.shape[0]):
            r = pltpu.roll(dconv, C - i, 0)
            p = pltpu.roll(nxt, 8 - i, 0)
            tailrows = jnp.where(row8 >= 8 - i, p, r[C - 8:])
            m = jnp.concatenate([r[:C - 8], tailrows], axis=0) * aux[:, 5 + i:6 + i]
            d = d + m * w[i:i + 1]
            dw.append(jnp.sum((dconv * sh[i - 1]).reshape(C // 8, 8, 128), axis=0))
        return d, dw

    def stage_c(j, carry):
        nq, nk, nv, dws = carry
        c = steps - 1 - j
        lo = pl.multiple_of(c * C, C)
        rows = pl.ds(lo, C)
        aux = aux_ref[0, rows, :]
        carried = aux[:, 1:2]
        tail = aux[:, 2:3]
        xq = q_ref[0, rows, :].astype(f32)
        xk = k_ref[0, rows, :].astype(f32)
        xv = v_ref[0, rows, :].astype(f32)
        cq, sq, q, rq, shq = act_stage(xq, prev_rows(q_ref, lo), aux, w_ref[0], True)
        ck, sk, k, rk, shk = act_stage(xk, prev_rows(k_ref, lo), aux, w_ref[1], True)
        cv, sv, v, _, shv = act_stage(xv, prev_rows(v_ref, lo), aux, w_ref[2], False)
        bblock = b_ref[0, rows, :].astype(f32)
        beta = beta_column(bblock, h)
        strict, inclusive = masks(aux, seg_ref[0, 0:1, rows])
        kb = k.astype(bf)
        qb = q.astype(bf)
        st = s_ref[0, 0, rows, :]
        dst = ds_s[rows, :]
        fresh = fresh_ref[0, 0, rows, :]
        do = do_s[rows, :]
        gram = nt(kb, kb)
        kk = nn(kb, jnp.concatenate([dst, st], axis=1))
        dfresh = pd_s[rows, :] + tail * kk[:, :128]
        x = v - carried * kk[:, 128:]
        y = tn(t_ref[0, 0, rows, :], dfresh)
        dx = beta * y
        cdx = (carried * dx).astype(bf)
        yb = y.astype(bf)
        dob = do.astype(bf)
        both = nt(jnp.concatenate([dob, yb], axis=0), fresh)
        dp = jnp.where(inclusive, both[:C], 0.0)
        da = jnp.where(strict, -both[C:], 0.0)
        dbeta = jnp.sum(y * x, axis=-1, keepdims=True) + jnp.sum(da * gram, axis=-1, keepdims=True)
        dg = beta * da
        dgs = dg + dg.T
        through = nt(jnp.concatenate([carried * do, -(carried * dx)], axis=0), st)
        dpb = dp.astype(bf)
        dq = through[:C] + nn(dpb, kb)
        dk = through[C:] + tn(dpb, qb) + nt(tail * fresh.astype(f32), dst) + nn(dgs, kb)
        dv = dx
        db = dbeta * beta * (1.0 - beta)
        bl = pl.ds(4 * heads * 128, 128)
        @pl.when(h == 0)
        def _():
            draw_ref[0, rows, bl] = jnp.where(lane == 0, db, 0.0).astype(bf)
        @pl.when(h > 0)
        def _():
            old = draw_ref[0, rows, bl]
            draw_ref[0, rows, bl] = jnp.where(lane == h, db.astype(bf).astype(f32), old.astype(f32)).astype(bf)
        dq = rq * (dq - q * jnp.sum(q * dq, axis=-1, keepdims=True))
        dk = rk * (dk - k * jnp.sum(k * dk, axis=-1, keepdims=True))
        dcq = dq * (sq * (1.0 + cq * (1.0 - sq)))
        dck = dk * (sk * (1.0 + ck * (1.0 - sk)))
        dcv = dv * (sv * (1.0 + cv * (1.0 - sv)))
        rq_, wq = conv_back(dcq, nq, aux, w_ref[0], xq, shq)
        rk_, wk = conv_back(dck, nk, aux, w_ref[1], xk, shk)
        rv_, wv = conv_back(dcv, nv, aux, w_ref[2], xv, shv)
        for t, val in ((0, rq_), (1, rk_), (2, rv_)):
            draw_ref[0, rows, pl.ds(pl.multiple_of((t * heads + h) * 128, 128), 128)] = val.astype(bf)
        dws = tuple(a + b for a, b in zip(dws, wq + wk + wv))
        return dcq[:8], dck[:8], dcv[:8], dws
    z8 = jnp.zeros((8, 128), f32)
    taps = w_ref.shape[1]
    _, _, _, dws = lax.fori_loop(0, steps, stage_c, (z8, z8, z8, (z8,) * (3 * taps)), unroll=2)
    for n, d in enumerate(dws):
        dconv_ref[0, 0, n] = d

def mixer_bwd(raw, aux, segrow, conv, gain, saved, dmixed):
    nb, length, width = raw.shape
    heads = (width - 128) // 512
    taps = conv.shape[1]
    per = pl.BlockSpec((1, 1, length, 128), lambda b, h: (b, h, 0, 0))
    sh = lambda d: jax.ShapeDtypeStruct((nb, heads, length, 128), d)
    draw, dconv, dgain = pl.pallas_call(
        bwd_kernel,
        grid=(nb, heads),
        in_specs=specs(length, heads, 0) + [
            pl.BlockSpec((1, length, aux.shape[2]), lambda b, h: (b, 0, 0)),
            pl.BlockSpec((1, 1, length), lambda b, h: (b, 0, 0)),
            pl.BlockSpec((3, taps, 128), lambda b, h: (0, 0, h)),
            pl.BlockSpec((1, 128), lambda b, h: (0, 0)),
        ] + [per] * 7 + [pl.BlockSpec((1, length, 128), lambda b, h: (b, 0, h))],
        out_specs=[pl.BlockSpec((1, length, width), lambda b, h: (b, 0, 0)),
                   pl.BlockSpec((1, 1, 3 * taps, 8, 128), lambda b, h: (b, h, 0, 0, 0)),
                   pl.BlockSpec((1, 1, 8, 128), lambda b, h: (b, h, 0, 0))],
        out_shape=[jax.ShapeDtypeStruct((nb, length, width), bf),
                   jax.ShapeDtypeStruct((nb, heads, 3 * taps, 8, 128), f32),
                   jax.ShapeDtypeStruct((nb, heads, 8, 128), f32)],
        scratch_shapes=[pltpu.VMEM((length, 128), f32)] * 3 + [pltpu.VMEM((length, 128), bf)],
        name="mixer_backward",
    )(raw, raw, raw, raw, raw, aux, segrow, conv, gain, *saved, dmixed)
    dconv = jnp.sum(dconv, axis=(0, 3)).reshape(heads, 3, taps, 128).transpose(1, 2, 0, 3).reshape(3, taps, heads * 128)
    return draw, dconv, jnp.sum(dgain, axis=(0, 1, 2))

def make_aux(segments):
    nb, length = segments.shape
    seg = segments.astype(f32)
    blocks = seg.reshape(nb, length // C, C)
    last = blocks[:, :, -1:]
    before = jnp.concatenate([jnp.full((nb, 1, 1), -1.0, f32), last[:, :-1]], axis=1)
    carried = (blocks == before).astype(f32).reshape(nb, length)
    tail = (blocks == last).astype(f32).reshape(nb, length)
    cols = [seg, carried, tail]
    for i in range(1, 4):
        cols.append((jnp.pad(seg, ((0, 0), (i, 0)), constant_values=-1.0)[:, :length] == seg).astype(f32))
    for i in range(1, 4):
        cols.append((jnp.pad(seg, ((0, 0), (0, i)), constant_values=-1.0)[:, i:] == seg).astype(f32))
    cols += [jnp.zeros_like(seg)] * (16 - len(cols))
    return jnp.stack(cols, axis=-1), seg[:, None, :]


SLOTS = ((0, 0, 0), (0, 0, 1), (1, 0, 0), (0, 1, 0), (1, 0, 1), (0, 1, 1), (1, 1, 0), (1, 1, 1))
MESH = pl.DeviceIdType.MESH
VM = pl.BlockSpec(memory_space=pltpu.VMEM)
ANY = pl.BlockSpec(memory_space=pl.ANY)


def slot_place(r, gx, gy):
    dx, dy, dc = SLOTS[r]
    hi, lo = gx // 2, gx % 2
    hi = 1 - hi if dy else hi
    lo = 1 - lo if dc else lo
    return hi * 2 + lo, (1 - gy if dx else gy)


def slot_peer(r, gx, gy):
    px, py = slot_place(r, gx, gy)
    return {"gx": px, "gy": py}


def entry_barrier(peers):
    sem = pltpu.get_barrier_semaphore()
    for peer in peers:
        pl.semaphore_signal(sem, inc=1, device_id=peer, device_id_type=MESH)
    pl.semaphore_wait(sem, len(peers))


def remote(src, dst, send, recv, peer):
    return pltpu.make_async_remote_copy(src, dst, send, recv, device_id=peer, device_id_type=MESH)


def nt_dot(a, b):
    return lax.dot_general(a, b, (((1,), (1,)), ((), ())), preferred_element_type=f32)


def nn_dot(a, b):
    return lax.dot_general(a, b, (((1,), (0,)), ((), ())), preferred_element_type=f32)


class Gather:
    COPIES = 13

    def __init__(self, buf, send, recv, gx, gy):
        rows = buf.shape[1]
        half = rows // 2
        a, b = pl.ds(0, half), pl.ds(half, half)
        core, xn, yn = (slot_peer(r, gx, gy) for r in (1, 2, 3))

        def make(i, src, dst, part, peer):
            return remote(buf.at[src, part], buf.at[dst, part], send.at[i], recv.at[i], peer)

        self.own = [
            make(0, 0, 2, a, xn),
            make(1, 0, 3, a, yn),
            make(2, 0, 2, b, xn),
            make(3, 0, 3, b, yn),
            remote(buf.at[0], buf.at[1], send.at[4], recv.at[4], core),
        ]
        self.diagonal = [make(5, 3, 6, a, xn), make(6, 2, 6, b, yn)]
        self.cross = [
            make(7, 2, 4, a, core),
            make(8, 2, 4, b, core),
            make(9, 3, 5, a, core),
            make(10, 3, 5, b, core),
            make(11, 6, 7, a, core),
            make(12, 6, 7, b, core),
        ]

    def start(self):
        for c in self.own:
            c.start()

    def step(self, i):
        if i == 1:
            self.own[4].wait_recv()
        elif i == 2:
            self.own[1].wait_recv()
            self.diagonal[0].start()
            self.cross[2].start()
            self.own[0].wait_recv()
            self.cross[0].start()
            self.own[2].wait_recv()
            self.diagonal[1].start()
            self.cross[1].start()
        elif i == 3:
            self.own[3].wait_recv()
            self.cross[3].start()
        elif i == 4:
            self.cross[0].wait_recv()
            self.cross[1].wait_recv()
        elif i == 5:
            self.cross[2].wait_recv()
            self.cross[3].wait_recv()
        elif i == 6:
            self.diagonal[0].wait_recv()
            self.cross[4].start()
            self.diagonal[1].wait_recv()
            self.cross[5].start()
        elif i == 7:
            self.cross[4].wait_recv()
            self.cross[5].wait_recv()

    def finish(self):
        for c in self.own + self.diagonal + self.cross:
            c.wait_send()


def mlp_kernel(
    mixed_ref, out_ref, x_ref, gain_ref, wgu_ref, wd_ref, y_ref,
    middle_ref, second_ref, hidden_ref, grads_ref, yrel_ref,
    mix_in, w_out, wgu, wd, buf, ybuf, hbuf, gbuf, mid, mine,
    load_sem, y_sem, y_out_sem, out_sem, a2a_send, a2a_recv, ag_send, ag_recv,
):
    gx, gy = lax.axis_index("gx"), lax.axis_index("gy")
    ngx, ngy = 4, 2
    me = gx * ngy + gy
    rows = x_ref.shape[0]
    feat = x_ref.shape[1]
    width = mixed_ref.shape[2]
    units = wd_ref.shape[0]
    tile = 256
    peers = [slot_peer(r, gx, gy) for r in range(1, 8)]
    entry_barrier(peers)
    sends = []
    for i, r in enumerate((6, 7, 2, 4, 3, 5, 1)):
        px, py = slot_place(r, gx, gy)
        sends.append(remote(mixed_ref.at[py * ngx + px], mix_in.at[me], a2a_send.at[r], a2a_recv.at[r], slot_peer(r, gx, gy)))
        sends[-1].start()
    loads = [
        pltpu.make_async_copy(mixed_ref.at[gy * ngx + gx], mine, load_sem.at[0]),
        pltpu.make_async_copy(out_ref, w_out, load_sem.at[1]),
        pltpu.make_async_copy(wgu_ref, wgu, load_sem.at[2]),
        pltpu.make_async_copy(wd_ref, wd, load_sem.at[3]),
    ]
    for c in loads:
        c.start()

    def y_load(r, n):
        px, py = slot_place(r, gx, gy)
        return [
            pltpu.make_async_copy(y_ref.at[px * ngy + h, py], ybuf.at[r % 2, :, pl.ds(h * (feat // 2), feat // 2)], y_sem.at[r % 2, h])
            for h in range(2)
        ]

    def y_store(r):
        return pltpu.make_async_copy(ybuf.at[r % 2], yrel_ref.at[r], y_out_sem.at[r % 2])

    for c in y_load(0, 0):
        c.start()
    loads[0].wait()
    mix_in[me] = mine[...]
    for c in sends:
        c.wait_recv()
    loads[1].wait()
    for h in range(ngy):
        cols = pl.ds(h * (feat // ngy), feat // ngy)
        total = x_ref[:, cols].astype(f32)
        for p in range(ngx):
            left = jnp.concatenate([mix_in[p * 2], mix_in[p * 2 + 1]], axis=1)
            total = total + nn_dot(left, w_out[p * 2 + h])
        mid[:, cols] = total
    middle = mid[...]
    rate = lax.rsqrt(jnp.mean(middle * middle, axis=-1, keepdims=True) + EPS)
    buf[0] = (middle * rate * gain_ref[...]).astype(bf)
    gather = Gather(buf, ag_send, ag_recv, gx, gy)
    gather.start()
    middle_ref[...] = mid[...]
    loads[2].wait()
    loads[3].wait()

    def outs(r):
        return [
            pltpu.make_async_copy(buf.at[r], second_ref.at[r], out_sem.at[0, r % 2]),
            pltpu.make_async_copy(hbuf.at[r % 2], hidden_ref.at[r], out_sem.at[1, r % 2]),
            pltpu.make_async_copy(gbuf.at[r % 2], grads_ref.at[r], out_sem.at[2, r % 2]),
        ]

    for r in range(8):
        gather.step(r)
        if r >= 2:
            for c in outs(r - 2):
                c.wait()
        if r + 1 < 8:
            if r >= 1:
                y_store(r - 1).wait()
            for c in y_load(r + 1, 0):
                c.start()
        for c in y_load(r, 0):
            c.wait()
        y_store(r).start()

        def body(t, _):
            cols = pl.ds(pl.multiple_of(t * tile, tile), tile)
            up_cols = pl.ds(pl.multiple_of(units + t * tile, tile), tile)
            gate = nn_dot(buf[r], wgu[:, cols])
            up = nn_dot(buf[r], wgu[:, up_cols])
            gh = nt_dot(ybuf[r % 2], wd[cols, :])
            s = jax.nn.sigmoid(gate)
            act = gate * s
            hbuf[r % 2, :, cols] = (act * up).astype(bf)
            gbuf[r % 2, :, up_cols] = (gh * act).astype(bf)
            gbuf[r % 2, :, cols] = (gh * up * s * (1.0 + gate * (1.0 - s))).astype(bf)
            return 0

        lax.fori_loop(0, units // tile, body, 0)
        for c in outs(r):
            c.start()
    for r in (6, 7):
        for c in outs(r):
            c.wait()
        y_store(r).wait()
    gather.finish()
    for c in sends:
        c.wait_send()


def mlp_forward(mixed, out_all, x_own, gain, gate_up, down, y_all, collective):
    rows, feat = x_own.shape
    width = mixed.shape[2]
    units = down.shape[0]
    sd = jax.ShapeDtypeStruct
    return pl.pallas_call(
        mlp_kernel,
        in_specs=[ANY, ANY, VM, VM, ANY, ANY, ANY],
        out_specs=[VM, ANY, ANY, ANY, ANY],
        out_shape=[
            sd((rows, feat), f32),
            sd((8, rows, feat), bf),
            sd((8, rows, units), bf),
            sd((8, rows, 2 * units), bf),
            sd((8, rows, feat), bf),
        ],
        scratch_shapes=[
            pltpu.VMEM((8, rows, width), bf),
            pltpu.VMEM(out_all.shape, bf),
            pltpu.VMEM(gate_up.shape, bf),
            pltpu.VMEM(down.shape, bf),
            pltpu.VMEM((8, rows, feat), bf),
            pltpu.VMEM((2, rows, feat), bf),
            pltpu.VMEM((2, rows, units), bf),
            pltpu.VMEM((2, rows, 2 * units), bf),
            pltpu.VMEM((rows, feat), f32),
            pltpu.VMEM((rows, width), bf),
            pltpu.SemaphoreType.DMA((4,)),
            pltpu.SemaphoreType.DMA((2, 2)),
            pltpu.SemaphoreType.DMA((2,)),
            pltpu.SemaphoreType.DMA((3, 2)),
            pltpu.SemaphoreType.DMA((8,)),
            pltpu.SemaphoreType.DMA((8,)),
            pltpu.SemaphoreType.DMA((13,)),
            pltpu.SemaphoreType.DMA((13,)),
        ],
        compiler_params=pltpu.CompilerParams(collective_id=collective, has_side_effects=True, vmem_limit_bytes=62 << 20),
        name="mlp_forward",
    )(mixed, out_all, x_own, gain, gate_up, down, y_all)


class Scatter:
    def __init__(self, give, take, acc, diag_in, last_in, s_core, r_core, s_link, r_link, gx, gy):
        self.give, self.take, self.acc, self.diag_in, self.last_in = give, take, acc, diag_in, last_in
        core, xn, yn = (slot_peer(r, gx, gy) for r in (1, 2, 3))
        rows = acc.shape[1]
        half = rows // 2
        a, b = pl.ds(0, half), pl.ds(half, half)
        self.a, self.b = a, b
        self.core = [remote(give.at[n], take.at[n], s_core.at[n], r_core.at[n], core) for n in range(4)]

        def link(i, src, dst, peer):
            return remote(src, dst, s_link.at[i], r_link.at[i], peer)

        self.link = [
            link(0, acc.at[0, a], diag_in.at[0], xn),
            link(1, acc.at[0, b], diag_in.at[1], yn),
            link(2, acc.at[1, a], last_in.at[0, a], xn),
            link(3, acc.at[2, b], last_in.at[1, b], yn),
            link(4, acc.at[1, b], last_in.at[0, b], xn),
            link(5, acc.at[2, a], last_in.at[1, a], yn),
        ]

    def run(self, product, self_acc):
        acc = self.acc

        def give_out(n, slot):
            def put(cols, value):
                self.give[n, :, cols] = value.astype(bf)

            product(slot, put)
            self.core[n].start()

        def keep(n, slot):
            def put(cols, value):
                acc[n, :, cols] = value.astype(bf)

            product(slot, put)

        def join(n):
            self.core[n].wait_recv()
            acc[n] = (acc[n].astype(f32) + self.take[n].astype(f32)).astype(bf)

        a, b = self.a, self.b
        give_out(0, 7)
        keep(0, 6)
        give_out(1, 4)
        join(0)
        self.link[0].start()
        self.link[1].start()
        give_out(2, 5)
        keep(1, 2)
        join(1)
        self.link[2].start()
        keep(2, 3)
        join(2)
        self.link[3].start()
        give_out(3, 1)

        def put_self(cols, value):
            self_acc[:, cols] = value

        product(0, put_self)
        self.link[1].wait_recv()
        acc[1, b] = (acc[1, b].astype(f32) + self.diag_in[1].astype(f32)).astype(bf)
        self.link[4].start()
        self.link[0].wait_recv()
        acc[2, a] = (acc[2, a].astype(f32) + self.diag_in[0].astype(f32)).astype(bf)
        self.link[5].start()
        self.core[3].wait_recv()
        self_acc[...] += self.take[3].astype(f32)
        for c in self.link[2:]:
            c.wait_recv()
        self_acc[...] += self.last_in[0].astype(f32) + self.last_in[1].astype(f32)

    def finish(self):
        for c in self.core + self.link:
            c.wait_send()


def scatter_scratch(rows, feat):
    return [
        pltpu.VMEM((4, rows, feat), bf),
        pltpu.VMEM((4, rows, feat), bf),
        pltpu.VMEM((3, rows, feat), bf),
        pltpu.VMEM((2, rows // 2, feat), bf),
        pltpu.VMEM((2, rows, feat), bf),
        pltpu.SemaphoreType.DMA((4,)),
        pltpu.SemaphoreType.DMA((4,)),
        pltpu.SemaphoreType.DMA((6,)),
        pltpu.SemaphoreType.DMA((6,)),
    ]


def back_kernel(
    grads_ref, wgu_ref, out_ref, middle_ref, y_ref, gain_ref,
    gm_ref, gmix_ref, dgain_ref,
    give, take, acc, diag_in, last_in, s_core, r_core, s_link, r_link,
    lhs, wgu, w_out, total, mid_low, gsend, load_sem, lhs_sem, a2a_send, a2a_recv, keep_sem,
):
    gx, gy = lax.axis_index("gx"), lax.axis_index("gy")
    ngx, ngy = 4, 2
    rows, feat = middle_ref.shape
    width = gmix_ref.shape[2]
    tile = 512
    order = (7, 6, 4, 5, 2, 3, 1, 0)
    loads = [pltpu.make_async_copy(wgu_ref, wgu, load_sem.at[0])]
    pulls = {r: pltpu.make_async_copy(grads_ref.at[r], lhs.at[r], lhs_sem.at[r]) for r in order}
    pulls[7].start()
    loads[0].start()
    for r in order[1:]:
        pulls[r].start()
    loads.append(pltpu.make_async_copy(out_ref, w_out, load_sem.at[1]))
    loads[1].start()
    entry_barrier([slot_peer(r, gx, gy) for r in range(1, 8)])
    loads[0].wait()

    def product(slot, put):
        pulls[slot].wait()

        def body(t, _):
            cols = pl.ds(pl.multiple_of(t * tile, tile), tile)
            put(cols, nt_dot(lhs[slot], wgu[cols, :]))
            return 0

        lax.fori_loop(0, feat // tile, body, 0)

    scatter = Scatter(give, take, acc, diag_in, last_in, s_core, r_core, s_link, r_link, gx, gy)
    scatter.run(product, total)
    middle = middle_ref[...]
    incoming = total[...]
    rate = lax.rsqrt(jnp.mean(middle * middle, axis=-1, keepdims=True) + EPS)
    scaled = gain_ref[...] * incoming
    inner = jnp.mean(middle * scaled, axis=-1, keepdims=True)
    dgain_ref[...] = jnp.sum((incoming * middle * rate).reshape(rows // 8, 8, feat), axis=0)
    gm = y_ref[...].astype(f32) + rate * scaled - middle * (rate * rate * rate) * inner
    mid_low[...] = gm.astype(bf)
    gm_ref[...] = mid_low[...]
    loads[1].wait()
    v = gy * ngx + gx
    sends = []
    for r in (6, 7, 2, 4, 3, 5, 1, 0):
        px, py = slot_place(r, gx, gy)
        rows_w = pl.ds(pl.multiple_of(py * width, width), width)
        part = nt_dot(mid_low[:, : feat // 2], w_out[px * 2, rows_w, :]) + nt_dot(mid_low[:, feat // 2 :], w_out[px * 2 + 1, rows_w, :])
        gsend[r] = part.astype(bf)
        if r == 0:
            keep = pltpu.make_async_copy(gsend.at[0], gmix_ref.at[v], keep_sem)
            keep.start()
        else:
            c = remote(gsend.at[r], gmix_ref.at[v], a2a_send.at[r], a2a_recv.at[r], slot_peer(r, gx, gy))
            c.start()
            sends.append(c)
    keep.wait()
    for c in sends:
        c.wait_recv()
    for c in sends:
        c.wait_send()
    scatter.finish()


def mlp_backward(grads, gate_up, out_all, middle, y_own, gain, width, collective):
    rows, feat = middle.shape
    sd = jax.ShapeDtypeStruct
    return pl.pallas_call(
        back_kernel,
        in_specs=[ANY, ANY, ANY, VM, VM, VM],
        out_specs=[VM, ANY, VM],
        out_shape=[sd((rows, feat), bf), sd((8, rows, width), bf), sd((8, feat), f32)],
        scratch_shapes=scatter_scratch(rows, feat)
        + [
            pltpu.VMEM(grads.shape, bf),
            pltpu.VMEM(gate_up.shape, bf),
            pltpu.VMEM(out_all.shape, bf),
            pltpu.VMEM((rows, feat), f32),
            pltpu.VMEM((rows, feat), bf),
            pltpu.VMEM((8, rows, width), bf),
            pltpu.SemaphoreType.DMA((2,)),
            pltpu.SemaphoreType.DMA((8,)),
            pltpu.SemaphoreType.DMA((8,)),
            pltpu.SemaphoreType.DMA((8,)),
            pltpu.SemaphoreType.DMA,
        ],
        compiler_params=pltpu.CompilerParams(collective_id=collective, has_side_effects=True, vmem_limit_bytes=63 << 20),
        name="mlp_backward",
    )(grads, gate_up, out_all, middle, y_own, gain)


def scatter_kernel(lhs_ref, w_ref, out_ref, give, take, acc, diag_in, last_in, s_core, r_core, s_link, r_link, lhs, w, total, load_sem, lhs_sem, *, slots, transposed):
    gx, gy = lax.axis_index("gx"), lax.axis_index("gy")
    rows, feat = out_ref.shape
    tile = 512
    load = pltpu.make_async_copy(w_ref, w, load_sem)

    def source(r):
        if slots:
            return lhs_ref.at[r]
        px, py = slot_place(r, gx, gy)
        return lhs_ref.at[py * 4 + px]

    order = (7, 6, 4, 5, 2, 3, 1, 0)
    pulls = {r: pltpu.make_async_copy(source(r), lhs.at[r], lhs_sem.at[r]) for r in order}
    pulls[7].start()
    load.start()
    for r in order[1:]:
        pulls[r].start()
    entry_barrier([slot_peer(r, gx, gy) for r in (1, 2, 3)])
    load.wait()

    def product(slot, put):
        pulls[slot].wait()

        def body(t, _):
            cols = pl.ds(pl.multiple_of(t * tile, tile), tile)
            put(cols, nn_dot(lhs[slot], w[:, cols]) if transposed else nt_dot(lhs[slot], w[cols, :]))
            return 0

        lax.fori_loop(0, feat // tile, body, 0)

    scatter = Scatter(give, take, acc, diag_in, last_in, s_core, r_core, s_link, r_link, gx, gy)
    scatter.run(product, total)
    out_ref[...] = total[...]
    scatter.finish()


def product_scatter(lhs, w, collective, slots, transposed):
    _, rows, depth = lhs.shape
    feat = w.shape[1] if transposed else w.shape[0]
    return pl.pallas_call(
        functools.partial(scatter_kernel, slots=slots, transposed=transposed),
        in_specs=[ANY, ANY],
        out_specs=VM,
        out_shape=jax.ShapeDtypeStruct((rows, feat), f32),
        scratch_shapes=scatter_scratch(rows, feat)
        + [
            pltpu.VMEM(lhs.shape, bf),
            pltpu.VMEM(w.shape, bf),
            pltpu.VMEM((rows, feat), f32),
            pltpu.SemaphoreType.DMA,
            pltpu.SemaphoreType.DMA((8,)),
        ],
        compiler_params=pltpu.CompilerParams(collective_id=collective, has_side_effects=True, vmem_limit_bytes=60 << 20),
        name="product_scatter",
    )(lhs, w)


TOKENS = ("gy", "gx")


def dot(a, b):
    return lax.dot_general(a, b, (((1,), (0,)), ((), ())), preferred_element_type=f32)


def dot_t(a, b):
    return lax.dot_general(a, b, (((1,), (1,)), ((), ())), preferred_element_type=f32)


def dot_w(a, b):
    return lax.dot_general(a, b, (((0,), (0,)), ((), ())), preferred_element_type=f32)


def swap(value):
    return lax.ppermute(value, "gy", [(0, 1), (1, 0)])


def in_order(mine, other, axis):
    first = lax.axis_index("gy") == 0
    return jnp.concatenate([jnp.where(first, mine, other), jnp.where(first, other, mine)], axis=axis)


def halves(value, axis):
    size = value.shape[axis] // 2
    mine = lax.axis_index("gy")
    return (
        lax.dynamic_slice_in_dim(value, mine * size, size, axis),
        lax.dynamic_slice_in_dim(value, (1 - mine) * size, size, axis),
    )


def gather_blocks(value):
    nb, rows, width = value.shape
    many = lax.all_gather(value, ("gx", "gy"), axis=0, tiled=False)
    ngx, ngy = lax.axis_size("gx"), lax.axis_size("gy")
    many = many.reshape(ngx, ngy, nb, rows, width)
    return many.transpose(2, 0, 3, 1, 4).reshape(nb, ngx * rows, ngy * width)


def to_final(own):
    mine, other = halves(own, 1)
    return in_order(mine[None], swap(other)[None], 0)


def rate_of(value):
    return lax.rsqrt(jnp.mean(value * value, axis=-1, keepdims=True) + EPS)


def scatter_dp(value):
    return lax.psum_scatter(value.astype(bf), "dp", scatter_dimension=0, tiled=True)


def rows_to_dp(grad, ndp):
    rows, cols = grad.shape
    parts = grad.astype(bf).reshape(2, ndp, rows // (2 * ndp), cols).transpose(1, 0, 2, 3)
    summed = scatter_dp(parts.reshape(rows, cols))
    mine, other = halves(summed, 0)
    return mine, swap(other)


def sum_axis(value, axis):
    size = lax.axis_size(axis)
    step = 1
    while step < size:
        value = value + lax.ppermute(value, axis, [(i, i ^ step) for i in range(size)])
        step *= 2
    return value


def spread(value, ndp):
    part = value.shape[0] // ndp
    dp = lax.axis_index("dp")
    piece = swap(lax.dynamic_slice_in_dim(value, dp * part, part, 0))
    if ndp & (ndp - 1) or ndp > 4:
        return lax.all_gather(piece, "dp", axis=0, tiled=True)
    out = lax.dynamic_update_slice_in_dim(jnp.zeros(value.shape, value.dtype), piece, dp * part, 0)
    for step in range(1, ndp):
        got = lax.ppermute(piece, "dp", [(i, i ^ step) for i in range(ndp)])
        out = lax.dynamic_update_slice_in_dim(out, got, (dp ^ step) * part, 0)
    return out


def shards(
    inputs,
    segments,
    norm_gain,
    w_query,
    w_key,
    w_value,
    w_beta,
    w_gate_head,
    conv_kernel,
    head_gain,
    w_out,
    mlp_gain,
    w_gate,
    w_up,
    w_down,
    grad_y,
):
    ngx, ngy, ndp = lax.axis_size("gx"), lax.axis_size("gy"), lax.axis_size("dp")
    gx, gy = lax.axis_index("gx"), lax.axis_index("gy")
    x_all = gather_blocks(inputs)
    nb, length, feat = x_all.shape
    tokens = nb * length
    own_rows = tokens // (ngx * ngy)
    own_start = (gy * ngx + gx) * own_rows
    heads = w_beta.shape[1] // ngy
    width = w_query.shape[1] // ngy

    cat = [halves(w, 1) for w in (w_query, w_key, w_value, w_gate_head)]
    pad = ((0, 0), (0, 128 - heads))
    beta_mine, beta_other = halves(w_beta, 1)
    head_w = in_order(
        jnp.concatenate([m for m, _ in cat] + [jnp.pad(beta_mine, pad)], axis=1),
        swap(jnp.concatenate([o for _, o in cat] + [jnp.pad(beta_other, pad)], axis=1)),
        0,
    )

    block = w_gate.shape[1]
    units = -(-block // (ngy * 256)) * 256
    unit_mine, unit_other = gy * (block - units), (1 - gy) * (block - units)

    def pick(w, start, axis):
        return lax.dynamic_slice_in_dim(w, start, units, axis)

    fresh_unit = (lax.broadcasted_iota(jnp.int32, (1, units), 1) >= gy * (2 * units - block)).astype(bf)
    gate_up = in_order(
        jnp.concatenate([pick(w_gate, unit_mine, 1), pick(w_up, unit_mine, 1)], axis=1),
        spread(jnp.concatenate([pick(w_gate, unit_other, 1), pick(w_up, unit_other, 1)], axis=1), ndp),
        0,
    ) * jnp.concatenate([fresh_unit, fresh_unit], axis=1)
    down_w = in_order(pick(w_down, unit_mine, 0), spread(pick(w_down, unit_other, 0), ndp), 1)
    out_all = lax.all_gather(w_out, ("gx", "gy"), axis=0, tiled=False)
    y_all = lax.all_gather(grad_y, ("gx", "gy"), axis=0, tiled=False)

    aux, segrow = make_aux(segments)
    x_flat = x_all.reshape(tokens, feat)
    x_wide = x_flat.astype(f32)
    rate_first = rate_of(x_wide)
    normed = (x_wide * rate_first * norm_gain).astype(bf)
    raw = dot(normed, head_w).reshape(nb, length, -1)
    conv_start = (gx * ngy + gy) * width
    conv_local = lax.dynamic_slice_in_dim(conv_kernel, conv_start, width, 2)
    gain_row = head_gain[None]
    mixed, *saved = mixer_fwd(raw, aux, segrow, conv_local, gain_row)
    x_own = lax.dynamic_slice_in_dim(x_flat, own_start, own_rows, 0)
    middle, second, hidden, grads, y_rel = mlp_forward(
        mixed.reshape(8, own_rows, width), out_all, x_own, mlp_gain[None], gate_up, down_w, y_all, 1
    )
    second_flat, hidden_flat = second.reshape(tokens, feat), hidden.reshape(tokens, units)
    grads_flat, y_flat = grads.reshape(tokens, 2 * units), y_rel.reshape(tokens, feat)
    down_keep, down_send = halves(dot_w(hidden_flat, y_flat).astype(bf), 1)
    down_both = jnp.stack([down_keep, swap(down_send)])
    first, last = down_both[gy], down_both[1 - gy]
    down_rows = jnp.concatenate([first, last[2 * units - block :]], axis=0)
    sum_down = scatter_dp(down_rows).astype(f32)
    grad_gu_mine, grad_gu_other = rows_to_dp(dot_w(second_flat, grads_flat), ndp)

    mid_low, grad_mixed, mlp_gain_parts = mlp_backward(
        grads, gate_up, out_all, middle, y_rel[0], mlp_gain[None], width, 2
    )
    draw, conv_grad, gain_grad = mixer_bwd(
        raw, aux, segrow, conv_local, gain_row, saved, grad_mixed.reshape(nb, length, width)
    )
    draw = draw.reshape(tokens, -1)
    grad_head_w = dot_w(normed, draw)
    norm_gain_grad = jnp.sum(grad_head_w * head_w.astype(f32), axis=1) / norm_gain
    head_mine, head_other = rows_to_dp(grad_head_w, ndp)
    mid_all = lax.all_gather(mid_low, TOKENS, axis=0, tiled=True)
    grad_normed = product_scatter(draw.reshape(8, own_rows, -1), head_w, 3, False, False)
    x_wide_own = x_own.astype(f32)
    rate_own = rate_of(x_wide_own)
    scaled = norm_gain * grad_normed
    inner = jnp.mean(x_wide_own * scaled, axis=-1, keepdims=True)
    norm_one = rate_own * scaled - x_wide_own * (rate_own * rate_own * rate_own) * inner
    grad_inputs = to_final((mid_low.astype(f32) + norm_one).astype(bf))
    layer_out = to_final((middle + product_scatter(hidden, down_w, 4, True, True)).astype(bf))

    out_keep, out_send = halves(dot_w(mixed.reshape(tokens, width), mid_all).astype(bf), 1)
    sum_out = scatter_dp(in_order(out_keep, swap(out_send), 0)).astype(f32)

    def unit_columns(i):
        part = slice(i * units, (i + 1) * units)
        both = jnp.stack([grad_gu_mine[:, part], grad_gu_other[:, part]])
        return jnp.concatenate([both[gy], both[1 - gy][:, 2 * units - block :]], axis=1).astype(f32)

    sum_gate, sum_up = unit_columns(0), unit_columns(1)

    def head_part(i, n):
        return in_order(head_mine[:, i : i + n], head_other[:, i : i + n], 1).astype(f32)

    sum_query, sum_key, sum_value, sum_head_gate = (head_part(i * width, width) for i in range(4))
    sum_beta = head_part(4 * width, heads)

    small = jnp.concatenate([conv_grad.reshape(-1), norm_gain_grad, jnp.sum(mlp_gain_parts, axis=0), gain_grad])
    small = sum_axis(small, "dp")
    n_conv = conv_grad.size
    conv_full = lax.dynamic_update_slice_in_dim(
        jnp.zeros(conv_kernel.shape, f32), small[:n_conv].reshape(conv_grad.shape), conv_start, 2
    )
    small = sum_axis(sum_axis(jnp.concatenate([conv_full.reshape(-1), small[n_conv:]]), "gx"), "gy")
    n_conv = conv_full.size
    conv_sum = small[:n_conv].reshape(conv_kernel.shape)
    norm_sum, mlp_sum, gain_sum = jnp.split(small[n_conv:], [feat, 2 * feat])
    return (
        layer_out,
        grad_inputs,
        norm_sum,
        sum_query,
        sum_key,
        sum_value,
        sum_beta,
        sum_head_gate,
        conv_sum,
        gain_sum,
        sum_out,
        mlp_sum,
        sum_gate,
        sum_up,
        sum_down,
    )


def solution(mesh):
    cols = P("gy", "gx")
    rows = P("gx", "gy")
    acts = P("dp", "gx", "gy")
    cols_out = P(("gy", "dp"), "gx")
    rows_out = P(("gx", "dp"), "gy")
    return jax.shard_map(
        shards,
        mesh=mesh,
        in_specs=(acts, P("dp", None), P(), cols, cols, cols, cols, cols, P(), P(), rows, P(), cols, cols, rows, acts),
        out_specs=(
            acts,
            acts,
            P(),
            cols_out,
            cols_out,
            cols_out,
            cols_out,
            cols_out,
            P(),
            P(),
            rows_out,
            P(),
            cols_out,
            cols_out,
            rows_out,
        ),
        check_vma=False,
    )
```

```python
import jax, jax.numpy as jnp
from jax import lax
from jax.experimental import pallas as pl
from jax.experimental.pallas import tpu as pltpu
import functools
from jax.sharding import PartitionSpec as P
EPS = 1e-6
HEAD_EPS = 0.01
C = 128
bf = jnp.bfloat16
f32 = jnp.float32
GROUP = 8

def lasting(us):
    return pl.CostEstimate(flops=int(us * 1.15e9), bytes_accessed=1 << 20, transcendentals=0)

def nn(a, b):
    return lax.dot_general(a.astype(bf), b.astype(bf), (((1,), (0,)), ((), ())), preferred_element_type=f32)
def nt(a, b):
    return lax.dot_general(a.astype(bf), b.astype(bf), (((1,), (1,)), ((), ())), preferred_element_type=f32)
def tn(a, b):
    return lax.dot_general(a.astype(bf), b.astype(bf), (((0,), (0,)), ((), ())), preferred_element_type=f32)

def level_masks(n):
    row = lax.broadcasted_iota(jnp.int32, (n, n), 0)
    col = lax.broadcasted_iota(jnp.int32, (n, n), 1)
    out = []
    size = 1
    while size < n:
        out.append(((row ^ col) & (-size) == size).astype(f32).astype(bf))
        size *= 2
    return (row == col).astype(f32).astype(bf), out

def inverse_many(many, eye, levels):
    totals = [eye - a * levels[0] for a in many]
    for mask in levels[1:]:
        inner = [nn(a * mask, t).astype(bf) for a, t in zip(many, totals)]
        outer = [nn(t, x).astype(bf) for t, x in zip(totals, inner)]
        totals = [t - x for t, x in zip(totals, outer)]
    return totals

def act_stage(x, prev, aux, w, norm):
    row8 = lax.broadcasted_iota(jnp.int32, (8, 128), 0)
    conv = x * w[0:1]
    sh = []
    for i in range(1, w.shape[0]):
        r = pltpu.roll(x, i, 0)
        p = pltpu.roll(prev, i, 0)
        head = jnp.where(row8 < i, p, r[:8])
        m = jnp.concatenate([head, r[8:]], axis=0) * aux[:, 2 + i:3 + i]
        sh.append(m)
        conv = conv + m * w[i:i + 1]
    s = jax.nn.sigmoid(conv)
    act = conv * s
    if norm:
        rate = lax.rsqrt(jnp.sum(act * act, axis=-1, keepdims=True) + EPS)
        return conv, s, act * rate, rate, sh
    return conv, s, act, None, sh

def masks(aux, segrow):
    n = aux.shape[0]
    row = lax.broadcasted_iota(jnp.int32, (n, n), 0)
    col = lax.broadcasted_iota(jnp.int32, (n, n), 1)
    same = aux[:, 0:1] == segrow
    return same & (row > col), same & (row >= col)

def aux_columns(ref, rows):
    block = ref[0, :, rows]
    return jnp.concatenate([block, jnp.zeros((C - block.shape[0], C), f32)], axis=0).T

def beta_column(block, h):
    lane = lax.broadcasted_iota(jnp.int32, block.shape, 1)
    return jnp.sum(jnp.where(lane == h, jax.nn.sigmoid(block), 0.0), axis=1, keepdims=True)

def prev_rows(ref, lo):
    start = pl.multiple_of(jnp.maximum(lo - 8, 0), 8)
    return jnp.where(lo > 0, ref[0, pl.ds(start, 8), :].astype(f32), 0.0)

def fwd_kernel(q_ref, k_ref, v_ref, g_ref, b_ref, aux_ref, w_ref, gain_ref,
               mixed_ref, t_ref, w_out, p_ref, f_ref, s_ref, fresh_ref, o_ref,
               q_s, u_s, b_s):
    h = pl.program_id(1)
    length = q_ref.shape[1]
    steps = length // C
    eye, levels = level_masks(C)
    def stage_a(group, _):
        lows = [pl.multiple_of((group * GROUP + n) * C, C) for n in range(GROUP)]
        spans = [pl.ds(lo, C) for lo in lows]
        many, keys, right = [], [], []
        for lo, rows in zip(lows, spans):
            aux = aux_columns(aux_ref, rows)
            q = act_stage(q_ref[0, rows, :].astype(f32), prev_rows(q_ref, lo), aux, w_ref[0], True)[2]
            k = act_stage(k_ref[0, rows, :].astype(f32), prev_rows(k_ref, lo), aux, w_ref[1], True)[2]
            v = act_stage(v_ref[0, rows, :].astype(f32), prev_rows(v_ref, lo), aux, w_ref[2], False)[2]
            beta = beta_column(b_ref[0, rows, :].astype(f32), h)
            strict, inclusive = masks(aux, aux_ref[0, 0:1, rows])
            kb = k.astype(bf)
            qb = q.astype(bf)
            both = nt(jnp.concatenate([kb, qb], axis=0), kb)
            many.append(jnp.where(strict, beta * both[:C], 0.0).astype(bf))
            p_ref[0, 0, rows, :] = jnp.where(inclusive, both[C:], 0.0).astype(bf)
            q_s[rows, :] = qb
            keys.append((k * aux[:, 2:3]).astype(bf))
            right.append(jnp.concatenate([(beta * k).astype(bf), (beta * v).astype(bf)], axis=1))
        totals = inverse_many(many, eye, levels)
        wus = [nn(t, r) for t, r in zip(totals, right)]
        kwus = [tn(k, wu) for k, wu in zip(keys, wus)]
        for rows, t, wu, kwu in zip(spans, totals, wus, kwus):
            clast = aux_ref[0, 1:2, rows][:, C - 1:C]
            f_ref[0, 0, rows, :] = (clast * (eye.astype(f32) - kwu[:, :C])).astype(bf)
            b_s[rows, :] = kwu[:, C:]
            t_ref[0, 0, rows, :] = t
            w_out[0, 0, rows, :] = wu[:, :C].astype(bf)
            u_s[rows, :] = wu[:, C:]
        return 0
    lax.fori_loop(0, steps // GROUP, stage_a, 0)
    def scan(c, state):
        rows = pl.ds(pl.multiple_of(c * C, C), C)
        sb = state.astype(bf)
        s_ref[0, 0, rows, :] = sb
        return nn(f_ref[0, 0, rows, :], sb) + b_s[rows, :]
    lax.fori_loop(0, steps, scan, jnp.zeros((C, C), f32), unroll=True)
    def stage_c(c, _):
        rows = pl.ds(pl.multiple_of(c * C, C), C)
        aux = aux_columns(aux_ref, rows)
        carried = aux[:, 1:2]
        ws = nn(jnp.concatenate([w_out[0, 0, rows, :], q_s[rows, :]], axis=0), s_ref[0, 0, rows, :])
        fresh = (u_s[rows, :] - carried * ws[:C]).astype(bf)
        out = carried * ws[C:] + nn(p_ref[0, 0, rows, :], fresh)
        fresh_ref[0, 0, rows, :] = fresh
        o_ref[0, 0, rows, :] = out
        g = g_ref[0, rows, :].astype(f32)
        r = lax.rsqrt(jnp.mean(out * out, axis=-1, keepdims=True) + HEAD_EPS)
        mixed_ref[0, rows, :] = (out * r * gain_ref[0:1] * (g * jax.nn.sigmoid(g))).astype(bf)
        return 0
    lax.fori_loop(0, steps, stage_c, 0, unroll=4)

def specs(length, heads, off):
    return [pl.BlockSpec((1, length, 128), functools.partial(lambda t, b, h: (b, 0, t * heads + h), t)) for t in range(4)] + [
        pl.BlockSpec((1, length, 128), lambda b, h: (b, 0, 4 * heads))]

def mixer_fwd(raw, aux, conv, gain):
    nb, length, width = raw.shape
    heads = (width - 128) // 512
    per = pl.BlockSpec((1, 1, length, 128), lambda b, h: (b, h, 0, 0))
    sh = lambda d: jax.ShapeDtypeStruct((nb, heads, length, 128), d)
    return pl.pallas_call(
        fwd_kernel,
        grid=(nb, heads),
        in_specs=specs(length, heads, 0) + [
            pl.BlockSpec((1, aux.shape[1], length), lambda b, h: (b, 0, 0)),
            pl.BlockSpec((3, conv.shape[1], 128), lambda b, h: (0, 0, h)),
            pl.BlockSpec((1, 128), lambda b, h: (0, 0)),
        ],
        out_specs=[pl.BlockSpec((1, length, 128), lambda b, h: (b, 0, h))] + [per] * 7,
        out_shape=[jax.ShapeDtypeStruct((nb, length, heads * 128), bf)] + [sh(bf)] * 6 + [sh(f32)],
        scratch_shapes=[pltpu.VMEM((length, 128), bf), pltpu.VMEM((length, 128), f32), pltpu.VMEM((length, 128), f32)],
        cost_estimate=lasting(33),
        name="mixer_forward",
    )(raw, raw, raw, raw, raw, aux, conv, gain)

def bwd_kernel(q_ref, k_ref, v_ref, g_ref, b_ref, aux_ref, w_ref, gain_ref,
               t_ref, w_in, p_ref, f_ref, s_ref, fresh_ref, o_ref, dm_ref,
               draw_ref, dconv_ref, dgain_ref,
               do_s, pd_s, base_s, ds_s):
    h = pl.program_id(1)
    heads = pl.num_programs(1)
    length = q_ref.shape[1]
    steps = length // C
    gain = gain_ref[0:1]
    def stage_a(c, dgain):
        lo = pl.multiple_of(c * C, C)
        rows = pl.ds(lo, C)
        aux = aux_columns(aux_ref, rows)
        carried = aux[:, 1:2]
        q = act_stage(q_ref[0, rows, :].astype(f32), prev_rows(q_ref, lo), aux, w_ref[0], True)[2]
        out = o_ref[0, 0, rows, :]
        g = g_ref[0, rows, :].astype(f32)
        dm = dm_ref[0, rows, :].astype(f32)
        s = jax.nn.sigmoid(g)
        r = lax.rsqrt(jnp.mean(out * out, axis=-1, keepdims=True) + HEAD_EPS)
        scaled = out * r
        dn = dm * (g * s)
        dg = dm * scaled * gain * (s * (1.0 + g * (1.0 - s)))
        draw_ref[0, rows, pl.ds(pl.multiple_of((3 * heads + h) * 128, 128), 128)] = dg.astype(bf)
        e = dn * gain
        do = r * (e - scaled * jnp.mean(e * scaled, axis=-1, keepdims=True))
        pd = tn(p_ref[0, 0, rows, :], do)
        do_s[rows, :] = do
        pd_s[rows, :] = pd
        base_s[rows, :] = tn(jnp.concatenate([q.astype(bf), w_in[0, 0, rows, :]], axis=0),
                             jnp.concatenate([carried * do, -carried * pd], axis=0))
        return dgain + jnp.sum((dn * scaled).reshape(C // 8, 8, 128), axis=0)
    dgain = lax.fori_loop(0, steps, stage_a, jnp.zeros((8, 128), f32), unroll=2)
    dgain_ref[0, 0] = dgain
    def scan(j, state):
        c = steps - 1 - j
        rows = pl.ds(pl.multiple_of(c * C, C), C)
        sb = state.astype(bf)
        ds_s[rows, :] = sb
        return tn(f_ref[0, 0, rows, :], sb) + base_s[rows, :]
    lax.fori_loop(0, steps, scan, jnp.zeros((C, C), f32), unroll=True)
    row8 = lax.broadcasted_iota(jnp.int32, (8, 128), 0)
    lane = lax.broadcasted_iota(jnp.int32, (C, 128), 1)

    def conv_back(dconv, nxt, aux, w, raw, sh):
        d = dconv * w[0:1]
        dw = [jnp.sum((dconv * raw).reshape(C // 8, 8, 128), axis=0)]
        for i in range(1, w.shape[0]):
            r = pltpu.roll(dconv, C - i, 0)
            p = pltpu.roll(nxt, 8 - i, 0)
            tailrows = jnp.where(row8 >= 8 - i, p, r[C - 8:])
            m = jnp.concatenate([r[:C - 8], tailrows], axis=0) * aux[:, 5 + i:6 + i]
            d = d + m * w[i:i + 1]
            dw.append(jnp.sum((dconv * sh[i - 1]).reshape(C // 8, 8, 128), axis=0))
        return d, dw

    def stage_c(j, carry):
        nq, nk, nv, dws = carry
        c = steps - 1 - j
        lo = pl.multiple_of(c * C, C)
        rows = pl.ds(lo, C)
        aux = aux_columns(aux_ref, rows)
        carried = aux[:, 1:2]
        tail = aux[:, 2:3]
        xq = q_ref[0, rows, :].astype(f32)
        xk = k_ref[0, rows, :].astype(f32)
        xv = v_ref[0, rows, :].astype(f32)
        cq, sq, q, rq, shq = act_stage(xq, prev_rows(q_ref, lo), aux, w_ref[0], True)
        ck, sk, k, rk, shk = act_stage(xk, prev_rows(k_ref, lo), aux, w_ref[1], True)
        cv, sv, v, _, shv = act_stage(xv, prev_rows(v_ref, lo), aux, w_ref[2], False)
        bblock = b_ref[0, rows, :].astype(f32)
        beta = beta_column(bblock, h)
        strict, inclusive = masks(aux, aux_ref[0, 0:1, rows])
        kb = k.astype(bf)
        qb = q.astype(bf)
        st = s_ref[0, 0, rows, :]
        dst = ds_s[rows, :]
        fresh = fresh_ref[0, 0, rows, :]
        do = do_s[rows, :]
        gram = nt(kb, kb)
        kk = nn(kb, jnp.concatenate([dst, st], axis=1))
        dfresh = pd_s[rows, :] + tail * kk[:, :128]
        x = v - carried * kk[:, 128:]
        y = tn(t_ref[0, 0, rows, :], dfresh)
        dx = beta * y
        cdx = (carried * dx).astype(bf)
        yb = y.astype(bf)
        dob = do.astype(bf)
        both = nt(jnp.concatenate([dob, yb], axis=0), fresh)
        dp = jnp.where(inclusive, both[:C], 0.0)
        da = jnp.where(strict, -both[C:], 0.0)
        dbeta = jnp.sum(y * x, axis=-1, keepdims=True) + jnp.sum(da * gram, axis=-1, keepdims=True)
        dg = beta * da
        dgs = dg + dg.T
        through = nt(jnp.concatenate([carried * do, -(carried * dx)], axis=0), st)
        dpb = dp.astype(bf)
        dq = through[:C] + nn(dpb, kb)
        dk = through[C:] + tn(dpb, qb) + nt(tail * fresh.astype(f32), dst) + nn(dgs, kb)
        dv = dx
        db = dbeta * beta * (1.0 - beta)
        bl = pl.ds(4 * heads * 128, 128)
        @pl.when(h == 0)
        def _():
            draw_ref[0, rows, bl] = jnp.where(lane == 0, db, 0.0).astype(bf)
        @pl.when(h > 0)
        def _():
            old = draw_ref[0, rows, bl]
            draw_ref[0, rows, bl] = jnp.where(lane == h, db.astype(bf).astype(f32), old.astype(f32)).astype(bf)
        dq = rq * (dq - q * jnp.sum(q * dq, axis=-1, keepdims=True))
        dk = rk * (dk - k * jnp.sum(k * dk, axis=-1, keepdims=True))
        dcq = dq * (sq * (1.0 + cq * (1.0 - sq)))
        dck = dk * (sk * (1.0 + ck * (1.0 - sk)))
        dcv = dv * (sv * (1.0 + cv * (1.0 - sv)))
        rq_, wq = conv_back(dcq, nq, aux, w_ref[0], xq, shq)
        rk_, wk = conv_back(dck, nk, aux, w_ref[1], xk, shk)
        rv_, wv = conv_back(dcv, nv, aux, w_ref[2], xv, shv)
        for t, val in ((0, rq_), (1, rk_), (2, rv_)):
            draw_ref[0, rows, pl.ds(pl.multiple_of((t * heads + h) * 128, 128), 128)] = val.astype(bf)
        dws = tuple(a + b for a, b in zip(dws, wq + wk + wv))
        return dcq[:8], dck[:8], dcv[:8], dws
    z8 = jnp.zeros((8, 128), f32)
    taps = w_ref.shape[1]
    _, _, _, dws = lax.fori_loop(0, steps, stage_c, (z8, z8, z8, (z8,) * (3 * taps)), unroll=2)
    for n, d in enumerate(dws):
        dconv_ref[0, 0, n] = d

def mixer_bwd(raw, aux, conv, gain, saved, dmixed):
    nb, length, width = raw.shape
    heads = (width - 128) // 512
    taps = conv.shape[1]
    per = pl.BlockSpec((1, 1, length, 128), lambda b, h: (b, h, 0, 0))
    sh = lambda d: jax.ShapeDtypeStruct((nb, heads, length, 128), d)
    draw, dconv, dgain = pl.pallas_call(
        bwd_kernel,
        grid=(nb, heads),
        in_specs=specs(length, heads, 0) + [
            pl.BlockSpec((1, aux.shape[1], length), lambda b, h: (b, 0, 0)),
            pl.BlockSpec((3, taps, 128), lambda b, h: (0, 0, h)),
            pl.BlockSpec((1, 128), lambda b, h: (0, 0)),
        ] + [per] * 7 + [pl.BlockSpec((1, length, 128), lambda b, h: (b, 0, h))],
        out_specs=[pl.BlockSpec((1, length, width), lambda b, h: (b, 0, 0)),
                   pl.BlockSpec((1, 1, 3 * taps, 8, 128), lambda b, h: (b, h, 0, 0, 0)),
                   pl.BlockSpec((1, 1, 8, 128), lambda b, h: (b, h, 0, 0))],
        out_shape=[jax.ShapeDtypeStruct((nb, length, width), bf),
                   jax.ShapeDtypeStruct((nb, heads, 3 * taps, 8, 128), f32),
                   jax.ShapeDtypeStruct((nb, heads, 8, 128), f32)],
        scratch_shapes=[pltpu.VMEM((length, 128), f32)] * 3 + [pltpu.VMEM((length, 128), bf)],
        cost_estimate=lasting(2),
        name="mixer_backward",
    )(raw, raw, raw, raw, raw, aux, conv, gain, *saved, dmixed)
    dconv = jnp.sum(dconv, axis=(0, 3)).reshape(heads, 3, taps, 128).transpose(1, 2, 0, 3).reshape(3, taps, heads * 128)
    return draw, dconv, jnp.sum(dgain, axis=(0, 1, 2))

def make_aux(segments):
    nb, length = segments.shape
    seg = segments.astype(f32)
    blocks = seg.reshape(nb, length // C, C)
    last = blocks[:, :, -1:]
    before = jnp.concatenate([jnp.full((nb, 1, 1), -1.0, f32), last[:, :-1]], axis=1)
    carried = (blocks == before).astype(f32).reshape(nb, length)
    tail = (blocks == last).astype(f32).reshape(nb, length)
    cols = [seg, carried, tail]
    for i in range(1, 4):
        cols.append((jnp.pad(seg, ((0, 0), (i, 0)), constant_values=-1.0)[:, :length] == seg).astype(f32))
    for i in range(1, 4):
        cols.append((jnp.pad(seg, ((0, 0), (0, i)), constant_values=-1.0)[:, i:] == seg).astype(f32))
    cols += [jnp.zeros_like(seg)] * (16 - len(cols))
    return jnp.stack(cols, axis=1)


SLOTS = ((0, 0, 0), (0, 0, 1), (1, 0, 0), (0, 1, 0), (1, 0, 1), (0, 1, 1), (1, 1, 0), (1, 1, 1))
MESH = pl.DeviceIdType.MESH
VM = pl.BlockSpec(memory_space=pltpu.VMEM)
ANY = pl.BlockSpec(memory_space=pl.ANY)


def slot_place(r, gx, gy):
    dx, dy, dc = SLOTS[r]
    hi, lo = gx // 2, gx % 2
    hi = 1 - hi if dy else hi
    lo = 1 - lo if dc else lo
    return hi * 2 + lo, (1 - gy if dx else gy)


def slot_peer(r, gx, gy):
    px, py = slot_place(r, gx, gy)
    return {"gx": px, "gy": py}


def flipped(index, n, size):
    out, bit = 0, 1
    while bit < size:
        digit = index // bit % 2
        out = out + bit * (1 - digit if n & bit else digit)
        bit *= 2
    return out


def entry_barrier(peers):
    sem = pltpu.get_barrier_semaphore()
    for peer in peers:
        pl.semaphore_signal(sem, inc=1, device_id=peer, device_id_type=MESH)
    pl.semaphore_wait(sem, len(peers))


def remote(src, dst, send, recv, peer):
    return pltpu.make_async_remote_copy(src, dst, send, recv, device_id=peer, device_id_type=MESH)


def nt_dot(a, b):
    return lax.dot_general(a, b, (((1,), (1,)), ((), ())), preferred_element_type=f32)


def nn_dot(a, b):
    return lax.dot_general(a, b, (((1,), (0,)), ((), ())), preferred_element_type=f32)


class Gather:
    COPIES = 13

    def __init__(self, buf, send, recv, gx, gy, over_gx=False):
        rows = buf.shape[1]
        half = rows // 2
        a, b = pl.ds(0, half), pl.ds(half, half)
        core, xn, yn = (slot_peer(r, gx, gy) for r in (1, 2, 3))

        def make(i, src, dst, part, peer):
            return remote(buf.at[src, part], buf.at[dst, part], send.at[i], recv.at[i], peer)

        self.own = [
            make(0, 0, 2, a, xn),
            make(1, 0, 3, a, yn),
            make(2, 0, 2, b, xn),
            make(3, 0, 3, b, yn),
            remote(buf.at[0], buf.at[1], send.at[4], recv.at[4], core),
        ]
        self.over_gx = over_gx
        self.diagonal = [make(5, 2, 6, a, yn) if over_gx else make(5, 3, 6, a, xn), make(6, 2, 6, b, yn)]
        self.cross = [
            make(7, 2, 4, a, core),
            make(8, 2, 4, b, core),
            make(9, 3, 5, a, core),
            make(10, 3, 5, b, core),
            make(11, 6, 7, a, core),
            make(12, 6, 7, b, core),
        ]

    def start(self):
        for c in self.own:
            c.start()

    def step(self, i):
        if i == 1:
            self.own[4].wait_recv()
        elif i == 2:
            self.own[1].wait_recv()
            if not self.over_gx:
                self.diagonal[0].start()
            self.cross[2].start()
            self.own[0].wait_recv()
            if self.over_gx:
                self.diagonal[0].start()
            self.cross[0].start()
            self.own[2].wait_recv()
            self.diagonal[1].start()
            self.cross[1].start()
        elif i == 3:
            self.own[3].wait_recv()
            self.cross[3].start()
        elif i == 4:
            self.cross[0].wait_recv()
            self.cross[1].wait_recv()
        elif i == 5:
            self.cross[2].wait_recv()
            self.cross[3].wait_recv()
        elif i == 6:
            self.diagonal[0].wait_recv()
            self.cross[4].start()
            self.diagonal[1].wait_recv()
            self.cross[5].start()
        elif i == 7:
            self.cross[4].wait_recv()
            self.cross[5].wait_recv()

    def finish(self):
        for c in self.own + self.diagonal + self.cross:
            c.wait_send()


def head_kernel(
    x_ref, wq_ref, wk_ref, wv_ref, wg_ref, wb_ref, gate_ref, up_ref, out_ref, gain_ref,
    normed_ref, raw_ref, hw_ref, own_ref, gu_ref, wo_ref,
    buf, w, low, acc, ag_send, ag_recv, w_send, w_recv, load_sem, out_sem, raw_sem, hw_sem, z_send, z_recv, u_send, u_recv,
):
    gx, gy, dp = lax.axis_index("gx"), lax.axis_index("gy"), lax.axis_index("dp")
    ngx = 4
    piece = gu_ref.shape[0]
    parts = x_ref.shape[1] // piece
    units = gu_ref.shape[1] // 2
    unit_other = pl.multiple_of((1 - gy) * (gate_ref.shape[1] - units), 128)
    turn = flipped(dp, 0, parts)
    rows_sent = pl.ds(pl.multiple_of(turn * piece, piece), piece)
    rows = own_ref.shape[0]
    part = x_ref.shape[1]
    width = wq_ref.shape[1] // 2
    weights = ((wq_ref, width), (wk_ref, width), (wv_ref, width), (wg_ref, width), (wb_ref, 128))
    starts = [0, width, 2 * width, 3 * width, 4 * width]
    xn = slot_peer(2, gx, gy)
    loads = [pltpu.make_async_copy(x_ref, buf.at[0], load_sem.at[5])]
    for i, (ref, n) in enumerate(weights):
        src = ref.at[:, pl.ds(pl.multiple_of(gy * n, 128), n)]
        loads.append(pltpu.make_async_copy(src, w.at[0, :, pl.ds(starts[i], n)], load_sem.at[i]))
    for c in loads:
        c.start()
    peers = [slot_peer(r, gx, gy) for r in (1, 2, 3)] + [{"dp": flipped(dp, n, parts)} for n in range(1, parts)]
    entry_barrier(peers)
    swaps = []
    for i, (ref, n) in enumerate(weights):
        src = ref.at[rows_sent, pl.ds(pl.multiple_of((1 - gy) * n, 128), n)]
        swaps.append(remote(src, w.at[1, rows_sent, pl.ds(starts[i], n)], w_send.at[i], w_recv.at[i], xn))
        swaps[-1].start()
    loads[0].wait()
    gather = Gather(buf, ag_send, ag_recv, gx, gy, True)
    gather.start()
    extra = [
        remote(gate_ref.at[rows_sent, pl.ds(unit_other, units)], gu_ref.at[:, pl.ds(0, units)], u_send.at[0], u_recv.at[0], xn),
        remote(up_ref.at[rows_sent, pl.ds(unit_other, units)], gu_ref.at[:, pl.ds(units, units)], u_send.at[1], u_recv.at[1], xn),
        remote(out_ref.at[pl.ds(pl.multiple_of((1 - gy) * width, width), width), :], wo_ref, u_send.at[2], u_recv.at[2], xn),
    ]
    for c in extra:
        c.start()
    for c in swaps:
        c.wait_recv()
    spread = [
        remote(w.at[1, rows_sent], w.at[1, rows_sent], z_send.at[n], z_recv.at[n], {"dp": flipped(dp, n, parts)}) for n in range(1, parts)
    ]
    for c in spread:
        c.start()
    for c in loads[1:]:
        c.wait()
    keep = pltpu.make_async_copy(w.at[0], hw_ref.at[pl.ds(pl.multiple_of(gy * part, part), part)], hw_sem.at[0])
    keep.start()
    near = pl.ds(pl.multiple_of(gy * part, part), part)
    far = pl.ds(pl.multiple_of((1 - gy) * part, part), part)
    stores = []
    blocks = []

    def pair(n, first, second):
        px, _ = slot_place(first, gx, gy)
        for s in range(2):
            span = pl.ds(s * rows, rows)
            v = s * ngx + px
            i = 2 * n + s
            x0 = buf[first, span, :].astype(f32)
            x1 = buf[second, span, :].astype(f32)
            total = jnp.sum(x0 * x0, axis=-1, keepdims=True) + jnp.sum(x1 * x1, axis=-1, keepdims=True)
            rate = lax.rsqrt(total / (2 * part) + EPS)
            low[i, :, near] = (x0 * rate * gain_ref[:, near]).astype(bf)
            low[i, :, far] = (x1 * rate * gain_ref[:, far]).astype(bf)
            c = pltpu.make_async_copy(low.at[i], normed_ref.at[v], out_sem.at[i])
            c.start()
            stores.append(c)
            acc[i] = nn_dot(low[i, :, near], w[0])
            blocks.append((i, v))

    for step in (1, 2, 3, 4):
        gather.step(step)
        if step == 2:
            pair(0, 0, 2)
            mine = pl.ds(pl.multiple_of(gy * rows, rows), rows)
            own_ref[:, near] = buf[0, mine, :]
            own_ref[:, far] = buf[2, mine, :]
    pair(1, 1, 4)
    gather.step(5)
    gather.step(6)
    pair(2, 3, 6)
    gather.step(7)
    pair(3, 5, 7)
    for c in spread:
        c.wait_recv()
    give = pltpu.make_async_copy(w.at[1], hw_ref.at[far], hw_sem.at[1])
    give.start()

    for i, v in blocks:
        acc[i] += nn_dot(low[i, :, far], w[1])
        c = pltpu.make_async_copy(acc.at[i], raw_ref.at[v], raw_sem.at[i])
        c.start()
        stores.append(c)
    keep.wait()
    give.wait()
    for c in stores:
        c.wait()
    for c in extra:
        c.wait_recv()
    for c in swaps + spread + extra:
        c.wait_send()
    gather.finish()


def head_project(inputs, w_query, w_key, w_value, w_gate_head, w_beta, w_gate, w_up, w_out, gain, units, parts, collective):
    total, part = inputs.shape
    rows = total // 2
    feat = 2 * part
    cols = 2 * w_query.shape[1] + 128
    sd = jax.ShapeDtypeStruct
    return pl.pallas_call(
        head_kernel,
        in_specs=[ANY] * 9 + [VM],
        out_specs=[ANY, ANY, ANY, VM, ANY, ANY],
        out_shape=[
            sd((8, rows, feat), bf),
            sd((8, rows, cols), f32),
            sd((feat, cols), bf),
            sd((rows, feat), bf),
            sd((part // parts, 2 * units), bf),
            sd((w_out.shape[0] // 2, w_out.shape[1]), bf),
        ],
        scratch_shapes=[
            pltpu.VMEM((8, total, part), bf),
            pltpu.VMEM((2, part, cols), bf),
            pltpu.VMEM((8, rows, feat), bf),
            pltpu.VMEM((8, rows, cols), f32),
            pltpu.SemaphoreType.DMA((13,)),
            pltpu.SemaphoreType.DMA((13,)),
            pltpu.SemaphoreType.DMA((5,)),
            pltpu.SemaphoreType.DMA((5,)),
            pltpu.SemaphoreType.DMA((6,)),
            pltpu.SemaphoreType.DMA((8,)),
            pltpu.SemaphoreType.DMA((8,)),
            pltpu.SemaphoreType.DMA((2,)),
            pltpu.SemaphoreType.DMA((4,)),
            pltpu.SemaphoreType.DMA((4,)),
            pltpu.SemaphoreType.DMA((3,)),
            pltpu.SemaphoreType.DMA((3,)),
        ],
        compiler_params=pltpu.CompilerParams(collective_id=collective, has_side_effects=True, vmem_limit_bytes=60 << 20),
        cost_estimate=lasting(80),
        name="head_project",
    )(inputs, w_query, w_key, w_value, w_gate_head, w_beta, w_gate, w_up, w_out, gain)


def mlp_kernel(x_ref, gate_ref, up_ref, down_ref, y_ref, *refs, parts):
    gu_refs, piece_ref, refs = refs[:parts], refs[parts], refs[parts + 1 :]
    mlp_body(parts, x_ref, gate_ref, up_ref, down_ref, y_ref, gu_refs, piece_ref, *refs)


def mlp_body(
    parts, x_ref, gate_ref, up_ref, down_ref, y_ref, gu_refs, piece_ref,
    second_ref, hidden_ref, grads_ref, yrel_ref, gu_out, dn_out,
    wgu, wd, buf, ybuf, hbuf, gbuf, load_sem, w_sem, keep_sem, y_sem, y_out_sem, out_sem, ag_send, ag_recv,
):
    gx, gy = lax.axis_index("gx"), lax.axis_index("gy")
    ngy = 2
    rows = x_ref.shape[0]
    feat = x_ref.shape[1]
    units = wd.shape[0]
    half = feat // 2
    tile = 256
    dp = lax.axis_index("dp")
    unit_mine = pl.multiple_of(gy * (gate_ref.shape[1] - units), 128)
    doubled = gy * (2 * units - gate_ref.shape[1])
    load = pltpu.make_async_copy(x_ref, buf.at[0], load_sem)
    load.start()
    near = pl.ds(pl.multiple_of(gy * half, half), half)
    far = pl.multiple_of((1 - gy) * half, half)
    own_units = pl.ds(unit_mine, units)
    w_loads = [
        pltpu.make_async_copy(gate_ref.at[:, own_units], wgu.at[near, pl.ds(0, units)], w_sem.at[0]),
        pltpu.make_async_copy(up_ref.at[:, own_units], wgu.at[near, pl.ds(units, units)], w_sem.at[1]),
        pltpu.make_async_copy(down_ref.at[own_units, :], wd.at[:, near], w_sem.at[2]),
    ]
    w_loads.append(pltpu.make_async_copy(piece_ref, wd.at[:, pl.ds(far, half)], w_sem.at[3]))
    for n in range(parts):
        turn = flipped(dp, n, parts)
        piece = half // parts
        w_loads.append(
            pltpu.make_async_copy(gu_refs[n], wgu.at[pl.ds(pl.multiple_of(far + turn * piece, piece), piece), :], w_sem.at[4 + n])
        )
    for c in w_loads:
        c.start()
    entry_barrier([slot_peer(r, gx, gy) for r in (1, 2, 3)])
    load.wait()
    gather = Gather(buf, ag_send, ag_recv, gx, gy)
    gather.start()

    def y_load(r, n):
        px, py = slot_place(r, gx, gy)
        return [
            pltpu.make_async_copy(y_ref.at[px * ngy + h, py], ybuf.at[r % 2, :, pl.ds(h * (feat // 2), feat // 2)], y_sem.at[r % 2, h])
            for h in range(2)
        ]

    def y_store(r):
        return pltpu.make_async_copy(ybuf.at[r % 2], yrel_ref.at[r], y_out_sem.at[r % 2])

    for c in y_load(0, 0):
        c.start()
    for c in w_loads:
        c.wait()
    keeps = [pltpu.make_async_copy(wgu, gu_out, keep_sem.at[0]), pltpu.make_async_copy(wd, dn_out, keep_sem.at[1])]
    for c in keeps:
        c.start()

    def outs(r):
        return [
            pltpu.make_async_copy(buf.at[r], second_ref.at[r], out_sem.at[0, r % 2]),
            pltpu.make_async_copy(hbuf.at[r % 2], hidden_ref.at[r], out_sem.at[1, r % 2]),
            pltpu.make_async_copy(gbuf.at[r % 2], grads_ref.at[r], out_sem.at[2, r % 2]),
        ]

    for r in range(8):
        gather.step(r)
        if r >= 2:
            for c in outs(r - 2):
                c.wait()
        if r + 1 < 8:
            if r >= 1:
                y_store(r - 1).wait()
            for c in y_load(r + 1, 0):
                c.start()
        for c in y_load(r, 0):
            c.wait()
        y_store(r).start()

        def body(t, _):
            cols = pl.ds(pl.multiple_of(t * tile, tile), tile)
            up_cols = pl.ds(pl.multiple_of(units + t * tile, tile), tile)
            gate = nn_dot(buf[r], wgu[:, cols])
            up = nn_dot(buf[r], wgu[:, up_cols])
            gh = nt_dot(ybuf[r % 2], wd[cols, :])
            s = jax.nn.sigmoid(gate)
            keep = lax.broadcasted_iota(jnp.int32, gate.shape, 1) + t * tile >= doubled
            act = jnp.where(keep, gate * s, 0.0)
            up = jnp.where(keep, up, 0.0)
            hbuf[r % 2, :, cols] = (act * up).astype(bf)
            gbuf[r % 2, :, up_cols] = (gh * act).astype(bf)
            gbuf[r % 2, :, cols] = (gh * up * s * (1.0 + gate * (1.0 - s))).astype(bf)
            return 0

        lax.fori_loop(0, units // tile, body, 0)
        for c in outs(r):
            c.start()
    for r in (6, 7):
        for c in outs(r):
            c.wait()
        y_store(r).wait()
    gather.finish()
    for c in keeps:
        c.wait()


def mlp_forward(x_own, w_gate, w_up, w_down, y_all, gu_pieces, down_piece, units, collective):
    rows, feat = x_own.shape
    parts = len(gu_pieces)
    sd = jax.ShapeDtypeStruct
    return pl.pallas_call(
        functools.partial(mlp_kernel, parts=parts),
        in_specs=[ANY] * (6 + parts),
        out_specs=[ANY] * 6,
        out_shape=[
            sd((8, rows, feat), bf),
            sd((8, rows, units), bf),
            sd((8, rows, 2 * units), bf),
            sd((8, rows, feat), bf),
            sd((feat, 2 * units), bf),
            sd((units, feat), bf),
        ],
        scratch_shapes=[
            pltpu.VMEM((feat, 2 * units), bf),
            pltpu.VMEM((units, feat), bf),
            pltpu.VMEM((8, rows, feat), bf),
            pltpu.VMEM((2, rows, feat), bf),
            pltpu.VMEM((2, rows, units), bf),
            pltpu.VMEM((2, rows, 2 * units), bf),
            pltpu.SemaphoreType.DMA,
            pltpu.SemaphoreType.DMA((4 + parts,)),
            pltpu.SemaphoreType.DMA((2,)),
            pltpu.SemaphoreType.DMA((2, 2)),
            pltpu.SemaphoreType.DMA((2,)),
            pltpu.SemaphoreType.DMA((3, 2)),
            pltpu.SemaphoreType.DMA((13,)),
            pltpu.SemaphoreType.DMA((13,)),
        ],
        compiler_params=pltpu.CompilerParams(collective_id=collective, has_side_effects=True, vmem_limit_bytes=62 << 20),
        cost_estimate=lasting(68),
        name="mlp_forward",
    )(x_own, w_gate, w_up, w_down, y_all, *gu_pieces, down_piece)


class Scatter:
    def __init__(self, give, take, acc, diag_in, last_in, s_core, r_core, s_link, r_link, gx, gy):
        self.give, self.take, self.acc, self.diag_in, self.last_in = give, take, acc, diag_in, last_in
        core, xn, yn = (slot_peer(r, gx, gy) for r in (1, 2, 3))
        rows = acc.shape[1]
        half = rows // 2
        a, b = pl.ds(0, half), pl.ds(half, half)
        self.a, self.b = a, b
        self.core = [remote(give.at[n], take.at[n], s_core.at[n], r_core.at[n], core) for n in range(4)]

        def link(i, src, dst, peer):
            return remote(src, dst, s_link.at[i], r_link.at[i], peer)

        self.link = [
            link(0, acc.at[0, a], diag_in.at[0], xn),
            link(1, acc.at[0, b], diag_in.at[1], yn),
            link(2, acc.at[1, a], last_in.at[0, a], xn),
            link(3, acc.at[2, b], last_in.at[1, b], yn),
            link(4, acc.at[1, b], last_in.at[0, b], xn),
            link(5, acc.at[2, a], last_in.at[1, a], yn),
        ]

    def run(self, product, self_acc):
        acc = self.acc

        def give_out(n, slot):
            def put(cols, value):
                self.give[n, :, cols] = value.astype(bf)

            product(slot, put)
            self.core[n].start()

        def keep(n, slot):
            def put(cols, value):
                acc[n, :, cols] = value.astype(bf)

            product(slot, put)

        def join(n):
            self.core[n].wait_recv()
            acc[n] = (acc[n].astype(f32) + self.take[n].astype(f32)).astype(bf)

        a, b = self.a, self.b
        give_out(0, 7)
        keep(0, 6)
        give_out(1, 4)
        join(0)
        self.link[0].start()
        self.link[1].start()
        give_out(2, 5)
        keep(1, 2)
        join(1)
        self.link[2].start()
        keep(2, 3)
        join(2)
        self.link[3].start()
        give_out(3, 1)

        def put_self(cols, value):
            self_acc[:, cols] = value

        product(0, put_self)
        self.link[1].wait_recv()
        acc[1, b] = (acc[1, b].astype(f32) + self.diag_in[1].astype(f32)).astype(bf)
        self.link[4].start()
        self.link[0].wait_recv()
        acc[2, a] = (acc[2, a].astype(f32) + self.diag_in[0].astype(f32)).astype(bf)
        self.link[5].start()
        self.core[3].wait_recv()
        self_acc[...] += self.take[3].astype(f32)
        for c in self.link[2:]:
            c.wait_recv()
        self_acc[...] += self.last_in[0].astype(f32) + self.last_in[1].astype(f32)

    def finish(self):
        for c in self.core + self.link:
            c.wait_send()


def scatter_scratch(rows, feat):
    return [
        pltpu.VMEM((4, rows, feat), bf),
        pltpu.VMEM((4, rows, feat), bf),
        pltpu.VMEM((3, rows, feat), bf),
        pltpu.VMEM((2, rows // 2, feat), bf),
        pltpu.VMEM((2, rows, feat), bf),
        pltpu.SemaphoreType.DMA((4,)),
        pltpu.SemaphoreType.DMA((4,)),
        pltpu.SemaphoreType.DMA((6,)),
        pltpu.SemaphoreType.DMA((6,)),
    ]


def own_out_rows(out_ref, piece_ref, w, sem, gy):
    width, part = piece_ref.shape
    near = pl.ds(pl.multiple_of(gy * part, part), part)
    far = pl.ds(pl.multiple_of((1 - gy) * part, part), part)
    return [
        pltpu.make_async_copy(out_ref.at[pl.ds(pl.multiple_of(gy * width, width), width), :], w.at[:, near], sem.at[0]),
        pltpu.make_async_copy(piece_ref, w.at[:, far], sem.at[1]),
    ]


def out_kernel(
    mixed_ref, out_ref, piece_ref, x_ref, gain_ref,
    middle_ref, normed_ref, slots_ref,
    give, take, acc, diag_in, last_in, s_core, r_core, s_link, r_link, lhs, w, total, load_sem, lhs_sem, keep_sem,
):
    gx, gy = lax.axis_index("gx"), lax.axis_index("gy")
    feat = x_ref.shape[1]
    tile = 512
    loads = own_out_rows(out_ref, piece_ref, w, load_sem, gy)
    pulls = {}
    for r in (7, 6, 4, 5, 2, 3, 1, 0):
        px, py = slot_place(r, gx, gy)
        pulls[r] = pltpu.make_async_copy(mixed_ref.at[py * 4 + px], lhs.at[r], lhs_sem.at[r])
    for c in loads + list(pulls.values()):
        c.start()
    entry_barrier([slot_peer(r, gx, gy) for r in (1, 2, 3)])
    for c in loads:
        c.wait()

    def product(slot, put):
        pulls[slot].wait()

        def body(t, _):
            cols = pl.ds(pl.multiple_of(t * tile, tile), tile)
            put(cols, nn_dot(lhs[slot], w[:, cols]))
            return 0

        lax.fori_loop(0, feat // tile, body, 0)

    scatter = Scatter(give, take, acc, diag_in, last_in, s_core, r_core, s_link, r_link, gx, gy)
    scatter.run(product, total)
    keep = pltpu.make_async_copy(lhs, slots_ref, keep_sem)
    keep.start()
    middle = x_ref[...].astype(f32) + total[...]
    middle_ref[...] = middle
    rate = lax.rsqrt(jnp.mean(middle * middle, axis=-1, keepdims=True) + EPS)
    normed_ref[...] = (middle * rate * gain_ref[...]).astype(bf)
    keep.wait()
    scatter.finish()


def out_project(mixed, w_out, piece, x_own, gain, collective):
    rows, feat = x_own.shape
    width = mixed.shape[2]
    sd = jax.ShapeDtypeStruct
    return pl.pallas_call(
        out_kernel,
        in_specs=[ANY, ANY, ANY, VM, VM],
        out_specs=[VM, VM, ANY],
        out_shape=[sd((rows, feat), f32), sd((rows, feat), bf), sd(mixed.shape, bf)],
        scratch_shapes=scatter_scratch(rows, feat)
        + [
            pltpu.VMEM(mixed.shape, bf),
            pltpu.VMEM((width, feat), bf),
            pltpu.VMEM((rows, feat), f32),
            pltpu.SemaphoreType.DMA((2,)),
            pltpu.SemaphoreType.DMA((8,)),
            pltpu.SemaphoreType.DMA,
        ],
        compiler_params=pltpu.CompilerParams(collective_id=collective, has_side_effects=True, vmem_limit_bytes=60 << 20),
        cost_estimate=lasting(44),
        name="out_project",
    )(mixed, w_out, piece, x_own, gain)


def back_kernel(
    grads_ref, wgu_ref, out_ref, piece_ref, middle_ref, y_ref, gain_ref,
    mid_ref, gmix_ref, dgain_ref,
    give, take, acc, diag_in, last_in, s_core, r_core, s_link, r_link,
    lhs, wgu, w, total, buf, gstage, y_own, load_sem, lhs_sem, ag_send, ag_recv, mid_sem, gmix_sem,
):
    gx, gy = lax.axis_index("gx"), lax.axis_index("gy")
    rows, feat = middle_ref.shape
    tile = 512
    load = pltpu.make_async_copy(wgu_ref, wgu, load_sem.at[2])
    outs = own_out_rows(out_ref, piece_ref, w, load_sem, gy)
    order = (7, 6, 4, 5, 2, 3, 1, 0)
    pulls = {r: pltpu.make_async_copy(grads_ref.at[r], lhs.at[r], lhs_sem.at[r]) for r in order}
    pulls[7].start()
    load.start()
    for r in order[1:]:
        pulls[r].start()
    outs.append(pltpu.make_async_copy(y_ref.at[0], y_own, load_sem.at[3]))
    for c in outs:
        c.start()
    entry_barrier([slot_peer(r, gx, gy) for r in (1, 2, 3)])
    load.wait()

    def product(slot, put):
        pulls[slot].wait()

        def body(t, _):
            cols = pl.ds(pl.multiple_of(t * tile, tile), tile)
            put(cols, nt_dot(lhs[slot], wgu[cols, :]))
            return 0

        lax.fori_loop(0, feat // tile, body, 0)

    scatter = Scatter(give, take, acc, diag_in, last_in, s_core, r_core, s_link, r_link, gx, gy)
    scatter.run(product, total)
    middle = middle_ref[...]
    incoming = total[...]
    rate = lax.rsqrt(jnp.mean(middle * middle, axis=-1, keepdims=True) + EPS)
    scaled = gain_ref[...] * incoming
    inner = jnp.mean(middle * scaled, axis=-1, keepdims=True)
    for c in outs:
        c.wait()
    buf[0] = (y_own[...].astype(f32) + rate * scaled - middle * (rate * rate * rate) * inner).astype(bf)
    gather = Gather(buf, ag_send, ag_recv, gx, gy)
    gather.start()
    dgain_ref[...] = jnp.sum((incoming * middle * rate).reshape(rows // 8, 8, feat), axis=0)
    stores = []
    for r in range(8):
        gather.step(r)
        px, py = slot_place(r, gx, gy)
        gstage[r] = nt_dot(buf[r], w[...]).astype(bf)
        stores.append(pltpu.make_async_copy(gstage.at[r], gmix_ref.at[py * 4 + px], gmix_sem.at[r]))
        stores.append(pltpu.make_async_copy(buf.at[r], mid_ref.at[r], mid_sem.at[r]))
        for c in stores[-2:]:
            c.start()
    for c in stores:
        c.wait()
    gather.finish()
    scatter.finish()


def mlp_backward(grads, gate_up, w_out, piece, middle, y_rel, gain, collective):
    rows, feat = middle.shape
    width = piece.shape[0]
    sd = jax.ShapeDtypeStruct
    return pl.pallas_call(
        back_kernel,
        in_specs=[ANY, ANY, ANY, ANY, VM, ANY, VM],
        out_specs=[ANY, ANY, VM],
        out_shape=[sd((8, rows, feat), bf), sd((8, rows, width), bf), sd((8, feat), f32)],
        scratch_shapes=scatter_scratch(rows, feat)
        + [
            pltpu.VMEM(grads.shape, bf),
            pltpu.VMEM(gate_up.shape, bf),
            pltpu.VMEM((width, feat), bf),
            pltpu.VMEM((rows, feat), f32),
            pltpu.VMEM((8, rows, feat), bf),
            pltpu.VMEM((8, rows, width), bf),
            pltpu.VMEM((rows, feat), bf),
            pltpu.SemaphoreType.DMA((4,)),
            pltpu.SemaphoreType.DMA((8,)),
            pltpu.SemaphoreType.DMA((13,)),
            pltpu.SemaphoreType.DMA((13,)),
            pltpu.SemaphoreType.DMA((8,)),
            pltpu.SemaphoreType.DMA((8,)),
        ],
        compiler_params=pltpu.CompilerParams(collective_id=collective, has_side_effects=True, vmem_limit_bytes=63 << 20),
        cost_estimate=lasting(20),
        name="mlp_backward",
    )(grads, gate_up, w_out, piece, middle, y_rel, gain)


def scatter_kernel(lhs_ref, w_ref, out_ref, give, take, acc, diag_in, last_in, s_core, r_core, s_link, r_link, lhs, w, total, load_sem, lhs_sem, *, slots, transposed):
    gx, gy = lax.axis_index("gx"), lax.axis_index("gy")
    rows, feat = out_ref.shape
    tile = 512
    load = pltpu.make_async_copy(w_ref, w, load_sem)

    def source(r):
        if slots:
            return lhs_ref.at[r]
        px, py = slot_place(r, gx, gy)
        return lhs_ref.at[py * 4 + px]

    order = (7, 6, 4, 5, 2, 3, 1, 0)
    pulls = {r: pltpu.make_async_copy(source(r), lhs.at[r], lhs_sem.at[r]) for r in order}
    pulls[7].start()
    load.start()
    for r in order[1:]:
        pulls[r].start()
    entry_barrier([slot_peer(r, gx, gy) for r in (1, 2, 3)])
    load.wait()

    def product(slot, put):
        pulls[slot].wait()

        def body(t, _):
            cols = pl.ds(pl.multiple_of(t * tile, tile), tile)
            put(cols, nn_dot(lhs[slot], w[:, cols]) if transposed else nt_dot(lhs[slot], w[cols, :]))
            return 0

        lax.fori_loop(0, feat // tile, body, 0)

    scatter = Scatter(give, take, acc, diag_in, last_in, s_core, r_core, s_link, r_link, gx, gy)
    scatter.run(product, total)
    out_ref[...] = total[...]
    scatter.finish()


def product_scatter(lhs, w, collective, slots, transposed):
    _, rows, depth = lhs.shape
    feat = w.shape[1] if transposed else w.shape[0]
    return pl.pallas_call(
        functools.partial(scatter_kernel, slots=slots, transposed=transposed),
        in_specs=[ANY, ANY],
        out_specs=VM,
        out_shape=jax.ShapeDtypeStruct((rows, feat), f32),
        scratch_shapes=scatter_scratch(rows, feat)
        + [
            pltpu.VMEM(lhs.shape, bf),
            pltpu.VMEM(w.shape, bf),
            pltpu.VMEM((rows, feat), f32),
            pltpu.SemaphoreType.DMA,
            pltpu.SemaphoreType.DMA((8,)),
        ],
        compiler_params=pltpu.CompilerParams(collective_id=collective, has_side_effects=True, vmem_limit_bytes=60 << 20),
        cost_estimate=lasting(5),
        name="product_scatter",
    )(lhs, w)


def dot(a, b):
    return lax.dot_general(a, b, (((1,), (0,)), ((), ())), preferred_element_type=f32)


def dot_t(a, b):
    return lax.dot_general(a, b, (((1,), (1,)), ((), ())), preferred_element_type=f32)


def dot_w(a, b):
    return lax.dot_general(a, b, (((0,), (0,)), ((), ())), preferred_element_type=f32)


def swap(value):
    return lax.ppermute(value, "gy", [(0, 1), (1, 0)])


def in_order(mine, other, axis):
    first = lax.axis_index("gy") == 0
    return jnp.concatenate([jnp.where(first, mine, other), jnp.where(first, other, mine)], axis=axis)


def halves(value, axis):
    size = value.shape[axis] // 2
    mine = lax.axis_index("gy")
    return (
        lax.dynamic_slice_in_dim(value, mine * size, size, axis),
        lax.dynamic_slice_in_dim(value, (1 - mine) * size, size, axis),
    )


def to_final(own):
    mine, other = halves(own, 1)
    return in_order(mine[None], swap(other)[None], 0)


def rate_of(value):
    return lax.rsqrt(jnp.mean(value * value, axis=-1, keepdims=True) + EPS)


def scatter_dp(value):
    return lax.psum_scatter(value.astype(bf), "dp", scatter_dimension=0, tiled=True)


def rows_to_dp(left, right):
    part = left.shape[1] // 2
    halves_of = [dot_w(left[:, i * part : (i + 1) * part], right).astype(bf) for i in range(2)]
    return halves_of


def sort_halves(parts):
    first = lax.axis_index("gy") == 0
    return jnp.where(first, parts[0], parts[1]), swap(jnp.where(first, parts[1], parts[0]))


def sum_axis(value, axis):
    size = lax.axis_size(axis)
    step = 1
    while step < size:
        value = value + lax.ppermute(value, axis, [(i, i ^ step) for i in range(size)])
        step *= 2
    return value


def shards(
    inputs,
    segments,
    norm_gain,
    w_query,
    w_key,
    w_value,
    w_beta,
    w_gate_head,
    conv_kernel,
    head_gain,
    w_out,
    mlp_gain,
    w_gate,
    w_up,
    w_down,
    grad_y,
):
    ngx, ngy, ndp = lax.axis_size("gx"), lax.axis_size("gy"), lax.axis_size("dp")
    gx, gy = lax.axis_index("gx"), lax.axis_index("gy")
    nb, part_rows, part_feat = inputs.shape
    length, feat = part_rows * ngx, part_feat * ngy
    tokens = nb * length
    own_rows = tokens // (ngx * ngy)
    heads = w_beta.shape[1] // ngy
    width = w_query.shape[1] // ngy
    beta_w = jnp.pad(w_beta.T.reshape(ngy, heads, part_feat), ((0, 0), (0, 128 - heads), (0, 0))).reshape(ngy * 128, part_feat).T
    block = w_gate.shape[1]
    units = -(-block // (ngy * 256)) * 256
    parts = ndp if ndp == 4 else 1
    normed, raw, head_w, x_own, gu_piece, out_piece = head_project(
        inputs.reshape(nb * part_rows, part_feat), w_query, w_key, w_value, w_gate_head, beta_w, w_gate, w_up, w_out,
        norm_gain[None], units, parts, 5,
    )
    normed = normed.reshape(tokens, feat)
    raw = raw.reshape(nb, length, -1)

    def around(value):
        return [value] + [lax.ppermute(value, "dp", [(i, i ^ n) for i in range(ndp)]) for n in range(1, parts)]

    gu_pieces = around(gu_piece)
    x_own, grad_y, w_down = lax.optimization_barrier((x_own, grad_y, w_down))
    down_piece = swap(lax.dynamic_slice_in_dim(w_down, (1 - gy) * (block - units), units, 0))
    y_all = lax.all_gather(grad_y, ("gx", "gy"), axis=0, tiled=False)

    aux = make_aux(segments)
    conv_start = (gx * ngy + gy) * width
    conv_local = lax.dynamic_slice_in_dim(conv_kernel, conv_start, width, 2)
    gain_row = head_gain[None]
    mixed, *saved = mixer_fwd(raw, aux, conv_local, gain_row)
    middle, second_own, mixed_slots = out_project(
        mixed.reshape(8, own_rows, width), w_out, out_piece, x_own, mlp_gain[None], 1
    )
    second, hidden, grads, y_rel, gate_up, down_w = mlp_forward(
        second_own, w_gate, w_up, w_down, y_all, gu_pieces, down_piece, units, 6
    )
    second_flat, hidden_flat = second.reshape(tokens, feat), hidden.reshape(tokens, units)
    grads_flat, y_flat = grads.reshape(tokens, 2 * units), y_rel.reshape(tokens, feat)
    half = feat // 2
    gu_first = dot_w(second_flat[:, :half], grads_flat).astype(bf)
    hidden_flat, gu_first = lax.optimization_barrier((hidden_flat, gu_first))
    down_grad = dot_w(hidden_flat, y_flat).astype(bf)
    second_flat, down_grad = lax.optimization_barrier((second_flat, down_grad))
    down_keep, down_send = halves(down_grad, 1)
    down_both = jnp.stack([down_keep, swap(down_send)])
    gu_second = dot_w(second_flat[:, half:], grads_flat).astype(bf)
    grads, gu_second = lax.optimization_barrier((grads, gu_second))
    gu_sums = [scatter_dp(gu_first), scatter_dp(gu_second)]
    first, last = down_both[gy], down_both[1 - gy]
    down_rows = jnp.concatenate([first, last[2 * units - block :]], axis=0)

    mid_slots, grad_mixed, mlp_gain_parts = mlp_backward(
        grads, gate_up, w_out, out_piece, middle, y_rel, mlp_gain[None], 2
    )
    grad_mixed, mid_slots, down_rows, *gu_sums = lax.optimization_barrier((grad_mixed, mid_slots, down_rows, *gu_sums))
    down_sum = scatter_dp(down_rows)
    mid_low = mid_slots[0]
    out_grad = dot_w(mixed_slots.reshape(tokens, width), mid_slots.reshape(tokens, feat)).astype(bf)
    out_keep, out_send = halves(out_grad, 1)
    out_rows = in_order(out_keep, swap(out_send), 0)
    draw, conv_grad, gain_grad = mixer_bwd(
        raw, aux, conv_local, gain_row, saved, grad_mixed.reshape(nb, length, width)
    )
    draw = draw.reshape(tokens, -1)
    draw, down_sum, out_rows = lax.optimization_barrier((draw, down_sum, out_rows))
    out_sum = scatter_dp(out_rows)
    main = 4 * width
    head_grads = rows_to_dp(normed, draw[:, :main])
    beta_grad = dot_w(normed, draw[:, main:])
    norm_gain_grad = (
        jnp.sum(jnp.concatenate(head_grads, axis=0).astype(f32) * head_w[:, :main].astype(f32), axis=1)
        + jnp.sum(beta_grad * head_w[:, main:].astype(f32), axis=1)
    ) / norm_gain
    draw, hidden, out_sum, *head_grads = lax.optimization_barrier((draw, hidden, out_sum, *head_grads))
    sum_down, sum_out = down_sum.astype(f32), out_sum.astype(f32)
    grad_gu_mine, grad_gu_other = sort_halves(gu_sums)
    head_sums = [scatter_dp(g) for g in head_grads]
    grad_normed = product_scatter(draw.reshape(8, own_rows, -1), head_w, 3, False, False)
    x_wide_own = x_own.astype(f32)
    rate_own = rate_of(x_wide_own)
    scaled = norm_gain * grad_normed
    inner = jnp.mean(x_wide_own * scaled, axis=-1, keepdims=True)
    norm_one = rate_own * scaled - x_wide_own * (rate_own * rate_own * rate_own) * inner
    grad_inputs = to_final((mid_low.astype(f32) + norm_one).astype(bf))
    layer_out = to_final((middle + product_scatter(hidden, down_w, 4, True, True)).astype(bf))

    head_mine, head_other = sort_halves(head_sums)

    def unit_columns(i):
        part = slice(i * units, (i + 1) * units)
        both = jnp.stack([grad_gu_mine[:, part], grad_gu_other[:, part]])
        return jnp.concatenate([both[gy], both[1 - gy][:, 2 * units - block :]], axis=1).astype(f32)

    sum_gate, sum_up = unit_columns(0), unit_columns(1)

    def head_part(i, n):
        return in_order(head_mine[:, i : i + n], head_other[:, i : i + n], 1).astype(f32)

    sum_query, sum_key, sum_value, sum_head_gate = (head_part(i * width, width) for i in range(4))

    small = jnp.concatenate(
        [beta_grad[:, :heads].T.reshape(-1), conv_grad.reshape(-1), norm_gain_grad, jnp.sum(mlp_gain_parts, axis=0), gain_grad]
    )
    small = sum_axis(small, "dp")
    beta_sum, small = small[: heads * feat].reshape(heads, feat), small[heads * feat :]
    beta_rows = feat // (ngy * ndp)
    beta_mine, beta_other = (
        lax.dynamic_slice_in_dim(beta_sum, (side * ndp + lax.axis_index("dp")) * beta_rows, beta_rows, 1) for side in (gy, 1 - gy)
    )
    sum_beta = in_order(beta_mine, swap(beta_other), 0).T
    n_conv = conv_grad.size
    conv_full = lax.dynamic_update_slice_in_dim(
        jnp.zeros(conv_kernel.shape, f32), small[:n_conv].reshape(conv_grad.shape), conv_start, 2
    )
    small = sum_axis(sum_axis(jnp.concatenate([conv_full.reshape(-1), small[n_conv:]]), "gx"), "gy")
    n_conv = conv_full.size
    conv_sum = small[:n_conv].reshape(conv_kernel.shape)
    norm_sum, mlp_sum, gain_sum = jnp.split(small[n_conv:], [feat, 2 * feat])
    return (
        layer_out,
        grad_inputs,
        norm_sum,
        sum_query,
        sum_key,
        sum_value,
        sum_beta,
        sum_head_gate,
        conv_sum,
        gain_sum,
        sum_out,
        mlp_sum,
        sum_gate,
        sum_up,
        sum_down,
    )


def solution(mesh):
    cols = P("gy", "gx")
    rows = P("gx", "gy")
    acts = P("dp", "gx", "gy")
    cols_out = P(("gy", "dp"), "gx")
    rows_out = P(("gx", "dp"), "gy")
    return jax.shard_map(
        shards,
        mesh=mesh,
        in_specs=(acts, P("dp", None), P(), cols, cols, cols, cols, cols, P(), P(), rows, P(), cols, cols, rows, acts),
        out_specs=(
            acts,
            acts,
            P(),
            cols_out,
            cols_out,
            cols_out,
            cols_out,
            cols_out,
            P(),
            P(),
            rows_out,
            P(),
            cols_out,
            cols_out,
            rows_out,
        ),
        check_vma=False,
    )
```

```python
import jax, jax.numpy as jnp
from jax import lax
from jax.experimental import pallas as pl
from jax.experimental.pallas import tpu as pltpu
import functools
from jax.sharding import PartitionSpec as P
EPS = 1e-6
HEAD_EPS = 0.01
C = 128
bf = jnp.bfloat16
f32 = jnp.float32
GROUP = 8

def lasting(us):
    return pl.CostEstimate(flops=int(us * 1.15e9), bytes_accessed=1 << 20, transcendentals=0)

def nn(a, b):
    return lax.dot_general(a.astype(bf), b.astype(bf), (((1,), (0,)), ((), ())), preferred_element_type=f32)
def nt(a, b):
    return lax.dot_general(a.astype(bf), b.astype(bf), (((1,), (1,)), ((), ())), preferred_element_type=f32)
def tn(a, b):
    return lax.dot_general(a.astype(bf), b.astype(bf), (((0,), (0,)), ((), ())), preferred_element_type=f32)

def level_masks(n):
    row = lax.broadcasted_iota(jnp.int32, (n, n), 0)
    col = lax.broadcasted_iota(jnp.int32, (n, n), 1)
    out = []
    size = 1
    while size < n:
        out.append(((row ^ col) & (-size) == size).astype(f32).astype(bf))
        size *= 2
    return (row == col).astype(f32).astype(bf), out

def inverse_many(many, eye, levels):
    totals = [eye - a * levels[0] for a in many]
    for mask in levels[1:]:
        inner = [nn(a * mask, t).astype(bf) for a, t in zip(many, totals)]
        outer = [nn(t, x).astype(bf) for t, x in zip(totals, inner)]
        totals = [t - x for t, x in zip(totals, outer)]
    return totals

def act_stage(x, prev, aux, w, norm):
    row8 = lax.broadcasted_iota(jnp.int32, (8, 128), 0)
    conv = x * w[0:1]
    sh = []
    for i in range(1, w.shape[0]):
        r = pltpu.roll(x, i, 0)
        p = pltpu.roll(prev, i, 0)
        head = jnp.where(row8 < i, p, r[:8])
        m = jnp.concatenate([head, r[8:]], axis=0) * aux[:, 2 + i:3 + i]
        sh.append(m)
        conv = conv + m * w[i:i + 1]
    s = jax.nn.sigmoid(conv)
    act = conv * s
    if norm:
        rate = lax.rsqrt(jnp.sum(act * act, axis=-1, keepdims=True) + EPS)
        return conv, s, act * rate, rate, sh
    return conv, s, act, None, sh

def masks(aux, segrow):
    n = aux.shape[0]
    row = lax.broadcasted_iota(jnp.int32, (n, n), 0)
    col = lax.broadcasted_iota(jnp.int32, (n, n), 1)
    same = aux[:, 0:1] == segrow
    return same & (row > col), same & (row >= col)

def aux_columns(ref, rows):
    block = ref[0, :, rows]
    return jnp.concatenate([block, jnp.zeros((C - block.shape[0], C), f32)], axis=0).T

def beta_column(block, h):
    lane = lax.broadcasted_iota(jnp.int32, block.shape, 1)
    return jnp.sum(jnp.where(lane == h, jax.nn.sigmoid(block), 0.0), axis=1, keepdims=True)

def prev_rows(ref, lo):
    start = pl.multiple_of(jnp.maximum(lo - 8, 0), 8)
    return jnp.where(lo > 0, ref[0, pl.ds(start, 8), :].astype(f32), 0.0)

def fwd_kernel(q_ref, k_ref, v_ref, g_ref, b_ref, aux_ref, w_ref, gain_ref,
               mixed_ref, t_ref, w_out, p_ref, f_ref, s_ref, fresh_ref, o_ref,
               q_s, u_s, b_s):
    h = pl.program_id(1)
    length = q_ref.shape[1]
    steps = length // C
    eye, levels = level_masks(C)
    def stage_a(group, _):
        lows = [pl.multiple_of((group * GROUP + n) * C, C) for n in range(GROUP)]
        spans = [pl.ds(lo, C) for lo in lows]
        many, keys, right = [], [], []
        for lo, rows in zip(lows, spans):
            aux = aux_columns(aux_ref, rows)
            q = act_stage(q_ref[0, rows, :].astype(f32), prev_rows(q_ref, lo), aux, w_ref[0], True)[2]
            k = act_stage(k_ref[0, rows, :].astype(f32), prev_rows(k_ref, lo), aux, w_ref[1], True)[2]
            v = act_stage(v_ref[0, rows, :].astype(f32), prev_rows(v_ref, lo), aux, w_ref[2], False)[2]
            beta = beta_column(b_ref[0, rows, :].astype(f32), h)
            strict, inclusive = masks(aux, aux_ref[0, 0:1, rows])
            kb = k.astype(bf)
            qb = q.astype(bf)
            both = nt(jnp.concatenate([kb, qb], axis=0), kb)
            many.append(jnp.where(strict, beta * both[:C], 0.0).astype(bf))
            p_ref[0, 0, rows, :] = jnp.where(inclusive, both[C:], 0.0).astype(bf)
            q_s[rows, :] = qb
            keys.append((k * aux[:, 2:3]).astype(bf))
            right.append(jnp.concatenate([(beta * k).astype(bf), (beta * v).astype(bf)], axis=1))
        totals = inverse_many(many, eye, levels)
        wus = [nn(t, r) for t, r in zip(totals, right)]
        kwus = [tn(k, wu) for k, wu in zip(keys, wus)]
        for rows, t, wu, kwu in zip(spans, totals, wus, kwus):
            clast = aux_ref[0, 1:2, rows][:, C - 1:C]
            f_ref[0, 0, rows, :] = (clast * (eye.astype(f32) - kwu[:, :C])).astype(bf)
            b_s[rows, :] = kwu[:, C:]
            t_ref[0, 0, rows, :] = t
            w_out[0, 0, rows, :] = wu[:, :C].astype(bf)
            u_s[rows, :] = wu[:, C:]
        return 0
    lax.fori_loop(0, steps // GROUP, stage_a, 0)
    def scan(c, state):
        rows = pl.ds(pl.multiple_of(c * C, C), C)
        sb = state.astype(bf)
        s_ref[0, 0, rows, :] = sb
        return nn(f_ref[0, 0, rows, :], sb) + b_s[rows, :]
    lax.fori_loop(0, steps, scan, jnp.zeros((C, C), f32), unroll=True)
    def stage_c(c, _):
        rows = pl.ds(pl.multiple_of(c * C, C), C)
        aux = aux_columns(aux_ref, rows)
        carried = aux[:, 1:2]
        ws = nn(jnp.concatenate([w_out[0, 0, rows, :], q_s[rows, :]], axis=0), s_ref[0, 0, rows, :])
        fresh = (u_s[rows, :] - carried * ws[:C]).astype(bf)
        out = carried * ws[C:] + nn(p_ref[0, 0, rows, :], fresh)
        fresh_ref[0, 0, rows, :] = fresh
        o_ref[0, 0, rows, :] = out
        g = g_ref[0, rows, :].astype(f32)
        r = lax.rsqrt(jnp.mean(out * out, axis=-1, keepdims=True) + HEAD_EPS)
        mixed_ref[0, rows, :] = (out * r * gain_ref[0:1] * (g * jax.nn.sigmoid(g))).astype(bf)
        return 0
    lax.fori_loop(0, steps, stage_c, 0, unroll=4)

def specs(length, heads, off):
    return [pl.BlockSpec((1, length, 128), functools.partial(lambda t, b, h: (b, 0, t * heads + h), t)) for t in range(4)] + [
        pl.BlockSpec((1, length, 128), lambda b, h: (b, 0, 4 * heads))]

def mixer_fwd(raw, aux, conv, gain):
    nb, length, width = raw.shape
    heads = (width - 128) // 512
    per = pl.BlockSpec((1, 1, length, 128), lambda b, h: (b, h, 0, 0))
    sh = lambda d: jax.ShapeDtypeStruct((nb, heads, length, 128), d)
    return pl.pallas_call(
        fwd_kernel,
        grid=(nb, heads),
        in_specs=specs(length, heads, 0) + [
            pl.BlockSpec((1, aux.shape[1], length), lambda b, h: (b, 0, 0)),
            pl.BlockSpec((3, conv.shape[1], 128), lambda b, h: (0, 0, h)),
            pl.BlockSpec((1, 128), lambda b, h: (0, 0)),
        ],
        out_specs=[pl.BlockSpec((1, length, 128), lambda b, h: (b, 0, h))] + [per] * 7,
        out_shape=[jax.ShapeDtypeStruct((nb, length, heads * 128), bf)] + [sh(bf)] * 6 + [sh(f32)],
        scratch_shapes=[pltpu.VMEM((length, 128), bf), pltpu.VMEM((length, 128), f32), pltpu.VMEM((length, 128), f32)],
        cost_estimate=lasting(33),
        name="mixer_forward",
    )(raw, raw, raw, raw, raw, aux, conv, gain)

def bwd_kernel(q_ref, k_ref, v_ref, g_ref, b_ref, aux_ref, w_ref, gain_ref,
               t_ref, w_in, p_ref, f_ref, s_ref, fresh_ref, o_ref, dm_ref,
               draw_ref, dconv_ref, dgain_ref,
               do_s, pd_s, base_s, ds_s):
    h = pl.program_id(1)
    heads = pl.num_programs(1)
    length = q_ref.shape[1]
    steps = length // C
    gain = gain_ref[0:1]
    def stage_a(c, dgain):
        lo = pl.multiple_of(c * C, C)
        rows = pl.ds(lo, C)
        aux = aux_columns(aux_ref, rows)
        carried = aux[:, 1:2]
        q = act_stage(q_ref[0, rows, :].astype(f32), prev_rows(q_ref, lo), aux, w_ref[0], True)[2]
        out = o_ref[0, 0, rows, :]
        g = g_ref[0, rows, :].astype(f32)
        dm = dm_ref[0, rows, :].astype(f32)
        s = jax.nn.sigmoid(g)
        r = lax.rsqrt(jnp.mean(out * out, axis=-1, keepdims=True) + HEAD_EPS)
        scaled = out * r
        dn = dm * (g * s)
        dg = dm * scaled * gain * (s * (1.0 + g * (1.0 - s)))
        draw_ref[0, rows, pl.ds(pl.multiple_of((3 * heads + h) * 128, 128), 128)] = dg.astype(bf)
        e = dn * gain
        do = r * (e - scaled * jnp.mean(e * scaled, axis=-1, keepdims=True))
        pd = tn(p_ref[0, 0, rows, :], do)
        do_s[rows, :] = do
        pd_s[rows, :] = pd
        base_s[rows, :] = tn(jnp.concatenate([q.astype(bf), w_in[0, 0, rows, :]], axis=0),
                             jnp.concatenate([carried * do, -carried * pd], axis=0))
        return dgain + jnp.sum((dn * scaled).reshape(C // 8, 8, 128), axis=0)
    dgain = lax.fori_loop(0, steps, stage_a, jnp.zeros((8, 128), f32), unroll=2)
    dgain_ref[0, 0] = dgain
    def scan(j, state):
        c = steps - 1 - j
        rows = pl.ds(pl.multiple_of(c * C, C), C)
        sb = state.astype(bf)
        ds_s[rows, :] = sb
        return tn(f_ref[0, 0, rows, :], sb) + base_s[rows, :]
    lax.fori_loop(0, steps, scan, jnp.zeros((C, C), f32), unroll=True)
    row8 = lax.broadcasted_iota(jnp.int32, (8, 128), 0)
    lane = lax.broadcasted_iota(jnp.int32, (C, 128), 1)

    def conv_back(dconv, nxt, aux, w, raw, sh):
        d = dconv * w[0:1]
        dw = [jnp.sum((dconv * raw).reshape(C // 8, 8, 128), axis=0)]
        for i in range(1, w.shape[0]):
            r = pltpu.roll(dconv, C - i, 0)
            p = pltpu.roll(nxt, 8 - i, 0)
            tailrows = jnp.where(row8 >= 8 - i, p, r[C - 8:])
            m = jnp.concatenate([r[:C - 8], tailrows], axis=0) * aux[:, 5 + i:6 + i]
            d = d + m * w[i:i + 1]
            dw.append(jnp.sum((dconv * sh[i - 1]).reshape(C // 8, 8, 128), axis=0))
        return d, dw

    def stage_c(j, carry):
        nq, nk, nv, dws = carry
        c = steps - 1 - j
        lo = pl.multiple_of(c * C, C)
        rows = pl.ds(lo, C)
        aux = aux_columns(aux_ref, rows)
        carried = aux[:, 1:2]
        tail = aux[:, 2:3]
        xq = q_ref[0, rows, :].astype(f32)
        xk = k_ref[0, rows, :].astype(f32)
        xv = v_ref[0, rows, :].astype(f32)
        cq, sq, q, rq, shq = act_stage(xq, prev_rows(q_ref, lo), aux, w_ref[0], True)
        ck, sk, k, rk, shk = act_stage(xk, prev_rows(k_ref, lo), aux, w_ref[1], True)
        cv, sv, v, _, shv = act_stage(xv, prev_rows(v_ref, lo), aux, w_ref[2], False)
        bblock = b_ref[0, rows, :].astype(f32)
        beta = beta_column(bblock, h)
        strict, inclusive = masks(aux, aux_ref[0, 0:1, rows])
        kb = k.astype(bf)
        qb = q.astype(bf)
        st = s_ref[0, 0, rows, :]
        dst = ds_s[rows, :]
        fresh = fresh_ref[0, 0, rows, :]
        do = do_s[rows, :]
        gram = nt(kb, kb)
        kk = nn(kb, jnp.concatenate([dst, st], axis=1))
        dfresh = pd_s[rows, :] + tail * kk[:, :128]
        x = v - carried * kk[:, 128:]
        y = tn(t_ref[0, 0, rows, :], dfresh)
        dx = beta * y
        cdx = (carried * dx).astype(bf)
        yb = y.astype(bf)
        dob = do.astype(bf)
        both = nt(jnp.concatenate([dob, yb], axis=0), fresh)
        dp = jnp.where(inclusive, both[:C], 0.0)
        da = jnp.where(strict, -both[C:], 0.0)
        dbeta = jnp.sum(y * x, axis=-1, keepdims=True) + jnp.sum(da * gram, axis=-1, keepdims=True)
        dg = beta * da
        dgs = dg + dg.T
        through = nt(jnp.concatenate([carried * do, -(carried * dx)], axis=0), st)
        dpb = dp.astype(bf)
        dq = through[:C] + nn(dpb, kb)
        dk = through[C:] + tn(dpb, qb) + nt(tail * fresh.astype(f32), dst) + nn(dgs, kb)
        dv = dx
        db = dbeta * beta * (1.0 - beta)
        bl = pl.ds(4 * heads * 128, 128)
        @pl.when(h == 0)
        def _():
            draw_ref[0, rows, bl] = jnp.where(lane == 0, db, 0.0).astype(bf)
        @pl.when(h > 0)
        def _():
            old = draw_ref[0, rows, bl]
            draw_ref[0, rows, bl] = jnp.where(lane == h, db.astype(bf).astype(f32), old.astype(f32)).astype(bf)
        dq = rq * (dq - q * jnp.sum(q * dq, axis=-1, keepdims=True))
        dk = rk * (dk - k * jnp.sum(k * dk, axis=-1, keepdims=True))
        dcq = dq * (sq * (1.0 + cq * (1.0 - sq)))
        dck = dk * (sk * (1.0 + ck * (1.0 - sk)))
        dcv = dv * (sv * (1.0 + cv * (1.0 - sv)))
        rq_, wq = conv_back(dcq, nq, aux, w_ref[0], xq, shq)
        rk_, wk = conv_back(dck, nk, aux, w_ref[1], xk, shk)
        rv_, wv = conv_back(dcv, nv, aux, w_ref[2], xv, shv)
        for t, val in ((0, rq_), (1, rk_), (2, rv_)):
            draw_ref[0, rows, pl.ds(pl.multiple_of((t * heads + h) * 128, 128), 128)] = val.astype(bf)
        dws = tuple(a + b for a, b in zip(dws, wq + wk + wv))
        return dcq[:8], dck[:8], dcv[:8], dws
    z8 = jnp.zeros((8, 128), f32)
    taps = w_ref.shape[1]
    _, _, _, dws = lax.fori_loop(0, steps, stage_c, (z8, z8, z8, (z8,) * (3 * taps)), unroll=2)
    for n, d in enumerate(dws):
        dconv_ref[0, 0, n] = d

def mixer_bwd(raw, aux, conv, gain, saved, dmixed):
    nb, length, width = raw.shape
    heads = (width - 128) // 512
    taps = conv.shape[1]
    per = pl.BlockSpec((1, 1, length, 128), lambda b, h: (b, h, 0, 0))
    sh = lambda d: jax.ShapeDtypeStruct((nb, heads, length, 128), d)
    draw, dconv, dgain = pl.pallas_call(
        bwd_kernel,
        grid=(nb, heads),
        in_specs=specs(length, heads, 0) + [
            pl.BlockSpec((1, aux.shape[1], length), lambda b, h: (b, 0, 0)),
            pl.BlockSpec((3, taps, 128), lambda b, h: (0, 0, h)),
            pl.BlockSpec((1, 128), lambda b, h: (0, 0)),
        ] + [per] * 7 + [pl.BlockSpec((1, length, 128), lambda b, h: (b, 0, h))],
        out_specs=[pl.BlockSpec((1, length, width), lambda b, h: (b, 0, 0)),
                   pl.BlockSpec((1, 1, 3 * taps, 8, 128), lambda b, h: (b, h, 0, 0, 0)),
                   pl.BlockSpec((1, 1, 8, 128), lambda b, h: (b, h, 0, 0))],
        out_shape=[jax.ShapeDtypeStruct((nb, length, width), bf),
                   jax.ShapeDtypeStruct((nb, heads, 3 * taps, 8, 128), f32),
                   jax.ShapeDtypeStruct((nb, heads, 8, 128), f32)],
        scratch_shapes=[pltpu.VMEM((length, 128), f32)] * 3 + [pltpu.VMEM((length, 128), bf)],
        cost_estimate=lasting(2),
        name="mixer_backward",
    )(raw, raw, raw, raw, raw, aux, conv, gain, *saved, dmixed)
    dconv = jnp.sum(dconv, axis=(0, 3)).reshape(heads, 3, taps, 128).transpose(1, 2, 0, 3).reshape(3, taps, heads * 128)
    return draw, dconv, jnp.sum(dgain, axis=(0, 1, 2))

def make_aux(segments):
    nb, length = segments.shape
    seg = segments.astype(f32)
    blocks = seg.reshape(nb, length // C, C)
    last = blocks[:, :, -1:]
    before = jnp.concatenate([jnp.full((nb, 1, 1), -1.0, f32), last[:, :-1]], axis=1)
    carried = (blocks == before).astype(f32).reshape(nb, length)
    tail = (blocks == last).astype(f32).reshape(nb, length)
    cols = [seg, carried, tail]
    for i in range(1, 4):
        cols.append((jnp.pad(seg, ((0, 0), (i, 0)), constant_values=-1.0)[:, :length] == seg).astype(f32))
    for i in range(1, 4):
        cols.append((jnp.pad(seg, ((0, 0), (0, i)), constant_values=-1.0)[:, i:] == seg).astype(f32))
    cols += [jnp.zeros_like(seg)] * (16 - len(cols))
    return jnp.stack(cols, axis=1)


SLOTS = ((0, 0, 0), (0, 0, 1), (1, 0, 0), (0, 1, 0), (1, 0, 1), (0, 1, 1), (1, 1, 0), (1, 1, 1))
MESH = pl.DeviceIdType.MESH
VM = pl.BlockSpec(memory_space=pltpu.VMEM)
ANY = pl.BlockSpec(memory_space=pl.ANY)


def slot_place(r, gx, gy):
    dx, dy, dc = SLOTS[r]
    hi, lo = gx // 2, gx % 2
    hi = 1 - hi if dy else hi
    lo = 1 - lo if dc else lo
    return hi * 2 + lo, (1 - gy if dx else gy)


def slot_peer(r, gx, gy):
    px, py = slot_place(r, gx, gy)
    return {"gx": px, "gy": py}


def flipped(index, n, size):
    out, bit = 0, 1
    while bit < size:
        digit = index // bit % 2
        out = out + bit * (1 - digit if n & bit else digit)
        bit *= 2
    return out


def entry_barrier(peers):
    sem = pltpu.get_barrier_semaphore()
    for peer in peers:
        pl.semaphore_signal(sem, inc=1, device_id=peer, device_id_type=MESH)
    pl.semaphore_wait(sem, len(peers))


def remote(src, dst, send, recv, peer):
    return pltpu.make_async_remote_copy(src, dst, send, recv, device_id=peer, device_id_type=MESH)


def nt_dot(a, b):
    return lax.dot_general(a, b, (((1,), (1,)), ((), ())), preferred_element_type=f32)


def nn_dot(a, b):
    return lax.dot_general(a, b, (((1,), (0,)), ((), ())), preferred_element_type=f32)


class Gather:
    COPIES = 13

    def __init__(self, buf, send, recv, gx, gy, over_gx=False):
        rows = buf.shape[1]
        half = rows // 2
        a, b = pl.ds(0, half), pl.ds(half, half)
        core, xn, yn = (slot_peer(r, gx, gy) for r in (1, 2, 3))

        def make(i, src, dst, part, peer):
            return remote(buf.at[src, part], buf.at[dst, part], send.at[i], recv.at[i], peer)

        self.own = [
            make(0, 0, 2, a, xn),
            make(1, 0, 3, a, yn),
            make(2, 0, 2, b, xn),
            make(3, 0, 3, b, yn),
            remote(buf.at[0], buf.at[1], send.at[4], recv.at[4], core),
        ]
        self.over_gx = over_gx
        self.diagonal = [make(5, 2, 6, a, yn) if over_gx else make(5, 3, 6, a, xn), make(6, 2, 6, b, yn)]
        self.cross = [
            make(7, 2, 4, a, core),
            make(8, 2, 4, b, core),
            make(9, 3, 5, a, core),
            make(10, 3, 5, b, core),
            make(11, 6, 7, a, core),
            make(12, 6, 7, b, core),
        ]

    def start(self):
        for c in self.own:
            c.start()

    def step(self, i):
        if i == 1:
            self.own[4].wait_recv()
        elif i == 2:
            self.own[1].wait_recv()
            if not self.over_gx:
                self.diagonal[0].start()
            self.cross[2].start()
            self.own[0].wait_recv()
            if self.over_gx:
                self.diagonal[0].start()
            self.cross[0].start()
            self.own[2].wait_recv()
            self.diagonal[1].start()
            self.cross[1].start()
        elif i == 3:
            self.own[3].wait_recv()
            self.cross[3].start()
        elif i == 4:
            self.cross[0].wait_recv()
            self.cross[1].wait_recv()
        elif i == 5:
            self.cross[2].wait_recv()
            self.cross[3].wait_recv()
        elif i == 6:
            self.diagonal[0].wait_recv()
            self.cross[4].start()
            self.diagonal[1].wait_recv()
            self.cross[5].start()
        elif i == 7:
            self.cross[4].wait_recv()
            self.cross[5].wait_recv()

    def finish(self):
        for c in self.own + self.diagonal + self.cross:
            c.wait_send()


def head_kernel(
    x_ref, wq_ref, wk_ref, wv_ref, wg_ref, wb_ref, gate_ref, up_ref, out_ref, gain_ref,
    normed_ref, raw_ref, hw_ref, own_ref, gu_ref, wo_ref,
    buf, w, low, acc, ag_send, ag_recv, w_send, w_recv, load_sem, out_sem, raw_sem, hw_sem, z_send, z_recv, u_send, u_recv,
):
    gx, gy, dp = lax.axis_index("gx"), lax.axis_index("gy"), lax.axis_index("dp")
    ngx = 4
    piece = gu_ref.shape[0]
    parts = x_ref.shape[1] // piece
    units = gu_ref.shape[1] // 2
    unit_other = pl.multiple_of((1 - gy) * (gate_ref.shape[1] - units), 128)
    turn = flipped(dp, 0, parts)
    rows_sent = pl.ds(pl.multiple_of(turn * piece, piece), piece)
    rows = own_ref.shape[0]
    part = x_ref.shape[1]
    width = wq_ref.shape[1] // 2
    weights = ((wq_ref, width), (wk_ref, width), (wv_ref, width), (wg_ref, width), (wb_ref, 128))
    starts = [0, width, 2 * width, 3 * width, 4 * width]
    xn = slot_peer(2, gx, gy)
    loads = [pltpu.make_async_copy(x_ref, buf.at[0], load_sem.at[5])]
    for i, (ref, n) in enumerate(weights):
        src = ref.at[:, pl.ds(pl.multiple_of(gy * n, 128), n)]
        loads.append(pltpu.make_async_copy(src, w.at[0, :, pl.ds(starts[i], n)], load_sem.at[i]))
    for c in loads:
        c.start()
    peers = [slot_peer(r, gx, gy) for r in (1, 2, 3)] + [{"dp": flipped(dp, n, parts)} for n in range(1, parts)]
    entry_barrier(peers)
    swaps = []
    for i, (ref, n) in enumerate(weights):
        src = ref.at[rows_sent, pl.ds(pl.multiple_of((1 - gy) * n, 128), n)]
        swaps.append(remote(src, w.at[1, rows_sent, pl.ds(starts[i], n)], w_send.at[i], w_recv.at[i], xn))
        swaps[-1].start()
    loads[0].wait()
    gather = Gather(buf, ag_send, ag_recv, gx, gy, True)
    gather.start()
    extra = [
        remote(gate_ref.at[rows_sent, pl.ds(unit_other, units)], gu_ref.at[:, pl.ds(0, units)], u_send.at[0], u_recv.at[0], xn),
        remote(up_ref.at[rows_sent, pl.ds(unit_other, units)], gu_ref.at[:, pl.ds(units, units)], u_send.at[1], u_recv.at[1], xn),
        remote(out_ref.at[pl.ds(pl.multiple_of((1 - gy) * width, width), width), :], wo_ref, u_send.at[2], u_recv.at[2], xn),
    ]
    for c in extra:
        c.start()
    for c in swaps:
        c.wait_recv()
    spread = [
        remote(w.at[1, rows_sent], w.at[1, rows_sent], z_send.at[n], z_recv.at[n], {"dp": flipped(dp, n, parts)}) for n in range(1, parts)
    ]
    for c in spread:
        c.start()
    for c in loads[1:]:
        c.wait()
    keep = pltpu.make_async_copy(w.at[0], hw_ref.at[pl.ds(pl.multiple_of(gy * part, part), part)], hw_sem.at[0])
    keep.start()
    near = pl.ds(pl.multiple_of(gy * part, part), part)
    far = pl.ds(pl.multiple_of((1 - gy) * part, part), part)
    stores = []
    blocks = []

    def pair(n, first, second):
        px, _ = slot_place(first, gx, gy)
        for s in range(2):
            span = pl.ds(s * rows, rows)
            v = s * ngx + px
            i = 2 * n + s
            x0 = buf[first, span, :].astype(f32)
            x1 = buf[second, span, :].astype(f32)
            total = jnp.sum(x0 * x0, axis=-1, keepdims=True) + jnp.sum(x1 * x1, axis=-1, keepdims=True)
            rate = lax.rsqrt(total / (2 * part) + EPS)
            low[i, :, near] = (x0 * rate * gain_ref[:, near]).astype(bf)
            low[i, :, far] = (x1 * rate * gain_ref[:, far]).astype(bf)
            c = pltpu.make_async_copy(low.at[i], normed_ref.at[v], out_sem.at[i])
            c.start()
            stores.append(c)
            acc[i] = nn_dot(low[i, :, near], w[0])
            blocks.append((i, v))

    for step in (1, 2, 3, 4):
        gather.step(step)
        if step == 2:
            pair(0, 0, 2)
            mine = pl.ds(pl.multiple_of(gy * rows, rows), rows)
            own_ref[:, near] = buf[0, mine, :]
            own_ref[:, far] = buf[2, mine, :]
    pair(1, 1, 4)
    gather.step(5)
    gather.step(6)
    pair(2, 3, 6)
    gather.step(7)
    pair(3, 5, 7)
    for c in spread:
        c.wait_recv()
    give = pltpu.make_async_copy(w.at[1], hw_ref.at[far], hw_sem.at[1])
    give.start()

    for i, v in blocks:
        acc[i] += nn_dot(low[i, :, far], w[1])
        c = pltpu.make_async_copy(acc.at[i], raw_ref.at[v], raw_sem.at[i])
        c.start()
        stores.append(c)
    keep.wait()
    give.wait()
    for c in stores:
        c.wait()
    for c in extra:
        c.wait_recv()
    for c in swaps + spread + extra:
        c.wait_send()
    gather.finish()


def head_project(inputs, w_query, w_key, w_value, w_gate_head, w_beta, w_gate, w_up, w_out, gain, units, parts, collective):
    total, part = inputs.shape
    rows = total // 2
    feat = 2 * part
    cols = 2 * w_query.shape[1] + 128
    sd = jax.ShapeDtypeStruct
    return pl.pallas_call(
        head_kernel,
        in_specs=[ANY] * 9 + [VM],
        out_specs=[ANY, ANY, ANY, VM, ANY, ANY],
        out_shape=[
            sd((8, rows, feat), bf),
            sd((8, rows, cols), f32),
            sd((feat, cols), bf),
            sd((rows, feat), bf),
            sd((part // parts, 2 * units), bf),
            sd((w_out.shape[0] // 2, w_out.shape[1]), bf),
        ],
        scratch_shapes=[
            pltpu.VMEM((8, total, part), bf),
            pltpu.VMEM((2, part, cols), bf),
            pltpu.VMEM((8, rows, feat), bf),
            pltpu.VMEM((8, rows, cols), f32),
            pltpu.SemaphoreType.DMA((13,)),
            pltpu.SemaphoreType.DMA((13,)),
            pltpu.SemaphoreType.DMA((5,)),
            pltpu.SemaphoreType.DMA((5,)),
            pltpu.SemaphoreType.DMA((6,)),
            pltpu.SemaphoreType.DMA((8,)),
            pltpu.SemaphoreType.DMA((8,)),
            pltpu.SemaphoreType.DMA((2,)),
            pltpu.SemaphoreType.DMA((4,)),
            pltpu.SemaphoreType.DMA((4,)),
            pltpu.SemaphoreType.DMA((3,)),
            pltpu.SemaphoreType.DMA((3,)),
        ],
        compiler_params=pltpu.CompilerParams(collective_id=collective, has_side_effects=True, vmem_limit_bytes=60 << 20),
        cost_estimate=lasting(80),
        name="head_project",
    )(inputs, w_query, w_key, w_value, w_gate_head, w_beta, w_gate, w_up, w_out, gain)


def mlp_kernel(x_ref, gate_ref, up_ref, down_ref, y_ref, *refs, parts):
    gu_refs, piece_ref, refs = refs[:parts], refs[parts], refs[parts + 1 :]
    mlp_body(parts, x_ref, gate_ref, up_ref, down_ref, y_ref, gu_refs, piece_ref, *refs)


def mlp_body(
    parts, x_ref, gate_ref, up_ref, down_ref, y_ref, gu_refs, piece_ref,
    second_ref, hidden_ref, grads_ref, yrel_ref, gu_out, dn_out,
    wgu, wd, buf, ybuf, hbuf, gbuf, load_sem, w_sem, keep_sem, y_sem, y_out_sem, out_sem, ag_send, ag_recv,
):
    gx, gy = lax.axis_index("gx"), lax.axis_index("gy")
    ngy = 2
    rows = x_ref.shape[0]
    feat = x_ref.shape[1]
    units = wd.shape[0]
    half = feat // 2
    tile = 256
    dp = lax.axis_index("dp")
    unit_mine = pl.multiple_of(gy * (gate_ref.shape[1] - units), 128)
    doubled = gy * (2 * units - gate_ref.shape[1])
    load = pltpu.make_async_copy(x_ref, buf.at[0], load_sem)
    load.start()
    near = pl.ds(pl.multiple_of(gy * half, half), half)
    far = pl.multiple_of((1 - gy) * half, half)
    own_units = pl.ds(unit_mine, units)
    w_loads = [
        pltpu.make_async_copy(gate_ref.at[:, own_units], wgu.at[near, pl.ds(0, units)], w_sem.at[0]),
        pltpu.make_async_copy(up_ref.at[:, own_units], wgu.at[near, pl.ds(units, units)], w_sem.at[1]),
        pltpu.make_async_copy(down_ref.at[own_units, :], wd.at[:, near], w_sem.at[2]),
    ]
    w_loads.append(pltpu.make_async_copy(piece_ref, wd.at[:, pl.ds(far, half)], w_sem.at[3]))
    for n in range(parts):
        turn = flipped(dp, n, parts)
        piece = half // parts
        w_loads.append(
            pltpu.make_async_copy(gu_refs[n], wgu.at[pl.ds(pl.multiple_of(far + turn * piece, piece), piece), :], w_sem.at[4 + n])
        )
    for c in w_loads:
        c.start()
    entry_barrier([slot_peer(r, gx, gy) for r in (1, 2, 3)])
    load.wait()
    gather = Gather(buf, ag_send, ag_recv, gx, gy)
    gather.start()

    def y_load(r, n):
        px, py = slot_place(r, gx, gy)
        return [
            pltpu.make_async_copy(y_ref.at[px * ngy + h, py], ybuf.at[r % 2, :, pl.ds(h * (feat // 2), feat // 2)], y_sem.at[r % 2, h])
            for h in range(2)
        ]

    def y_store(r):
        return pltpu.make_async_copy(ybuf.at[r % 2], yrel_ref.at[r], y_out_sem.at[r % 2])

    for c in y_load(0, 0):
        c.start()
    for c in w_loads:
        c.wait()
    keeps = [pltpu.make_async_copy(wgu, gu_out, keep_sem.at[0]), pltpu.make_async_copy(wd, dn_out, keep_sem.at[1])]
    for c in keeps:
        c.start()

    def outs(r):
        return [
            pltpu.make_async_copy(buf.at[r], second_ref.at[r], out_sem.at[0, r % 2]),
            pltpu.make_async_copy(hbuf.at[r % 2], hidden_ref.at[r], out_sem.at[1, r % 2]),
            pltpu.make_async_copy(gbuf.at[r % 2], grads_ref.at[r], out_sem.at[2, r % 2]),
        ]

    for r in range(8):
        gather.step(r)
        if r >= 2:
            for c in outs(r - 2):
                c.wait()
        if r + 1 < 8:
            if r >= 1:
                y_store(r - 1).wait()
            for c in y_load(r + 1, 0):
                c.start()
        for c in y_load(r, 0):
            c.wait()
        y_store(r).start()

        def body(t, _):
            cols = pl.ds(pl.multiple_of(t * tile, tile), tile)
            up_cols = pl.ds(pl.multiple_of(units + t * tile, tile), tile)
            gate = nn_dot(buf[r], wgu[:, cols])
            up = nn_dot(buf[r], wgu[:, up_cols])
            gh = nt_dot(ybuf[r % 2], wd[cols, :])
            s = jax.nn.sigmoid(gate)
            keep = lax.broadcasted_iota(jnp.int32, gate.shape, 1) + t * tile >= doubled
            act = jnp.where(keep, gate * s, 0.0)
            up = jnp.where(keep, up, 0.0)
            hbuf[r % 2, :, cols] = (act * up).astype(bf)
            gbuf[r % 2, :, up_cols] = (gh * act).astype(bf)
            gbuf[r % 2, :, cols] = (gh * up * s * (1.0 + gate * (1.0 - s))).astype(bf)
            return 0

        lax.fori_loop(0, units // tile, body, 0)
        for c in outs(r):
            c.start()
    for r in (6, 7):
        for c in outs(r):
            c.wait()
        y_store(r).wait()
    gather.finish()
    for c in keeps:
        c.wait()


def mlp_forward(x_own, w_gate, w_up, w_down, y_all, gu_pieces, down_piece, units, collective):
    rows, feat = x_own.shape
    parts = len(gu_pieces)
    sd = jax.ShapeDtypeStruct
    return pl.pallas_call(
        functools.partial(mlp_kernel, parts=parts),
        in_specs=[ANY] * (6 + parts),
        out_specs=[ANY] * 6,
        out_shape=[
            sd((8, rows, feat), bf),
            sd((8, rows, units), bf),
            sd((8, rows, 2 * units), bf),
            sd((8, rows, feat), bf),
            sd((feat, 2 * units), bf),
            sd((units, feat), bf),
        ],
        scratch_shapes=[
            pltpu.VMEM((feat, 2 * units), bf),
            pltpu.VMEM((units, feat), bf),
            pltpu.VMEM((8, rows, feat), bf),
            pltpu.VMEM((2, rows, feat), bf),
            pltpu.VMEM((2, rows, units), bf),
            pltpu.VMEM((2, rows, 2 * units), bf),
            pltpu.SemaphoreType.DMA,
            pltpu.SemaphoreType.DMA((4 + parts,)),
            pltpu.SemaphoreType.DMA((2,)),
            pltpu.SemaphoreType.DMA((2, 2)),
            pltpu.SemaphoreType.DMA((2,)),
            pltpu.SemaphoreType.DMA((3, 2)),
            pltpu.SemaphoreType.DMA((13,)),
            pltpu.SemaphoreType.DMA((13,)),
        ],
        compiler_params=pltpu.CompilerParams(collective_id=collective, has_side_effects=True, vmem_limit_bytes=62 << 20),
        cost_estimate=lasting(68),
        name="mlp_forward",
    )(x_own, w_gate, w_up, w_down, y_all, *gu_pieces, down_piece)


class Scatter:
    def __init__(self, give, take, acc, diag_in, last_in, s_core, r_core, s_link, r_link, gx, gy, over_gx=False):
        self.over_gx = over_gx
        self.give, self.take, self.acc, self.diag_in, self.last_in = give, take, acc, diag_in, last_in
        core, xn, yn = (slot_peer(r, gx, gy) for r in (1, 2, 3))
        rows = acc.shape[1]
        half = rows // 2
        a, b = pl.ds(0, half), pl.ds(half, half)
        self.a, self.b = a, b
        self.core = [remote(give.at[n], take.at[n], s_core.at[n], r_core.at[n], core) for n in range(4)]

        def link(i, src, dst, peer):
            return remote(src, dst, s_link.at[i], r_link.at[i], peer)

        self.link = [
            link(0, acc.at[0, a], diag_in.at[0], yn if over_gx else xn),
            link(1, acc.at[0, b], diag_in.at[1], yn),
            link(2, acc.at[1, a], last_in.at[0, a], xn),
            link(3, acc.at[2, b], last_in.at[1, b], yn),
            link(4, acc.at[1, b], last_in.at[0, b], xn),
            link(5, acc.at[2, a], last_in.at[1, a], yn),
        ]

    def begin(self, product, self_acc, between=None):
        acc = self.acc

        def give_out(n, slot):
            def put(cols, value):
                self.give[n, :, cols] = value.astype(bf)

            product(slot, put)
            self.core[n].start()

        def keep(n, slot):
            def put(cols, value):
                acc[n, :, cols] = value.astype(bf)

            product(slot, put)

        def join(n):
            self.core[n].wait_recv()
            acc[n] = (acc[n].astype(f32) + self.take[n].astype(f32)).astype(bf)

        give_out(0, 7)
        keep(0, 6)
        give_out(1, 4)
        if between is not None:
            between()
        join(0)
        self.link[0].start()
        self.link[1].start()
        give_out(2, 5)
        keep(1, 2)
        join(1)
        if not self.over_gx:
            self.link[2].start()
        keep(2, 3)
        join(2)
        self.link[3].start()
        if self.over_gx:
            self.link[5].start()
        give_out(3, 1)

        def put_self(cols, value):
            self_acc[:, cols] = value

        product(0, put_self)

    def forward(self):
        acc, a, b = self.acc, self.a, self.b
        if self.over_gx:
            for i, half, onward in ((0, a, 2), (1, b, 4)):
                self.link[i].wait_recv()
                acc[1, half] = (acc[1, half].astype(f32) + self.diag_in[i].astype(f32)).astype(bf)
                self.link[onward].start()
            return
        self.link[1].wait_recv()
        acc[1, b] = (acc[1, b].astype(f32) + self.diag_in[1].astype(f32)).astype(bf)
        self.link[4].start()
        self.link[0].wait_recv()
        acc[2, a] = (acc[2, a].astype(f32) + self.diag_in[0].astype(f32)).astype(bf)
        self.link[5].start()

    def end(self, self_acc):
        self.core[3].wait_recv()
        self_acc[...] += self.take[3].astype(f32)
        for c in self.link[2:]:
            c.wait_recv()
        self_acc[...] += self.last_in[0].astype(f32) + self.last_in[1].astype(f32)

    def run(self, product, self_acc):
        self.begin(product, self_acc)
        self.forward()
        self.end(self_acc)

    def finish(self):
        for c in self.core + self.link:
            c.wait_send()


def scatter_scratch(rows, feat):
    return [
        pltpu.VMEM((4, rows, feat), bf),
        pltpu.VMEM((4, rows, feat), bf),
        pltpu.VMEM((3, rows, feat), bf),
        pltpu.VMEM((2, rows // 2, feat), bf),
        pltpu.VMEM((2, rows, feat), bf),
        pltpu.SemaphoreType.DMA((4,)),
        pltpu.SemaphoreType.DMA((4,)),
        pltpu.SemaphoreType.DMA((6,)),
        pltpu.SemaphoreType.DMA((6,)),
    ]


def own_out_rows(out_ref, piece_ref, w, sem, gy):
    width, part = piece_ref.shape
    near = pl.ds(pl.multiple_of(gy * part, part), part)
    far = pl.ds(pl.multiple_of((1 - gy) * part, part), part)
    return [
        pltpu.make_async_copy(out_ref.at[pl.ds(pl.multiple_of(gy * width, width), width), :], w.at[:, near], sem.at[0]),
        pltpu.make_async_copy(piece_ref, w.at[:, far], sem.at[1]),
    ]


def out_kernel(
    mixed_ref, out_ref, piece_ref, x_ref, gain_ref,
    middle_ref, normed_ref, slots_ref,
    give, take, acc, diag_in, last_in, s_core, r_core, s_link, r_link, lhs, w, total, load_sem, lhs_sem, keep_sem,
):
    gx, gy = lax.axis_index("gx"), lax.axis_index("gy")
    feat = x_ref.shape[1]
    tile = 512
    loads = own_out_rows(out_ref, piece_ref, w, load_sem, gy)
    pulls = {}
    for r in (7, 6, 4, 5, 2, 3, 1, 0):
        px, py = slot_place(r, gx, gy)
        pulls[r] = pltpu.make_async_copy(mixed_ref.at[py * 4 + px], lhs.at[r], lhs_sem.at[r])
    for c in loads + list(pulls.values()):
        c.start()
    entry_barrier([slot_peer(r, gx, gy) for r in (1, 2, 3)])
    for c in loads:
        c.wait()

    def product(slot, put):
        pulls[slot].wait()

        def body(t, _):
            cols = pl.ds(pl.multiple_of(t * tile, tile), tile)
            put(cols, nn_dot(lhs[slot], w[:, cols]))
            return 0

        lax.fori_loop(0, feat // tile, body, 0)

    scatter = Scatter(give, take, acc, diag_in, last_in, s_core, r_core, s_link, r_link, gx, gy, True)
    scatter.run(product, total)
    keep = pltpu.make_async_copy(lhs, slots_ref, keep_sem)
    keep.start()
    middle = x_ref[...].astype(f32) + total[...]
    middle_ref[...] = middle
    rate = lax.rsqrt(jnp.mean(middle * middle, axis=-1, keepdims=True) + EPS)
    normed_ref[...] = (middle * rate * gain_ref[...]).astype(bf)
    keep.wait()
    scatter.finish()


def out_project(mixed, w_out, piece, x_own, gain, collective):
    rows, feat = x_own.shape
    width = mixed.shape[2]
    sd = jax.ShapeDtypeStruct
    return pl.pallas_call(
        out_kernel,
        in_specs=[ANY, ANY, ANY, VM, VM],
        out_specs=[VM, VM, ANY],
        out_shape=[sd((rows, feat), f32), sd((rows, feat), bf), sd(mixed.shape, bf)],
        scratch_shapes=scatter_scratch(rows, feat)
        + [
            pltpu.VMEM(mixed.shape, bf),
            pltpu.VMEM((width, feat), bf),
            pltpu.VMEM((rows, feat), f32),
            pltpu.SemaphoreType.DMA((2,)),
            pltpu.SemaphoreType.DMA((8,)),
            pltpu.SemaphoreType.DMA,
        ],
        compiler_params=pltpu.CompilerParams(collective_id=collective, has_side_effects=True, vmem_limit_bytes=60 << 20),
        cost_estimate=lasting(44),
        name="out_project",
    )(mixed, w_out, piece, x_own, gain)


def back_kernel(
    grads_ref, wgu_ref, out_ref, piece_ref, middle_ref, y_ref, gain_ref,
    mid_ref, gmix_ref, dgain_ref,
    give, take, acc, diag_in, last_in, s_core, r_core, s_link, r_link,
    lhs, wgu, w, total, buf, gstage, y_own, load_sem, lhs_sem, ag_send, ag_recv, mid_sem, gmix_sem,
):
    gx, gy = lax.axis_index("gx"), lax.axis_index("gy")
    rows, feat = middle_ref.shape
    tile = 512
    load = pltpu.make_async_copy(wgu_ref, wgu, load_sem.at[2])
    outs = own_out_rows(out_ref, piece_ref, w, load_sem, gy)
    order = (7, 6, 4, 5, 2, 3, 1, 0)
    pulls = {r: pltpu.make_async_copy(grads_ref.at[r], lhs.at[r], lhs_sem.at[r]) for r in order}
    pulls[7].start()
    load.start()
    for r in order[1:]:
        pulls[r].start()
    outs.append(pltpu.make_async_copy(y_ref.at[0], y_own, load_sem.at[3]))
    for c in outs:
        c.start()
    entry_barrier([slot_peer(r, gx, gy) for r in (1, 2, 3)])
    load.wait()

    def product(slot, put):
        pulls[slot].wait()

        def body(t, _):
            cols = pl.ds(pl.multiple_of(t * tile, tile), tile)
            put(cols, nt_dot(lhs[slot], wgu[cols, :]))
            return 0

        lax.fori_loop(0, feat // tile, body, 0)

    scatter = Scatter(give, take, acc, diag_in, last_in, s_core, r_core, s_link, r_link, gx, gy, True)
    scatter.run(product, total)
    middle = middle_ref[...]
    incoming = total[...]
    rate = lax.rsqrt(jnp.mean(middle * middle, axis=-1, keepdims=True) + EPS)
    scaled = gain_ref[...] * incoming
    inner = jnp.mean(middle * scaled, axis=-1, keepdims=True)
    for c in outs:
        c.wait()
    buf[0] = (y_own[...].astype(f32) + rate * scaled - middle * (rate * rate * rate) * inner).astype(bf)
    gather = Gather(buf, ag_send, ag_recv, gx, gy)
    gather.start()
    dgain_ref[...] = jnp.sum((incoming * middle * rate).reshape(rows // 8, 8, feat), axis=0)
    stores = []
    for r in range(8):
        gather.step(r)
        px, py = slot_place(r, gx, gy)
        gstage[r] = nt_dot(buf[r], w[...]).astype(bf)
        stores.append(pltpu.make_async_copy(gstage.at[r], gmix_ref.at[py * 4 + px], gmix_sem.at[r]))
        stores.append(pltpu.make_async_copy(buf.at[r], mid_ref.at[r], mid_sem.at[r]))
        for c in stores[-2:]:
            c.start()
    for c in stores:
        c.wait()
    gather.finish()
    scatter.finish()


def mlp_backward(grads, gate_up, w_out, piece, middle, y_rel, gain, collective):
    rows, feat = middle.shape
    width = piece.shape[0]
    sd = jax.ShapeDtypeStruct
    return pl.pallas_call(
        back_kernel,
        in_specs=[ANY, ANY, ANY, ANY, VM, ANY, VM],
        out_specs=[ANY, ANY, VM],
        out_shape=[sd((8, rows, feat), bf), sd((8, rows, width), bf), sd((8, feat), f32)],
        scratch_shapes=scatter_scratch(rows, feat)
        + [
            pltpu.VMEM(grads.shape, bf),
            pltpu.VMEM(gate_up.shape, bf),
            pltpu.VMEM((width, feat), bf),
            pltpu.VMEM((rows, feat), f32),
            pltpu.VMEM((8, rows, feat), bf),
            pltpu.VMEM((8, rows, width), bf),
            pltpu.VMEM((rows, feat), bf),
            pltpu.SemaphoreType.DMA((4,)),
            pltpu.SemaphoreType.DMA((8,)),
            pltpu.SemaphoreType.DMA((13,)),
            pltpu.SemaphoreType.DMA((13,)),
            pltpu.SemaphoreType.DMA((8,)),
            pltpu.SemaphoreType.DMA((8,)),
        ],
        compiler_params=pltpu.CompilerParams(collective_id=collective, has_side_effects=True, vmem_limit_bytes=63 << 20),
        cost_estimate=lasting(20),
        name="mlp_backward",
    )(grads, gate_up, w_out, piece, middle, y_rel, gain)


def final_kernel(
    draw_ref, hw_ref, hidden_ref, dn_ref, x_ref, mid_ref, middle_ref, other_ref, gain_ref, small_ref,
    gin_ref, lout_ref, all_ref,
    give1, take1, acc1, diag1, last1, sc1, rc1, sl1, rl1,
    give2, take2, acc2, diag2, last2, sc2, rc2, sl2, rl2,
    draw, hw, hidden, dn, x, mid, m_near, total1, total2, row_send, row_recv, z_in, z_sum, z_all,
    load_sem, draw_sem, hidden_sem, x_sem, row_sem, z_send, z_recv, p_send, p_recv,
    *, ndp,
):
    gx, gy, dp = lax.axis_index("gx"), lax.axis_index("gy"), lax.axis_index("dp")
    me = gx * 2 + gy
    rows, feat = middle_ref.shape
    part = feat // 2
    tile = 512
    near = pl.ds(pl.multiple_of(gy * part, part), part)
    xn = slot_peer(2, gx, gy)
    pairs = {0: (0, 2), 2: (0, 2), 1: (1, 4), 4: (1, 4), 3: (3, 6), 6: (3, 6), 5: (5, 7), 7: (5, 7)}
    load_hw = pltpu.make_async_copy(hw_ref, hw, load_sem.at[0])
    load_dn = pltpu.make_async_copy(dn_ref, dn, load_sem.at[1])
    order = (7, 5, 6, 3, 4, 1, 2, 0)
    draws = {}
    for r in order:
        px, py = slot_place(r, gx, gy)
        draws[r] = pltpu.make_async_copy(draw_ref.at[py * 4 + px], draw.at[r], draw_sem.at[r])
    hiddens = {r: pltpu.make_async_copy(hidden_ref.at[r], hidden.at[r], hidden_sem.at[r]) for r in order}
    draws[7].start()
    draws[5].start()
    load_hw.start()
    for r in order[2:]:
        draws[r].start()
    load_dn.start()
    for r in order:
        hiddens[r].start()
    finals = [
        pltpu.make_async_copy(x_ref, x, x_sem.at[0]),
        pltpu.make_async_copy(mid_ref.at[0, :, near], mid.at[gy], x_sem.at[1]),
        pltpu.make_async_copy(mid_ref.at[2, :, near], mid.at[1 - gy], x_sem.at[2]),
    ]
    for c in finals:
        c.start()
    finals.append(pltpu.make_async_copy(middle_ref.at[:, near], m_near, x_sem.at[3]))
    finals[-1].start()
    entry_barrier([slot_peer(r, gx, gy) for r in range(1, 8)] + [{"dp": flipped(dp, n, ndp)} for n in range(1, ndp)])
    around = [
        remote(small_ref, z_in.at[n], z_send.at[n], z_recv.at[n], {"dp": flipped(dp, n, ndp)}) for n in range(1, ndp)
    ]
    for c in around:
        c.start()

    def rows_pair(many, copies, slot, waited):
        for r in pairs[slot]:
            if r not in waited:
                copies[r].wait()
                waited.add(r)
        first, second = pairs[slot]
        low = first + (second - first) * gy
        return low, first + second - low

    def maker(many, copies, weights, weight_load, transposed):
        waited = set()

        def product(slot, put):
            low, high = rows_pair(many, copies, slot, waited)
            if weight_load is not None and "w" not in waited:
                weight_load.wait()
                waited.add("w")
            _, py = slot_place(slot, gx, gy)

            def body(t, _):
                cols = pl.ds(pl.multiple_of(t * tile, tile), tile)
                wide = pl.ds(pl.multiple_of(py * part + t * tile, tile), tile)
                if transposed:
                    w = weights[:, wide]
                    value = [nn_dot(many[low], w), nn_dot(many[high], w)]
                else:
                    w = weights[wide, :]
                    value = [nt_dot(many[low], w), nt_dot(many[high], w)]
                put(cols, jnp.concatenate(value, axis=0))
                return 0

            lax.fori_loop(0, part // tile, body, 0)

        return product

    first = Scatter(give1, take1, acc1, diag1, last1, sc1, rc1, sl1, rl1, gx, gy)
    second = Scatter(give2, take2, acc2, diag2, last2, sc2, rc2, sl2, rl2, gx, gy)
    first.begin(maker(draw, draws, hw, load_hw, False), total1)
    for c in around:
        c.wait_recv()
    summed = small_ref[...]
    for n in range(1, ndp):
        summed = summed + z_in[n]
    z_sum[...] = summed
    passes = [remote(z_sum, z_all.at[me], p_send.at[r], p_recv.at[r], slot_peer(r, gx, gy)) for r in range(1, 8)]
    for c in passes:
        c.start()
    second.begin(maker(hidden, hiddens, dn, load_dn, True), total2, first.forward)
    first.end(total1)
    for c in finals:
        c.wait()
    wide_x = x[...].astype(f32)
    scaled = gain_ref[:, near] * total1[...]
    sums = [jnp.sum(wide_x * wide_x, axis=-1, keepdims=True), jnp.sum(wide_x * scaled, axis=-1, keepdims=True)]
    lane = lax.broadcasted_iota(jnp.int32, (2 * rows, 128), 1)
    packed = jnp.where(lane == 0, sums[0], jnp.where(lane == 1, sums[1], 0.0)).T
    row_send[...] = packed[:8]
    row_copy = remote(row_send, row_recv, row_sem.at[0], row_sem.at[1], xn)
    row_copy.start()
    second.forward()
    second.end(total2)
    mine = pl.ds(pl.multiple_of(gy * rows, rows), rows)
    other = pl.ds(pl.multiple_of((1 - gy) * rows, rows), rows)
    lout_ref[gy] = (total2[mine, :] + m_near[...]).astype(bf)
    lout_ref[1 - gy] = (total2[other, :] + other_ref[...].astype(f32)).astype(bf)
    row_copy.wait_recv()
    both = jnp.concatenate([row_send[...] + row_recv[...], jnp.zeros((120, 2 * rows), f32)], axis=0).T
    rate = lax.rsqrt(both[:, 0:1] / feat + EPS)
    inner = both[:, 1:2] / feat
    gin = mid[...].reshape(2 * rows, part).astype(f32) + rate * scaled - wide_x * (rate * rate * rate) * inner
    gin_ref[...] = gin.astype(bf).reshape(2, rows, part)
    z_all[me] = z_sum[...]
    for c in passes:
        c.wait_recv()
    all_ref[...] = z_all[...]
    for c in around + passes + [row_copy]:
        c.wait_send()
    first.finish()
    second.finish()


def final_sums(draw, head_w, hidden, down, inputs, mid, middle, other, gain, small, ndp, collective):
    rows, feat = middle.shape
    part = feat // 2
    sd = jax.ShapeDtypeStruct
    dma = pltpu.SemaphoreType.DMA
    return pl.pallas_call(
        functools.partial(final_kernel, ndp=ndp),
        in_specs=[ANY] * 7 + [VM] * 3,
        out_specs=[VM] * 3,
        out_shape=[sd((2, rows, part), bf), sd((2, rows, part), bf), sd((8, *small.shape), f32)],
        scratch_shapes=scatter_scratch(2 * rows, part)
        + scatter_scratch(2 * rows, part)
        + [
            pltpu.VMEM(draw.shape, bf),
            pltpu.VMEM(head_w.shape, bf),
            pltpu.VMEM(hidden.shape, bf),
            pltpu.VMEM(down.shape, bf),
            pltpu.VMEM((2 * rows, part), bf),
            pltpu.VMEM((2, rows, part), bf),
            pltpu.VMEM((rows, part), f32),
            pltpu.VMEM((2 * rows, part), f32),
            pltpu.VMEM((2 * rows, part), f32),
            pltpu.VMEM((8, 2 * rows), f32),
            pltpu.VMEM((8, 2 * rows), f32),
            pltpu.VMEM((ndp, *small.shape), f32),
            pltpu.VMEM(small.shape, f32),
            pltpu.VMEM((8, *small.shape), f32),
            dma((2,)),
            dma((8,)),
            dma((8,)),
            dma((4,)),
            dma((2,)),
            dma((ndp,)),
            dma((ndp,)),
            dma((8,)),
            dma((8,)),
        ],
        compiler_params=pltpu.CompilerParams(collective_id=collective, has_side_effects=True, vmem_limit_bytes=63 << 20),
        cost_estimate=lasting(5),
        name="final_sums",
    )(draw, head_w, hidden, down, inputs, mid, middle, other, gain, small)


def dot(a, b):
    return lax.dot_general(a, b, (((1,), (0,)), ((), ())), preferred_element_type=f32)


def dot_t(a, b):
    return lax.dot_general(a, b, (((1,), (1,)), ((), ())), preferred_element_type=f32)


def dot_w(a, b):
    return lax.dot_general(a, b, (((0,), (0,)), ((), ())), preferred_element_type=f32)


def swap(value):
    return lax.ppermute(value, "gy", [(0, 1), (1, 0)])


def in_order(mine, other, axis):
    first = lax.axis_index("gy") == 0
    return jnp.concatenate([jnp.where(first, mine, other), jnp.where(first, other, mine)], axis=axis)


def halves(value, axis):
    size = value.shape[axis] // 2
    mine = lax.axis_index("gy")
    return (
        lax.dynamic_slice_in_dim(value, mine * size, size, axis),
        lax.dynamic_slice_in_dim(value, (1 - mine) * size, size, axis),
    )


def scatter_dp(value):
    return lax.psum_scatter(value.astype(bf), "dp", scatter_dimension=0, tiled=True)


def rows_to_dp(left, right):
    part = left.shape[1] // 2
    halves_of = [dot_w(left[:, i * part : (i + 1) * part], right).astype(bf) for i in range(2)]
    return halves_of


def sort_halves(parts):
    first = lax.axis_index("gy") == 0
    return jnp.where(first, parts[0], parts[1]), swap(jnp.where(first, parts[1], parts[0]))


def shards(
    inputs,
    segments,
    norm_gain,
    w_query,
    w_key,
    w_value,
    w_beta,
    w_gate_head,
    conv_kernel,
    head_gain,
    w_out,
    mlp_gain,
    w_gate,
    w_up,
    w_down,
    grad_y,
):
    ngx, ngy, ndp = lax.axis_size("gx"), lax.axis_size("gy"), lax.axis_size("dp")
    gx, gy = lax.axis_index("gx"), lax.axis_index("gy")
    nb, part_rows, part_feat = inputs.shape
    length, feat = part_rows * ngx, part_feat * ngy
    tokens = nb * length
    own_rows = tokens // (ngx * ngy)
    heads = w_beta.shape[1] // ngy
    width = w_query.shape[1] // ngy
    beta_w = jnp.pad(w_beta.T.reshape(ngy, heads, part_feat), ((0, 0), (0, 128 - heads), (0, 0))).reshape(ngy * 128, part_feat).T
    block = w_gate.shape[1]
    units = -(-block // (ngy * 256)) * 256
    parts = ndp if ndp == 4 else 1
    normed, raw, head_w, x_own, gu_piece, out_piece = head_project(
        inputs.reshape(nb * part_rows, part_feat), w_query, w_key, w_value, w_gate_head, beta_w, w_gate, w_up, w_out,
        norm_gain[None], units, parts, 5,
    )
    normed = normed.reshape(tokens, feat)
    raw = raw.reshape(nb, length, -1)

    def around(value):
        return [value] + [lax.ppermute(value, "dp", [(i, i ^ n) for i in range(ndp)]) for n in range(1, parts)]

    gu_pieces = around(gu_piece)
    x_own, grad_y, w_down = lax.optimization_barrier((x_own, grad_y, w_down))
    down_piece = swap(lax.dynamic_slice_in_dim(w_down, (1 - gy) * (block - units), units, 0))
    y_all = lax.all_gather(grad_y, ("gx", "gy"), axis=0, tiled=False)

    aux = make_aux(segments)
    conv_start = (gx * ngy + gy) * width
    conv_local = lax.dynamic_slice_in_dim(conv_kernel, conv_start, width, 2)
    gain_row = head_gain[None]
    mixed, *saved = mixer_fwd(raw, aux, conv_local, gain_row)
    middle, second_own, mixed_slots = out_project(
        mixed.reshape(8, own_rows, width), w_out, out_piece, x_own, mlp_gain[None], 1
    )
    second, hidden, grads, y_rel, gate_up, down_w = mlp_forward(
        second_own, w_gate, w_up, w_down, y_all, gu_pieces, down_piece, units, 6
    )
    second_flat, hidden_flat = second.reshape(tokens, feat), hidden.reshape(tokens, units)
    grads_flat, y_flat = grads.reshape(tokens, 2 * units), y_rel.reshape(tokens, feat)
    half = feat // 2
    gu_first = dot_w(second_flat[:, :half], grads_flat).astype(bf)
    hidden_flat, gu_first = lax.optimization_barrier((hidden_flat, gu_first))
    down_grad = dot_w(hidden_flat, y_flat).astype(bf)
    second_flat, down_grad = lax.optimization_barrier((second_flat, down_grad))
    down_keep, down_send = halves(down_grad, 1)
    down_both = jnp.stack([down_keep, swap(down_send)])
    gu_second = dot_w(second_flat[:, half:], grads_flat).astype(bf)
    grads, gu_second = lax.optimization_barrier((grads, gu_second))
    gu_sums = [scatter_dp(gu_first), scatter_dp(gu_second)]
    first, last = down_both[gy], down_both[1 - gy]
    down_rows = jnp.concatenate([first, last[2 * units - block :]], axis=0)

    mid_slots, grad_mixed, mlp_gain_parts = mlp_backward(
        grads, gate_up, w_out, out_piece, middle, y_rel, mlp_gain[None], 2
    )
    grad_mixed, mid_slots, down_rows, *gu_sums = lax.optimization_barrier((grad_mixed, mid_slots, down_rows, *gu_sums))
    down_sum = scatter_dp(down_rows)
    out_grad = dot_w(mixed_slots.reshape(tokens, width), mid_slots.reshape(tokens, feat)).astype(bf)
    out_keep, out_send = halves(out_grad, 1)
    out_rows = in_order(out_keep, swap(out_send), 0)
    draw, conv_grad, gain_grad = mixer_bwd(
        raw, aux, conv_local, gain_row, saved, grad_mixed.reshape(nb, length, width)
    )
    draw = draw.reshape(tokens, -1)
    gu_pair = sort_halves(gu_sums)
    middle_other = swap(lax.dynamic_slice_in_dim(middle, (1 - gy) * half, half, 1).astype(bf))
    draw, down_sum, out_rows, middle_other, *gu_pair = lax.optimization_barrier((draw, down_sum, out_rows, middle_other, *gu_pair))
    out_sum = scatter_dp(out_rows)
    main = 4 * width
    both = rows_to_dp(normed, draw)
    norm_gain_grad = jnp.sum(jnp.concatenate(both, axis=0).astype(f32) * head_w.astype(f32), axis=1) / norm_gain
    beta_grad = jnp.concatenate([g[:, main : main + heads] for g in both], axis=0).astype(f32)
    head_grads = [g[:, :main] for g in both]
    draw, hidden, *head_grads = lax.optimization_barrier((draw, hidden, *head_grads))
    head_sums = [scatter_dp(g) for g in head_grads]
    hidden, out_sum = lax.optimization_barrier((hidden, out_sum))
    sum_down, sum_out = down_sum.astype(f32), out_sum.astype(f32)
    grad_gu_mine, grad_gu_other = gu_pair
    flat = [beta_grad.T, conv_grad, norm_gain_grad, jnp.sum(mlp_gain_parts, axis=0), gain_grad]
    counts = [v.size // 128 for v in flat]
    small = jnp.concatenate([v.reshape(-1, 128) for v in flat])
    small = jnp.pad(small, ((0, -small.shape[0] % 8), (0, 0)))
    if parts == 1:
        small = lax.psum(small, "dp")
    grad_inputs, layer_out, gathered = final_sums(
        draw.reshape(8, own_rows, -1), head_w, hidden, down_w, inputs.reshape(nb * part_rows, part_feat), mid_slots, middle,
        middle_other, norm_gain[None], small, parts, 3,
    )

    head_mine, head_other = sort_halves(head_sums)

    def unit_columns(i):
        part = slice(i * units, (i + 1) * units)
        both = jnp.stack([grad_gu_mine[:, part], grad_gu_other[:, part]])
        return jnp.concatenate([both[gy], both[1 - gy][:, 2 * units - block :]], axis=1).astype(f32)

    sum_gate, sum_up = unit_columns(0), unit_columns(1)

    def head_part(i, n):
        return in_order(head_mine[:, i : i + n], head_other[:, i : i + n], 1).astype(f32)

    sum_query, sum_key, sum_value, sum_head_gate = (head_part(i * width, width) for i in range(4))

    n_beta, n_conv, n_norm, n_mlp, n_gain = counts
    beta_parts = gathered[:, :n_beta].reshape(8, heads, feat)
    beta_rows = feat // (ngy * ndp)
    beta_pair = lax.dynamic_slice(beta_parts, (gx * ngy, 0, (gy * ndp + lax.axis_index("dp")) * beta_rows), (ngy, heads, beta_rows))
    sum_beta = beta_pair.reshape(ngy * heads, beta_rows).T
    taps = conv_kernel.shape[1]
    conv_sum = gathered[:, n_beta : n_beta + n_conv].reshape(8, 3, taps, width).transpose(1, 2, 0, 3).reshape(conv_kernel.shape)
    rest = jnp.sum(gathered[:, n_beta + n_conv :], axis=0)
    norm_sum = rest[:n_norm].reshape(feat)
    mlp_sum = rest[n_norm : n_norm + n_mlp].reshape(feat)
    gain_sum = rest[n_norm + n_mlp : n_norm + n_mlp + n_gain].reshape(-1)
    return (
        layer_out,
        grad_inputs,
        norm_sum,
        sum_query,
        sum_key,
        sum_value,
        sum_beta,
        sum_head_gate,
        conv_sum,
        gain_sum,
        sum_out,
        mlp_sum,
        sum_gate,
        sum_up,
        sum_down,
    )


def solution(mesh):
    cols = P("gy", "gx")
    rows = P("gx", "gy")
    acts = P("dp", "gx", "gy")
    cols_out = P(("gy", "dp"), "gx")
    rows_out = P(("gx", "dp"), "gy")
    return jax.shard_map(
        shards,
        mesh=mesh,
        in_specs=(acts, P("dp", None), P(), cols, cols, cols, cols, cols, P(), P(), rows, P(), cols, cols, rows, acts),
        out_specs=(
            acts,
            acts,
            P(),
            cols_out,
            cols_out,
            cols_out,
            cols_out,
            cols_out,
            P(),
            P(),
            rows_out,
            P(),
            cols_out,
            cols_out,
            rows_out,
        ),
        check_vma=False,
    )
```

```python
import jax, jax.numpy as jnp
from jax import lax
from jax.experimental import pallas as pl
from jax.experimental.pallas import tpu as pltpu
import functools
from jax.sharding import PartitionSpec as P
EPS = 1e-6
HEAD_EPS = 0.01
C = 128
bf = jnp.bfloat16
f32 = jnp.float32
GROUP = 8
BACK_A = 8
BACK_C = 4

def lasting(us):
    return pl.CostEstimate(flops=int(us * 1.15e9), bytes_accessed=1 << 20, transcendentals=0)

def nn(a, b):
    return lax.dot_general(a.astype(bf), b.astype(bf), (((1,), (0,)), ((), ())), preferred_element_type=f32)
def nt(a, b):
    return lax.dot_general(a.astype(bf), b.astype(bf), (((1,), (1,)), ((), ())), preferred_element_type=f32)
def tn(a, b):
    return lax.dot_general(a.astype(bf), b.astype(bf), (((0,), (0,)), ((), ())), preferred_element_type=f32)

def level_masks(n):
    row = lax.broadcasted_iota(jnp.int32, (n, n), 0)
    col = lax.broadcasted_iota(jnp.int32, (n, n), 1)
    out = []
    size = 1
    while size < n:
        out.append(((row ^ col) & (-size) == size).astype(f32).astype(bf))
        size *= 2
    return (row == col).astype(f32).astype(bf), out

def inverse_many(many, eye, levels):
    totals = [eye - a * levels[0] for a in many]
    for mask in levels[1:]:
        inner = [nn(a * mask, t).astype(bf) for a, t in zip(many, totals)]
        outer = [nn(t, x).astype(bf) for t, x in zip(totals, inner)]
        totals = [t - x for t, x in zip(totals, outer)]
    return totals

def act_stage(x, prev, aux, w, norm):
    row8 = lax.broadcasted_iota(jnp.int32, (8, 128), 0)
    conv = x * w[0:1]
    sh = []
    for i in range(1, w.shape[0]):
        r = pltpu.roll(x, i, 0)
        p = pltpu.roll(prev, i, 0)
        head = jnp.where(row8 < i, p, r[:8])
        m = jnp.concatenate([head, r[8:]], axis=0) * aux[:, 2 + i:3 + i]
        sh.append(m)
        conv = conv + m * w[i:i + 1]
    s = jax.nn.sigmoid(conv)
    act = conv * s
    if norm:
        rate = lax.rsqrt(jnp.sum(act * act, axis=-1, keepdims=True) + EPS)
        return conv, s, act * rate, rate, sh
    return conv, s, act, None, sh

def masks(aux, segrow):
    n = aux.shape[0]
    row = lax.broadcasted_iota(jnp.int32, (n, n), 0)
    col = lax.broadcasted_iota(jnp.int32, (n, n), 1)
    same = aux[:, 0:1] == segrow
    return same & (row > col), same & (row >= col)

def aux_columns(ref, rows):
    block = ref[0, :, rows]
    return jnp.concatenate([block, jnp.zeros((C - block.shape[0], C), f32)], axis=0).T

def beta_column(block, h):
    lane = lax.broadcasted_iota(jnp.int32, block.shape, 1)
    return jnp.sum(jnp.where(lane == h, jax.nn.sigmoid(block), 0.0), axis=1, keepdims=True)

def prev_rows(ref, lo):
    start = pl.multiple_of(jnp.maximum(lo - 8, 0), 8)
    return jnp.where(lo > 0, ref[0, pl.ds(start, 8), :].astype(f32), 0.0)

def fwd_kernel(q_ref, k_ref, v_ref, g_ref, b_ref, aux_ref, w_ref, gain_ref,
               mixed_ref, t_ref, w_out, p_ref, f_ref, s_ref, fresh_ref, o_ref,
               q_s, u_s, b_s):
    h = pl.program_id(1)
    length = q_ref.shape[1]
    steps = length // C
    eye, levels = level_masks(C)
    def stage_a(group, _):
        lows = [pl.multiple_of((group * GROUP + n) * C, C) for n in range(GROUP)]
        spans = [pl.ds(lo, C) for lo in lows]
        many, keys, right = [], [], []
        for lo, rows in zip(lows, spans):
            aux = aux_columns(aux_ref, rows)
            q = act_stage(q_ref[0, rows, :].astype(f32), prev_rows(q_ref, lo), aux, w_ref[0], True)[2]
            k = act_stage(k_ref[0, rows, :].astype(f32), prev_rows(k_ref, lo), aux, w_ref[1], True)[2]
            v = act_stage(v_ref[0, rows, :].astype(f32), prev_rows(v_ref, lo), aux, w_ref[2], False)[2]
            beta = beta_column(b_ref[0, rows, :].astype(f32), h)
            strict, inclusive = masks(aux, aux_ref[0, 0:1, rows])
            kb = k.astype(bf)
            qb = q.astype(bf)
            both = nt(jnp.concatenate([kb, qb], axis=0), kb)
            many.append(jnp.where(strict, beta * both[:C], 0.0).astype(bf))
            p_ref[0, 0, rows, :] = jnp.where(inclusive, both[C:], 0.0).astype(bf)
            q_s[rows, :] = qb
            keys.append((k * aux[:, 2:3]).astype(bf))
            right.append(jnp.concatenate([(beta * k).astype(bf), (beta * v).astype(bf)], axis=1))
        totals = inverse_many(many, eye, levels)
        wus = [nn(t, r) for t, r in zip(totals, right)]
        kwus = [tn(k, wu) for k, wu in zip(keys, wus)]
        for rows, t, wu, kwu in zip(spans, totals, wus, kwus):
            clast = aux_ref[0, 1:2, rows][:, C - 1:C]
            f_ref[0, 0, rows, :] = (clast * (eye.astype(f32) - kwu[:, :C])).astype(bf)
            b_s[rows, :] = kwu[:, C:]
            t_ref[0, 0, rows, :] = t
            w_out[0, 0, rows, :] = wu[:, :C].astype(bf)
            u_s[rows, :] = wu[:, C:]
        return 0
    lax.fori_loop(0, steps // GROUP, stage_a, 0)
    def scan(c, state):
        rows = pl.ds(pl.multiple_of(c * C, C), C)
        sb = state.astype(bf)
        s_ref[0, 0, rows, :] = sb
        return nn(f_ref[0, 0, rows, :], sb) + b_s[rows, :]
    lax.fori_loop(0, steps, scan, jnp.zeros((C, C), f32), unroll=True)
    def stage_c(c, _):
        rows = pl.ds(pl.multiple_of(c * C, C), C)
        aux = aux_columns(aux_ref, rows)
        carried = aux[:, 1:2]
        ws = nn(jnp.concatenate([w_out[0, 0, rows, :], q_s[rows, :]], axis=0), s_ref[0, 0, rows, :])
        fresh = (u_s[rows, :] - carried * ws[:C]).astype(bf)
        out = carried * ws[C:] + nn(p_ref[0, 0, rows, :], fresh)
        fresh_ref[0, 0, rows, :] = fresh
        o_ref[0, 0, rows, :] = out
        g = g_ref[0, rows, :].astype(f32)
        r = lax.rsqrt(jnp.mean(out * out, axis=-1, keepdims=True) + HEAD_EPS)
        mixed_ref[0, rows, :] = (out * r * gain_ref[0:1] * (g * jax.nn.sigmoid(g))).astype(bf)
        return 0
    lax.fori_loop(0, steps, stage_c, 0, unroll=4)

def specs(length, heads, off):
    return [pl.BlockSpec((1, length, 128), functools.partial(lambda t, b, h: (b, 0, t * heads + h), t)) for t in range(4)] + [
        pl.BlockSpec((1, length, 128), lambda b, h: (b, 0, 4 * heads))]

def mixer_fwd(raw, aux, conv, gain):
    nb, length, width = raw.shape
    heads = (width - 128) // 512
    per = pl.BlockSpec((1, 1, length, 128), lambda b, h: (b, h, 0, 0))
    sh = lambda d: jax.ShapeDtypeStruct((nb, heads, length, 128), d)
    return pl.pallas_call(
        fwd_kernel,
        grid=(nb, heads),
        in_specs=specs(length, heads, 0) + [
            pl.BlockSpec((1, aux.shape[1], length), lambda b, h: (b, 0, 0)),
            pl.BlockSpec((3, conv.shape[1], 128), lambda b, h: (0, 0, h)),
            pl.BlockSpec((1, 128), lambda b, h: (0, 0)),
        ],
        out_specs=[pl.BlockSpec((1, length, 128), lambda b, h: (b, 0, h))] + [per] * 7,
        out_shape=[jax.ShapeDtypeStruct((nb, length, heads * 128), bf)] + [sh(bf)] * 6 + [sh(f32)],
        scratch_shapes=[pltpu.VMEM((length, 128), bf), pltpu.VMEM((length, 128), f32), pltpu.VMEM((length, 128), f32)],
        cost_estimate=lasting(33),
        name="mixer_forward",
    )(raw, raw, raw, raw, raw, aux, conv, gain)

def bwd_kernel(q_ref, k_ref, v_ref, g_ref, b_ref, aux_ref, w_ref, gain_ref,
               t_ref, w_in, p_ref, f_ref, s_ref, fresh_ref, o_ref, dm_ref,
               draw_ref, dconv_ref, dgain_ref,
               do_s, pd_s, base_s, ds_s):
    h = pl.program_id(1)
    heads = pl.num_programs(1)
    length = q_ref.shape[1]
    steps = length // C
    gain = gain_ref[0:1]
    def stage_a(group, dgain):
        spans, dos, lefts, carries = [], [], [], []
        for n in range(BACK_A):
            lo = pl.multiple_of((group * BACK_A + n) * C, C)
            rows = pl.ds(lo, C)
            aux = aux_columns(aux_ref, rows)
            q = act_stage(q_ref[0, rows, :].astype(f32), prev_rows(q_ref, lo), aux, w_ref[0], True)[2]
            out = o_ref[0, 0, rows, :]
            g = g_ref[0, rows, :].astype(f32)
            dm = dm_ref[0, rows, :].astype(f32)
            s = jax.nn.sigmoid(g)
            r = lax.rsqrt(jnp.mean(out * out, axis=-1, keepdims=True) + HEAD_EPS)
            scaled = out * r
            dn = dm * (g * s)
            dg = dm * scaled * gain * (s * (1.0 + g * (1.0 - s)))
            draw_ref[0, rows, pl.ds(pl.multiple_of((3 * heads + h) * 128, 128), 128)] = dg.astype(bf)
            e = dn * gain
            do = r * (e - scaled * jnp.mean(e * scaled, axis=-1, keepdims=True))
            do_s[rows, :] = do
            dgain = dgain + jnp.sum((dn * scaled).reshape(C // 8, 8, 128), axis=0)
            spans.append(rows)
            dos.append(do)
            lefts.append(q.astype(bf))
            carries.append(aux[:, 1:2])
        pds = [tn(p_ref[0, 0, rows, :], do) for rows, do in zip(spans, dos)]
        bases = [
            tn(jnp.concatenate([(c * do).astype(bf), (-c * pd).astype(bf)], axis=0), jnp.concatenate([q, w_in[0, 0, rows, :]], axis=0))
            for rows, do, pd, q, c in zip(spans, dos, pds, lefts, carries)
        ]
        for rows, pd, base in zip(spans, pds, bases):
            pd_s[rows, :] = pd
            base_s[rows, :] = base
        return dgain
    dgain = lax.fori_loop(0, steps // BACK_A, stage_a, jnp.zeros((8, 128), f32))
    dgain_ref[0, 0] = dgain
    def scan(j, state):
        c = steps - 1 - j
        rows = pl.ds(pl.multiple_of(c * C, C), C)
        sb = state.astype(bf)
        ds_s[rows, :] = sb
        return nn(sb, f_ref[0, 0, rows, :]) + base_s[rows, :]
    lax.fori_loop(0, steps, scan, jnp.zeros((C, C), f32), unroll=True)
    row8 = lax.broadcasted_iota(jnp.int32, (8, 128), 0)
    lane = lax.broadcasted_iota(jnp.int32, (C, 128), 1)

    def conv_back(dconv, nxt, aux, w, raw, sh):
        d = dconv * w[0:1]
        dw = [jnp.sum((dconv * raw).reshape(C // 8, 8, 128), axis=0)]
        for i in range(1, w.shape[0]):
            r = pltpu.roll(dconv, C - i, 0)
            p = pltpu.roll(nxt, 8 - i, 0)
            tailrows = jnp.where(row8 >= 8 - i, p, r[C - 8:])
            m = jnp.concatenate([r[:C - 8], tailrows], axis=0) * aux[:, 5 + i:6 + i]
            d = d + m * w[i:i + 1]
            dw.append(jnp.sum((dconv * sh[i - 1]).reshape(C // 8, 8, 128), axis=0))
        return d, dw

    def stage_c(j, carry):
        nq, nk, nv, dws = carry
        parts = []
        for n in range(BACK_C):
            lo = pl.multiple_of((steps - 1 - j * BACK_C - n) * C, C)
            rows = pl.ds(lo, C)
            aux = aux_columns(aux_ref, rows)
            xq = q_ref[0, rows, :].astype(f32)
            xk = k_ref[0, rows, :].astype(f32)
            xv = v_ref[0, rows, :].astype(f32)
            aq = act_stage(xq, prev_rows(q_ref, lo), aux, w_ref[0], True)
            ak = act_stage(xk, prev_rows(k_ref, lo), aux, w_ref[1], True)
            av = act_stage(xv, prev_rows(v_ref, lo), aux, w_ref[2], False)
            beta = beta_column(b_ref[0, rows, :].astype(f32), h)
            kb, qb = ak[2].astype(bf), aq[2].astype(bf)
            parts.append((rows, aux, xq, xk, xv, aq, ak, av, beta, kb, qb))
        grams = [nt(p[9], p[9]) for p in parts]
        from_next = [nt(p[9], ds_s[p[0], :]) for p in parts]
        from_state = [nn(p[9], s_ref[0, 0, p[0], :]) for p in parts]
        ys = [tn(t_ref[0, 0, p[0], :], pd_s[p[0], :] + p[1][:, 2:3] * d) for p, d in zip(parts, from_next)]
        boths = [
            nt(jnp.concatenate([do_s[p[0], :].astype(bf), y.astype(bf)], axis=0), fresh_ref[0, 0, p[0], :]) for p, y in zip(parts, ys)
        ]
        dxs = [p[8] * y for p, y in zip(parts, ys)]
        throughs = [
            nt(jnp.concatenate([p[1][:, 1:2] * do_s[p[0], :], -(p[1][:, 1:2] * dx)], axis=0), s_ref[0, 0, p[0], :])
            for p, dx in zip(parts, dxs)
        ]
        freshes = [nn(p[1][:, 2:3] * fresh_ref[0, 0, p[0], :].astype(f32), ds_s[p[0], :]) for p in parts]
        dps, dgss, dbetas = [], [], []
        for p, gram, state, y, both in zip(parts, grams, from_state, ys, boths):
            rows, aux, beta = p[0], p[1], p[8]
            strict, inclusive = masks(aux, aux_ref[0, 0:1, rows])
            x = p[7][2] - aux[:, 1:2] * state
            dps.append(jnp.where(inclusive, both[:C], 0.0).astype(bf))
            da = jnp.where(strict, -both[C:], 0.0)
            dbetas.append(jnp.sum(y * x, axis=-1, keepdims=True) + jnp.sum(da * gram, axis=-1, keepdims=True))
            dg = beta * da
            dgss.append(dg + dg.T)
        dqs = [t[:C] + nn(dp, p[9]) for p, t, dp in zip(parts, throughs, dps)]
        dks = [
            t[C:] + f + tn(dp, p[10]) + nn(dgs, p[9]) for p, t, f, dp, dgs in zip(parts, throughs, freshes, dps, dgss)
        ]
        for p, dq, dk, dv, dbeta in zip(parts, dqs, dks, dxs, dbetas):
            rows, aux, xq, xk, xv, (cq, sq, q, rq, shq), (ck, sk, k, rk, shk), (cv, sv, v, _, shv), beta = p[:9]
            db = dbeta * beta * (1.0 - beta)
            bl = pl.ds(4 * heads * 128, 128)
            @pl.when(h == 0)
            def _():
                draw_ref[0, rows, bl] = jnp.where(lane == 0, db, 0.0).astype(bf)
            @pl.when(h > 0)
            def _():
                old = draw_ref[0, rows, bl]
                draw_ref[0, rows, bl] = jnp.where(lane == h, db.astype(bf).astype(f32), old.astype(f32)).astype(bf)
            dq = rq * (dq - q * jnp.sum(q * dq, axis=-1, keepdims=True))
            dk = rk * (dk - k * jnp.sum(k * dk, axis=-1, keepdims=True))
            dcq = dq * (sq * (1.0 + cq * (1.0 - sq)))
            dck = dk * (sk * (1.0 + ck * (1.0 - sk)))
            dcv = dv * (sv * (1.0 + cv * (1.0 - sv)))
            rq_, wq = conv_back(dcq, nq, aux, w_ref[0], xq, shq)
            rk_, wk = conv_back(dck, nk, aux, w_ref[1], xk, shk)
            rv_, wv = conv_back(dcv, nv, aux, w_ref[2], xv, shv)
            for t, val in ((0, rq_), (1, rk_), (2, rv_)):
                draw_ref[0, rows, pl.ds(pl.multiple_of((t * heads + h) * 128, 128), 128)] = val.astype(bf)
            dws = tuple(a + b for a, b in zip(dws, wq + wk + wv))
            nq, nk, nv = dcq[:8], dck[:8], dcv[:8]
        return nq, nk, nv, dws
    z8 = jnp.zeros((8, 128), f32)
    taps = w_ref.shape[1]
    _, _, _, dws = lax.fori_loop(0, steps // BACK_C, stage_c, (z8, z8, z8, (z8,) * (3 * taps)))
    for n, d in enumerate(dws):
        dconv_ref[0, 0, n] = d

def mixer_bwd(raw, aux, conv, gain, saved, dmixed):
    nb, length, width = raw.shape
    heads = (width - 128) // 512
    taps = conv.shape[1]
    per = pl.BlockSpec((1, 1, length, 128), lambda b, h: (b, h, 0, 0))
    sh = lambda d: jax.ShapeDtypeStruct((nb, heads, length, 128), d)
    draw, dconv, dgain = pl.pallas_call(
        bwd_kernel,
        grid=(nb, heads),
        in_specs=specs(length, heads, 0) + [
            pl.BlockSpec((1, aux.shape[1], length), lambda b, h: (b, 0, 0)),
            pl.BlockSpec((3, taps, 128), lambda b, h: (0, 0, h)),
            pl.BlockSpec((1, 128), lambda b, h: (0, 0)),
        ] + [per] * 7 + [pl.BlockSpec((1, length, 128), lambda b, h: (b, 0, h))],
        out_specs=[pl.BlockSpec((1, length, width), lambda b, h: (b, 0, 0)),
                   pl.BlockSpec((1, 1, 3 * taps, 8, 128), lambda b, h: (b, h, 0, 0, 0)),
                   pl.BlockSpec((1, 1, 8, 128), lambda b, h: (b, h, 0, 0))],
        out_shape=[jax.ShapeDtypeStruct((nb, length, width), bf),
                   jax.ShapeDtypeStruct((nb, heads, 3 * taps, 8, 128), f32),
                   jax.ShapeDtypeStruct((nb, heads, 8, 128), f32)],
        scratch_shapes=[pltpu.VMEM((length, 128), f32)] * 3 + [pltpu.VMEM((length, 128), bf)],
        cost_estimate=lasting(2),
        name="mixer_backward",
    )(raw, raw, raw, raw, raw, aux, conv, gain, *saved, dmixed)
    dconv = jnp.sum(dconv, axis=(0, 3)).reshape(heads, 3, taps, 128).transpose(1, 2, 0, 3).reshape(3, taps, heads * 128)
    return draw, dconv, jnp.sum(dgain, axis=(0, 1, 2))

def make_aux(segments):
    nb, length = segments.shape
    seg = segments.astype(f32)
    blocks = seg.reshape(nb, length // C, C)
    last = blocks[:, :, -1:]
    before = jnp.concatenate([jnp.full((nb, 1, 1), -1.0, f32), last[:, :-1]], axis=1)
    carried = (blocks == before).astype(f32).reshape(nb, length)
    tail = (blocks == last).astype(f32).reshape(nb, length)
    cols = [seg, carried, tail]
    for i in range(1, 4):
        cols.append((jnp.pad(seg, ((0, 0), (i, 0)), constant_values=-1.0)[:, :length] == seg).astype(f32))
    for i in range(1, 4):
        cols.append((jnp.pad(seg, ((0, 0), (0, i)), constant_values=-1.0)[:, i:] == seg).astype(f32))
    cols += [jnp.zeros_like(seg)] * (16 - len(cols))
    return jnp.stack(cols, axis=1)


SLOTS = ((0, 0, 0), (0, 0, 1), (1, 0, 0), (0, 1, 0), (1, 0, 1), (0, 1, 1), (1, 1, 0), (1, 1, 1))
MESH = pl.DeviceIdType.MESH
VM = pl.BlockSpec(memory_space=pltpu.VMEM)
ANY = pl.BlockSpec(memory_space=pl.ANY)


def slot_place(r, gx, gy):
    dx, dy, dc = SLOTS[r]
    hi, lo = gx // 2, gx % 2
    hi = 1 - hi if dy else hi
    lo = 1 - lo if dc else lo
    return hi * 2 + lo, (1 - gy if dx else gy)


def slot_peer(r, gx, gy):
    px, py = slot_place(r, gx, gy)
    return {"gx": px, "gy": py}


def flipped(index, n, size):
    out, bit = 0, 1
    while bit < size:
        digit = index // bit % 2
        out = out + bit * (1 - digit if n & bit else digit)
        bit *= 2
    return out


def entry_barrier(peers):
    sem = pltpu.get_barrier_semaphore()
    for peer in peers:
        pl.semaphore_signal(sem, inc=1, device_id=peer, device_id_type=MESH)
    pl.semaphore_wait(sem, len(peers))


def remote(src, dst, send, recv, peer):
    return pltpu.make_async_remote_copy(src, dst, send, recv, device_id=peer, device_id_type=MESH)


def nt_dot(a, b):
    return lax.dot_general(a, b, (((1,), (1,)), ((), ())), preferred_element_type=f32)


def nn_dot(a, b):
    return lax.dot_general(a, b, (((1,), (0,)), ((), ())), preferred_element_type=f32)


class Gather:
    COPIES = 13

    def __init__(self, buf, send, recv, gx, gy, over_gx=False):
        rows = buf.shape[1]
        half = rows // 2
        a, b = pl.ds(0, half), pl.ds(half, half)
        core, xn, yn = (slot_peer(r, gx, gy) for r in (1, 2, 3))

        def make(i, src, dst, part, peer):
            return remote(buf.at[src, part], buf.at[dst, part], send.at[i], recv.at[i], peer)

        self.own = [
            make(0, 0, 2, a, xn),
            make(1, 0, 3, a, yn),
            make(2, 0, 2, b, xn),
            make(3, 0, 3, b, yn),
            remote(buf.at[0], buf.at[1], send.at[4], recv.at[4], core),
        ]
        self.over_gx = over_gx
        self.diagonal = [make(5, 2, 6, a, yn) if over_gx else make(5, 3, 6, a, xn), make(6, 2, 6, b, yn)]
        self.cross = [
            make(7, 2, 4, a, core),
            make(8, 2, 4, b, core),
            make(9, 3, 5, a, core),
            make(10, 3, 5, b, core),
            make(11, 6, 7, a, core),
            make(12, 6, 7, b, core),
        ]

    def start(self):
        for c in self.own:
            c.start()

    def step(self, i):
        if i == 1:
            self.own[4].wait_recv()
        elif i == 2:
            self.own[1].wait_recv()
            if not self.over_gx:
                self.diagonal[0].start()
            self.cross[2].start()
            self.own[0].wait_recv()
            if self.over_gx:
                self.diagonal[0].start()
            self.cross[0].start()
            self.own[2].wait_recv()
            self.diagonal[1].start()
            self.cross[1].start()
        elif i == 3:
            self.own[3].wait_recv()
            self.cross[3].start()
        elif i == 4:
            self.cross[0].wait_recv()
            self.cross[1].wait_recv()
        elif i == 5:
            self.cross[2].wait_recv()
            self.cross[3].wait_recv()
        elif i == 6:
            self.diagonal[0].wait_recv()
            self.cross[4].start()
            self.diagonal[1].wait_recv()
            self.cross[5].start()
        elif i == 7:
            self.cross[4].wait_recv()
            self.cross[5].wait_recv()

    def finish(self):
        for c in self.own + self.diagonal + self.cross:
            c.wait_send()


def head_kernel(
    x_ref, wq_ref, wk_ref, wv_ref, wg_ref, wb_ref, gate_ref, up_ref, down_ref, out_ref, gain_ref,
    normed_ref, raw_ref, hw_ref, own_ref, gu_ref, wo_ref,
    buf, w, low, acc, ag_send, ag_recv, w_send, w_recv, load_sem, out_sem, raw_sem, hw_sem, z_send, z_recv, u_send, u_recv,
):
    gx, gy, dp = lax.axis_index("gx"), lax.axis_index("gy"), lax.axis_index("dp")
    ngx = 4
    units = gu_ref.shape[1] // 2
    parts = (x_ref.shape[1] + units // 2) // gu_ref.shape[0]
    piece = x_ref.shape[1] // parts
    down_piece = units // 2 // parts
    unit_other = pl.multiple_of((1 - gy) * (gate_ref.shape[1] - units), 128)
    turn = flipped(dp, 0, parts)
    rows_sent = pl.ds(pl.multiple_of(turn * piece, piece), piece)
    rows = own_ref.shape[0]
    part = x_ref.shape[1]
    width = wq_ref.shape[1] // 2
    weights = ((wq_ref, width), (wk_ref, width), (wv_ref, width), (wg_ref, width), (wb_ref, 128))
    starts = [0, width, 2 * width, 3 * width, 4 * width]
    xn = slot_peer(2, gx, gy)
    loads = [pltpu.make_async_copy(x_ref, buf.at[0], load_sem.at[5])]
    for i, (ref, n) in enumerate(weights):
        src = ref.at[:, pl.ds(pl.multiple_of(gy * n, 128), n)]
        loads.append(pltpu.make_async_copy(src, w.at[0, :, pl.ds(starts[i], n)], load_sem.at[i]))
    for c in loads:
        c.start()
    peers = [slot_peer(r, gx, gy) for r in (1, 2, 3)] + [{"dp": flipped(dp, n, parts)} for n in range(1, parts)]
    entry_barrier(peers)
    swaps = []
    for i, (ref, n) in enumerate(weights):
        src = ref.at[rows_sent, pl.ds(pl.multiple_of((1 - gy) * n, 128), n)]
        swaps.append(remote(src, w.at[1, rows_sent, pl.ds(starts[i], n)], w_send.at[i], w_recv.at[i], xn))
        swaps[-1].start()
    loads[0].wait()
    gather = Gather(buf, ag_send, ag_recv, gx, gy, True)
    gather.start()
    extra = [
        remote(gate_ref.at[rows_sent, pl.ds(unit_other, units)], gu_ref.at[pl.ds(0, piece), pl.ds(0, units)], u_send.at[0], u_recv.at[0], xn),
        remote(up_ref.at[rows_sent, pl.ds(unit_other, units)], gu_ref.at[pl.ds(0, piece), pl.ds(units, units)], u_send.at[1], u_recv.at[1], xn),
        remote(
            down_ref.at[pl.ds(pl.multiple_of(unit_other + units // 2 + turn * down_piece, 32), down_piece), :],
            gu_ref.at[pl.ds(piece, down_piece), pl.ds(0, x_ref.shape[1])],
            u_send.at[3],
            u_recv.at[3],
            xn,
        ),
        remote(out_ref.at[pl.ds(pl.multiple_of((1 - gy) * width, width), width), :], wo_ref, u_send.at[2], u_recv.at[2], xn),
    ]
    for c in extra:
        c.start()
    for c in swaps:
        c.wait_recv()
    spread = [
        remote(w.at[1, rows_sent], w.at[1, rows_sent], z_send.at[n], z_recv.at[n], {"dp": flipped(dp, n, parts)}) for n in range(1, parts)
    ]
    for c in spread:
        c.start()
    for c in loads[1:]:
        c.wait()
    keep = pltpu.make_async_copy(w.at[0], hw_ref.at[pl.ds(pl.multiple_of(gy * part, part), part)], hw_sem.at[0])
    keep.start()
    near = pl.ds(pl.multiple_of(gy * part, part), part)
    far = pl.ds(pl.multiple_of((1 - gy) * part, part), part)
    stores = []
    blocks = []

    def pair(n, first, second):
        px, _ = slot_place(first, gx, gy)
        for s in range(2):
            span = pl.ds(s * rows, rows)
            v = s * ngx + px
            i = 2 * n + s
            x0 = buf[first, span, :].astype(f32)
            x1 = buf[second, span, :].astype(f32)
            total = jnp.sum(x0 * x0, axis=-1, keepdims=True) + jnp.sum(x1 * x1, axis=-1, keepdims=True)
            rate = lax.rsqrt(total / (2 * part) + EPS)
            low[i, :, near] = (x0 * rate * gain_ref[:, near]).astype(bf)
            low[i, :, far] = (x1 * rate * gain_ref[:, far]).astype(bf)
            c = pltpu.make_async_copy(low.at[i], normed_ref.at[v], out_sem.at[i])
            c.start()
            stores.append(c)
            acc[i] = nn_dot(low[i, :, near], w[0])
            blocks.append((i, v))

    for step in (1, 2, 3, 4):
        gather.step(step)
        if step == 2:
            pair(0, 0, 2)
            mine = pl.ds(pl.multiple_of(gy * rows, rows), rows)
            own_ref[:, near] = buf[0, mine, :]
            own_ref[:, far] = buf[2, mine, :]
    pair(1, 1, 4)
    gather.step(5)
    gather.step(6)
    pair(2, 3, 6)
    gather.step(7)
    pair(3, 5, 7)
    for c in spread:
        c.wait_recv()
    give = pltpu.make_async_copy(w.at[1], hw_ref.at[far], hw_sem.at[1])
    give.start()

    for i, v in blocks:
        acc[i] += nn_dot(low[i, :, far], w[1])
        c = pltpu.make_async_copy(acc.at[i], raw_ref.at[v], raw_sem.at[i])
        c.start()
        stores.append(c)
    keep.wait()
    give.wait()
    for c in stores:
        c.wait()
    for c in extra:
        c.wait_recv()
    for c in swaps + spread + extra:
        c.wait_send()
    gather.finish()


def head_project(inputs, w_query, w_key, w_value, w_gate_head, w_beta, w_gate, w_up, w_down, w_out, gain, units, parts, collective):
    total, part = inputs.shape
    rows = total // 2
    feat = 2 * part
    cols = 2 * w_query.shape[1] + 128
    sd = jax.ShapeDtypeStruct
    return pl.pallas_call(
        head_kernel,
        in_specs=[ANY] * 10 + [VM],
        out_specs=[ANY, ANY, ANY, VM, ANY, ANY],
        out_shape=[
            sd((8, rows, feat), bf),
            sd((8, rows, cols), f32),
            sd((feat, cols), bf),
            sd((rows, feat), bf),
            sd(((part + units // 2) // parts, 2 * units), bf),
            sd((w_out.shape[0] // 2, w_out.shape[1]), bf),
        ],
        scratch_shapes=[
            pltpu.VMEM((8, total, part), bf),
            pltpu.VMEM((2, part, cols), bf),
            pltpu.VMEM((8, rows, feat), bf),
            pltpu.VMEM((8, rows, cols), f32),
            pltpu.SemaphoreType.DMA((13,)),
            pltpu.SemaphoreType.DMA((13,)),
            pltpu.SemaphoreType.DMA((5,)),
            pltpu.SemaphoreType.DMA((5,)),
            pltpu.SemaphoreType.DMA((6,)),
            pltpu.SemaphoreType.DMA((8,)),
            pltpu.SemaphoreType.DMA((8,)),
            pltpu.SemaphoreType.DMA((2,)),
            pltpu.SemaphoreType.DMA((4,)),
            pltpu.SemaphoreType.DMA((4,)),
            pltpu.SemaphoreType.DMA((4,)),
            pltpu.SemaphoreType.DMA((4,)),
        ],
        compiler_params=pltpu.CompilerParams(collective_id=collective, has_side_effects=True, vmem_limit_bytes=60 << 20),
        cost_estimate=lasting(80),
        name="head_project",
    )(inputs, w_query, w_key, w_value, w_gate_head, w_beta, w_gate, w_up, w_down, w_out, gain)


def mlp_kernel(x_ref, gate_ref, up_ref, down_ref, y_ref, *refs, parts):
    gu_refs, piece_ref, refs = refs[:parts], refs[parts], refs[parts + 1 :]
    mlp_body(parts, x_ref, gate_ref, up_ref, down_ref, y_ref, gu_refs, piece_ref, *refs)


def mlp_body(
    parts, x_ref, gate_ref, up_ref, down_ref, y_ref, gu_refs, piece_ref,
    second_ref, hidden_ref, grads_ref, yrel_ref, gu_out, dn_out,
    wgu, wd, buf, ybuf, hbuf, gbuf, load_sem, w_sem, keep_sem, y_sem, y_out_sem, out_sem, ag_send, ag_recv,
):
    gx, gy = lax.axis_index("gx"), lax.axis_index("gy")
    ngy = 2
    rows = x_ref.shape[0]
    feat = x_ref.shape[1]
    units = wd.shape[0]
    half = feat // 2
    tile = 256
    dp = lax.axis_index("dp")
    unit_mine = pl.multiple_of(gy * (gate_ref.shape[1] - units), 128)
    doubled = gy * (2 * units - gate_ref.shape[1])
    load = pltpu.make_async_copy(x_ref, buf.at[0], load_sem)
    load.start()
    near = pl.ds(pl.multiple_of(gy * half, half), half)
    far = pl.multiple_of((1 - gy) * half, half)
    own_units = pl.ds(unit_mine, units)
    w_loads = [
        pltpu.make_async_copy(gate_ref.at[:, own_units], wgu.at[near, pl.ds(0, units)], w_sem.at[0]),
        pltpu.make_async_copy(up_ref.at[:, own_units], wgu.at[near, pl.ds(units, units)], w_sem.at[1]),
        pltpu.make_async_copy(down_ref.at[own_units, :], wd.at[:, near], w_sem.at[2]),
    ]
    w_loads.append(pltpu.make_async_copy(piece_ref, wd.at[pl.ds(0, units // 2), pl.ds(far, half)], w_sem.at[3]))
    for n in range(parts):
        turn = flipped(dp, n, parts)
        piece = half // parts
        down_piece = units // 2 // parts
        gu_rows = wgu.at[pl.ds(pl.multiple_of(far + turn * piece, piece), piece), :]
        down_rows = wd.at[pl.ds(pl.multiple_of(units // 2 + turn * down_piece, 32), down_piece), pl.ds(far, half)]
        w_loads.append(pltpu.make_async_copy(gu_refs[n].at[pl.ds(0, piece)], gu_rows, w_sem.at[4 + 2 * n]))
        w_loads.append(pltpu.make_async_copy(gu_refs[n].at[pl.ds(piece, down_piece), pl.ds(0, half)], down_rows, w_sem.at[5 + 2 * n]))
    for c in w_loads:
        c.start()
    entry_barrier([slot_peer(r, gx, gy) for r in (1, 2, 3)])
    load.wait()
    gather = Gather(buf, ag_send, ag_recv, gx, gy)
    gather.start()

    def y_load(r, n):
        px, py = slot_place(r, gx, gy)
        return [
            pltpu.make_async_copy(y_ref.at[px * ngy + h, py], ybuf.at[r % 2, :, pl.ds(h * (feat // 2), feat // 2)], y_sem.at[r % 2, h])
            for h in range(2)
        ]

    def y_store(r):
        return pltpu.make_async_copy(ybuf.at[r % 2], yrel_ref.at[r], y_out_sem.at[r % 2])

    for c in y_load(0, 0):
        c.start()
    for c in w_loads:
        c.wait()
    keeps = [pltpu.make_async_copy(wgu, gu_out, keep_sem.at[0]), pltpu.make_async_copy(wd, dn_out, keep_sem.at[1])]
    for c in keeps:
        c.start()

    def outs(r):
        return [
            pltpu.make_async_copy(buf.at[r], second_ref.at[r], out_sem.at[0, r % 2]),
            pltpu.make_async_copy(hbuf.at[r % 2], hidden_ref.at[r], out_sem.at[1, r % 2]),
            pltpu.make_async_copy(gbuf.at[r % 2], grads_ref.at[r], out_sem.at[2, r % 2]),
        ]

    for r in range(8):
        gather.step(r)
        if r >= 2:
            for c in outs(r - 2):
                c.wait()
        if r + 1 < 8:
            if r >= 1:
                y_store(r - 1).wait()
            for c in y_load(r + 1, 0):
                c.start()
        for c in y_load(r, 0):
            c.wait()
        y_store(r).start()

        def body(t, _):
            cols = pl.ds(pl.multiple_of(t * tile, tile), tile)
            up_cols = pl.ds(pl.multiple_of(units + t * tile, tile), tile)
            gate = nn_dot(buf[r], wgu[:, cols])
            up = nn_dot(buf[r], wgu[:, up_cols])
            gh = nt_dot(ybuf[r % 2], wd[cols, :])
            s = jax.nn.sigmoid(gate)
            keep = lax.broadcasted_iota(jnp.int32, gate.shape, 1) + t * tile >= doubled
            act = jnp.where(keep, gate * s, 0.0)
            up = jnp.where(keep, up, 0.0)
            hbuf[r % 2, :, cols] = (act * up).astype(bf)
            gbuf[r % 2, :, up_cols] = (gh * act).astype(bf)
            gbuf[r % 2, :, cols] = (gh * up * s * (1.0 + gate * (1.0 - s))).astype(bf)
            return 0

        lax.fori_loop(0, units // tile, body, 0)
        for c in outs(r):
            c.start()
    for r in (6, 7):
        for c in outs(r):
            c.wait()
        y_store(r).wait()
    gather.finish()
    for c in keeps:
        c.wait()


def mlp_forward(x_own, w_gate, w_up, w_down, y_all, gu_pieces, down_piece, units, collective):
    rows, feat = x_own.shape
    parts = len(gu_pieces)
    sd = jax.ShapeDtypeStruct
    return pl.pallas_call(
        functools.partial(mlp_kernel, parts=parts),
        in_specs=[ANY] * (6 + parts),
        out_specs=[ANY] * 6,
        out_shape=[
            sd((8, rows, feat), bf),
            sd((8, rows, units), bf),
            sd((8, rows, 2 * units), bf),
            sd((8, rows, feat), bf),
            sd((feat, 2 * units), bf),
            sd((units, feat), bf),
        ],
        scratch_shapes=[
            pltpu.VMEM((feat, 2 * units), bf),
            pltpu.VMEM((units, feat), bf),
            pltpu.VMEM((8, rows, feat), bf),
            pltpu.VMEM((2, rows, feat), bf),
            pltpu.VMEM((2, rows, units), bf),
            pltpu.VMEM((2, rows, 2 * units), bf),
            pltpu.SemaphoreType.DMA,
            pltpu.SemaphoreType.DMA((4 + 2 * parts,)),
            pltpu.SemaphoreType.DMA((2,)),
            pltpu.SemaphoreType.DMA((2, 2)),
            pltpu.SemaphoreType.DMA((2,)),
            pltpu.SemaphoreType.DMA((3, 2)),
            pltpu.SemaphoreType.DMA((13,)),
            pltpu.SemaphoreType.DMA((13,)),
        ],
        compiler_params=pltpu.CompilerParams(collective_id=collective, has_side_effects=True, vmem_limit_bytes=62 << 20),
        cost_estimate=lasting(68),
        name="mlp_forward",
    )(x_own, w_gate, w_up, w_down, y_all, *gu_pieces, down_piece)


class Scatter:
    def __init__(self, give, take, acc, diag_in, last_in, s_core, r_core, s_link, r_link, gx, gy, over_gx=False):
        self.over_gx = over_gx
        self.give, self.take, self.acc, self.diag_in, self.last_in = give, take, acc, diag_in, last_in
        core, xn, yn = (slot_peer(r, gx, gy) for r in (1, 2, 3))
        rows = acc.shape[1]
        half = rows // 2
        a, b = pl.ds(0, half), pl.ds(half, half)
        self.a, self.b = a, b
        self.core = [remote(give.at[n], take.at[n], s_core.at[n], r_core.at[n], core) for n in range(4)]

        def link(i, src, dst, peer):
            return remote(src, dst, s_link.at[i], r_link.at[i], peer)

        self.link = [
            link(0, acc.at[0, a], diag_in.at[0], yn if over_gx else xn),
            link(1, acc.at[0, b], diag_in.at[1], yn),
            link(2, acc.at[1, a], last_in.at[0, a], xn),
            link(3, acc.at[2, b], last_in.at[1, b], yn),
            link(4, acc.at[1, b], last_in.at[0, b], xn),
            link(5, acc.at[2, a], last_in.at[1, a], yn),
        ]

    def begin(self, product, self_acc, between=None):
        acc = self.acc

        def give_out(n, slot):
            def put(cols, value):
                self.give[n, :, cols] = value.astype(bf)

            product(slot, put)
            self.core[n].start()

        def keep(n, slot):
            def put(cols, value):
                acc[n, :, cols] = value.astype(bf)

            product(slot, put)

        def join(n):
            self.core[n].wait_recv()
            acc[n] = (acc[n].astype(f32) + self.take[n].astype(f32)).astype(bf)

        give_out(0, 7)
        keep(0, 6)
        give_out(1, 4)
        if between is not None:
            between()
        join(0)
        self.link[0].start()
        self.link[1].start()
        give_out(2, 5)
        keep(1, 2)
        join(1)
        if not self.over_gx:
            self.link[2].start()
        keep(2, 3)
        join(2)
        self.link[3].start()
        if self.over_gx:
            self.link[5].start()
        give_out(3, 1)

        def put_self(cols, value):
            self_acc[:, cols] = value

        product(0, put_self)

    def forward(self):
        acc, a, b = self.acc, self.a, self.b
        if self.over_gx:
            for i, half, onward in ((0, a, 2), (1, b, 4)):
                self.link[i].wait_recv()
                acc[1, half] = (acc[1, half].astype(f32) + self.diag_in[i].astype(f32)).astype(bf)
                self.link[onward].start()
            return
        self.link[1].wait_recv()
        acc[1, b] = (acc[1, b].astype(f32) + self.diag_in[1].astype(f32)).astype(bf)
        self.link[4].start()
        self.link[0].wait_recv()
        acc[2, a] = (acc[2, a].astype(f32) + self.diag_in[0].astype(f32)).astype(bf)
        self.link[5].start()

    def end(self, self_acc):
        self.core[3].wait_recv()
        self_acc[...] += self.take[3].astype(f32)
        for c in self.link[2:]:
            c.wait_recv()
        self_acc[...] += self.last_in[0].astype(f32) + self.last_in[1].astype(f32)

    def run(self, product, self_acc):
        self.begin(product, self_acc)
        self.forward()
        self.end(self_acc)

    def finish(self):
        for c in self.core + self.link:
            c.wait_send()


def scatter_scratch(rows, feat):
    return [
        pltpu.VMEM((4, rows, feat), bf),
        pltpu.VMEM((4, rows, feat), bf),
        pltpu.VMEM((3, rows, feat), bf),
        pltpu.VMEM((2, rows // 2, feat), bf),
        pltpu.VMEM((2, rows, feat), bf),
        pltpu.SemaphoreType.DMA((4,)),
        pltpu.SemaphoreType.DMA((4,)),
        pltpu.SemaphoreType.DMA((6,)),
        pltpu.SemaphoreType.DMA((6,)),
    ]


def own_out_rows(out_ref, piece_ref, w, sem, gy):
    width, part = piece_ref.shape
    near = pl.ds(pl.multiple_of(gy * part, part), part)
    far = pl.ds(pl.multiple_of((1 - gy) * part, part), part)
    return [
        pltpu.make_async_copy(out_ref.at[pl.ds(pl.multiple_of(gy * width, width), width), :], w.at[:, near], sem.at[0]),
        pltpu.make_async_copy(piece_ref, w.at[:, far], sem.at[1]),
    ]


def out_kernel(
    mixed_ref, out_ref, piece_ref, x_ref, gain_ref,
    middle_ref, normed_ref, slots_ref, other_ref,
    give, take, acc, diag_in, last_in, s_core, r_core, s_link, r_link, lhs, w, total, load_sem, lhs_sem, keep_sem,
):
    gx, gy = lax.axis_index("gx"), lax.axis_index("gy")
    feat = x_ref.shape[1]
    tile = 512
    loads = own_out_rows(out_ref, piece_ref, w, load_sem, gy)
    pulls = {}
    for r in (7, 6, 4, 5, 2, 3, 1, 0):
        px, py = slot_place(r, gx, gy)
        pulls[r] = pltpu.make_async_copy(mixed_ref.at[py * 4 + px], lhs.at[r], lhs_sem.at[r])
    for c in loads + list(pulls.values()):
        c.start()
    entry_barrier([slot_peer(r, gx, gy) for r in (1, 2, 3)])
    for c in loads:
        c.wait()

    def product(slot, put):
        pulls[slot].wait()

        def body(t, _):
            cols = pl.ds(pl.multiple_of(t * tile, tile), tile)
            put(cols, nn_dot(lhs[slot], w[:, cols]))
            return 0

        lax.fori_loop(0, feat // tile, body, 0)

    scatter = Scatter(give, take, acc, diag_in, last_in, s_core, r_core, s_link, r_link, gx, gy)
    scatter.run(product, total)
    keep = pltpu.make_async_copy(lhs, slots_ref, keep_sem)
    keep.start()
    middle = x_ref[...].astype(f32) + total[...]
    middle_ref[...] = middle
    other_ref[...] = middle_ref[:, pl.ds(pl.multiple_of((1 - gy) * (feat // 2), feat // 2), feat // 2)].astype(bf)
    rate = lax.rsqrt(jnp.mean(middle * middle, axis=-1, keepdims=True) + EPS)
    normed_ref[...] = (middle * rate * gain_ref[...]).astype(bf)
    keep.wait()
    scatter.finish()


def out_project(mixed, w_out, piece, x_own, gain, collective):
    rows, feat = x_own.shape
    width = mixed.shape[2]
    sd = jax.ShapeDtypeStruct
    return pl.pallas_call(
        out_kernel,
        in_specs=[ANY, ANY, ANY, VM, VM],
        out_specs=[VM, VM, ANY, VM],
        out_shape=[sd((rows, feat), f32), sd((rows, feat), bf), sd(mixed.shape, bf), sd((rows, feat // 2), bf)],
        scratch_shapes=scatter_scratch(rows, feat)
        + [
            pltpu.VMEM(mixed.shape, bf),
            pltpu.VMEM((width, feat), bf),
            pltpu.VMEM((rows, feat), f32),
            pltpu.SemaphoreType.DMA((2,)),
            pltpu.SemaphoreType.DMA((8,)),
            pltpu.SemaphoreType.DMA,
        ],
        compiler_params=pltpu.CompilerParams(collective_id=collective, has_side_effects=True, vmem_limit_bytes=60 << 20),
        cost_estimate=lasting(44),
        name="out_project",
    )(mixed, w_out, piece, x_own, gain)


def back_kernel(
    grads_ref, wgu_ref, out_ref, piece_ref, middle_ref, y_ref, gain_ref,
    mid_ref, gmix_ref, dgain_ref,
    give, take, acc, diag_in, last_in, s_core, r_core, s_link, r_link,
    lhs, wgu, w, total, buf, gstage, y_own, load_sem, lhs_sem, ag_send, ag_recv, mid_sem, gmix_sem,
):
    gx, gy = lax.axis_index("gx"), lax.axis_index("gy")
    rows, feat = middle_ref.shape
    tile = 512
    load = pltpu.make_async_copy(wgu_ref, wgu, load_sem.at[2])
    outs = own_out_rows(out_ref, piece_ref, w, load_sem, gy)
    order = (7, 6, 4, 5, 2, 3, 1, 0)
    pulls = {r: pltpu.make_async_copy(grads_ref.at[r], lhs.at[r], lhs_sem.at[r]) for r in order}
    pulls[7].start()
    load.start()
    for r in order[1:]:
        pulls[r].start()
    outs.append(pltpu.make_async_copy(y_ref.at[0], y_own, load_sem.at[3]))
    for c in outs:
        c.start()
    entry_barrier([slot_peer(r, gx, gy) for r in (1, 2, 3)])
    load.wait()

    def product(slot, put):
        pulls[slot].wait()

        def body(t, _):
            cols = pl.ds(pl.multiple_of(t * tile, tile), tile)
            put(cols, nt_dot(lhs[slot], wgu[cols, :]))
            return 0

        lax.fori_loop(0, feat // tile, body, 0)

    scatter = Scatter(give, take, acc, diag_in, last_in, s_core, r_core, s_link, r_link, gx, gy, True)
    scatter.run(product, total)
    middle = middle_ref[...]
    incoming = total[...]
    rate = lax.rsqrt(jnp.mean(middle * middle, axis=-1, keepdims=True) + EPS)
    scaled = gain_ref[...] * incoming
    inner = jnp.mean(middle * scaled, axis=-1, keepdims=True)
    for c in outs:
        c.wait()
    buf[0] = (y_own[...].astype(f32) + rate * scaled - middle * (rate * rate * rate) * inner).astype(bf)
    gather = Gather(buf, ag_send, ag_recv, gx, gy)
    gather.start()
    dgain_ref[...] = jnp.sum((incoming * middle * rate).reshape(rows // 8, 8, feat), axis=0)
    stores = []
    for r in range(8):
        gather.step(r)
        px, py = slot_place(r, gx, gy)
        gstage[r] = nt_dot(buf[r], w[...]).astype(bf)
        stores.append(pltpu.make_async_copy(gstage.at[r], gmix_ref.at[py * 4 + px], gmix_sem.at[r]))
        stores.append(pltpu.make_async_copy(buf.at[r], mid_ref.at[r], mid_sem.at[r]))
        for c in stores[-2:]:
            c.start()
    for c in stores:
        c.wait()
    gather.finish()
    scatter.finish()


def mlp_backward(grads, gate_up, w_out, piece, middle, y_rel, gain, collective):
    rows, feat = middle.shape
    width = piece.shape[0]
    sd = jax.ShapeDtypeStruct
    return pl.pallas_call(
        back_kernel,
        in_specs=[ANY, ANY, ANY, ANY, VM, ANY, VM],
        out_specs=[ANY, ANY, VM],
        out_shape=[sd((8, rows, feat), bf), sd((8, rows, width), bf), sd((8, feat), f32)],
        scratch_shapes=scatter_scratch(rows, feat)
        + [
            pltpu.VMEM(grads.shape, bf),
            pltpu.VMEM(gate_up.shape, bf),
            pltpu.VMEM((width, feat), bf),
            pltpu.VMEM((rows, feat), f32),
            pltpu.VMEM((8, rows, feat), bf),
            pltpu.VMEM((8, rows, width), bf),
            pltpu.VMEM((rows, feat), bf),
            pltpu.SemaphoreType.DMA((4,)),
            pltpu.SemaphoreType.DMA((8,)),
            pltpu.SemaphoreType.DMA((13,)),
            pltpu.SemaphoreType.DMA((13,)),
            pltpu.SemaphoreType.DMA((8,)),
            pltpu.SemaphoreType.DMA((8,)),
        ],
        compiler_params=pltpu.CompilerParams(collective_id=collective, has_side_effects=True, vmem_limit_bytes=63 << 20),
        cost_estimate=lasting(20),
        name="mlp_backward",
    )(grads, gate_up, w_out, piece, middle, y_rel, gain)


def final_kernel(
    draw_ref, hw_ref, hidden_ref, dn_ref, x_ref, mid_ref, middle_ref, other_ref, gain_ref, small_ref,
    gin_ref, lout_ref, all_ref,
    give1, take1, acc1, diag1, last1, sc1, rc1, sl1, rl1,
    give2, take2, acc2, diag2, last2, sc2, rc2, sl2, rl2,
    draw, hw, hidden, dn, x, mid, m_near, total1, total2, row_send, row_recv, z_in, z_sum, z_all,
    load_sem, draw_sem, hidden_sem, x_sem, row_sem, z_send, z_recv, p_send, p_recv,
    *, ndp,
):
    gx, gy, dp = lax.axis_index("gx"), lax.axis_index("gy"), lax.axis_index("dp")
    me = gx * 2 + gy
    rows, feat = middle_ref.shape
    part = feat // 2
    tile = 512
    near = pl.ds(pl.multiple_of(gy * part, part), part)
    xn = slot_peer(2, gx, gy)
    pairs = {0: (0, 2), 2: (0, 2), 1: (1, 4), 4: (1, 4), 3: (3, 6), 6: (3, 6), 5: (5, 7), 7: (5, 7)}
    load_hw = pltpu.make_async_copy(hw_ref, hw, load_sem.at[0])
    load_dn = pltpu.make_async_copy(dn_ref, dn, load_sem.at[1])
    order = (7, 5, 6, 3, 4, 1, 2, 0)
    draws = {}
    for r in order:
        px, py = slot_place(r, gx, gy)
        draws[r] = pltpu.make_async_copy(draw_ref.at[py * 4 + px], draw.at[r], draw_sem.at[r])
    hiddens = {r: pltpu.make_async_copy(hidden_ref.at[r], hidden.at[r], hidden_sem.at[r]) for r in order}
    draws[7].start()
    draws[5].start()
    load_hw.start()
    for r in order[2:]:
        draws[r].start()
    load_dn.start()
    for r in order:
        hiddens[r].start()
    finals = [
        pltpu.make_async_copy(x_ref, x, x_sem.at[0]),
        pltpu.make_async_copy(mid_ref.at[0, :, near], mid.at[gy], x_sem.at[1]),
        pltpu.make_async_copy(mid_ref.at[2, :, near], mid.at[1 - gy], x_sem.at[2]),
    ]
    for c in finals:
        c.start()
    finals.append(pltpu.make_async_copy(middle_ref.at[:, near], m_near, x_sem.at[3]))
    finals[-1].start()
    entry_barrier([slot_peer(r, gx, gy) for r in range(1, 8)] + [{"dp": flipped(dp, n, ndp)} for n in range(1, ndp)])
    around = [
        remote(small_ref, z_in.at[n], z_send.at[n], z_recv.at[n], {"dp": flipped(dp, n, ndp)}) for n in range(1, ndp)
    ]
    for c in around:
        c.start()

    def rows_pair(many, copies, slot, waited):
        for r in pairs[slot]:
            if r not in waited:
                copies[r].wait()
                waited.add(r)
        first, second = pairs[slot]
        low = first + (second - first) * gy
        return low, first + second - low

    def maker(many, copies, weights, weight_load, transposed):
        waited = set()

        def product(slot, put):
            low, high = rows_pair(many, copies, slot, waited)
            if weight_load is not None and "w" not in waited:
                weight_load.wait()
                waited.add("w")
            _, py = slot_place(slot, gx, gy)

            def body(t, _):
                cols = pl.ds(pl.multiple_of(t * tile, tile), tile)
                wide = pl.ds(pl.multiple_of(py * part + t * tile, tile), tile)
                if transposed:
                    w = weights[:, wide]
                    value = [nn_dot(many[low], w), nn_dot(many[high], w)]
                else:
                    w = weights[wide, :]
                    value = [nt_dot(many[low], w), nt_dot(many[high], w)]
                put(cols, jnp.concatenate(value, axis=0))
                return 0

            lax.fori_loop(0, part // tile, body, 0)

        return product

    first = Scatter(give1, take1, acc1, diag1, last1, sc1, rc1, sl1, rl1, gx, gy)
    second = Scatter(give2, take2, acc2, diag2, last2, sc2, rc2, sl2, rl2, gx, gy)
    first.begin(maker(draw, draws, hw, load_hw, False), total1)
    for c in around:
        c.wait_recv()
    summed = small_ref[...]
    for n in range(1, ndp):
        summed = summed + z_in[n]
    z_sum[...] = summed
    passes = [remote(z_sum, z_all.at[me], p_send.at[r], p_recv.at[r], slot_peer(r, gx, gy)) for r in range(1, 8)]
    for c in passes:
        c.start()
    second.begin(maker(hidden, hiddens, dn, load_dn, True), total2, first.forward)
    first.end(total1)
    for c in finals:
        c.wait()
    wide_x = x[...].astype(f32)
    scaled = gain_ref[:, near] * total1[...]
    sums = [jnp.sum(wide_x * wide_x, axis=-1, keepdims=True), jnp.sum(wide_x * scaled, axis=-1, keepdims=True)]
    lane = lax.broadcasted_iota(jnp.int32, (2 * rows, 128), 1)
    packed = jnp.where(lane == 0, sums[0], jnp.where(lane == 1, sums[1], 0.0)).T
    row_send[...] = packed[:8]
    row_copy = remote(row_send, row_recv, row_sem.at[0], row_sem.at[1], xn)
    row_copy.start()
    second.forward()
    second.end(total2)
    mine = pl.ds(pl.multiple_of(gy * rows, rows), rows)
    other = pl.ds(pl.multiple_of((1 - gy) * rows, rows), rows)
    lout_ref[gy] = (total2[mine, :] + m_near[...]).astype(bf)
    lout_ref[1 - gy] = (total2[other, :] + other_ref[...].astype(f32)).astype(bf)
    row_copy.wait_recv()
    both = jnp.concatenate([row_send[...] + row_recv[...], jnp.zeros((120, 2 * rows), f32)], axis=0).T
    rate = lax.rsqrt(both[:, 0:1] / feat + EPS)
    inner = both[:, 1:2] / feat
    gin = mid[...].reshape(2 * rows, part).astype(f32) + rate * scaled - wide_x * (rate * rate * rate) * inner
    gin_ref[...] = gin.astype(bf).reshape(2, rows, part)
    z_all[me] = z_sum[...]
    for c in passes:
        c.wait_recv()
    all_ref[...] = z_all[...]
    for c in around + passes + [row_copy]:
        c.wait_send()
    first.finish()
    second.finish()


def final_sums(draw, head_w, hidden, down, inputs, mid, middle, other, gain, small, ndp, collective):
    rows, feat = middle.shape
    part = feat // 2
    sd = jax.ShapeDtypeStruct
    dma = pltpu.SemaphoreType.DMA
    return pl.pallas_call(
        functools.partial(final_kernel, ndp=ndp),
        in_specs=[ANY] * 7 + [VM] * 3,
        out_specs=[VM] * 3,
        out_shape=[sd((2, rows, part), bf), sd((2, rows, part), bf), sd((8, *small.shape), f32)],
        scratch_shapes=scatter_scratch(2 * rows, part)
        + scatter_scratch(2 * rows, part)
        + [
            pltpu.VMEM(draw.shape, bf),
            pltpu.VMEM(head_w.shape, bf),
            pltpu.VMEM(hidden.shape, bf),
            pltpu.VMEM(down.shape, bf),
            pltpu.VMEM((2 * rows, part), bf),
            pltpu.VMEM((2, rows, part), bf),
            pltpu.VMEM((rows, part), f32),
            pltpu.VMEM((2 * rows, part), f32),
            pltpu.VMEM((2 * rows, part), f32),
            pltpu.VMEM((8, 2 * rows), f32),
            pltpu.VMEM((8, 2 * rows), f32),
            pltpu.VMEM((ndp, *small.shape), f32),
            pltpu.VMEM(small.shape, f32),
            pltpu.VMEM((8, *small.shape), f32),
            dma((2,)),
            dma((8,)),
            dma((8,)),
            dma((4,)),
            dma((2,)),
            dma((ndp,)),
            dma((ndp,)),
            dma((8,)),
            dma((8,)),
        ],
        compiler_params=pltpu.CompilerParams(collective_id=collective, has_side_effects=True, vmem_limit_bytes=63 << 20),
        cost_estimate=lasting(5),
        name="final_sums",
    )(draw, head_w, hidden, down, inputs, mid, middle, other, gain, small)


def dot(a, b):
    return lax.dot_general(a, b, (((1,), (0,)), ((), ())), preferred_element_type=f32)


def dot_t(a, b):
    return lax.dot_general(a, b, (((1,), (1,)), ((), ())), preferred_element_type=f32)


def dot_w(a, b):
    return lax.dot_general(a, b, (((0,), (0,)), ((), ())), preferred_element_type=f32)


def swap(value):
    return lax.ppermute(value, "gy", [(0, 1), (1, 0)])


def in_order(mine, other, axis):
    first = lax.axis_index("gy") == 0
    return jnp.concatenate([jnp.where(first, mine, other), jnp.where(first, other, mine)], axis=axis)


def halves(value, axis):
    size = value.shape[axis] // 2
    mine = lax.axis_index("gy")
    return (
        lax.dynamic_slice_in_dim(value, mine * size, size, axis),
        lax.dynamic_slice_in_dim(value, (1 - mine) * size, size, axis),
    )


def scatter_dp(value):
    return lax.psum_scatter(value.astype(bf), "dp", scatter_dimension=0, tiled=True)


def sort_halves(parts):
    first = lax.axis_index("gy") == 0
    return jnp.where(first, parts[0], parts[1]), swap(jnp.where(first, parts[1], parts[0]))


def shards(
    inputs,
    segments,
    norm_gain,
    w_query,
    w_key,
    w_value,
    w_beta,
    w_gate_head,
    conv_kernel,
    head_gain,
    w_out,
    mlp_gain,
    w_gate,
    w_up,
    w_down,
    grad_y,
):
    ngx, ngy, ndp = lax.axis_size("gx"), lax.axis_size("gy"), lax.axis_size("dp")
    gx, gy = lax.axis_index("gx"), lax.axis_index("gy")
    nb, part_rows, part_feat = inputs.shape
    length, feat = part_rows * ngx, part_feat * ngy
    tokens = nb * length
    own_rows = tokens // (ngx * ngy)
    heads = w_beta.shape[1] // ngy
    width = w_query.shape[1] // ngy
    beta_w = jnp.pad(w_beta.T.reshape(ngy, heads, part_feat), ((0, 0), (0, 128 - heads), (0, 0))).reshape(ngy * 128, part_feat).T
    block = w_gate.shape[1]
    units = -(-block // (ngy * 256)) * 256
    parts = ndp if ndp == 4 else 1
    normed, raw, head_w, x_own, gu_piece, out_piece = head_project(
        inputs.reshape(nb * part_rows, part_feat), w_query, w_key, w_value, w_gate_head, beta_w, w_gate, w_up, w_down, w_out,
        norm_gain[None], units, parts, 5,
    )
    normed = normed.reshape(tokens, feat)
    raw = raw.reshape(nb, length, -1)

    def around(value):
        return [value] + [lax.ppermute(value, "dp", [(i, i ^ n) for i in range(ndp)]) for n in range(1, parts)]

    gu_pieces = around(gu_piece)
    x_own, grad_y, w_down = lax.optimization_barrier((x_own, grad_y, w_down))
    down_piece = swap(lax.dynamic_slice_in_dim(w_down, (1 - gy) * (block - units), units // 2, 0))
    y_all = lax.all_gather(grad_y, ("gx", "gy"), axis=0, tiled=False)

    aux = make_aux(segments)
    conv_start = (gx * ngy + gy) * width
    conv_local = lax.dynamic_slice_in_dim(conv_kernel, conv_start, width, 2)
    gain_row = head_gain[None]
    mixed, *saved = mixer_fwd(raw, aux, conv_local, gain_row)
    middle, second_own, mixed_slots, middle_half = out_project(
        mixed.reshape(8, own_rows, width), w_out, out_piece, x_own, mlp_gain[None], 1
    )
    second, hidden, grads, y_rel, gate_up, down_w = mlp_forward(
        second_own, w_gate, w_up, w_down, y_all, gu_pieces, down_piece, units, 6
    )
    second_flat, hidden_flat = second.reshape(tokens, feat), hidden.reshape(tokens, units)
    grads_flat, y_flat = grads.reshape(tokens, 2 * units), y_rel.reshape(tokens, feat)
    half = feat // 2
    gu_first = dot_w(second_flat[:, :half], grads_flat).astype(bf)
    hidden_flat, gu_first = lax.optimization_barrier((hidden_flat, gu_first))
    down_grad = dot_w(hidden_flat, y_flat).astype(bf)
    second_flat, down_grad = lax.optimization_barrier((second_flat, down_grad))
    down_keep, down_send = halves(down_grad, 1)
    down_both = jnp.stack([down_keep, swap(down_send)])
    gu_second = dot_w(second_flat[:, half:], grads_flat).astype(bf)
    grads, gu_second = lax.optimization_barrier((grads, gu_second))
    gu_sums = [scatter_dp(gu_first), scatter_dp(gu_second)]
    first, last = down_both[gy], down_both[1 - gy]
    down_rows = jnp.concatenate([first, last[2 * units - block :]], axis=0)

    mid_slots, grad_mixed, mlp_gain_parts = mlp_backward(
        grads, gate_up, w_out, out_piece, middle, y_rel, mlp_gain[None], 2
    )
    grad_mixed, mid_slots, down_rows, *gu_sums = lax.optimization_barrier((grad_mixed, mid_slots, down_rows, *gu_sums))
    down_sum = scatter_dp(down_rows)
    out_grad = dot_w(mixed_slots.reshape(tokens, width), mid_slots.reshape(tokens, feat)).astype(bf)
    out_keep, out_send = halves(out_grad, 1)
    out_rows = in_order(out_keep, swap(out_send), 0)
    draw, conv_grad, gain_grad = mixer_bwd(
        raw, aux, conv_local, gain_row, saved, grad_mixed.reshape(nb, length, width)
    )
    draw = draw.reshape(tokens, -1)
    gu_pair = sort_halves(gu_sums)
    middle_other = swap(middle_half)
    draw, down_sum, out_rows, middle_other, *gu_pair = lax.optimization_barrier((draw, down_sum, out_rows, middle_other, *gu_pair))
    out_sum = scatter_dp(out_rows)
    main = 4 * width
    both = dot_w(normed, draw).astype(bf)
    norm_gain_grad = jnp.sum(both.astype(f32) * head_w.astype(f32), axis=1) / norm_gain
    beta_grad = both[:, main : main + heads].astype(f32)
    head_grads = both[:, :main].reshape(2, half, main)
    draw, hidden, head_grads = lax.optimization_barrier((draw, hidden, head_grads))
    head_sums = list(lax.psum_scatter(head_grads, "dp", scatter_dimension=1, tiled=True))
    hidden, out_sum = lax.optimization_barrier((hidden, out_sum))
    flat = [beta_grad.T, conv_grad, norm_gain_grad, jnp.sum(mlp_gain_parts, axis=0), gain_grad]
    counts = [v.size // 128 for v in flat]
    small = jnp.concatenate([v.reshape(-1, 128) for v in flat])
    small = jnp.pad(small, ((0, -small.shape[0] % 8), (0, 0)))
    if parts == 1:
        small = lax.psum(small, "dp")
    grad_inputs, layer_out, gathered = final_sums(
        draw.reshape(8, own_rows, -1), head_w, hidden, down_w, inputs.reshape(nb * part_rows, part_feat), mid_slots, middle,
        middle_other, norm_gain[None], small, parts, 3,
    )

    grad_inputs, layer_out, down_sum, out_sum, *gu_pair = lax.optimization_barrier((grad_inputs, layer_out, down_sum, out_sum, *gu_pair))
    sum_down, sum_out = down_sum.astype(f32), out_sum.astype(f32)
    grad_gu_mine, grad_gu_other = gu_pair
    head_mine, head_other = sort_halves(head_sums)

    def unit_columns(i):
        part = slice(i * units, (i + 1) * units)
        both = jnp.stack([grad_gu_mine[:, part], grad_gu_other[:, part]])
        return jnp.concatenate([both[gy], both[1 - gy][:, 2 * units - block :]], axis=1).astype(f32)

    sum_gate, sum_up = unit_columns(0), unit_columns(1)

    def head_part(i, n):
        return in_order(head_mine[:, i : i + n], head_other[:, i : i + n], 1).astype(f32)

    sum_query, sum_key, sum_value, sum_head_gate = (head_part(i * width, width) for i in range(4))

    n_beta, n_conv, n_norm, n_mlp, n_gain = counts
    beta_parts = gathered[:, :n_beta].reshape(8, heads, feat)
    beta_rows = feat // (ngy * ndp)
    beta_pair = lax.dynamic_slice(beta_parts, (gx * ngy, 0, (gy * ndp + lax.axis_index("dp")) * beta_rows), (ngy, heads, beta_rows))
    sum_beta = beta_pair.reshape(ngy * heads, beta_rows).T
    taps = conv_kernel.shape[1]
    conv_sum = gathered[:, n_beta : n_beta + n_conv].reshape(8, 3, taps, width).transpose(1, 2, 0, 3).reshape(conv_kernel.shape)
    rest = jnp.sum(gathered[:, n_beta + n_conv :], axis=0)
    norm_sum = rest[:n_norm].reshape(feat)
    mlp_sum = rest[n_norm : n_norm + n_mlp].reshape(feat)
    gain_sum = rest[n_norm + n_mlp : n_norm + n_mlp + n_gain].reshape(-1)
    return (
        layer_out,
        grad_inputs,
        norm_sum,
        sum_query,
        sum_key,
        sum_value,
        sum_beta,
        sum_head_gate,
        conv_sum,
        gain_sum,
        sum_out,
        mlp_sum,
        sum_gate,
        sum_up,
        sum_down,
    )


def solution(mesh):
    cols = P("gy", "gx")
    rows = P("gx", "gy")
    acts = P("dp", "gx", "gy")
    cols_out = P(("gy", "dp"), "gx")
    rows_out = P(("gx", "dp"), "gy")
    return jax.shard_map(
        shards,
        mesh=mesh,
        in_specs=(acts, P("dp", None), P(), cols, cols, cols, cols, cols, P(), P(), rows, P(), cols, cols, rows, acts),
        out_specs=(
            acts,
            acts,
            P(),
            cols_out,
            cols_out,
            cols_out,
            cols_out,
            cols_out,
            P(),
            P(),
            rows_out,
            P(),
            cols_out,
            cols_out,
            rows_out,
        ),
        check_vma=False,
    )
```

```python
import jax, jax.numpy as jnp
from jax import lax
from jax.experimental import pallas as pl
from jax.experimental.pallas import tpu as pltpu
import functools
from jax.sharding import PartitionSpec as P
EPS = 1e-6
HEAD_EPS = 0.01
C = 128
bf = jnp.bfloat16
f32 = jnp.float32
GROUP = 8
BACK_A = 8
BACK_C = 4

def lasting(us):
    return pl.CostEstimate(flops=int(us * 1.15e9), bytes_accessed=1 << 20, transcendentals=0)

def nn(a, b):
    return lax.dot_general(a.astype(bf), b.astype(bf), (((1,), (0,)), ((), ())), preferred_element_type=f32)
def nt(a, b):
    return lax.dot_general(a.astype(bf), b.astype(bf), (((1,), (1,)), ((), ())), preferred_element_type=f32)
def tn(a, b):
    return lax.dot_general(a.astype(bf), b.astype(bf), (((0,), (0,)), ((), ())), preferred_element_type=f32)

def level_masks(n):
    row = lax.broadcasted_iota(jnp.int32, (n, n), 0)
    col = lax.broadcasted_iota(jnp.int32, (n, n), 1)
    out = []
    size = 1
    while size < n:
        out.append(((row ^ col) & (-size) == size).astype(f32).astype(bf))
        size *= 2
    return (row == col).astype(f32).astype(bf), out

def inverse_many(many, eye, levels):
    totals = [eye - a * levels[0] for a in many]
    for mask in levels[1:]:
        inner = [nn(a * mask, t).astype(bf) for a, t in zip(many, totals)]
        outer = [nn(t, x).astype(bf) for t, x in zip(totals, inner)]
        totals = [t - x for t, x in zip(totals, outer)]
    return totals

def act_stage(x, prev, aux, w, norm):
    row8 = lax.broadcasted_iota(jnp.int32, (8, 128), 0)
    conv = x * w[0:1]
    sh = []
    for i in range(1, w.shape[0]):
        r = pltpu.roll(x, i, 0)
        p = pltpu.roll(prev, i, 0)
        head = jnp.where(row8 < i, p, r[:8])
        m = jnp.concatenate([head, r[8:]], axis=0) * aux[:, 2 + i:3 + i]
        sh.append(m)
        conv = conv + m * w[i:i + 1]
    s = jax.nn.sigmoid(conv)
    act = conv * s
    if norm:
        rate = lax.rsqrt(jnp.sum(act * act, axis=-1, keepdims=True) + EPS)
        return conv, s, act * rate, rate, sh
    return conv, s, act, None, sh

def masks(aux, segrow):
    n = aux.shape[0]
    row = lax.broadcasted_iota(jnp.int32, (n, n), 0)
    col = lax.broadcasted_iota(jnp.int32, (n, n), 1)
    same = aux[:, 0:1] == segrow
    return same & (row > col), same & (row >= col)

def aux_columns(ref, rows):
    block = ref[0, :, rows]
    return jnp.concatenate([block, jnp.zeros((C - block.shape[0], C), f32)], axis=0).T

def beta_column(block, h):
    lane = lax.broadcasted_iota(jnp.int32, block.shape, 1)
    return jnp.sum(jnp.where(lane == h, jax.nn.sigmoid(block), 0.0), axis=1, keepdims=True)

def prev_rows(ref, lo):
    start = pl.multiple_of(jnp.maximum(lo - 8, 0), 8)
    return jnp.where(lo > 0, ref[0, pl.ds(start, 8), :].astype(f32), 0.0)

def fwd_kernel(q_ref, k_ref, v_ref, g_ref, b_ref, aux_ref, w_ref, gain_ref,
               mixed_ref, t_ref, w_out, p_ref, f_ref, s_ref, fresh_ref, o_ref,
               q_s, u_s, b_s):
    h = pl.program_id(1)
    length = q_ref.shape[1]
    steps = length // C
    eye, levels = level_masks(C)
    def stage_a(group, _):
        lows = [pl.multiple_of((group * GROUP + n) * C, C) for n in range(GROUP)]
        spans = [pl.ds(lo, C) for lo in lows]
        many, keys, right = [], [], []
        for lo, rows in zip(lows, spans):
            aux = aux_columns(aux_ref, rows)
            q = act_stage(q_ref[0, rows, :].astype(f32), prev_rows(q_ref, lo), aux, w_ref[0], True)[2]
            k = act_stage(k_ref[0, rows, :].astype(f32), prev_rows(k_ref, lo), aux, w_ref[1], True)[2]
            v = act_stage(v_ref[0, rows, :].astype(f32), prev_rows(v_ref, lo), aux, w_ref[2], False)[2]
            beta = beta_column(b_ref[0, rows, :].astype(f32), h)
            strict, inclusive = masks(aux, aux_ref[0, 0:1, rows])
            kb = k.astype(bf)
            qb = q.astype(bf)
            both = nt(jnp.concatenate([kb, qb], axis=0), kb)
            many.append(jnp.where(strict, beta * both[:C], 0.0).astype(bf))
            p_ref[0, 0, rows, :] = jnp.where(inclusive, both[C:], 0.0).astype(bf)
            q_s[rows, :] = qb
            keys.append((k * aux[:, 2:3]).astype(bf))
            right.append(jnp.concatenate([(beta * k).astype(bf), (beta * v).astype(bf)], axis=1))
        totals = inverse_many(many, eye, levels)
        wus = [nn(t, r) for t, r in zip(totals, right)]
        kwus = [tn(k, wu) for k, wu in zip(keys, wus)]
        for rows, t, wu, kwu in zip(spans, totals, wus, kwus):
            clast = aux_ref[0, 1:2, rows][:, C - 1:C]
            f_ref[0, 0, rows, :] = (clast * (eye.astype(f32) - kwu[:, :C])).astype(bf)
            b_s[rows, :] = kwu[:, C:]
            t_ref[0, 0, rows, :] = t
            w_out[0, 0, rows, :] = wu[:, :C].astype(bf)
            u_s[rows, :] = wu[:, C:]
        return 0
    lax.fori_loop(0, steps // GROUP, stage_a, 0)
    def scan(c, state):
        rows = pl.ds(pl.multiple_of(c * C, C), C)
        sb = state.astype(bf)
        s_ref[0, 0, rows, :] = sb
        return nn(f_ref[0, 0, rows, :], sb) + b_s[rows, :]
    lax.fori_loop(0, steps, scan, jnp.zeros((C, C), f32), unroll=True)
    def stage_c(c, _):
        rows = pl.ds(pl.multiple_of(c * C, C), C)
        aux = aux_columns(aux_ref, rows)
        carried = aux[:, 1:2]
        ws = nn(jnp.concatenate([w_out[0, 0, rows, :], q_s[rows, :]], axis=0), s_ref[0, 0, rows, :])
        fresh = (u_s[rows, :] - carried * ws[:C]).astype(bf)
        out = carried * ws[C:] + nn(p_ref[0, 0, rows, :], fresh)
        fresh_ref[0, 0, rows, :] = fresh
        o_ref[0, 0, rows, :] = out
        g = g_ref[0, rows, :].astype(f32)
        r = lax.rsqrt(jnp.mean(out * out, axis=-1, keepdims=True) + HEAD_EPS)
        mixed_ref[0, rows, :] = (out * r * gain_ref[0:1] * (g * jax.nn.sigmoid(g))).astype(bf)
        return 0
    lax.fori_loop(0, steps, stage_c, 0, unroll=4)

def specs(length, heads, off):
    return [pl.BlockSpec((1, length, 128), functools.partial(lambda t, b, h: (b, 0, t * heads + h), t)) for t in range(4)] + [
        pl.BlockSpec((1, length, 128), lambda b, h: (b, 0, 4 * heads))]

def mixer_fwd(raw, aux, conv, gain):
    nb, length, width = raw.shape
    heads = (width - 128) // 512
    per = pl.BlockSpec((1, 1, length, 128), lambda b, h: (b, h, 0, 0))
    sh = lambda d: jax.ShapeDtypeStruct((nb, heads, length, 128), d)
    return pl.pallas_call(
        fwd_kernel,
        grid=(nb, heads),
        in_specs=specs(length, heads, 0) + [
            pl.BlockSpec((1, aux.shape[1], length), lambda b, h: (b, 0, 0)),
            pl.BlockSpec((3, conv.shape[1], 128), lambda b, h: (0, 0, h)),
            pl.BlockSpec((1, 128), lambda b, h: (0, 0)),
        ],
        out_specs=[pl.BlockSpec((1, length, 128), lambda b, h: (b, 0, h))] + [per] * 7,
        out_shape=[jax.ShapeDtypeStruct((nb, length, heads * 128), bf)] + [sh(bf)] * 6 + [sh(f32)],
        scratch_shapes=[pltpu.VMEM((length, 128), bf), pltpu.VMEM((length, 128), f32), pltpu.VMEM((length, 128), f32)],
        cost_estimate=lasting(33),
        name="mixer_forward",
    )(raw, raw, raw, raw, raw, aux, conv, gain)

def bwd_kernel(q_ref, k_ref, v_ref, g_ref, b_ref, aux_ref, w_ref, gain_ref,
               t_ref, w_in, p_ref, f_ref, s_ref, fresh_ref, o_ref, dm_ref,
               draw_ref, dconv_ref, dgain_ref,
               do_s, pd_s, base_s, ds_s):
    h = pl.program_id(1)
    heads = pl.num_programs(1)
    length = q_ref.shape[1]
    steps = length // C
    gain = gain_ref[0:1]
    def stage_a(group, dgain):
        spans, dos, lefts, carries = [], [], [], []
        for n in range(BACK_A):
            lo = pl.multiple_of((group * BACK_A + n) * C, C)
            rows = pl.ds(lo, C)
            aux = aux_columns(aux_ref, rows)
            q = act_stage(q_ref[0, rows, :].astype(f32), prev_rows(q_ref, lo), aux, w_ref[0], True)[2]
            out = o_ref[0, 0, rows, :]
            g = g_ref[0, rows, :].astype(f32)
            dm = dm_ref[0, rows, :].astype(f32)
            s = jax.nn.sigmoid(g)
            r = lax.rsqrt(jnp.mean(out * out, axis=-1, keepdims=True) + HEAD_EPS)
            scaled = out * r
            dn = dm * (g * s)
            dg = dm * scaled * gain * (s * (1.0 + g * (1.0 - s)))
            draw_ref[0, rows, pl.ds(pl.multiple_of((3 * heads + h) * 128, 128), 128)] = dg.astype(bf)
            e = dn * gain
            do = r * (e - scaled * jnp.mean(e * scaled, axis=-1, keepdims=True))
            do_s[rows, :] = do
            dgain = dgain + jnp.sum((dn * scaled).reshape(C // 8, 8, 128), axis=0)
            spans.append(rows)
            dos.append(do)
            lefts.append(q.astype(bf))
            carries.append(aux[:, 1:2])
        pds = [tn(p_ref[0, 0, rows, :], do) for rows, do in zip(spans, dos)]
        bases = [
            tn(jnp.concatenate([(c * do).astype(bf), (-c * pd).astype(bf)], axis=0), jnp.concatenate([q, w_in[0, 0, rows, :]], axis=0))
            for rows, do, pd, q, c in zip(spans, dos, pds, lefts, carries)
        ]
        for rows, pd, base in zip(spans, pds, bases):
            pd_s[rows, :] = pd
            base_s[rows, :] = base
        return dgain
    dgain = lax.fori_loop(0, steps // BACK_A, stage_a, jnp.zeros((8, 128), f32))
    dgain_ref[0, 0] = dgain
    def scan(j, state):
        c = steps - 1 - j
        rows = pl.ds(pl.multiple_of(c * C, C), C)
        sb = state.astype(bf)
        ds_s[rows, :] = sb
        return nn(sb, f_ref[0, 0, rows, :]) + base_s[rows, :]
    lax.fori_loop(0, steps, scan, jnp.zeros((C, C), f32), unroll=True)
    row8 = lax.broadcasted_iota(jnp.int32, (8, 128), 0)
    lane = lax.broadcasted_iota(jnp.int32, (C, 128), 1)

    def conv_back(dconv, nxt, aux, w, raw, sh):
        d = dconv * w[0:1]
        dw = [jnp.sum((dconv * raw).reshape(C // 8, 8, 128), axis=0)]
        for i in range(1, w.shape[0]):
            r = pltpu.roll(dconv, C - i, 0)
            p = pltpu.roll(nxt, 8 - i, 0)
            tailrows = jnp.where(row8 >= 8 - i, p, r[C - 8:])
            m = jnp.concatenate([r[:C - 8], tailrows], axis=0) * aux[:, 5 + i:6 + i]
            d = d + m * w[i:i + 1]
            dw.append(jnp.sum((dconv * sh[i - 1]).reshape(C // 8, 8, 128), axis=0))
        return d, dw

    def stage_c(j, carry):
        nq, nk, nv, dws = carry
        parts = []
        for n in range(BACK_C):
            lo = pl.multiple_of((steps - 1 - j * BACK_C - n) * C, C)
            rows = pl.ds(lo, C)
            aux = aux_columns(aux_ref, rows)
            xq = q_ref[0, rows, :].astype(f32)
            xk = k_ref[0, rows, :].astype(f32)
            xv = v_ref[0, rows, :].astype(f32)
            aq = act_stage(xq, prev_rows(q_ref, lo), aux, w_ref[0], True)
            ak = act_stage(xk, prev_rows(k_ref, lo), aux, w_ref[1], True)
            av = act_stage(xv, prev_rows(v_ref, lo), aux, w_ref[2], False)
            beta = beta_column(b_ref[0, rows, :].astype(f32), h)
            kb, qb = ak[2].astype(bf), aq[2].astype(bf)
            parts.append((rows, aux, xq, xk, xv, aq, ak, av, beta, kb, qb))
        grams = [nt(p[9], p[9]) for p in parts]
        from_next = [nt(p[9], ds_s[p[0], :]) for p in parts]
        from_state = [nn(p[9], s_ref[0, 0, p[0], :]) for p in parts]
        ys = [tn(t_ref[0, 0, p[0], :], pd_s[p[0], :] + p[1][:, 2:3] * d) for p, d in zip(parts, from_next)]
        boths = [
            nt(jnp.concatenate([do_s[p[0], :].astype(bf), y.astype(bf)], axis=0), fresh_ref[0, 0, p[0], :]) for p, y in zip(parts, ys)
        ]
        dxs = [p[8] * y for p, y in zip(parts, ys)]
        throughs = [
            nt(jnp.concatenate([p[1][:, 1:2] * do_s[p[0], :], -(p[1][:, 1:2] * dx)], axis=0), s_ref[0, 0, p[0], :])
            for p, dx in zip(parts, dxs)
        ]
        freshes = [nn(p[1][:, 2:3] * fresh_ref[0, 0, p[0], :].astype(f32), ds_s[p[0], :]) for p in parts]
        dps, dgss, dbetas = [], [], []
        for p, gram, state, y, both in zip(parts, grams, from_state, ys, boths):
            rows, aux, beta = p[0], p[1], p[8]
            strict, inclusive = masks(aux, aux_ref[0, 0:1, rows])
            x = p[7][2] - aux[:, 1:2] * state
            dps.append(jnp.where(inclusive, both[:C], 0.0).astype(bf))
            da = jnp.where(strict, -both[C:], 0.0)
            dbetas.append(jnp.sum(y * x, axis=-1, keepdims=True) + jnp.sum(da * gram, axis=-1, keepdims=True))
            dg = beta * da
            dgss.append(dg + dg.T)
        dqs = [t[:C] + nn(dp, p[9]) for p, t, dp in zip(parts, throughs, dps)]
        dks = [
            t[C:] + f + tn(dp, p[10]) + nn(dgs, p[9]) for p, t, f, dp, dgs in zip(parts, throughs, freshes, dps, dgss)
        ]
        for p, dq, dk, dv, dbeta in zip(parts, dqs, dks, dxs, dbetas):
            rows, aux, xq, xk, xv, (cq, sq, q, rq, shq), (ck, sk, k, rk, shk), (cv, sv, v, _, shv), beta = p[:9]
            db = dbeta * beta * (1.0 - beta)
            bl = pl.ds(4 * heads * 128, 128)
            @pl.when(h == 0)
            def _():
                draw_ref[0, rows, bl] = jnp.where(lane == 0, db, 0.0).astype(bf)
            @pl.when(h > 0)
            def _():
                old = draw_ref[0, rows, bl]
                draw_ref[0, rows, bl] = jnp.where(lane == h, db.astype(bf).astype(f32), old.astype(f32)).astype(bf)
            dq = rq * (dq - q * jnp.sum(q * dq, axis=-1, keepdims=True))
            dk = rk * (dk - k * jnp.sum(k * dk, axis=-1, keepdims=True))
            dcq = dq * (sq * (1.0 + cq * (1.0 - sq)))
            dck = dk * (sk * (1.0 + ck * (1.0 - sk)))
            dcv = dv * (sv * (1.0 + cv * (1.0 - sv)))
            rq_, wq = conv_back(dcq, nq, aux, w_ref[0], xq, shq)
            rk_, wk = conv_back(dck, nk, aux, w_ref[1], xk, shk)
            rv_, wv = conv_back(dcv, nv, aux, w_ref[2], xv, shv)
            for t, val in ((0, rq_), (1, rk_), (2, rv_)):
                draw_ref[0, rows, pl.ds(pl.multiple_of((t * heads + h) * 128, 128), 128)] = val.astype(bf)
            dws = tuple(a + b for a, b in zip(dws, wq + wk + wv))
            nq, nk, nv = dcq[:8], dck[:8], dcv[:8]
        return nq, nk, nv, dws
    z8 = jnp.zeros((8, 128), f32)
    taps = w_ref.shape[1]
    _, _, _, dws = lax.fori_loop(0, steps // BACK_C, stage_c, (z8, z8, z8, (z8,) * (3 * taps)))
    for n, d in enumerate(dws):
        dconv_ref[0, 0, n] = d

def mixer_bwd(raw, aux, conv, gain, saved, dmixed):
    nb, length, width = raw.shape
    heads = (width - 128) // 512
    taps = conv.shape[1]
    per = pl.BlockSpec((1, 1, length, 128), lambda b, h: (b, h, 0, 0))
    sh = lambda d: jax.ShapeDtypeStruct((nb, heads, length, 128), d)
    draw, dconv, dgain = pl.pallas_call(
        bwd_kernel,
        grid=(nb, heads),
        in_specs=specs(length, heads, 0) + [
            pl.BlockSpec((1, aux.shape[1], length), lambda b, h: (b, 0, 0)),
            pl.BlockSpec((3, taps, 128), lambda b, h: (0, 0, h)),
            pl.BlockSpec((1, 128), lambda b, h: (0, 0)),
        ] + [per] * 7 + [pl.BlockSpec((1, length, 128), lambda b, h: (b, 0, h))],
        out_specs=[pl.BlockSpec((1, length, width), lambda b, h: (b, 0, 0)),
                   pl.BlockSpec((1, 1, 3 * taps, 8, 128), lambda b, h: (b, h, 0, 0, 0)),
                   pl.BlockSpec((1, 1, 8, 128), lambda b, h: (b, h, 0, 0))],
        out_shape=[jax.ShapeDtypeStruct((nb, length, width), bf),
                   jax.ShapeDtypeStruct((nb, heads, 3 * taps, 8, 128), f32),
                   jax.ShapeDtypeStruct((nb, heads, 8, 128), f32)],
        scratch_shapes=[pltpu.VMEM((length, 128), f32)] * 3 + [pltpu.VMEM((length, 128), bf)],
        cost_estimate=lasting(2),
        name="mixer_backward",
    )(raw, raw, raw, raw, raw, aux, conv, gain, *saved, dmixed)
    dconv = jnp.sum(dconv, axis=(0, 3)).reshape(heads, 3, taps, 128).transpose(1, 2, 0, 3).reshape(3, taps, heads * 128)
    return draw, dconv, jnp.sum(dgain, axis=(0, 1, 2))

def make_aux(segments):
    nb, length = segments.shape
    seg = segments.astype(f32)
    blocks = seg.reshape(nb, length // C, C)
    last = blocks[:, :, -1:]
    before = jnp.concatenate([jnp.full((nb, 1, 1), -1.0, f32), last[:, :-1]], axis=1)
    carried = (blocks == before).astype(f32).reshape(nb, length)
    tail = (blocks == last).astype(f32).reshape(nb, length)
    cols = [seg, carried, tail]
    for i in range(1, 4):
        cols.append((jnp.pad(seg, ((0, 0), (i, 0)), constant_values=-1.0)[:, :length] == seg).astype(f32))
    for i in range(1, 4):
        cols.append((jnp.pad(seg, ((0, 0), (0, i)), constant_values=-1.0)[:, i:] == seg).astype(f32))
    cols += [jnp.zeros_like(seg)] * (16 - len(cols))
    return jnp.stack(cols, axis=1)


SLOTS = ((0, 0, 0), (0, 0, 1), (1, 0, 0), (0, 1, 0), (1, 0, 1), (0, 1, 1), (1, 1, 0), (1, 1, 1))
MESH = pl.DeviceIdType.MESH
VM = pl.BlockSpec(memory_space=pltpu.VMEM)
ANY = pl.BlockSpec(memory_space=pl.ANY)


def slot_place(r, gx, gy):
    dx, dy, dc = SLOTS[r]
    hi, lo = gx // 2, gx % 2
    hi = 1 - hi if dy else hi
    lo = 1 - lo if dc else lo
    return hi * 2 + lo, (1 - gy if dx else gy)


def slot_peer(r, gx, gy):
    px, py = slot_place(r, gx, gy)
    return {"gx": px, "gy": py}


def flipped(index, n, size):
    out, bit = 0, 1
    while bit < size:
        digit = index // bit % 2
        out = out + bit * (1 - digit if n & bit else digit)
        bit *= 2
    return out


def entry_barrier(peers):
    sem = pltpu.get_barrier_semaphore()
    for peer in peers:
        pl.semaphore_signal(sem, inc=1, device_id=peer, device_id_type=MESH)
    pl.semaphore_wait(sem, len(peers))


def remote(src, dst, send, recv, peer):
    return pltpu.make_async_remote_copy(src, dst, send, recv, device_id=peer, device_id_type=MESH)


def nt_dot(a, b):
    return lax.dot_general(a, b, (((1,), (1,)), ((), ())), preferred_element_type=f32)


def nn_dot(a, b):
    return lax.dot_general(a, b, (((1,), (0,)), ((), ())), preferred_element_type=f32)


class Gather:
    COPIES = 13

    def __init__(self, buf, send, recv, gx, gy, over_gx=False):
        rows = buf.shape[1]
        half = rows // 2
        a, b = pl.ds(0, half), pl.ds(half, half)
        core, xn, yn = (slot_peer(r, gx, gy) for r in (1, 2, 3))

        def make(i, src, dst, part, peer):
            return remote(buf.at[src, part], buf.at[dst, part], send.at[i], recv.at[i], peer)

        self.own = [
            make(0, 0, 2, a, xn),
            make(1, 0, 3, a, yn),
            make(2, 0, 2, b, xn),
            make(3, 0, 3, b, yn),
            remote(buf.at[0], buf.at[1], send.at[4], recv.at[4], core),
        ]
        self.over_gx = over_gx
        self.diagonal = [make(5, 2, 6, a, yn) if over_gx else make(5, 3, 6, a, xn), make(6, 2, 6, b, yn)]
        self.cross = [
            make(7, 2, 4, a, core),
            make(8, 2, 4, b, core),
            make(9, 3, 5, a, core),
            make(10, 3, 5, b, core),
            make(11, 6, 7, a, core),
            make(12, 6, 7, b, core),
        ]

    def start(self):
        for c in self.own:
            c.start()

    def step(self, i):
        if i == 1:
            self.own[4].wait_recv()
        elif i == 2:
            self.own[1].wait_recv()
            if not self.over_gx:
                self.diagonal[0].start()
            self.cross[2].start()
            self.own[0].wait_recv()
            if self.over_gx:
                self.diagonal[0].start()
            self.cross[0].start()
            self.own[2].wait_recv()
            self.diagonal[1].start()
            self.cross[1].start()
        elif i == 3:
            self.own[3].wait_recv()
            self.cross[3].start()
        elif i == 4:
            self.cross[0].wait_recv()
            self.cross[1].wait_recv()
        elif i == 5:
            self.cross[2].wait_recv()
            self.cross[3].wait_recv()
        elif i == 6:
            self.diagonal[0].wait_recv()
            self.cross[4].start()
            self.diagonal[1].wait_recv()
            self.cross[5].start()
        elif i == 7:
            self.cross[4].wait_recv()
            self.cross[5].wait_recv()

    def finish(self):
        for c in self.own + self.diagonal + self.cross:
            c.wait_send()


def head_kernel(
    x_ref, wq_ref, wk_ref, wv_ref, wg_ref, wb_ref, gate_ref, up_ref, down_ref, out_ref, gain_ref,
    normed_ref, raw_ref, hw_ref, own_ref, gu_ref, wo_ref,
    buf, w, low, acc, ag_send, ag_recv, w_send, w_recv, load_sem, out_sem, raw_sem, hw_sem, z_send, z_recv, u_send, u_recv,
):
    gx, gy, dp = lax.axis_index("gx"), lax.axis_index("gy"), lax.axis_index("dp")
    ngx = 4
    units = gu_ref.shape[1] // 2
    parts = (x_ref.shape[1] + units // 2) // gu_ref.shape[0]
    piece = x_ref.shape[1] // parts
    down_piece = units // 2 // parts
    unit_other = pl.multiple_of((1 - gy) * (gate_ref.shape[1] - units), 128)
    turn = flipped(dp, 0, parts)
    rows_sent = pl.ds(pl.multiple_of(turn * piece, piece), piece)
    rows = own_ref.shape[0]
    part = x_ref.shape[1]
    width = wq_ref.shape[1] // 2
    weights = ((wq_ref, width), (wk_ref, width), (wv_ref, width), (wg_ref, width), (wb_ref, 128))
    starts = [0, width, 2 * width, 3 * width, 4 * width]
    xn = slot_peer(2, gx, gy)
    loads = [pltpu.make_async_copy(x_ref, buf.at[0], load_sem.at[5])]
    for i, (ref, n) in enumerate(weights):
        src = ref.at[:, pl.ds(pl.multiple_of(gy * n, 128), n)]
        loads.append(pltpu.make_async_copy(src, w.at[0, :, pl.ds(starts[i], n)], load_sem.at[i]))
    for c in loads:
        c.start()
    peers = [slot_peer(r, gx, gy) for r in (1, 2, 3)] + [{"dp": flipped(dp, n, parts)} for n in range(1, parts)]
    entry_barrier(peers)
    swaps = []
    for i, (ref, n) in enumerate(weights):
        src = ref.at[rows_sent, pl.ds(pl.multiple_of((1 - gy) * n, 128), n)]
        swaps.append(remote(src, w.at[1, rows_sent, pl.ds(starts[i], n)], w_send.at[i], w_recv.at[i], xn))
        swaps[-1].start()
    loads[0].wait()
    gather = Gather(buf, ag_send, ag_recv, gx, gy, True)
    gather.start()
    extra = [
        remote(gate_ref.at[rows_sent, pl.ds(unit_other, units)], gu_ref.at[pl.ds(0, piece), pl.ds(0, units)], u_send.at[0], u_recv.at[0], xn),
        remote(up_ref.at[rows_sent, pl.ds(unit_other, units)], gu_ref.at[pl.ds(0, piece), pl.ds(units, units)], u_send.at[1], u_recv.at[1], xn),
        remote(
            down_ref.at[pl.ds(pl.multiple_of(unit_other + units // 2 + turn * down_piece, 32), down_piece), :],
            gu_ref.at[pl.ds(piece, down_piece), pl.ds(0, x_ref.shape[1])],
            u_send.at[3],
            u_recv.at[3],
            xn,
        ),
        remote(out_ref.at[pl.ds(pl.multiple_of((1 - gy) * width, width), width), :], wo_ref, u_send.at[2], u_recv.at[2], xn),
    ]
    for c in extra:
        c.start()
    for c in swaps:
        c.wait_recv()
    spread = [
        remote(w.at[1, rows_sent], w.at[1, rows_sent], z_send.at[n], z_recv.at[n], {"dp": flipped(dp, n, parts)}) for n in range(1, parts)
    ]
    for c in spread:
        c.start()
    for c in loads[1:]:
        c.wait()
    keep = pltpu.make_async_copy(w.at[0], hw_ref.at[pl.ds(pl.multiple_of(gy * part, part), part)], hw_sem.at[0])
    keep.start()
    near = pl.ds(pl.multiple_of(gy * part, part), part)
    far = pl.ds(pl.multiple_of((1 - gy) * part, part), part)
    stores = []
    blocks = []

    def pair(n, first, second):
        px, _ = slot_place(first, gx, gy)
        for s in range(2):
            span = pl.ds(s * rows, rows)
            v = s * ngx + px
            i = 2 * n + s
            x0 = buf[first, span, :].astype(f32)
            x1 = buf[second, span, :].astype(f32)
            total = jnp.sum(x0 * x0, axis=-1, keepdims=True) + jnp.sum(x1 * x1, axis=-1, keepdims=True)
            rate = lax.rsqrt(total / (2 * part) + EPS)
            low[i, :, near] = (x0 * rate * gain_ref[:, near]).astype(bf)
            low[i, :, far] = (x1 * rate * gain_ref[:, far]).astype(bf)
            c = pltpu.make_async_copy(low.at[i], normed_ref.at[v], out_sem.at[i])
            c.start()
            stores.append(c)
            acc[i] = nn_dot(low[i, :, near], w[0])
            blocks.append((i, v))

    for step in (1, 2, 3, 4):
        gather.step(step)
        if step == 2:
            pair(0, 0, 2)
            mine = pl.ds(pl.multiple_of(gy * rows, rows), rows)
            own_ref[:, near] = buf[0, mine, :]
            own_ref[:, far] = buf[2, mine, :]
    pair(1, 1, 4)
    gather.step(5)
    gather.step(6)
    pair(2, 3, 6)
    gather.step(7)
    pair(3, 5, 7)
    for c in spread:
        c.wait_recv()
    give = pltpu.make_async_copy(w.at[1], hw_ref.at[far], hw_sem.at[1])
    give.start()

    for i, v in blocks:
        acc[i] += nn_dot(low[i, :, far], w[1])
        c = pltpu.make_async_copy(acc.at[i], raw_ref.at[v], raw_sem.at[i])
        c.start()
        stores.append(c)
    keep.wait()
    give.wait()
    for c in stores:
        c.wait()
    for c in extra:
        c.wait_recv()
    for c in swaps + spread + extra:
        c.wait_send()
    gather.finish()


def head_project(inputs, w_query, w_key, w_value, w_gate_head, w_beta, w_gate, w_up, w_down, w_out, gain, units, parts, collective):
    total, part = inputs.shape
    rows = total // 2
    feat = 2 * part
    cols = 2 * w_query.shape[1] + 128
    sd = jax.ShapeDtypeStruct
    return pl.pallas_call(
        head_kernel,
        in_specs=[ANY] * 10 + [VM],
        out_specs=[ANY, ANY, ANY, VM, ANY, ANY],
        out_shape=[
            sd((8, rows, feat), bf),
            sd((8, rows, cols), f32),
            sd((feat, cols), bf),
            sd((rows, feat), bf),
            sd(((part + units // 2) // parts, 2 * units), bf),
            sd((w_out.shape[0] // 2, w_out.shape[1]), bf),
        ],
        scratch_shapes=[
            pltpu.VMEM((8, total, part), bf),
            pltpu.VMEM((2, part, cols), bf),
            pltpu.VMEM((8, rows, feat), bf),
            pltpu.VMEM((8, rows, cols), f32),
            pltpu.SemaphoreType.DMA((13,)),
            pltpu.SemaphoreType.DMA((13,)),
            pltpu.SemaphoreType.DMA((5,)),
            pltpu.SemaphoreType.DMA((5,)),
            pltpu.SemaphoreType.DMA((6,)),
            pltpu.SemaphoreType.DMA((8,)),
            pltpu.SemaphoreType.DMA((8,)),
            pltpu.SemaphoreType.DMA((2,)),
            pltpu.SemaphoreType.DMA((4,)),
            pltpu.SemaphoreType.DMA((4,)),
            pltpu.SemaphoreType.DMA((4,)),
            pltpu.SemaphoreType.DMA((4,)),
        ],
        compiler_params=pltpu.CompilerParams(collective_id=collective, has_side_effects=True, vmem_limit_bytes=60 << 20),
        cost_estimate=lasting(80),
        name="head_project",
    )(inputs, w_query, w_key, w_value, w_gate_head, w_beta, w_gate, w_up, w_down, w_out, gain)


def mlp_kernel(x_ref, gate_ref, up_ref, down_ref, y_ref, *refs, parts):
    gu_refs, piece_ref, refs = refs[:parts], refs[parts], refs[parts + 1 :]
    mlp_body(parts, x_ref, gate_ref, up_ref, down_ref, y_ref, gu_refs, piece_ref, *refs)


def mlp_body(
    parts, x_ref, gate_ref, up_ref, down_ref, y_ref, gu_refs, piece_ref,
    second_ref, hidden_ref, grads_ref, yrel_ref, gu_out, dn_out,
    wgu, wd, buf, ybuf, hbuf, gbuf, load_sem, w_sem, keep_sem, y_sem, y_out_sem, out_sem, ag_send, ag_recv,
):
    gx, gy = lax.axis_index("gx"), lax.axis_index("gy")
    ngy = 2
    rows = x_ref.shape[0]
    feat = x_ref.shape[1]
    units = wd.shape[0]
    half = feat // 2
    tile = 256
    dp = lax.axis_index("dp")
    unit_mine = pl.multiple_of(gy * (gate_ref.shape[1] - units), 128)
    doubled = gy * (2 * units - gate_ref.shape[1])
    load = pltpu.make_async_copy(x_ref, buf.at[0], load_sem)
    load.start()
    near = pl.ds(pl.multiple_of(gy * half, half), half)
    far = pl.multiple_of((1 - gy) * half, half)
    own_units = pl.ds(unit_mine, units)
    w_loads = [
        pltpu.make_async_copy(gate_ref.at[:, own_units], wgu.at[near, pl.ds(0, units)], w_sem.at[0]),
        pltpu.make_async_copy(up_ref.at[:, own_units], wgu.at[near, pl.ds(units, units)], w_sem.at[1]),
        pltpu.make_async_copy(down_ref.at[own_units, :], wd.at[:, near], w_sem.at[2]),
    ]
    w_loads.append(pltpu.make_async_copy(piece_ref, wd.at[pl.ds(0, units // 2), pl.ds(far, half)], w_sem.at[3]))
    for n in range(parts):
        turn = flipped(dp, n, parts)
        piece = half // parts
        down_piece = units // 2 // parts
        gu_rows = wgu.at[pl.ds(pl.multiple_of(far + turn * piece, piece), piece), :]
        down_rows = wd.at[pl.ds(pl.multiple_of(units // 2 + turn * down_piece, 32), down_piece), pl.ds(far, half)]
        w_loads.append(pltpu.make_async_copy(gu_refs[n].at[pl.ds(0, piece)], gu_rows, w_sem.at[4 + 2 * n]))
        w_loads.append(pltpu.make_async_copy(gu_refs[n].at[pl.ds(piece, down_piece), pl.ds(0, half)], down_rows, w_sem.at[5 + 2 * n]))
    for c in w_loads:
        c.start()
    entry_barrier([slot_peer(r, gx, gy) for r in (1, 2, 3)])
    load.wait()
    gather = Gather(buf, ag_send, ag_recv, gx, gy)
    gather.start()

    def y_load(r, n):
        px, py = slot_place(r, gx, gy)
        return [
            pltpu.make_async_copy(y_ref.at[px * ngy + h, py], ybuf.at[r % 2, :, pl.ds(h * (feat // 2), feat // 2)], y_sem.at[r % 2, h])
            for h in range(2)
        ]

    def y_store(r):
        return pltpu.make_async_copy(ybuf.at[r % 2], yrel_ref.at[r], y_out_sem.at[r % 2])

    for c in y_load(0, 0):
        c.start()
    for c in w_loads:
        c.wait()
    keeps = [pltpu.make_async_copy(wgu, gu_out, keep_sem.at[0]), pltpu.make_async_copy(wd, dn_out, keep_sem.at[1])]
    for c in keeps:
        c.start()

    def outs(r):
        return [
            pltpu.make_async_copy(buf.at[r], second_ref.at[r], out_sem.at[0, r % 2]),
            pltpu.make_async_copy(hbuf.at[r % 2], hidden_ref.at[r], out_sem.at[1, r % 2]),
            pltpu.make_async_copy(gbuf.at[r % 2], grads_ref.at[r], out_sem.at[2, r % 2]),
        ]

    for r in range(8):
        gather.step(r)
        if r >= 2:
            for c in outs(r - 2):
                c.wait()
        if r + 1 < 8:
            if r >= 1:
                y_store(r - 1).wait()
            for c in y_load(r + 1, 0):
                c.start()
        for c in y_load(r, 0):
            c.wait()
        y_store(r).start()

        def body(t, _):
            cols = pl.ds(pl.multiple_of(t * tile, tile), tile)
            up_cols = pl.ds(pl.multiple_of(units + t * tile, tile), tile)
            gate = nn_dot(buf[r], wgu[:, cols])
            up = nn_dot(buf[r], wgu[:, up_cols])
            gh = nt_dot(ybuf[r % 2], wd[cols, :])
            s = jax.nn.sigmoid(gate)
            keep = lax.broadcasted_iota(jnp.int32, gate.shape, 1) + t * tile >= doubled
            act = jnp.where(keep, gate * s, 0.0)
            up = jnp.where(keep, up, 0.0)
            hbuf[r % 2, :, cols] = (act * up).astype(bf)
            gbuf[r % 2, :, up_cols] = (gh * act).astype(bf)
            gbuf[r % 2, :, cols] = (gh * up * s * (1.0 + gate * (1.0 - s))).astype(bf)
            return 0

        lax.fori_loop(0, units // tile, body, 0)
        for c in outs(r):
            c.start()
    for r in (6, 7):
        for c in outs(r):
            c.wait()
        y_store(r).wait()
    gather.finish()
    for c in keeps:
        c.wait()


def mlp_forward(x_own, w_gate, w_up, w_down, y_all, gu_pieces, down_piece, units, collective):
    rows, feat = x_own.shape
    parts = len(gu_pieces)
    sd = jax.ShapeDtypeStruct
    return pl.pallas_call(
        functools.partial(mlp_kernel, parts=parts),
        in_specs=[ANY] * (6 + parts),
        out_specs=[ANY] * 6,
        out_shape=[
            sd((8, rows, feat), bf),
            sd((8, rows, units), bf),
            sd((8, rows, 2 * units), bf),
            sd((8, rows, feat), bf),
            sd((feat, 2 * units), bf),
            sd((units, feat), bf),
        ],
        scratch_shapes=[
            pltpu.VMEM((feat, 2 * units), bf),
            pltpu.VMEM((units, feat), bf),
            pltpu.VMEM((8, rows, feat), bf),
            pltpu.VMEM((2, rows, feat), bf),
            pltpu.VMEM((2, rows, units), bf),
            pltpu.VMEM((2, rows, 2 * units), bf),
            pltpu.SemaphoreType.DMA,
            pltpu.SemaphoreType.DMA((4 + 2 * parts,)),
            pltpu.SemaphoreType.DMA((2,)),
            pltpu.SemaphoreType.DMA((2, 2)),
            pltpu.SemaphoreType.DMA((2,)),
            pltpu.SemaphoreType.DMA((3, 2)),
            pltpu.SemaphoreType.DMA((13,)),
            pltpu.SemaphoreType.DMA((13,)),
        ],
        compiler_params=pltpu.CompilerParams(collective_id=collective, has_side_effects=True, vmem_limit_bytes=62 << 20),
        cost_estimate=lasting(68),
        name="mlp_forward",
    )(x_own, w_gate, w_up, w_down, y_all, *gu_pieces, down_piece)


class Scatter:
    def __init__(self, give, take, acc, diag_in, last_in, s_core, r_core, s_link, r_link, gx, gy, over_gx=False):
        self.over_gx = over_gx
        self.give, self.take, self.acc, self.diag_in, self.last_in = give, take, acc, diag_in, last_in
        core, xn, yn = (slot_peer(r, gx, gy) for r in (1, 2, 3))
        rows = acc.shape[1]
        half = rows // 2
        a, b = pl.ds(0, half), pl.ds(half, half)
        self.a, self.b = a, b
        self.core = [remote(give.at[n], take.at[n], s_core.at[n], r_core.at[n], core) for n in range(4)]

        def link(i, src, dst, peer):
            return remote(src, dst, s_link.at[i], r_link.at[i], peer)

        self.link = [
            link(0, acc.at[0, a], diag_in.at[0], yn if over_gx else xn),
            link(1, acc.at[0, b], diag_in.at[1], yn),
            link(2, acc.at[1, a], last_in.at[0, a], xn),
            link(3, acc.at[2, b], last_in.at[1, b], yn),
            link(4, acc.at[1, b], last_in.at[0, b], xn),
            link(5, acc.at[2, a], last_in.at[1, a], yn),
        ]

    def begin(self, product, self_acc, between=None):
        acc = self.acc

        def give_out(n, slot):
            def put(cols, value):
                self.give[n, :, cols] = value.astype(bf)

            product(slot, put)
            self.core[n].start()

        def keep(n, slot):
            def put(cols, value):
                acc[n, :, cols] = value.astype(bf)

            product(slot, put)

        def join(n):
            self.core[n].wait_recv()
            acc[n] = (acc[n].astype(f32) + self.take[n].astype(f32)).astype(bf)

        give_out(0, 7)
        keep(0, 6)
        give_out(1, 4)
        if between is not None:
            between()
        join(0)
        self.link[0].start()
        self.link[1].start()
        give_out(2, 5)
        keep(1, 2)
        join(1)
        if not self.over_gx:
            self.link[2].start()
        keep(2, 3)
        join(2)
        self.link[3].start()
        if self.over_gx:
            self.link[5].start()
        give_out(3, 1)

        def put_self(cols, value):
            self_acc[:, cols] = value

        product(0, put_self)

    def forward(self):
        acc, a, b = self.acc, self.a, self.b
        if self.over_gx:
            for i, half, onward in ((0, a, 2), (1, b, 4)):
                self.link[i].wait_recv()
                acc[1, half] = (acc[1, half].astype(f32) + self.diag_in[i].astype(f32)).astype(bf)
                self.link[onward].start()
            return
        self.link[1].wait_recv()
        acc[1, b] = (acc[1, b].astype(f32) + self.diag_in[1].astype(f32)).astype(bf)
        self.link[4].start()
        self.link[0].wait_recv()
        acc[2, a] = (acc[2, a].astype(f32) + self.diag_in[0].astype(f32)).astype(bf)
        self.link[5].start()

    def end(self, self_acc):
        self.core[3].wait_recv()
        self_acc[...] += self.take[3].astype(f32)
        for c in self.link[2:]:
            c.wait_recv()
        self_acc[...] += self.last_in[0].astype(f32) + self.last_in[1].astype(f32)

    def run(self, product, self_acc):
        self.begin(product, self_acc)
        self.forward()
        self.end(self_acc)

    def finish(self):
        for c in self.core + self.link:
            c.wait_send()


def scatter_scratch(rows, feat):
    return [
        pltpu.VMEM((4, rows, feat), bf),
        pltpu.VMEM((4, rows, feat), bf),
        pltpu.VMEM((3, rows, feat), bf),
        pltpu.VMEM((2, rows // 2, feat), bf),
        pltpu.VMEM((2, rows, feat), bf),
        pltpu.SemaphoreType.DMA((4,)),
        pltpu.SemaphoreType.DMA((4,)),
        pltpu.SemaphoreType.DMA((6,)),
        pltpu.SemaphoreType.DMA((6,)),
    ]


def own_out_rows(out_ref, piece_ref, w, sem, gy):
    width, part = piece_ref.shape
    near = pl.ds(pl.multiple_of(gy * part, part), part)
    far = pl.ds(pl.multiple_of((1 - gy) * part, part), part)
    return [
        pltpu.make_async_copy(out_ref.at[pl.ds(pl.multiple_of(gy * width, width), width), :], w.at[:, near], sem.at[0]),
        pltpu.make_async_copy(piece_ref, w.at[:, far], sem.at[1]),
    ]


def out_kernel(
    mixed_ref, out_ref, piece_ref, x_ref, gain_ref,
    middle_ref, normed_ref, slots_ref, other_ref,
    give, take, acc, diag_in, last_in, s_core, r_core, s_link, r_link, lhs, w, total, load_sem, lhs_sem, keep_sem,
):
    gx, gy = lax.axis_index("gx"), lax.axis_index("gy")
    feat = x_ref.shape[1]
    tile = 512
    loads = own_out_rows(out_ref, piece_ref, w, load_sem, gy)
    pulls = {}
    for r in (7, 6, 4, 5, 2, 3, 1, 0):
        px, py = slot_place(r, gx, gy)
        pulls[r] = pltpu.make_async_copy(mixed_ref.at[py * 4 + px], lhs.at[r], lhs_sem.at[r])
    for c in loads + list(pulls.values()):
        c.start()
    entry_barrier([slot_peer(r, gx, gy) for r in (1, 2, 3)])
    for c in loads:
        c.wait()

    def product(slot, put):
        pulls[slot].wait()

        def body(t, _):
            cols = pl.ds(pl.multiple_of(t * tile, tile), tile)
            put(cols, nn_dot(lhs[slot], w[:, cols]))
            return 0

        lax.fori_loop(0, feat // tile, body, 0)

    scatter = Scatter(give, take, acc, diag_in, last_in, s_core, r_core, s_link, r_link, gx, gy)
    scatter.run(product, total)
    keep = pltpu.make_async_copy(lhs, slots_ref, keep_sem)
    keep.start()
    middle = x_ref[...].astype(f32) + total[...]
    middle_ref[...] = middle
    other_ref[...] = middle_ref[:, pl.ds(pl.multiple_of((1 - gy) * (feat // 2), feat // 2), feat // 2)].astype(bf)
    rate = lax.rsqrt(jnp.mean(middle * middle, axis=-1, keepdims=True) + EPS)
    normed_ref[...] = (middle * rate * gain_ref[...]).astype(bf)
    keep.wait()
    scatter.finish()


def out_project(mixed, w_out, piece, x_own, gain, collective):
    rows, feat = x_own.shape
    width = mixed.shape[2]
    sd = jax.ShapeDtypeStruct
    return pl.pallas_call(
        out_kernel,
        in_specs=[ANY, ANY, ANY, VM, VM],
        out_specs=[VM, VM, ANY, VM],
        out_shape=[sd((rows, feat), f32), sd((rows, feat), bf), sd(mixed.shape, bf), sd((rows, feat // 2), bf)],
        scratch_shapes=scatter_scratch(rows, feat)
        + [
            pltpu.VMEM(mixed.shape, bf),
            pltpu.VMEM((width, feat), bf),
            pltpu.VMEM((rows, feat), f32),
            pltpu.SemaphoreType.DMA((2,)),
            pltpu.SemaphoreType.DMA((8,)),
            pltpu.SemaphoreType.DMA,
        ],
        compiler_params=pltpu.CompilerParams(collective_id=collective, has_side_effects=True, vmem_limit_bytes=60 << 20),
        cost_estimate=lasting(44),
        name="out_project",
    )(mixed, w_out, piece, x_own, gain)


def back_kernel(
    grads_ref, wgu_ref, out_ref, piece_ref, middle_ref, y_ref, gain_ref,
    mid_ref, gmix_ref, dgain_ref,
    give, take, acc, diag_in, last_in, s_core, r_core, s_link, r_link,
    lhs, wgu, w, total, buf, gstage, y_own, load_sem, lhs_sem, ag_send, ag_recv, mid_sem, gmix_sem,
):
    gx, gy = lax.axis_index("gx"), lax.axis_index("gy")
    rows, feat = middle_ref.shape
    tile = 512
    load = pltpu.make_async_copy(wgu_ref, wgu, load_sem.at[2])
    outs = own_out_rows(out_ref, piece_ref, w, load_sem, gy)
    order = (7, 6, 4, 5, 2, 3, 1, 0)
    pulls = {r: pltpu.make_async_copy(grads_ref.at[r], lhs.at[r], lhs_sem.at[r]) for r in order}
    pulls[7].start()
    load.start()
    for r in order[1:]:
        pulls[r].start()
    outs.append(pltpu.make_async_copy(y_ref.at[0], y_own, load_sem.at[3]))
    for c in outs:
        c.start()
    entry_barrier([slot_peer(r, gx, gy) for r in (1, 2, 3)])
    load.wait()

    def product(slot, put):
        pulls[slot].wait()

        def body(t, _):
            cols = pl.ds(pl.multiple_of(t * tile, tile), tile)
            put(cols, nt_dot(lhs[slot], wgu[cols, :]))
            return 0

        lax.fori_loop(0, feat // tile, body, 0)

    scatter = Scatter(give, take, acc, diag_in, last_in, s_core, r_core, s_link, r_link, gx, gy, True)
    scatter.run(product, total)
    middle = middle_ref[...]
    incoming = total[...]
    rate = lax.rsqrt(jnp.mean(middle * middle, axis=-1, keepdims=True) + EPS)
    scaled = gain_ref[...] * incoming
    inner = jnp.mean(middle * scaled, axis=-1, keepdims=True)
    for c in outs:
        c.wait()
    buf[0] = (y_own[...].astype(f32) + rate * scaled - middle * (rate * rate * rate) * inner).astype(bf)
    gather = Gather(buf, ag_send, ag_recv, gx, gy)
    gather.start()
    dgain_ref[...] = jnp.sum((incoming * middle * rate).reshape(rows // 8, 8, feat), axis=0)
    stores = []
    for r in range(8):
        gather.step(r)
        px, py = slot_place(r, gx, gy)
        gstage[r] = nt_dot(buf[r], w[...]).astype(bf)
        stores.append(pltpu.make_async_copy(gstage.at[r], gmix_ref.at[py * 4 + px], gmix_sem.at[r]))
        stores.append(pltpu.make_async_copy(buf.at[r], mid_ref.at[r], mid_sem.at[r]))
        for c in stores[-2:]:
            c.start()
    for c in stores:
        c.wait()
    gather.finish()
    scatter.finish()


def mlp_backward(grads, gate_up, w_out, piece, middle, y_rel, gain, collective):
    rows, feat = middle.shape
    width = piece.shape[0]
    sd = jax.ShapeDtypeStruct
    return pl.pallas_call(
        back_kernel,
        in_specs=[ANY, ANY, ANY, ANY, VM, ANY, VM],
        out_specs=[ANY, ANY, VM],
        out_shape=[sd((8, rows, feat), bf), sd((8, rows, width), bf), sd((8, feat), f32)],
        scratch_shapes=scatter_scratch(rows, feat)
        + [
            pltpu.VMEM(grads.shape, bf),
            pltpu.VMEM(gate_up.shape, bf),
            pltpu.VMEM((width, feat), bf),
            pltpu.VMEM((rows, feat), f32),
            pltpu.VMEM((8, rows, feat), bf),
            pltpu.VMEM((8, rows, width), bf),
            pltpu.VMEM((rows, feat), bf),
            pltpu.SemaphoreType.DMA((4,)),
            pltpu.SemaphoreType.DMA((8,)),
            pltpu.SemaphoreType.DMA((13,)),
            pltpu.SemaphoreType.DMA((13,)),
            pltpu.SemaphoreType.DMA((8,)),
            pltpu.SemaphoreType.DMA((8,)),
        ],
        compiler_params=pltpu.CompilerParams(collective_id=collective, has_side_effects=True, vmem_limit_bytes=63 << 20),
        cost_estimate=lasting(1),
        name="mlp_backward",
    )(grads, gate_up, w_out, piece, middle, y_rel, gain)


def final_kernel(
    draw_ref, hw_ref, hidden_ref, dn_ref, x_ref, mid_ref, middle_ref, other_ref, gain_ref, small_ref,
    gin_ref, lout_ref, all_ref,
    give1, take1, acc1, diag1, last1, sc1, rc1, sl1, rl1,
    give2, take2, acc2, diag2, last2, sc2, rc2, sl2, rl2,
    draw, hw, hidden, dn, x, mid, m_near, total1, total2, row_send, row_recv, z_in, z_sum, z_all,
    load_sem, draw_sem, hidden_sem, x_sem, row_sem, z_send, z_recv, p_send, p_recv,
    *, ndp,
):
    gx, gy, dp = lax.axis_index("gx"), lax.axis_index("gy"), lax.axis_index("dp")
    me = gx * 2 + gy
    rows, feat = middle_ref.shape
    part = feat // 2
    tile = 512
    near = pl.ds(pl.multiple_of(gy * part, part), part)
    xn = slot_peer(2, gx, gy)
    pairs = {0: (0, 2), 2: (0, 2), 1: (1, 4), 4: (1, 4), 3: (3, 6), 6: (3, 6), 5: (5, 7), 7: (5, 7)}
    load_hw = pltpu.make_async_copy(hw_ref, hw, load_sem.at[0])
    load_dn = pltpu.make_async_copy(dn_ref, dn, load_sem.at[1])
    order = (7, 5, 6, 3, 4, 1, 2, 0)
    draws = {}
    for r in order:
        px, py = slot_place(r, gx, gy)
        draws[r] = pltpu.make_async_copy(draw_ref.at[py * 4 + px], draw.at[r], draw_sem.at[r])
    hiddens = {r: pltpu.make_async_copy(hidden_ref.at[r], hidden.at[r], hidden_sem.at[r]) for r in order}
    draws[7].start()
    draws[5].start()
    load_hw.start()
    for r in order[2:]:
        draws[r].start()
    load_dn.start()
    for r in order:
        hiddens[r].start()
    finals = [
        pltpu.make_async_copy(x_ref, x, x_sem.at[0]),
        pltpu.make_async_copy(mid_ref.at[0, :, near], mid.at[gy], x_sem.at[1]),
        pltpu.make_async_copy(mid_ref.at[2, :, near], mid.at[1 - gy], x_sem.at[2]),
    ]
    for c in finals:
        c.start()
    finals.append(pltpu.make_async_copy(middle_ref.at[:, near], m_near, x_sem.at[3]))
    finals[-1].start()
    entry_barrier([slot_peer(r, gx, gy) for r in range(1, 8)] + [{"dp": flipped(dp, n, ndp)} for n in range(1, ndp)])
    around = [
        remote(small_ref, z_in.at[n], z_send.at[n], z_recv.at[n], {"dp": flipped(dp, n, ndp)}) for n in range(1, ndp)
    ]
    for c in around:
        c.start()

    def rows_pair(many, copies, slot, waited):
        for r in pairs[slot]:
            if r not in waited:
                copies[r].wait()
                waited.add(r)
        first, second = pairs[slot]
        low = first + (second - first) * gy
        return low, first + second - low

    def maker(many, copies, weights, weight_load, transposed):
        waited = set()

        def product(slot, put):
            low, high = rows_pair(many, copies, slot, waited)
            if weight_load is not None and "w" not in waited:
                weight_load.wait()
                waited.add("w")
            _, py = slot_place(slot, gx, gy)

            def body(t, _):
                cols = pl.ds(pl.multiple_of(t * tile, tile), tile)
                wide = pl.ds(pl.multiple_of(py * part + t * tile, tile), tile)
                if transposed:
                    w = weights[:, wide]
                    value = [nn_dot(many[low], w), nn_dot(many[high], w)]
                else:
                    w = weights[wide, :]
                    value = [nt_dot(many[low], w), nt_dot(many[high], w)]
                put(cols, jnp.concatenate(value, axis=0))
                return 0

            lax.fori_loop(0, part // tile, body, 0)

        return product

    first = Scatter(give1, take1, acc1, diag1, last1, sc1, rc1, sl1, rl1, gx, gy)
    second = Scatter(give2, take2, acc2, diag2, last2, sc2, rc2, sl2, rl2, gx, gy)
    first.begin(maker(draw, draws, hw, load_hw, False), total1)
    for c in around:
        c.wait_recv()
    summed = small_ref[...]
    for n in range(1, ndp):
        summed = summed + z_in[n]
    z_sum[...] = summed
    passes = [remote(z_sum, z_all.at[me], p_send.at[r], p_recv.at[r], slot_peer(r, gx, gy)) for r in range(1, 8)]
    for c in passes:
        c.start()
    second.begin(maker(hidden, hiddens, dn, load_dn, True), total2, first.forward)
    first.end(total1)
    for c in finals:
        c.wait()
    wide_x = x[...].astype(f32)
    scaled = gain_ref[:, near] * total1[...]
    sums = [jnp.sum(wide_x * wide_x, axis=-1, keepdims=True), jnp.sum(wide_x * scaled, axis=-1, keepdims=True)]
    lane = lax.broadcasted_iota(jnp.int32, (2 * rows, 128), 1)
    packed = jnp.where(lane == 0, sums[0], jnp.where(lane == 1, sums[1], 0.0)).T
    row_send[...] = packed[:8]
    row_copy = remote(row_send, row_recv, row_sem.at[0], row_sem.at[1], xn)
    row_copy.start()
    second.forward()
    second.end(total2)
    mine = pl.ds(pl.multiple_of(gy * rows, rows), rows)
    other = pl.ds(pl.multiple_of((1 - gy) * rows, rows), rows)
    lout_ref[gy] = (total2[mine, :] + m_near[...]).astype(bf)
    lout_ref[1 - gy] = (total2[other, :] + other_ref[...].astype(f32)).astype(bf)
    row_copy.wait_recv()
    both = jnp.concatenate([row_send[...] + row_recv[...], jnp.zeros((120, 2 * rows), f32)], axis=0).T
    rate = lax.rsqrt(both[:, 0:1] / feat + EPS)
    inner = both[:, 1:2] / feat
    gin = mid[...].reshape(2 * rows, part).astype(f32) + rate * scaled - wide_x * (rate * rate * rate) * inner
    gin_ref[...] = gin.astype(bf).reshape(2, rows, part)
    z_all[me] = z_sum[...]
    for c in passes:
        c.wait_recv()
    all_ref[...] = z_all[...]
    for c in around + passes + [row_copy]:
        c.wait_send()
    first.finish()
    second.finish()


def final_sums(draw, head_w, hidden, down, inputs, mid, middle, other, gain, small, ndp, collective):
    rows, feat = middle.shape
    part = feat // 2
    sd = jax.ShapeDtypeStruct
    dma = pltpu.SemaphoreType.DMA
    return pl.pallas_call(
        functools.partial(final_kernel, ndp=ndp),
        in_specs=[ANY] * 7 + [VM] * 3,
        out_specs=[VM] * 3,
        out_shape=[sd((2, rows, part), bf), sd((2, rows, part), bf), sd((8, *small.shape), f32)],
        scratch_shapes=scatter_scratch(2 * rows, part)
        + scatter_scratch(2 * rows, part)
        + [
            pltpu.VMEM(draw.shape, bf),
            pltpu.VMEM(head_w.shape, bf),
            pltpu.VMEM(hidden.shape, bf),
            pltpu.VMEM(down.shape, bf),
            pltpu.VMEM((2 * rows, part), bf),
            pltpu.VMEM((2, rows, part), bf),
            pltpu.VMEM((rows, part), f32),
            pltpu.VMEM((2 * rows, part), f32),
            pltpu.VMEM((2 * rows, part), f32),
            pltpu.VMEM((8, 2 * rows), f32),
            pltpu.VMEM((8, 2 * rows), f32),
            pltpu.VMEM((ndp, *small.shape), f32),
            pltpu.VMEM(small.shape, f32),
            pltpu.VMEM((8, *small.shape), f32),
            dma((2,)),
            dma((8,)),
            dma((8,)),
            dma((4,)),
            dma((2,)),
            dma((ndp,)),
            dma((ndp,)),
            dma((8,)),
            dma((8,)),
        ],
        compiler_params=pltpu.CompilerParams(collective_id=collective, has_side_effects=True, vmem_limit_bytes=63 << 20),
        cost_estimate=lasting(5),
        name="final_sums",
    )(draw, head_w, hidden, down, inputs, mid, middle, other, gain, small)


def dot(a, b):
    return lax.dot_general(a, b, (((1,), (0,)), ((), ())), preferred_element_type=f32)


def dot_t(a, b):
    return lax.dot_general(a, b, (((1,), (1,)), ((), ())), preferred_element_type=f32)


def dot_w(a, b):
    return lax.dot_general(a, b, (((0,), (0,)), ((), ())), preferred_element_type=f32)


def swap(value):
    return lax.ppermute(value, "gy", [(0, 1), (1, 0)])


def in_order(mine, other, axis):
    first = lax.axis_index("gy") == 0
    return jnp.concatenate([jnp.where(first, mine, other), jnp.where(first, other, mine)], axis=axis)


def halves(value, axis):
    size = value.shape[axis] // 2
    mine = lax.axis_index("gy")
    return (
        lax.dynamic_slice_in_dim(value, mine * size, size, axis),
        lax.dynamic_slice_in_dim(value, (1 - mine) * size, size, axis),
    )


def scatter_dp(value):
    return lax.psum_scatter(value.astype(bf), "dp", scatter_dimension=0, tiled=True)


def sort_halves(parts):
    first = lax.axis_index("gy") == 0
    return jnp.where(first, parts[0], parts[1]), swap(jnp.where(first, parts[1], parts[0]))


def shards(
    inputs,
    segments,
    norm_gain,
    w_query,
    w_key,
    w_value,
    w_beta,
    w_gate_head,
    conv_kernel,
    head_gain,
    w_out,
    mlp_gain,
    w_gate,
    w_up,
    w_down,
    grad_y,
):
    ngx, ngy, ndp = lax.axis_size("gx"), lax.axis_size("gy"), lax.axis_size("dp")
    gx, gy = lax.axis_index("gx"), lax.axis_index("gy")
    nb, part_rows, part_feat = inputs.shape
    length, feat = part_rows * ngx, part_feat * ngy
    tokens = nb * length
    own_rows = tokens // (ngx * ngy)
    heads = w_beta.shape[1] // ngy
    width = w_query.shape[1] // ngy
    beta_w = jnp.pad(w_beta.T.reshape(ngy, heads, part_feat), ((0, 0), (0, 128 - heads), (0, 0))).reshape(ngy * 128, part_feat).T
    block = w_gate.shape[1]
    units = -(-block // (ngy * 256)) * 256
    parts = ndp if ndp == 4 else 1
    normed, raw, head_w, x_own, gu_piece, out_piece = head_project(
        inputs.reshape(nb * part_rows, part_feat), w_query, w_key, w_value, w_gate_head, beta_w, w_gate, w_up, w_down, w_out,
        norm_gain[None], units, parts, 5,
    )
    normed = normed.reshape(tokens, feat)
    raw = raw.reshape(nb, length, -1)

    def around(value):
        return [value] + [lax.ppermute(value, "dp", [(i, i ^ n) for i in range(ndp)]) for n in range(1, parts)]

    gu_pieces = around(gu_piece)
    x_own, grad_y, w_down = lax.optimization_barrier((x_own, grad_y, w_down))
    down_piece = swap(lax.dynamic_slice_in_dim(w_down, (1 - gy) * (block - units), units // 2, 0))
    y_all = lax.all_gather(grad_y, ("gx", "gy"), axis=0, tiled=False)

    aux = make_aux(segments)
    conv_start = (gx * ngy + gy) * width
    conv_local = lax.dynamic_slice_in_dim(conv_kernel, conv_start, width, 2)
    gain_row = head_gain[None]
    mixed, *saved = mixer_fwd(raw, aux, conv_local, gain_row)
    middle, second_own, mixed_slots, middle_half = out_project(
        mixed.reshape(8, own_rows, width), w_out, out_piece, x_own, mlp_gain[None], 1
    )
    second, hidden, grads, y_rel, gate_up, down_w = mlp_forward(
        second_own, w_gate, w_up, w_down, y_all, gu_pieces, down_piece, units, 6
    )
    second_flat, hidden_flat = second.reshape(tokens, feat), hidden.reshape(tokens, units)
    grads_flat, y_flat = grads.reshape(tokens, 2 * units), y_rel.reshape(tokens, feat)
    half = feat // 2
    gu_first = dot_w(second_flat[:, :half], grads_flat).astype(bf)
    hidden_flat, gu_first = lax.optimization_barrier((hidden_flat, gu_first))
    down_grad = dot_w(hidden_flat, y_flat).astype(bf)
    down_keep, down_send = halves(down_grad, 1)
    second_flat, down_keep, down_send = lax.optimization_barrier((second_flat, down_keep, down_send))
    down_both = jnp.stack([down_keep, swap(down_send)])
    gu_second = dot_w(second_flat[:, half:], grads_flat).astype(bf)
    grads, gu_second = lax.optimization_barrier((grads, gu_second))
    gu_sums = [scatter_dp(gu_first), scatter_dp(gu_second)]
    first, last = down_both[gy], down_both[1 - gy]
    down_rows = jnp.concatenate([first, last[2 * units - block :]], axis=0)

    mid_slots, grad_mixed, mlp_gain_parts = mlp_backward(
        grads, gate_up, w_out, out_piece, middle, y_rel, mlp_gain[None], 2
    )
    grad_mixed, mid_slots, down_rows, *gu_sums = lax.optimization_barrier((grad_mixed, mid_slots, down_rows, *gu_sums))
    down_sum = scatter_dp(down_rows)
    out_grad = dot_w(mixed_slots.reshape(tokens, width), mid_slots.reshape(tokens, feat)).astype(bf)
    out_keep, out_send = halves(out_grad, 1)
    out_rows = in_order(out_keep, swap(out_send), 0)
    draw, conv_grad, gain_grad = mixer_bwd(
        raw, aux, conv_local, gain_row, saved, grad_mixed.reshape(nb, length, width)
    )
    draw = draw.reshape(tokens, -1)
    gu_pair = sort_halves(gu_sums)
    middle_other = swap(middle_half)
    draw, down_sum, out_rows, middle_other, *gu_pair = lax.optimization_barrier((draw, down_sum, out_rows, middle_other, *gu_pair))
    out_sum = scatter_dp(out_rows)
    main = 4 * width
    both = dot_w(normed, draw).astype(bf)
    norm_gain_grad = jnp.sum(both.astype(f32) * head_w.astype(f32), axis=1) / norm_gain
    beta_grad = both[:, main : main + heads].astype(f32)
    head_grads = both[:, :main].reshape(2, half, main)
    draw, hidden, head_grads = lax.optimization_barrier((draw, hidden, head_grads))
    head_sums = list(lax.psum_scatter(head_grads, "dp", scatter_dimension=1, tiled=True))
    hidden, out_sum = lax.optimization_barrier((hidden, out_sum))
    flat = [beta_grad.T, conv_grad, norm_gain_grad, jnp.sum(mlp_gain_parts, axis=0), gain_grad]
    counts = [v.size // 128 for v in flat]
    small = jnp.concatenate([v.reshape(-1, 128) for v in flat])
    small = jnp.pad(small, ((0, -small.shape[0] % 8), (0, 0)))
    if parts == 1:
        small = lax.psum(small, "dp")
    grad_inputs, layer_out, gathered = final_sums(
        draw.reshape(8, own_rows, -1), head_w, hidden, down_w, inputs.reshape(nb * part_rows, part_feat), mid_slots, middle,
        middle_other, norm_gain[None], small, parts, 3,
    )

    grad_inputs, layer_out, down_sum, out_sum, *gu_pair = lax.optimization_barrier((grad_inputs, layer_out, down_sum, out_sum, *gu_pair))
    sum_down, sum_out = down_sum.astype(f32), out_sum.astype(f32)
    grad_gu_mine, grad_gu_other = gu_pair
    head_mine, head_other = sort_halves(head_sums)

    def unit_columns(i):
        part = slice(i * units, (i + 1) * units)
        both = jnp.stack([grad_gu_mine[:, part], grad_gu_other[:, part]])
        return jnp.concatenate([both[gy], both[1 - gy][:, 2 * units - block :]], axis=1).astype(f32)

    sum_gate, sum_up = unit_columns(0), unit_columns(1)

    def head_part(i, n):
        return in_order(head_mine[:, i : i + n], head_other[:, i : i + n], 1).astype(f32)

    sum_query, sum_key, sum_value, sum_head_gate = (head_part(i * width, width) for i in range(4))

    n_beta, n_conv, n_norm, n_mlp, n_gain = counts
    beta_parts = gathered[:, :n_beta].reshape(8, heads, feat)
    beta_rows = feat // (ngy * ndp)
    beta_pair = lax.dynamic_slice(beta_parts, (gx * ngy, 0, (gy * ndp + lax.axis_index("dp")) * beta_rows), (ngy, heads, beta_rows))
    sum_beta = beta_pair.reshape(ngy * heads, beta_rows).T
    taps = conv_kernel.shape[1]
    conv_sum = gathered[:, n_beta : n_beta + n_conv].reshape(8, 3, taps, width).transpose(1, 2, 0, 3).reshape(conv_kernel.shape)
    rest = jnp.sum(gathered[:, n_beta + n_conv :], axis=0)
    norm_sum = rest[:n_norm].reshape(feat)
    mlp_sum = rest[n_norm : n_norm + n_mlp].reshape(feat)
    gain_sum = rest[n_norm + n_mlp : n_norm + n_mlp + n_gain].reshape(-1)
    return (
        layer_out,
        grad_inputs,
        norm_sum,
        sum_query,
        sum_key,
        sum_value,
        sum_beta,
        sum_head_gate,
        conv_sum,
        gain_sum,
        sum_out,
        mlp_sum,
        sum_gate,
        sum_up,
        sum_down,
    )


def solution(mesh):
    cols = P("gy", "gx")
    rows = P("gx", "gy")
    acts = P("dp", "gx", "gy")
    cols_out = P(("gy", "dp"), "gx")
    rows_out = P(("gx", "dp"), "gy")
    return jax.shard_map(
        shards,
        mesh=mesh,
        in_specs=(acts, P("dp", None), P(), cols, cols, cols, cols, cols, P(), P(), rows, P(), cols, cols, rows, acts),
        out_specs=(
            acts,
            acts,
            P(),
            cols_out,
            cols_out,
            cols_out,
            cols_out,
            cols_out,
            P(),
            P(),
            rows_out,
            P(),
            cols_out,
            cols_out,
            rows_out,
        ),
        check_vma=False,
    )
```

```python
import jax, jax.numpy as jnp
from jax import lax
from jax.experimental import pallas as pl
from jax.experimental.pallas import tpu as pltpu
import functools
from jax.sharding import PartitionSpec as P
EPS = 1e-6
HEAD_EPS = 0.01
C = 128
bf = jnp.bfloat16
f32 = jnp.float32
GROUP = 8
BACK_A = 8
BACK_C = 4

def lasting(us):
    return pl.CostEstimate(flops=int(us * 1.15e9), bytes_accessed=1 << 20, transcendentals=0)

def nn(a, b):
    return lax.dot_general(a.astype(bf), b.astype(bf), (((1,), (0,)), ((), ())), preferred_element_type=f32)
def nt(a, b):
    return lax.dot_general(a.astype(bf), b.astype(bf), (((1,), (1,)), ((), ())), preferred_element_type=f32)
def tn(a, b):
    return lax.dot_general(a.astype(bf), b.astype(bf), (((0,), (0,)), ((), ())), preferred_element_type=f32)

def level_masks(n):
    row = lax.broadcasted_iota(jnp.int32, (n, n), 0)
    col = lax.broadcasted_iota(jnp.int32, (n, n), 1)
    out = []
    size = 1
    while size < n:
        out.append(((row ^ col) & (-size) == size).astype(f32).astype(bf))
        size *= 2
    return (row == col).astype(f32).astype(bf), out

def inverse_many(many, eye, levels):
    totals = [eye - a * levels[0] for a in many]
    for mask in levels[1:]:
        inner = [nn(a * mask, t).astype(bf) for a, t in zip(many, totals)]
        outer = [nn(t, x).astype(bf) for t, x in zip(totals, inner)]
        totals = [t - x for t, x in zip(totals, outer)]
    return totals

def act_stage(x, prev, aux, w, norm):
    row8 = lax.broadcasted_iota(jnp.int32, (8, 128), 0)
    conv = x * w[0:1]
    sh = []
    for i in range(1, w.shape[0]):
        r = pltpu.roll(x, i, 0)
        p = pltpu.roll(prev, i, 0)
        head = jnp.where(row8 < i, p, r[:8])
        m = jnp.concatenate([head, r[8:]], axis=0) * aux[:, 2 + i:3 + i]
        sh.append(m)
        conv = conv + m * w[i:i + 1]
    s = jax.nn.sigmoid(conv)
    act = conv * s
    if norm:
        rate = lax.rsqrt(jnp.sum(act * act, axis=-1, keepdims=True) + EPS)
        return conv, s, act * rate, rate, sh
    return conv, s, act, None, sh

def masks(aux, segrow):
    n = aux.shape[0]
    row = lax.broadcasted_iota(jnp.int32, (n, n), 0)
    col = lax.broadcasted_iota(jnp.int32, (n, n), 1)
    same = aux[:, 0:1] == segrow
    return same & (row > col), same & (row >= col)

def aux_columns(ref, rows):
    block = ref[0, :, rows]
    return jnp.concatenate([block, jnp.zeros((C - block.shape[0], C), f32)], axis=0).T

def beta_column(block, h):
    lane = lax.broadcasted_iota(jnp.int32, block.shape, 1)
    return jnp.sum(jnp.where(lane == h, jax.nn.sigmoid(block), 0.0), axis=1, keepdims=True)

def prev_rows(ref, lo):
    start = pl.multiple_of(jnp.maximum(lo - 8, 0), 8)
    return jnp.where(lo > 0, ref[0, pl.ds(start, 8), :].astype(f32), 0.0)

def fwd_kernel(q_ref, k_ref, v_ref, g_ref, b_ref, aux_ref, w_ref, gain_ref,
               mixed_ref, t_ref, w_out, p_ref, f_ref, s_ref, fresh_ref, o_ref,
               q_s, u_s, b_s):
    h = pl.program_id(1)
    length = q_ref.shape[1]
    steps = length // C
    eye, levels = level_masks(C)
    def stage_a(group, _):
        lows = [pl.multiple_of((group * GROUP + n) * C, C) for n in range(GROUP)]
        spans = [pl.ds(lo, C) for lo in lows]
        many, keys, right = [], [], []
        for lo, rows in zip(lows, spans):
            aux = aux_columns(aux_ref, rows)
            q = act_stage(q_ref[0, rows, :].astype(f32), prev_rows(q_ref, lo), aux, w_ref[0], True)[2]
            k = act_stage(k_ref[0, rows, :].astype(f32), prev_rows(k_ref, lo), aux, w_ref[1], True)[2]
            v = act_stage(v_ref[0, rows, :].astype(f32), prev_rows(v_ref, lo), aux, w_ref[2], False)[2]
            beta = beta_column(b_ref[0, rows, :].astype(f32), h)
            strict, inclusive = masks(aux, aux_ref[0, 0:1, rows])
            kb = k.astype(bf)
            qb = q.astype(bf)
            both = nt(jnp.concatenate([kb, qb], axis=0), kb)
            many.append(jnp.where(strict, beta * both[:C], 0.0).astype(bf))
            p_ref[0, 0, rows, :] = jnp.where(inclusive, both[C:], 0.0).astype(bf)
            q_s[rows, :] = qb
            keys.append((k * aux[:, 2:3]).astype(bf))
            right.append(jnp.concatenate([(beta * k).astype(bf), (beta * v).astype(bf)], axis=1))
        totals = inverse_many(many, eye, levels)
        wus = [nn(t, r) for t, r in zip(totals, right)]
        kwus = [tn(k, wu) for k, wu in zip(keys, wus)]
        for rows, t, wu, kwu in zip(spans, totals, wus, kwus):
            clast = aux_ref[0, 1:2, rows][:, C - 1:C]
            f_ref[0, 0, rows, :] = (clast * (eye.astype(f32) - kwu[:, :C])).astype(bf)
            b_s[rows, :] = kwu[:, C:]
            t_ref[0, 0, rows, :] = t
            w_out[0, 0, rows, :] = wu[:, :C].astype(bf)
            u_s[rows, :] = wu[:, C:]
        return 0
    lax.fori_loop(0, steps // GROUP, stage_a, 0)
    def scan(c, state):
        rows = pl.ds(pl.multiple_of(c * C, C), C)
        sb = state.astype(bf)
        s_ref[0, 0, rows, :] = sb
        return nn(f_ref[0, 0, rows, :], sb) + b_s[rows, :]
    lax.fori_loop(0, steps, scan, jnp.zeros((C, C), f32), unroll=True)
    def stage_c(c, _):
        rows = pl.ds(pl.multiple_of(c * C, C), C)
        aux = aux_columns(aux_ref, rows)
        carried = aux[:, 1:2]
        ws = nn(jnp.concatenate([w_out[0, 0, rows, :], q_s[rows, :]], axis=0), s_ref[0, 0, rows, :])
        fresh = (u_s[rows, :] - carried * ws[:C]).astype(bf)
        out = carried * ws[C:] + nn(p_ref[0, 0, rows, :], fresh)
        fresh_ref[0, 0, rows, :] = fresh
        o_ref[0, 0, rows, :] = out
        g = g_ref[0, rows, :].astype(f32)
        r = lax.rsqrt(jnp.mean(out * out, axis=-1, keepdims=True) + HEAD_EPS)
        mixed_ref[0, rows, :] = (out * r * gain_ref[0:1] * (g * jax.nn.sigmoid(g))).astype(bf)
        return 0
    lax.fori_loop(0, steps, stage_c, 0, unroll=8)

def specs(length, heads, off):
    return [pl.BlockSpec((1, length, 128), functools.partial(lambda t, b, h: (b, 0, t * heads + h), t)) for t in range(4)] + [
        pl.BlockSpec((1, length, 128), lambda b, h: (b, 0, 4 * heads))]

def mixer_fwd(raw, aux, conv, gain):
    nb, length, width = raw.shape
    heads = (width - 128) // 512
    per = pl.BlockSpec((1, 1, length, 128), lambda b, h: (b, h, 0, 0))
    sh = lambda d: jax.ShapeDtypeStruct((nb, heads, length, 128), d)
    return pl.pallas_call(
        fwd_kernel,
        grid=(nb, heads),
        in_specs=specs(length, heads, 0) + [
            pl.BlockSpec((1, aux.shape[1], length), lambda b, h: (b, 0, 0)),
            pl.BlockSpec((3, conv.shape[1], 128), lambda b, h: (0, 0, h)),
            pl.BlockSpec((1, 128), lambda b, h: (0, 0)),
        ],
        out_specs=[pl.BlockSpec((1, length, 128), lambda b, h: (b, 0, h))] + [per] * 7,
        out_shape=[jax.ShapeDtypeStruct((nb, length, heads * 128), bf)] + [sh(bf)] * 6 + [sh(f32)],
        scratch_shapes=[pltpu.VMEM((length, 128), bf), pltpu.VMEM((length, 128), f32), pltpu.VMEM((length, 128), f32)],
        cost_estimate=lasting(33),
        name="mixer_forward",
    )(raw, raw, raw, raw, raw, aux, conv, gain)

def bwd_kernel(q_ref, k_ref, v_ref, g_ref, b_ref, aux_ref, w_ref, gain_ref,
               t_ref, w_in, p_ref, f_ref, s_ref, fresh_ref, o_ref, dm_ref,
               draw_ref, dconv_ref, dgain_ref,
               do_s, pd_s, base_s, ds_s):
    h = pl.program_id(1)
    heads = pl.num_programs(1)
    length = q_ref.shape[1]
    steps = length // C
    gain = gain_ref[0:1]
    def stage_a(group, dgain):
        spans, dos, lefts, carries = [], [], [], []
        for n in range(BACK_A):
            lo = pl.multiple_of((group * BACK_A + n) * C, C)
            rows = pl.ds(lo, C)
            aux = aux_columns(aux_ref, rows)
            q = act_stage(q_ref[0, rows, :].astype(f32), prev_rows(q_ref, lo), aux, w_ref[0], True)[2]
            out = o_ref[0, 0, rows, :]
            g = g_ref[0, rows, :].astype(f32)
            dm = dm_ref[0, rows, :].astype(f32)
            s = jax.nn.sigmoid(g)
            r = lax.rsqrt(jnp.mean(out * out, axis=-1, keepdims=True) + HEAD_EPS)
            scaled = out * r
            dn = dm * (g * s)
            dg = dm * scaled * gain * (s * (1.0 + g * (1.0 - s)))
            draw_ref[0, rows, pl.ds(pl.multiple_of((3 * heads + h) * 128, 128), 128)] = dg.astype(bf)
            e = dn * gain
            do = r * (e - scaled * jnp.mean(e * scaled, axis=-1, keepdims=True))
            do_s[rows, :] = do
            dgain = dgain + jnp.sum((dn * scaled).reshape(C // 8, 8, 128), axis=0)
            spans.append(rows)
            dos.append(do)
            lefts.append(q.astype(bf))
            carries.append(aux[:, 1:2])
        pds = [tn(p_ref[0, 0, rows, :], do) for rows, do in zip(spans, dos)]
        bases = [
            tn(jnp.concatenate([(c * do).astype(bf), (-c * pd).astype(bf)], axis=0), jnp.concatenate([q, w_in[0, 0, rows, :]], axis=0))
            for rows, do, pd, q, c in zip(spans, dos, pds, lefts, carries)
        ]
        for rows, pd, base in zip(spans, pds, bases):
            pd_s[rows, :] = pd
            base_s[rows, :] = base
        return dgain
    dgain = lax.fori_loop(0, steps // BACK_A, stage_a, jnp.zeros((8, 128), f32))
    dgain_ref[0, 0] = dgain
    def scan(j, state):
        c = steps - 1 - j
        rows = pl.ds(pl.multiple_of(c * C, C), C)
        sb = state.astype(bf)
        ds_s[rows, :] = sb
        return nn(sb, f_ref[0, 0, rows, :]) + base_s[rows, :]
    lax.fori_loop(0, steps, scan, jnp.zeros((C, C), f32), unroll=True)
    row8 = lax.broadcasted_iota(jnp.int32, (8, 128), 0)
    lane = lax.broadcasted_iota(jnp.int32, (C, 128), 1)

    def conv_back(dconv, nxt, aux, w, raw, sh):
        d = dconv * w[0:1]
        dw = [jnp.sum((dconv * raw).reshape(C // 8, 8, 128), axis=0)]
        for i in range(1, w.shape[0]):
            r = pltpu.roll(dconv, C - i, 0)
            p = pltpu.roll(nxt, 8 - i, 0)
            tailrows = jnp.where(row8 >= 8 - i, p, r[C - 8:])
            m = jnp.concatenate([r[:C - 8], tailrows], axis=0) * aux[:, 5 + i:6 + i]
            d = d + m * w[i:i + 1]
            dw.append(jnp.sum((dconv * sh[i - 1]).reshape(C // 8, 8, 128), axis=0))
        return d, dw

    def stage_c(j, carry):
        nq, nk, nv, dws = carry
        parts = []
        for n in range(BACK_C):
            lo = pl.multiple_of((steps - 1 - j * BACK_C - n) * C, C)
            rows = pl.ds(lo, C)
            aux = aux_columns(aux_ref, rows)
            xq = q_ref[0, rows, :].astype(f32)
            xk = k_ref[0, rows, :].astype(f32)
            xv = v_ref[0, rows, :].astype(f32)
            aq = act_stage(xq, prev_rows(q_ref, lo), aux, w_ref[0], True)
            ak = act_stage(xk, prev_rows(k_ref, lo), aux, w_ref[1], True)
            av = act_stage(xv, prev_rows(v_ref, lo), aux, w_ref[2], False)
            beta = beta_column(b_ref[0, rows, :].astype(f32), h)
            kb, qb = ak[2].astype(bf), aq[2].astype(bf)
            parts.append((rows, aux, xq, xk, xv, aq, ak, av, beta, kb, qb))
        grams = [nt(p[9], p[9]) for p in parts]
        from_next = [nt(p[9], ds_s[p[0], :]) for p in parts]
        from_state = [nn(p[9], s_ref[0, 0, p[0], :]) for p in parts]
        ys = [tn(t_ref[0, 0, p[0], :], pd_s[p[0], :] + p[1][:, 2:3] * d) for p, d in zip(parts, from_next)]
        boths = [
            nt(jnp.concatenate([do_s[p[0], :].astype(bf), y.astype(bf)], axis=0), fresh_ref[0, 0, p[0], :]) for p, y in zip(parts, ys)
        ]
        dxs = [p[8] * y for p, y in zip(parts, ys)]
        throughs = [
            nt(jnp.concatenate([p[1][:, 1:2] * do_s[p[0], :], -(p[1][:, 1:2] * dx)], axis=0), s_ref[0, 0, p[0], :])
            for p, dx in zip(parts, dxs)
        ]
        freshes = [nn(p[1][:, 2:3] * fresh_ref[0, 0, p[0], :].astype(f32), ds_s[p[0], :]) for p in parts]
        dps, dgss, dbetas = [], [], []
        for p, gram, state, y, both in zip(parts, grams, from_state, ys, boths):
            rows, aux, beta = p[0], p[1], p[8]
            strict, inclusive = masks(aux, aux_ref[0, 0:1, rows])
            x = p[7][2] - aux[:, 1:2] * state
            dps.append(jnp.where(inclusive, both[:C], 0.0).astype(bf))
            da = jnp.where(strict, -both[C:], 0.0)
            dbetas.append(jnp.sum(y * x, axis=-1, keepdims=True) + jnp.sum(da * gram, axis=-1, keepdims=True))
            dg = beta * da
            dgss.append(dg + dg.T)
        dqs = [t[:C] + nn(dp, p[9]) for p, t, dp in zip(parts, throughs, dps)]
        dks = [
            t[C:] + f + tn(dp, p[10]) + nn(dgs, p[9]) for p, t, f, dp, dgs in zip(parts, throughs, freshes, dps, dgss)
        ]
        for p, dq, dk, dv, dbeta in zip(parts, dqs, dks, dxs, dbetas):
            rows, aux, xq, xk, xv, (cq, sq, q, rq, shq), (ck, sk, k, rk, shk), (cv, sv, v, _, shv), beta = p[:9]
            db = dbeta * beta * (1.0 - beta)
            bl = pl.ds(4 * heads * 128, 128)
            @pl.when(h == 0)
            def _():
                draw_ref[0, rows, bl] = jnp.where(lane == 0, db, 0.0).astype(bf)
            @pl.when(h > 0)
            def _():
                old = draw_ref[0, rows, bl]
                draw_ref[0, rows, bl] = jnp.where(lane == h, db.astype(bf).astype(f32), old.astype(f32)).astype(bf)
            dq = rq * (dq - q * jnp.sum(q * dq, axis=-1, keepdims=True))
            dk = rk * (dk - k * jnp.sum(k * dk, axis=-1, keepdims=True))
            dcq = dq * (sq * (1.0 + cq * (1.0 - sq)))
            dck = dk * (sk * (1.0 + ck * (1.0 - sk)))
            dcv = dv * (sv * (1.0 + cv * (1.0 - sv)))
            rq_, wq = conv_back(dcq, nq, aux, w_ref[0], xq, shq)
            rk_, wk = conv_back(dck, nk, aux, w_ref[1], xk, shk)
            rv_, wv = conv_back(dcv, nv, aux, w_ref[2], xv, shv)
            for t, val in ((0, rq_), (1, rk_), (2, rv_)):
                draw_ref[0, rows, pl.ds(pl.multiple_of((t * heads + h) * 128, 128), 128)] = val.astype(bf)
            dws = tuple(a + b for a, b in zip(dws, wq + wk + wv))
            nq, nk, nv = dcq[:8], dck[:8], dcv[:8]
        return nq, nk, nv, dws
    z8 = jnp.zeros((8, 128), f32)
    taps = w_ref.shape[1]
    _, _, _, dws = lax.fori_loop(0, steps // BACK_C, stage_c, (z8, z8, z8, (z8,) * (3 * taps)))
    for n, d in enumerate(dws):
        dconv_ref[0, 0, n] = d

def mixer_bwd(raw, aux, conv, gain, saved, dmixed):
    nb, length, width = raw.shape
    heads = (width - 128) // 512
    taps = conv.shape[1]
    per = pl.BlockSpec((1, 1, length, 128), lambda b, h: (b, h, 0, 0))
    sh = lambda d: jax.ShapeDtypeStruct((nb, heads, length, 128), d)
    draw, dconv, dgain = pl.pallas_call(
        bwd_kernel,
        grid=(nb, heads),
        in_specs=specs(length, heads, 0) + [
            pl.BlockSpec((1, aux.shape[1], length), lambda b, h: (b, 0, 0)),
            pl.BlockSpec((3, taps, 128), lambda b, h: (0, 0, h)),
            pl.BlockSpec((1, 128), lambda b, h: (0, 0)),
        ] + [per] * 7 + [pl.BlockSpec((1, length, 128), lambda b, h: (b, 0, h))],
        out_specs=[pl.BlockSpec((1, length, width), lambda b, h: (b, 0, 0)),
                   pl.BlockSpec((1, 1, 3 * taps, 8, 128), lambda b, h: (b, h, 0, 0, 0)),
                   pl.BlockSpec((1, 1, 8, 128), lambda b, h: (b, h, 0, 0))],
        out_shape=[jax.ShapeDtypeStruct((nb, length, width), bf),
                   jax.ShapeDtypeStruct((nb, heads, 3 * taps, 8, 128), f32),
                   jax.ShapeDtypeStruct((nb, heads, 8, 128), f32)],
        scratch_shapes=[pltpu.VMEM((length, 128), f32)] * 3 + [pltpu.VMEM((length, 128), bf)],
        cost_estimate=lasting(2),
        name="mixer_backward",
    )(raw, raw, raw, raw, raw, aux, conv, gain, *saved, dmixed)
    dconv = jnp.sum(dconv, axis=(0, 3)).reshape(heads, 3, taps, 128).transpose(1, 2, 0, 3).reshape(3, taps, heads * 128)
    return draw, dconv, jnp.sum(dgain, axis=(0, 1, 2))

def make_aux(segments):
    nb, length = segments.shape
    seg = segments.astype(f32)
    blocks = seg.reshape(nb, length // C, C)
    last = blocks[:, :, -1:]
    before = jnp.concatenate([jnp.full((nb, 1, 1), -1.0, f32), last[:, :-1]], axis=1)
    carried = (blocks == before).astype(f32).reshape(nb, length)
    tail = (blocks == last).astype(f32).reshape(nb, length)
    cols = [seg, carried, tail]
    for i in range(1, 4):
        cols.append((jnp.pad(seg, ((0, 0), (i, 0)), constant_values=-1.0)[:, :length] == seg).astype(f32))
    for i in range(1, 4):
        cols.append((jnp.pad(seg, ((0, 0), (0, i)), constant_values=-1.0)[:, i:] == seg).astype(f32))
    cols += [jnp.zeros_like(seg)] * (16 - len(cols))
    return jnp.stack(cols, axis=1)


SLOTS = ((0, 0, 0), (0, 0, 1), (1, 0, 0), (0, 1, 0), (1, 0, 1), (0, 1, 1), (1, 1, 0), (1, 1, 1))
MESH = pl.DeviceIdType.MESH
VM = pl.BlockSpec(memory_space=pltpu.VMEM)
ANY = pl.BlockSpec(memory_space=pl.ANY)


def slot_place(r, gx, gy):
    dx, dy, dc = SLOTS[r]
    hi, lo = gx // 2, gx % 2
    hi = 1 - hi if dy else hi
    lo = 1 - lo if dc else lo
    return hi * 2 + lo, (1 - gy if dx else gy)


def slot_peer(r, gx, gy):
    px, py = slot_place(r, gx, gy)
    return {"gx": px, "gy": py}


def flipped(index, n, size):
    out, bit = 0, 1
    while bit < size:
        digit = index // bit % 2
        out = out + bit * (1 - digit if n & bit else digit)
        bit *= 2
    return out


def entry_barrier(peers):
    sem = pltpu.get_barrier_semaphore()
    for peer in peers:
        pl.semaphore_signal(sem, inc=1, device_id=peer, device_id_type=MESH)
    pl.semaphore_wait(sem, len(peers))


def remote(src, dst, send, recv, peer):
    return pltpu.make_async_remote_copy(src, dst, send, recv, device_id=peer, device_id_type=MESH)


def nt_dot(a, b):
    return lax.dot_general(a, b, (((1,), (1,)), ((), ())), preferred_element_type=f32)


def nn_dot(a, b):
    return lax.dot_general(a, b, (((1,), (0,)), ((), ())), preferred_element_type=f32)


class Gather:
    COPIES = 13

    def __init__(self, buf, send, recv, gx, gy, over_gx=False):
        rows = buf.shape[1]
        half = rows // 2
        a, b = pl.ds(0, half), pl.ds(half, half)
        core, xn, yn = (slot_peer(r, gx, gy) for r in (1, 2, 3))

        def make(i, src, dst, part, peer):
            return remote(buf.at[src, part], buf.at[dst, part], send.at[i], recv.at[i], peer)

        self.own = [
            make(0, 0, 2, a, xn),
            make(1, 0, 3, a, yn),
            make(2, 0, 2, b, xn),
            make(3, 0, 3, b, yn),
            remote(buf.at[0], buf.at[1], send.at[4], recv.at[4], core),
        ]
        self.over_gx = over_gx
        self.diagonal = [make(5, 2, 6, a, yn) if over_gx else make(5, 3, 6, a, xn), make(6, 2, 6, b, yn)]
        self.cross = [
            make(7, 2, 4, a, core),
            make(8, 2, 4, b, core),
            make(9, 3, 5, a, core),
            make(10, 3, 5, b, core),
            make(11, 6, 7, a, core),
            make(12, 6, 7, b, core),
        ]

    def start(self):
        for c in self.own:
            c.start()

    def step(self, i):
        if i == 1:
            self.own[4].wait_recv()
        elif i == 2:
            self.own[1].wait_recv()
            if not self.over_gx:
                self.diagonal[0].start()
            self.cross[2].start()
            self.own[0].wait_recv()
            if self.over_gx:
                self.diagonal[0].start()
            self.cross[0].start()
            self.own[2].wait_recv()
            self.diagonal[1].start()
            self.cross[1].start()
        elif i == 3:
            self.own[3].wait_recv()
            self.cross[3].start()
        elif i == 4:
            self.cross[0].wait_recv()
            self.cross[1].wait_recv()
        elif i == 5:
            self.cross[2].wait_recv()
            self.cross[3].wait_recv()
        elif i == 6:
            self.diagonal[0].wait_recv()
            self.cross[4].start()
            self.diagonal[1].wait_recv()
            self.cross[5].start()
        elif i == 7:
            self.cross[4].wait_recv()
            self.cross[5].wait_recv()

    def finish(self):
        for c in self.own + self.diagonal + self.cross:
            c.wait_send()


def head_kernel(
    x_ref, wq_ref, wk_ref, wv_ref, wg_ref, wb_ref, gate_ref, up_ref, down_ref, out_ref, gain_ref,
    normed_ref, raw_ref, hw_ref, own_ref, gu_ref, wo_ref,
    buf, w, low, acc, ag_send, ag_recv, w_send, w_recv, load_sem, out_sem, raw_sem, hw_sem, z_send, z_recv, u_send, u_recv,
):
    gx, gy, dp = lax.axis_index("gx"), lax.axis_index("gy"), lax.axis_index("dp")
    ngx = 4
    units = gu_ref.shape[1] // 2
    parts = (x_ref.shape[1] + units // 2) // gu_ref.shape[0]
    piece = x_ref.shape[1] // parts
    down_piece = units // 2 // parts
    unit_other = pl.multiple_of((1 - gy) * (gate_ref.shape[1] - units), 128)
    turn = flipped(dp, 0, parts)
    rows_sent = pl.ds(pl.multiple_of(turn * piece, piece), piece)
    rows = own_ref.shape[0]
    part = x_ref.shape[1]
    width = wq_ref.shape[1] // 2
    weights = ((wq_ref, width), (wk_ref, width), (wv_ref, width), (wg_ref, width), (wb_ref, 128))
    starts = [0, width, 2 * width, 3 * width, 4 * width]
    xn = slot_peer(2, gx, gy)
    loads = [pltpu.make_async_copy(x_ref, buf.at[0], load_sem.at[5])]
    for i, (ref, n) in enumerate(weights):
        src = ref.at[:, pl.ds(pl.multiple_of(gy * n, 128), n)]
        loads.append(pltpu.make_async_copy(src, w.at[0, :, pl.ds(starts[i], n)], load_sem.at[i]))
    for c in loads:
        c.start()
    peers = [slot_peer(r, gx, gy) for r in (1, 2, 3)] + [{"dp": flipped(dp, n, parts)} for n in range(1, parts)]
    entry_barrier(peers)
    swaps = []
    for i, (ref, n) in enumerate(weights):
        src = ref.at[rows_sent, pl.ds(pl.multiple_of((1 - gy) * n, 128), n)]
        swaps.append(remote(src, w.at[1, rows_sent, pl.ds(starts[i], n)], w_send.at[i], w_recv.at[i], xn))
        swaps[-1].start()
    loads[0].wait()
    gather = Gather(buf, ag_send, ag_recv, gx, gy, True)
    gather.start()
    extra = [
        remote(gate_ref.at[rows_sent, pl.ds(unit_other, units)], gu_ref.at[pl.ds(0, piece), pl.ds(0, units)], u_send.at[0], u_recv.at[0], xn),
        remote(up_ref.at[rows_sent, pl.ds(unit_other, units)], gu_ref.at[pl.ds(0, piece), pl.ds(units, units)], u_send.at[1], u_recv.at[1], xn),
        remote(
            down_ref.at[pl.ds(pl.multiple_of(unit_other + units // 2 + turn * down_piece, 32), down_piece), :],
            gu_ref.at[pl.ds(piece, down_piece), pl.ds(0, x_ref.shape[1])],
            u_send.at[3],
            u_recv.at[3],
            xn,
        ),
        remote(out_ref.at[pl.ds(pl.multiple_of((1 - gy) * width, width), width), :], wo_ref, u_send.at[2], u_recv.at[2], xn),
    ]
    for c in extra:
        c.start()
    for c in swaps:
        c.wait_recv()
    spread = [
        remote(w.at[1, rows_sent], w.at[1, rows_sent], z_send.at[n], z_recv.at[n], {"dp": flipped(dp, n, parts)}) for n in range(1, parts)
    ]
    for c in spread:
        c.start()
    for c in loads[1:]:
        c.wait()
    keep = pltpu.make_async_copy(w.at[0], hw_ref.at[pl.ds(pl.multiple_of(gy * part, part), part)], hw_sem.at[0])
    keep.start()
    near = pl.ds(pl.multiple_of(gy * part, part), part)
    far = pl.ds(pl.multiple_of((1 - gy) * part, part), part)
    stores = []
    blocks = []

    def pair(n, first, second):
        px, _ = slot_place(first, gx, gy)
        for s in range(2):
            span = pl.ds(s * rows, rows)
            v = s * ngx + px
            i = 2 * n + s
            x0 = buf[first, span, :].astype(f32)
            x1 = buf[second, span, :].astype(f32)
            total = jnp.sum(x0 * x0, axis=-1, keepdims=True) + jnp.sum(x1 * x1, axis=-1, keepdims=True)
            rate = lax.rsqrt(total / (2 * part) + EPS)
            low[i, :, near] = (x0 * rate * gain_ref[:, near]).astype(bf)
            low[i, :, far] = (x1 * rate * gain_ref[:, far]).astype(bf)
            c = pltpu.make_async_copy(low.at[i], normed_ref.at[v], out_sem.at[i])
            c.start()
            stores.append(c)
            acc[i] = nn_dot(low[i, :, near], w[0])
            blocks.append((i, v))

    for step in (1, 2, 3, 4):
        gather.step(step)
        if step == 2:
            pair(0, 0, 2)
            mine = pl.ds(pl.multiple_of(gy * rows, rows), rows)
            own_ref[:, near] = buf[0, mine, :]
            own_ref[:, far] = buf[2, mine, :]
    pair(1, 1, 4)
    gather.step(5)
    gather.step(6)
    pair(2, 3, 6)
    gather.step(7)
    pair(3, 5, 7)
    for c in spread:
        c.wait_recv()
    give = pltpu.make_async_copy(w.at[1], hw_ref.at[far], hw_sem.at[1])
    give.start()

    for i, v in blocks:
        acc[i] += nn_dot(low[i, :, far], w[1])
        c = pltpu.make_async_copy(acc.at[i], raw_ref.at[v], raw_sem.at[i])
        c.start()
        stores.append(c)
    keep.wait()
    give.wait()
    for c in stores:
        c.wait()
    for c in extra:
        c.wait_recv()
    for c in swaps + spread + extra:
        c.wait_send()
    gather.finish()


def head_project(inputs, w_query, w_key, w_value, w_gate_head, w_beta, w_gate, w_up, w_down, w_out, gain, units, parts, collective):
    total, part = inputs.shape
    rows = total // 2
    feat = 2 * part
    cols = 2 * w_query.shape[1] + 128
    sd = jax.ShapeDtypeStruct
    return pl.pallas_call(
        head_kernel,
        in_specs=[ANY] * 10 + [VM],
        out_specs=[ANY, ANY, ANY, VM, ANY, ANY],
        out_shape=[
            sd((8, rows, feat), bf),
            sd((8, rows, cols), f32),
            sd((feat, cols), bf),
            sd((rows, feat), bf),
            sd(((part + units // 2) // parts, 2 * units), bf),
            sd((w_out.shape[0] // 2, w_out.shape[1]), bf),
        ],
        scratch_shapes=[
            pltpu.VMEM((8, total, part), bf),
            pltpu.VMEM((2, part, cols), bf),
            pltpu.VMEM((8, rows, feat), bf),
            pltpu.VMEM((8, rows, cols), f32),
            pltpu.SemaphoreType.DMA((13,)),
            pltpu.SemaphoreType.DMA((13,)),
            pltpu.SemaphoreType.DMA((5,)),
            pltpu.SemaphoreType.DMA((5,)),
            pltpu.SemaphoreType.DMA((6,)),
            pltpu.SemaphoreType.DMA((8,)),
            pltpu.SemaphoreType.DMA((8,)),
            pltpu.SemaphoreType.DMA((2,)),
            pltpu.SemaphoreType.DMA((4,)),
            pltpu.SemaphoreType.DMA((4,)),
            pltpu.SemaphoreType.DMA((4,)),
            pltpu.SemaphoreType.DMA((4,)),
        ],
        compiler_params=pltpu.CompilerParams(collective_id=collective, has_side_effects=True, vmem_limit_bytes=60 << 20),
        cost_estimate=lasting(80),
        name="head_project",
    )(inputs, w_query, w_key, w_value, w_gate_head, w_beta, w_gate, w_up, w_down, w_out, gain)


def mlp_kernel(x_ref, gate_ref, up_ref, down_ref, y_ref, *refs, parts):
    gu_refs, piece_ref, refs = refs[:parts], refs[parts], refs[parts + 1 :]
    mlp_body(parts, x_ref, gate_ref, up_ref, down_ref, y_ref, gu_refs, piece_ref, *refs)


def mlp_body(
    parts, x_ref, gate_ref, up_ref, down_ref, y_ref, gu_refs, piece_ref,
    second_ref, hidden_ref, grads_ref, yrel_ref, gu_out, dn_out,
    wgu, wd, buf, ybuf, hbuf, gbuf, load_sem, w_sem, keep_sem, y_sem, y_out_sem, out_sem, ag_send, ag_recv,
):
    gx, gy = lax.axis_index("gx"), lax.axis_index("gy")
    ngy = 2
    rows = x_ref.shape[0]
    feat = x_ref.shape[1]
    units = wd.shape[0]
    half = feat // 2
    tile = 256
    dp = lax.axis_index("dp")
    unit_mine = pl.multiple_of(gy * (gate_ref.shape[1] - units), 128)
    doubled = gy * (2 * units - gate_ref.shape[1])
    load = pltpu.make_async_copy(x_ref, buf.at[0], load_sem)
    load.start()
    near = pl.ds(pl.multiple_of(gy * half, half), half)
    far = pl.multiple_of((1 - gy) * half, half)
    own_units = pl.ds(unit_mine, units)
    w_loads = [
        pltpu.make_async_copy(gate_ref.at[:, own_units], wgu.at[near, pl.ds(0, units)], w_sem.at[0]),
        pltpu.make_async_copy(up_ref.at[:, own_units], wgu.at[near, pl.ds(units, units)], w_sem.at[1]),
        pltpu.make_async_copy(down_ref.at[own_units, :], wd.at[:, near], w_sem.at[2]),
    ]
    w_loads.append(pltpu.make_async_copy(piece_ref, wd.at[pl.ds(0, units // 2), pl.ds(far, half)], w_sem.at[3]))
    for n in range(parts):
        turn = flipped(dp, n, parts)
        piece = half // parts
        down_piece = units // 2 // parts
        gu_rows = wgu.at[pl.ds(pl.multiple_of(far + turn * piece, piece), piece), :]
        down_rows = wd.at[pl.ds(pl.multiple_of(units // 2 + turn * down_piece, 32), down_piece), pl.ds(far, half)]
        w_loads.append(pltpu.make_async_copy(gu_refs[n].at[pl.ds(0, piece)], gu_rows, w_sem.at[4 + 2 * n]))
        w_loads.append(pltpu.make_async_copy(gu_refs[n].at[pl.ds(piece, down_piece), pl.ds(0, half)], down_rows, w_sem.at[5 + 2 * n]))
    for c in w_loads:
        c.start()
    entry_barrier([slot_peer(r, gx, gy) for r in (1, 2, 3)])
    load.wait()
    gather = Gather(buf, ag_send, ag_recv, gx, gy)
    gather.start()

    def y_load(r, n):
        px, py = slot_place(r, gx, gy)
        return [
            pltpu.make_async_copy(y_ref.at[px * ngy + h, py], ybuf.at[r % 2, :, pl.ds(h * (feat // 2), feat // 2)], y_sem.at[r % 2, h])
            for h in range(2)
        ]

    def y_store(r):
        return pltpu.make_async_copy(ybuf.at[r % 2], yrel_ref.at[r], y_out_sem.at[r % 2])

    for c in y_load(0, 0):
        c.start()
    for c in w_loads:
        c.wait()
    keeps = [pltpu.make_async_copy(wgu, gu_out, keep_sem.at[0]), pltpu.make_async_copy(wd, dn_out, keep_sem.at[1])]
    for c in keeps:
        c.start()

    def outs(r):
        return [
            pltpu.make_async_copy(buf.at[r], second_ref.at[r], out_sem.at[0, r % 2]),
            pltpu.make_async_copy(hbuf.at[r % 2], hidden_ref.at[r], out_sem.at[1, r % 2]),
            pltpu.make_async_copy(gbuf.at[r % 2], grads_ref.at[r], out_sem.at[2, r % 2]),
        ]

    for r in range(8):
        gather.step(r)
        if r >= 2:
            for c in outs(r - 2):
                c.wait()
        if r + 1 < 8:
            if r >= 1:
                y_store(r - 1).wait()
            for c in y_load(r + 1, 0):
                c.start()
        for c in y_load(r, 0):
            c.wait()
        y_store(r).start()

        def body(t, _):
            cols = pl.ds(pl.multiple_of(t * tile, tile), tile)
            up_cols = pl.ds(pl.multiple_of(units + t * tile, tile), tile)
            gate = nn_dot(buf[r], wgu[:, cols])
            up = nn_dot(buf[r], wgu[:, up_cols])
            gh = nt_dot(ybuf[r % 2], wd[cols, :])
            s = jax.nn.sigmoid(gate)
            keep = lax.broadcasted_iota(jnp.int32, gate.shape, 1) + t * tile >= doubled
            act = jnp.where(keep, gate * s, 0.0)
            up = jnp.where(keep, up, 0.0)
            hbuf[r % 2, :, cols] = (act * up).astype(bf)
            gbuf[r % 2, :, up_cols] = (gh * act).astype(bf)
            gbuf[r % 2, :, cols] = (gh * up * s * (1.0 + gate * (1.0 - s))).astype(bf)
            return 0

        lax.fori_loop(0, units // tile, body, 0)
        for c in outs(r):
            c.start()
    for r in (6, 7):
        for c in outs(r):
            c.wait()
        y_store(r).wait()
    gather.finish()
    for c in keeps:
        c.wait()


def mlp_forward(x_own, w_gate, w_up, w_down, y_all, gu_pieces, down_piece, units, collective):
    rows, feat = x_own.shape
    parts = len(gu_pieces)
    sd = jax.ShapeDtypeStruct
    return pl.pallas_call(
        functools.partial(mlp_kernel, parts=parts),
        in_specs=[ANY] * (6 + parts),
        out_specs=[ANY] * 6,
        out_shape=[
            sd((8, rows, feat), bf),
            sd((8, rows, units), bf),
            sd((8, rows, 2 * units), bf),
            sd((8, rows, feat), bf),
            sd((feat, 2 * units), bf),
            sd((units, feat), bf),
        ],
        scratch_shapes=[
            pltpu.VMEM((feat, 2 * units), bf),
            pltpu.VMEM((units, feat), bf),
            pltpu.VMEM((8, rows, feat), bf),
            pltpu.VMEM((2, rows, feat), bf),
            pltpu.VMEM((2, rows, units), bf),
            pltpu.VMEM((2, rows, 2 * units), bf),
            pltpu.SemaphoreType.DMA,
            pltpu.SemaphoreType.DMA((4 + 2 * parts,)),
            pltpu.SemaphoreType.DMA((2,)),
            pltpu.SemaphoreType.DMA((2, 2)),
            pltpu.SemaphoreType.DMA((2,)),
            pltpu.SemaphoreType.DMA((3, 2)),
            pltpu.SemaphoreType.DMA((13,)),
            pltpu.SemaphoreType.DMA((13,)),
        ],
        compiler_params=pltpu.CompilerParams(collective_id=collective, has_side_effects=True, vmem_limit_bytes=62 << 20),
        cost_estimate=lasting(68),
        name="mlp_forward",
    )(x_own, w_gate, w_up, w_down, y_all, *gu_pieces, down_piece)


class Scatter:
    def __init__(self, give, take, acc, diag_in, last_in, s_core, r_core, s_link, r_link, gx, gy, over_gx=False):
        self.over_gx = over_gx
        self.give, self.take, self.acc, self.diag_in, self.last_in = give, take, acc, diag_in, last_in
        core, xn, yn = (slot_peer(r, gx, gy) for r in (1, 2, 3))
        rows = acc.shape[1]
        half = rows // 2
        a, b = pl.ds(0, half), pl.ds(half, half)
        self.a, self.b = a, b
        self.core = [remote(give.at[n], take.at[n], s_core.at[n], r_core.at[n], core) for n in range(4)]

        def link(i, src, dst, peer):
            return remote(src, dst, s_link.at[i], r_link.at[i], peer)

        self.link = [
            link(0, acc.at[0, a], diag_in.at[0], yn if over_gx else xn),
            link(1, acc.at[0, b], diag_in.at[1], yn),
            link(2, acc.at[1, a], last_in.at[0, a], xn),
            link(3, acc.at[2, b], last_in.at[1, b], yn),
            link(4, acc.at[1, b], last_in.at[0, b], xn),
            link(5, acc.at[2, a], last_in.at[1, a], yn),
        ]

    def begin(self, product, self_acc, between=None):
        acc = self.acc

        def give_out(n, slot):
            def put(cols, value):
                self.give[n, :, cols] = value.astype(bf)

            product(slot, put)
            self.core[n].start()

        def keep(n, slot):
            def put(cols, value):
                acc[n, :, cols] = value.astype(bf)

            product(slot, put)

        def join(n):
            self.core[n].wait_recv()
            acc[n] = (acc[n].astype(f32) + self.take[n].astype(f32)).astype(bf)

        give_out(0, 7)
        keep(0, 6)
        give_out(1, 4)
        if between is not None:
            between()
        join(0)
        self.link[0].start()
        self.link[1].start()
        give_out(2, 5)
        keep(1, 2)
        join(1)
        if not self.over_gx:
            self.link[2].start()
        keep(2, 3)
        join(2)
        self.link[3].start()
        if self.over_gx:
            self.link[5].start()
        give_out(3, 1)

        def put_self(cols, value):
            self_acc[:, cols] = value

        product(0, put_self)

    def forward(self):
        acc, a, b = self.acc, self.a, self.b
        if self.over_gx:
            for i, half, onward in ((0, a, 2), (1, b, 4)):
                self.link[i].wait_recv()
                acc[1, half] = (acc[1, half].astype(f32) + self.diag_in[i].astype(f32)).astype(bf)
                self.link[onward].start()
            return
        self.link[1].wait_recv()
        acc[1, b] = (acc[1, b].astype(f32) + self.diag_in[1].astype(f32)).astype(bf)
        self.link[4].start()
        self.link[0].wait_recv()
        acc[2, a] = (acc[2, a].astype(f32) + self.diag_in[0].astype(f32)).astype(bf)
        self.link[5].start()

    def end(self, self_acc):
        self.core[3].wait_recv()
        self_acc[...] += self.take[3].astype(f32)
        for c in self.link[2:]:
            c.wait_recv()
        self_acc[...] += self.last_in[0].astype(f32) + self.last_in[1].astype(f32)

    def run(self, product, self_acc):
        self.begin(product, self_acc)
        self.forward()
        self.end(self_acc)

    def finish(self):
        for c in self.core + self.link:
            c.wait_send()


def scatter_scratch(rows, feat):
    return [
        pltpu.VMEM((4, rows, feat), bf),
        pltpu.VMEM((4, rows, feat), bf),
        pltpu.VMEM((3, rows, feat), bf),
        pltpu.VMEM((2, rows // 2, feat), bf),
        pltpu.VMEM((2, rows, feat), bf),
        pltpu.SemaphoreType.DMA((4,)),
        pltpu.SemaphoreType.DMA((4,)),
        pltpu.SemaphoreType.DMA((6,)),
        pltpu.SemaphoreType.DMA((6,)),
    ]


def own_out_rows(out_ref, piece_ref, w, sem, gy):
    width, part = piece_ref.shape
    near = pl.ds(pl.multiple_of(gy * part, part), part)
    far = pl.ds(pl.multiple_of((1 - gy) * part, part), part)
    return [
        pltpu.make_async_copy(out_ref.at[pl.ds(pl.multiple_of(gy * width, width), width), :], w.at[:, near], sem.at[0]),
        pltpu.make_async_copy(piece_ref, w.at[:, far], sem.at[1]),
    ]


def out_kernel(
    mixed_ref, out_ref, piece_ref, x_ref, gain_ref,
    middle_ref, normed_ref, slots_ref, other_ref,
    give, take, acc, diag_in, last_in, s_core, r_core, s_link, r_link, lhs, w, total, load_sem, lhs_sem, keep_sem,
):
    gx, gy = lax.axis_index("gx"), lax.axis_index("gy")
    feat = x_ref.shape[1]
    tile = 512
    loads = own_out_rows(out_ref, piece_ref, w, load_sem, gy)
    pulls = {}
    for r in (7, 6, 4, 5, 2, 3, 1, 0):
        px, py = slot_place(r, gx, gy)
        pulls[r] = pltpu.make_async_copy(mixed_ref.at[py * 4 + px], lhs.at[r], lhs_sem.at[r])
    for c in loads + list(pulls.values()):
        c.start()
    entry_barrier([slot_peer(r, gx, gy) for r in (1, 2, 3)])
    for c in loads:
        c.wait()

    def product(slot, put):
        pulls[slot].wait()

        def body(t, _):
            cols = pl.ds(pl.multiple_of(t * tile, tile), tile)
            put(cols, nn_dot(lhs[slot], w[:, cols]))
            return 0

        lax.fori_loop(0, feat // tile, body, 0)

    scatter = Scatter(give, take, acc, diag_in, last_in, s_core, r_core, s_link, r_link, gx, gy)
    scatter.run(product, total)
    keep = pltpu.make_async_copy(lhs, slots_ref, keep_sem)
    keep.start()
    middle = x_ref[...].astype(f32) + total[...]
    middle_ref[...] = middle
    other_ref[...] = middle_ref[:, pl.ds(pl.multiple_of((1 - gy) * (feat // 2), feat // 2), feat // 2)].astype(bf)
    rate = lax.rsqrt(jnp.mean(middle * middle, axis=-1, keepdims=True) + EPS)
    normed_ref[...] = (middle * rate * gain_ref[...]).astype(bf)
    keep.wait()
    scatter.finish()


def out_project(mixed, w_out, piece, x_own, gain, collective):
    rows, feat = x_own.shape
    width = mixed.shape[2]
    sd = jax.ShapeDtypeStruct
    return pl.pallas_call(
        out_kernel,
        in_specs=[ANY, ANY, ANY, VM, VM],
        out_specs=[VM, VM, ANY, VM],
        out_shape=[sd((rows, feat), f32), sd((rows, feat), bf), sd(mixed.shape, bf), sd((rows, feat // 2), bf)],
        scratch_shapes=scatter_scratch(rows, feat)
        + [
            pltpu.VMEM(mixed.shape, bf),
            pltpu.VMEM((width, feat), bf),
            pltpu.VMEM((rows, feat), f32),
            pltpu.SemaphoreType.DMA((2,)),
            pltpu.SemaphoreType.DMA((8,)),
            pltpu.SemaphoreType.DMA,
        ],
        compiler_params=pltpu.CompilerParams(collective_id=collective, has_side_effects=True, vmem_limit_bytes=60 << 20),
        cost_estimate=lasting(44),
        name="out_project",
    )(mixed, w_out, piece, x_own, gain)


def back_kernel(
    grads_ref, wgu_ref, out_ref, piece_ref, middle_ref, y_ref, gain_ref,
    mid_ref, gmix_ref, dgain_ref,
    give, take, acc, diag_in, last_in, s_core, r_core, s_link, r_link,
    lhs, wgu, w, total, buf, gstage, y_own, load_sem, lhs_sem, ag_send, ag_recv, mid_sem, gmix_sem,
):
    gx, gy = lax.axis_index("gx"), lax.axis_index("gy")
    rows, feat = middle_ref.shape
    tile = 512
    load = pltpu.make_async_copy(wgu_ref, wgu, load_sem.at[2])
    outs = own_out_rows(out_ref, piece_ref, w, load_sem, gy)
    order = (7, 6, 4, 5, 2, 3, 1, 0)
    pulls = {r: pltpu.make_async_copy(grads_ref.at[r], lhs.at[r], lhs_sem.at[r]) for r in order}
    pulls[7].start()
    load.start()
    for r in order[1:]:
        pulls[r].start()
    outs.append(pltpu.make_async_copy(y_ref.at[0], y_own, load_sem.at[3]))
    for c in outs:
        c.start()
    entry_barrier([slot_peer(r, gx, gy) for r in (1, 2, 3)])
    load.wait()

    def product(slot, put):
        pulls[slot].wait()

        def body(t, _):
            cols = pl.ds(pl.multiple_of(t * tile, tile), tile)
            put(cols, nt_dot(lhs[slot], wgu[cols, :]))
            return 0

        lax.fori_loop(0, feat // tile, body, 0)

    scatter = Scatter(give, take, acc, diag_in, last_in, s_core, r_core, s_link, r_link, gx, gy, True)
    scatter.run(product, total)
    middle = middle_ref[...]
    incoming = total[...]
    rate = lax.rsqrt(jnp.mean(middle * middle, axis=-1, keepdims=True) + EPS)
    scaled = gain_ref[...] * incoming
    inner = jnp.mean(middle * scaled, axis=-1, keepdims=True)
    for c in outs:
        c.wait()
    buf[0] = (y_own[...].astype(f32) + rate * scaled - middle * (rate * rate * rate) * inner).astype(bf)
    gather = Gather(buf, ag_send, ag_recv, gx, gy)
    gather.start()
    dgain_ref[...] = jnp.sum((incoming * middle * rate).reshape(rows // 8, 8, feat), axis=0)
    stores = []
    for r in range(8):
        gather.step(r)
        px, py = slot_place(r, gx, gy)
        gstage[r] = nt_dot(buf[r], w[...]).astype(bf)
        stores.append(pltpu.make_async_copy(gstage.at[r], gmix_ref.at[py * 4 + px], gmix_sem.at[r]))
        stores.append(pltpu.make_async_copy(buf.at[r], mid_ref.at[r], mid_sem.at[r]))
        for c in stores[-2:]:
            c.start()
    for c in stores:
        c.wait()
    gather.finish()
    scatter.finish()


def mlp_backward(grads, gate_up, w_out, piece, middle, y_rel, gain, collective):
    rows, feat = middle.shape
    width = piece.shape[0]
    sd = jax.ShapeDtypeStruct
    return pl.pallas_call(
        back_kernel,
        in_specs=[ANY, ANY, ANY, ANY, VM, ANY, VM],
        out_specs=[ANY, ANY, VM],
        out_shape=[sd((8, rows, feat), bf), sd((8, rows, width), bf), sd((8, feat), f32)],
        scratch_shapes=scatter_scratch(rows, feat)
        + [
            pltpu.VMEM(grads.shape, bf),
            pltpu.VMEM(gate_up.shape, bf),
            pltpu.VMEM((width, feat), bf),
            pltpu.VMEM((rows, feat), f32),
            pltpu.VMEM((8, rows, feat), bf),
            pltpu.VMEM((8, rows, width), bf),
            pltpu.VMEM((rows, feat), bf),
            pltpu.SemaphoreType.DMA((4,)),
            pltpu.SemaphoreType.DMA((8,)),
            pltpu.SemaphoreType.DMA((13,)),
            pltpu.SemaphoreType.DMA((13,)),
            pltpu.SemaphoreType.DMA((8,)),
            pltpu.SemaphoreType.DMA((8,)),
        ],
        compiler_params=pltpu.CompilerParams(collective_id=collective, has_side_effects=True, vmem_limit_bytes=63 << 20),
        cost_estimate=lasting(1),
        name="mlp_backward",
    )(grads, gate_up, w_out, piece, middle, y_rel, gain)


def final_kernel(
    draw_ref, hw_ref, hidden_ref, dn_ref, x_ref, mid_ref, middle_ref, other_ref, gain_ref, small_ref,
    gin_ref, lout_ref, all_ref,
    give1, take1, acc1, diag1, last1, sc1, rc1, sl1, rl1,
    give2, take2, acc2, diag2, last2, sc2, rc2, sl2, rl2,
    draw, hw, hidden, dn, x, mid, m_near, total1, total2, row_send, row_recv, z_in, z_sum, z_all,
    load_sem, draw_sem, hidden_sem, x_sem, row_sem, z_send, z_recv, p_send, p_recv,
    *, ndp,
):
    gx, gy, dp = lax.axis_index("gx"), lax.axis_index("gy"), lax.axis_index("dp")
    me = gx * 2 + gy
    rows, feat = middle_ref.shape
    part = feat // 2
    tile = 512
    near = pl.ds(pl.multiple_of(gy * part, part), part)
    xn = slot_peer(2, gx, gy)
    pairs = {0: (0, 2), 2: (0, 2), 1: (1, 4), 4: (1, 4), 3: (3, 6), 6: (3, 6), 5: (5, 7), 7: (5, 7)}
    load_hw = pltpu.make_async_copy(hw_ref, hw, load_sem.at[0])
    load_dn = pltpu.make_async_copy(dn_ref, dn, load_sem.at[1])
    order = (7, 5, 6, 3, 4, 1, 2, 0)
    draws = {}
    for r in order:
        px, py = slot_place(r, gx, gy)
        draws[r] = pltpu.make_async_copy(draw_ref.at[py * 4 + px], draw.at[r], draw_sem.at[r])
    hiddens = {r: pltpu.make_async_copy(hidden_ref.at[r], hidden.at[r], hidden_sem.at[r]) for r in order}
    draws[7].start()
    draws[5].start()
    load_hw.start()
    for r in order[2:]:
        draws[r].start()
    load_dn.start()
    for r in order:
        hiddens[r].start()
    finals = [
        pltpu.make_async_copy(x_ref, x, x_sem.at[0]),
        pltpu.make_async_copy(mid_ref.at[0, :, near], mid.at[gy], x_sem.at[1]),
        pltpu.make_async_copy(mid_ref.at[2, :, near], mid.at[1 - gy], x_sem.at[2]),
    ]
    for c in finals:
        c.start()
    finals.append(pltpu.make_async_copy(middle_ref.at[:, near], m_near, x_sem.at[3]))
    finals[-1].start()
    entry_barrier([slot_peer(r, gx, gy) for r in range(1, 8)] + [{"dp": flipped(dp, n, ndp)} for n in range(1, ndp)])
    around = [
        remote(small_ref, z_in.at[n], z_send.at[n], z_recv.at[n], {"dp": flipped(dp, n, ndp)}) for n in range(1, ndp)
    ]
    for c in around:
        c.start()

    def rows_pair(many, copies, slot, waited):
        for r in pairs[slot]:
            if r not in waited:
                copies[r].wait()
                waited.add(r)
        first, second = pairs[slot]
        low = first + (second - first) * gy
        return low, first + second - low

    def maker(many, copies, weights, weight_load, transposed):
        waited = set()

        def product(slot, put):
            low, high = rows_pair(many, copies, slot, waited)
            if weight_load is not None and "w" not in waited:
                weight_load.wait()
                waited.add("w")
            _, py = slot_place(slot, gx, gy)

            def body(t, _):
                cols = pl.ds(pl.multiple_of(t * tile, tile), tile)
                wide = pl.ds(pl.multiple_of(py * part + t * tile, tile), tile)
                if transposed:
                    w = weights[:, wide]
                    value = [nn_dot(many[low], w), nn_dot(many[high], w)]
                else:
                    w = weights[wide, :]
                    value = [nt_dot(many[low], w), nt_dot(many[high], w)]
                put(cols, jnp.concatenate(value, axis=0))
                return 0

            lax.fori_loop(0, part // tile, body, 0)

        return product

    first = Scatter(give1, take1, acc1, diag1, last1, sc1, rc1, sl1, rl1, gx, gy)
    second = Scatter(give2, take2, acc2, diag2, last2, sc2, rc2, sl2, rl2, gx, gy)
    first.begin(maker(draw, draws, hw, load_hw, False), total1)
    for c in around:
        c.wait_recv()
    summed = small_ref[...]
    for n in range(1, ndp):
        summed = summed + z_in[n]
    z_sum[...] = summed
    passes = [remote(z_sum, z_all.at[me], p_send.at[r], p_recv.at[r], slot_peer(r, gx, gy)) for r in range(1, 8)]
    for c in passes:
        c.start()
    second.begin(maker(hidden, hiddens, dn, load_dn, True), total2, first.forward)
    first.end(total1)
    for c in finals:
        c.wait()
    wide_x = x[...].astype(f32)
    scaled = gain_ref[:, near] * total1[...]
    sums = [jnp.sum(wide_x * wide_x, axis=-1, keepdims=True), jnp.sum(wide_x * scaled, axis=-1, keepdims=True)]
    lane = lax.broadcasted_iota(jnp.int32, (2 * rows, 128), 1)
    packed = jnp.where(lane == 0, sums[0], jnp.where(lane == 1, sums[1], 0.0)).T
    row_send[...] = packed[:8]
    row_copy = remote(row_send, row_recv, row_sem.at[0], row_sem.at[1], xn)
    row_copy.start()
    second.forward()
    second.end(total2)
    mine = pl.ds(pl.multiple_of(gy * rows, rows), rows)
    other = pl.ds(pl.multiple_of((1 - gy) * rows, rows), rows)
    lout_ref[gy] = (total2[mine, :] + m_near[...]).astype(bf)
    lout_ref[1 - gy] = (total2[other, :] + other_ref[...].astype(f32)).astype(bf)
    row_copy.wait_recv()
    both = jnp.concatenate([row_send[...] + row_recv[...], jnp.zeros((120, 2 * rows), f32)], axis=0).T
    rate = lax.rsqrt(both[:, 0:1] / feat + EPS)
    inner = both[:, 1:2] / feat
    gin = mid[...].reshape(2 * rows, part).astype(f32) + rate * scaled - wide_x * (rate * rate * rate) * inner
    gin_ref[...] = gin.astype(bf).reshape(2, rows, part)
    z_all[me] = z_sum[...]
    for c in passes:
        c.wait_recv()
    all_ref[...] = z_all[...]
    for c in around + passes + [row_copy]:
        c.wait_send()
    first.finish()
    second.finish()


def final_sums(draw, head_w, hidden, down, inputs, mid, middle, other, gain, small, ndp, collective):
    rows, feat = middle.shape
    part = feat // 2
    sd = jax.ShapeDtypeStruct
    dma = pltpu.SemaphoreType.DMA
    return pl.pallas_call(
        functools.partial(final_kernel, ndp=ndp),
        in_specs=[ANY] * 7 + [VM] * 3,
        out_specs=[VM] * 3,
        out_shape=[sd((2, rows, part), bf), sd((2, rows, part), bf), sd((8, *small.shape), f32)],
        scratch_shapes=scatter_scratch(2 * rows, part)
        + scatter_scratch(2 * rows, part)
        + [
            pltpu.VMEM(draw.shape, bf),
            pltpu.VMEM(head_w.shape, bf),
            pltpu.VMEM(hidden.shape, bf),
            pltpu.VMEM(down.shape, bf),
            pltpu.VMEM((2 * rows, part), bf),
            pltpu.VMEM((2, rows, part), bf),
            pltpu.VMEM((rows, part), f32),
            pltpu.VMEM((2 * rows, part), f32),
            pltpu.VMEM((2 * rows, part), f32),
            pltpu.VMEM((8, 2 * rows), f32),
            pltpu.VMEM((8, 2 * rows), f32),
            pltpu.VMEM((ndp, *small.shape), f32),
            pltpu.VMEM(small.shape, f32),
            pltpu.VMEM((8, *small.shape), f32),
            dma((2,)),
            dma((8,)),
            dma((8,)),
            dma((4,)),
            dma((2,)),
            dma((ndp,)),
            dma((ndp,)),
            dma((8,)),
            dma((8,)),
        ],
        compiler_params=pltpu.CompilerParams(collective_id=collective, has_side_effects=True, vmem_limit_bytes=63 << 20),
        cost_estimate=lasting(5),
        name="final_sums",
    )(draw, head_w, hidden, down, inputs, mid, middle, other, gain, small)


def dot(a, b):
    return lax.dot_general(a, b, (((1,), (0,)), ((), ())), preferred_element_type=f32)


def dot_t(a, b):
    return lax.dot_general(a, b, (((1,), (1,)), ((), ())), preferred_element_type=f32)


def dot_w(a, b):
    return lax.dot_general(a, b, (((0,), (0,)), ((), ())), preferred_element_type=f32)


def swap(value):
    return lax.ppermute(value, "gy", [(0, 1), (1, 0)])


def in_order(mine, other, axis):
    first = lax.axis_index("gy") == 0
    return jnp.concatenate([jnp.where(first, mine, other), jnp.where(first, other, mine)], axis=axis)


def halves(value, axis):
    size = value.shape[axis] // 2
    mine = lax.axis_index("gy")
    return (
        lax.dynamic_slice_in_dim(value, mine * size, size, axis),
        lax.dynamic_slice_in_dim(value, (1 - mine) * size, size, axis),
    )


def scatter_dp(value):
    return lax.psum_scatter(value.astype(bf), "dp", scatter_dimension=0, tiled=True)


def sort_halves(parts):
    first = lax.axis_index("gy") == 0
    return jnp.where(first, parts[0], parts[1]), swap(jnp.where(first, parts[1], parts[0]))


def shards(
    inputs,
    segments,
    norm_gain,
    w_query,
    w_key,
    w_value,
    w_beta,
    w_gate_head,
    conv_kernel,
    head_gain,
    w_out,
    mlp_gain,
    w_gate,
    w_up,
    w_down,
    grad_y,
):
    ngx, ngy, ndp = lax.axis_size("gx"), lax.axis_size("gy"), lax.axis_size("dp")
    gx, gy = lax.axis_index("gx"), lax.axis_index("gy")
    nb, part_rows, part_feat = inputs.shape
    length, feat = part_rows * ngx, part_feat * ngy
    tokens = nb * length
    own_rows = tokens // (ngx * ngy)
    heads = w_beta.shape[1] // ngy
    width = w_query.shape[1] // ngy
    beta_w = jnp.pad(w_beta.T.reshape(ngy, heads, part_feat), ((0, 0), (0, 128 - heads), (0, 0))).reshape(ngy * 128, part_feat).T
    block = w_gate.shape[1]
    units = -(-block // (ngy * 256)) * 256
    parts = ndp if ndp == 4 else 1
    normed, raw, head_w, x_own, gu_piece, out_piece = head_project(
        inputs.reshape(nb * part_rows, part_feat), w_query, w_key, w_value, w_gate_head, beta_w, w_gate, w_up, w_down, w_out,
        norm_gain[None], units, parts, 5,
    )
    normed = normed.reshape(tokens, feat)
    raw = raw.reshape(nb, length, -1)

    def around(value):
        return [value] + [lax.ppermute(value, "dp", [(i, i ^ n) for i in range(ndp)]) for n in range(1, parts)]

    gu_pieces = around(gu_piece)
    x_own, grad_y, w_down = lax.optimization_barrier((x_own, grad_y, w_down))
    down_piece = swap(lax.dynamic_slice_in_dim(w_down, (1 - gy) * (block - units), units // 2, 0))
    y_all = lax.all_gather(grad_y, ("gx", "gy"), axis=0, tiled=False)

    aux = make_aux(segments)
    conv_start = (gx * ngy + gy) * width
    conv_local = lax.dynamic_slice_in_dim(conv_kernel, conv_start, width, 2)
    gain_row = head_gain[None]
    mixed, *saved = mixer_fwd(raw, aux, conv_local, gain_row)
    middle, second_own, mixed_slots, middle_half = out_project(
        mixed.reshape(8, own_rows, width), w_out, out_piece, x_own, mlp_gain[None], 1
    )
    second, hidden, grads, y_rel, gate_up, down_w = mlp_forward(
        second_own, w_gate, w_up, w_down, y_all, gu_pieces, down_piece, units, 6
    )
    second_flat, hidden_flat = second.reshape(tokens, feat), hidden.reshape(tokens, units)
    grads_flat, y_flat = grads.reshape(tokens, 2 * units), y_rel.reshape(tokens, feat)
    half = feat // 2
    gu_first = dot_w(second_flat[:, :half], grads_flat).astype(bf)
    hidden_flat, gu_first = lax.optimization_barrier((hidden_flat, gu_first))
    down_grad = dot_w(hidden_flat, y_flat).astype(bf)
    down_keep, down_send = halves(down_grad, 1)
    second_flat, down_keep, down_send = lax.optimization_barrier((second_flat, down_keep, down_send))
    down_both = jnp.stack([down_keep, swap(down_send)])
    gu_second = dot_w(second_flat[:, half:], grads_flat).astype(bf)
    grads, gu_second = lax.optimization_barrier((grads, gu_second))
    gu_sums = [scatter_dp(gu_first), scatter_dp(gu_second)]
    first, last = down_both[gy], down_both[1 - gy]
    down_rows = jnp.concatenate([first, last[2 * units - block :]], axis=0)

    mid_slots, grad_mixed, mlp_gain_parts = mlp_backward(
        grads, gate_up, w_out, out_piece, middle, y_rel, mlp_gain[None], 2
    )
    grad_mixed, mid_slots, down_rows, *gu_sums = lax.optimization_barrier((grad_mixed, mid_slots, down_rows, *gu_sums))
    down_sum = scatter_dp(down_rows)
    out_grad = dot_w(mixed_slots.reshape(tokens, width), mid_slots.reshape(tokens, feat)).astype(bf)
    out_keep, out_send = halves(out_grad, 1)
    out_rows = in_order(out_keep, swap(out_send), 0)
    draw, conv_grad, gain_grad = mixer_bwd(
        raw, aux, conv_local, gain_row, saved, grad_mixed.reshape(nb, length, width)
    )
    draw = draw.reshape(tokens, -1)
    gu_pair = sort_halves(gu_sums)
    middle_other = swap(middle_half)
    draw, down_sum, out_rows, middle_other, *gu_pair = lax.optimization_barrier((draw, down_sum, out_rows, middle_other, *gu_pair))
    out_sum = scatter_dp(out_rows)
    main = 4 * width
    both = dot_w(normed, draw).astype(bf)
    norm_gain_grad = jnp.sum(both.astype(f32) * head_w.astype(f32), axis=1) / norm_gain
    beta_grad = both[:, main : main + heads].astype(f32)
    head_grads = both[:, :main].reshape(2, half, main)
    draw, hidden, head_grads = lax.optimization_barrier((draw, hidden, head_grads))
    head_sums = list(lax.psum_scatter(head_grads, "dp", scatter_dimension=1, tiled=True))
    hidden, out_sum = lax.optimization_barrier((hidden, out_sum))
    flat = [beta_grad.T, conv_grad, norm_gain_grad, jnp.sum(mlp_gain_parts, axis=0), gain_grad]
    counts = [v.size // 128 for v in flat]
    small = jnp.concatenate([v.reshape(-1, 128) for v in flat])
    small = jnp.pad(small, ((0, -small.shape[0] % 8), (0, 0)))
    if parts == 1:
        small = lax.psum(small, "dp")
    grad_inputs, layer_out, gathered = final_sums(
        draw.reshape(8, own_rows, -1), head_w, hidden, down_w, inputs.reshape(nb * part_rows, part_feat), mid_slots, middle,
        middle_other, norm_gain[None], small, parts, 3,
    )

    grad_inputs, layer_out, down_sum, out_sum, *gu_pair = lax.optimization_barrier((grad_inputs, layer_out, down_sum, out_sum, *gu_pair))
    sum_down, sum_out = down_sum.astype(f32), out_sum.astype(f32)
    grad_gu_mine, grad_gu_other = gu_pair
    head_mine, head_other = sort_halves(head_sums)

    def unit_columns(i):
        part = slice(i * units, (i + 1) * units)
        both = jnp.stack([grad_gu_mine[:, part], grad_gu_other[:, part]])
        return jnp.concatenate([both[gy], both[1 - gy][:, 2 * units - block :]], axis=1).astype(f32)

    sum_gate, sum_up = unit_columns(0), unit_columns(1)

    def head_part(i, n):
        return in_order(head_mine[:, i : i + n], head_other[:, i : i + n], 1).astype(f32)

    sum_query, sum_key, sum_value, sum_head_gate = (head_part(i * width, width) for i in range(4))

    n_beta, n_conv, n_norm, n_mlp, n_gain = counts
    beta_parts = gathered[:, :n_beta].reshape(8, heads, feat)
    beta_rows = feat // (ngy * ndp)
    beta_pair = lax.dynamic_slice(beta_parts, (gx * ngy, 0, (gy * ndp + lax.axis_index("dp")) * beta_rows), (ngy, heads, beta_rows))
    sum_beta = beta_pair.reshape(ngy * heads, beta_rows).T
    taps = conv_kernel.shape[1]
    conv_sum = gathered[:, n_beta : n_beta + n_conv].reshape(8, 3, taps, width).transpose(1, 2, 0, 3).reshape(conv_kernel.shape)
    rest = jnp.sum(gathered[:, n_beta + n_conv :], axis=0)
    norm_sum = rest[:n_norm].reshape(feat)
    mlp_sum = rest[n_norm : n_norm + n_mlp].reshape(feat)
    gain_sum = rest[n_norm + n_mlp : n_norm + n_mlp + n_gain].reshape(-1)
    return (
        layer_out,
        grad_inputs,
        norm_sum,
        sum_query,
        sum_key,
        sum_value,
        sum_beta,
        sum_head_gate,
        conv_sum,
        gain_sum,
        sum_out,
        mlp_sum,
        sum_gate,
        sum_up,
        sum_down,
    )


def solution(mesh):
    cols = P("gy", "gx")
    rows = P("gx", "gy")
    acts = P("dp", "gx", "gy")
    cols_out = P(("gy", "dp"), "gx")
    rows_out = P(("gx", "dp"), "gy")
    return jax.shard_map(
        shards,
        mesh=mesh,
        in_specs=(acts, P("dp", None), P(), cols, cols, cols, cols, cols, P(), P(), rows, P(), cols, cols, rows, acts),
        out_specs=(
            acts,
            acts,
            P(),
            cols_out,
            cols_out,
            cols_out,
            cols_out,
            cols_out,
            P(),
            P(),
            rows_out,
            P(),
            cols_out,
            cols_out,
            rows_out,
        ),
        check_vma=False,
    )
```
